256 devices in a mesh: px: 8 (over y, core), py: 8 (over z), case: 4 (over x).
Axes of the slice: x: 4, y: 4, z: 8, core: 2. Of those that a mesh axis runs over, the one named last changes fastest.
Arguments:
- comp_type: int32 [8192], P(('px', 'py')), may hold values from 0 to 7
- stiffness: float32 [8192], P(('px', 'py')), may hold values from 0.3 to 3
- near_port: int32 [8192], P(('px', 'py')), may hold values from 0 to 127
- far_owner: int32 [8192, 1], P(('px', 'py')), may hold values from 0 to 63; in each aligned block of 128 rows (0 to 127, 128 to 255, ...) at most 3 rows name the same one
- far_port: int32 [8192], P(('px', 'py')), may hold values from 0 to 127
- bubble_load: float32 [64, 32, 8192], P(None, 'case', ('px', 'py')), may hold values from -6 to 6
- port_load: float32 [48, 32, 8192], P(None, 'case', ('px', 'py')), may hold values from -3 to 3
- bubble_inverse: float32 [8, 64, 64], replicated, may hold values from -1.5 to 2, as said below
- coupling: float32 [8, 96, 64], replicated, may hold values from -0.1 to 0.1
- port_block: float32 [8, 96, 96], replicated, may hold values from -3 to 8, as said below
Outputs:
- port_solution: float32 [48, 32, 8192], P(None, 'case', ('px', 'py'))
- port_residual: float32 [48, 32, 8192], P(None, 'case', ('px', 'py'))
- bubble_solution: float32 [64, 32, 8192], P(None, 'case', ('px', 'py'))
The draws below stay inside these ranges and needn't reach their ends.
Inputs may be any that keep to these rules, and one draw needn't show every extreme that they name: `far_owner`: among the 128 components of one partition, at most 3 name the same owner, a bound that some block reaches. `bubble_inverse`: each matrix is symmetric positive definite. `port_block`: each matrix is symmetric positive definite.
All inputs are finite; a program needn't handle non-finite values.
Results may differ from the reference program's by a relative error of at most 0.00016.
Values sent between devices are 32-bit elements; how exact they have to be, the bound alone decides.
No kernel may reach another device: no remote copies, remote signals or barrier semaphores. Data moves between devices by JAX's collectives and lax.ppermute only.
A program may use at most 64 MiB of HBM per device.

```python
import math
import jax
import jax.numpy as jnp
import numpy as np
from jax import lax

MODES = 64
PD = 48
TYPES = 8
ITERS = 2
COMP_DEV = 128
NPART = 64
PORT_DEV = 128
CAP = 3
COMPONENTS = 8192
PORTS = 8192
CASES = 32
N_PX = 8
N_PY = 8


def draw_bubble_inverse(key, part):
    base = jax.random.uniform(key, (TYPES, MODES, MODES), jnp.float32, -1.7, 1.7)
    square = jnp.einsum('tij,tkj->tik', base, base) / MODES
    return 0.5 * jnp.eye(MODES, dtype=jnp.float32)[None, :, :] + 0.5 * square


def draw_port_block(key, part):
    size_ports = 2 * PD
    base = jax.random.uniform(key, (TYPES, size_ports, size_ports), jnp.float32, -1.7, 1.7)
    square = jnp.einsum('tij,tkj->tik', base, base) / size_ports
    return 5.0 * jnp.eye(size_ports, dtype=jnp.float32)[None, :, :] + square


def place_ends(array, stream_key, low, largest):
    spot = [jax.random.randint(jax.random.fold_in(stream_key, axis), (), 0, length) for axis, length in enumerate(array.shape)]
    widest = array.shape.index(max(array.shape))
    neighbour = spot[:widest] + [(spot[widest] + 1) % array.shape[widest]] + spot[widest + 1:]
    return array.at[tuple(spot)].set(low).at[tuple(neighbour)].set(largest)


def shard_levels(rng, extent, pieces, least, largest):
    loudness, own = 1.0, jax.random.fold_in(rng, 6)
    for position, parts in pieces:
        draws = jnp.exp(jax.random.uniform(jax.random.fold_in(own, position), (parts,), jnp.float32, least / len(pieces), largest / len(pieces)))
        loudness = loudness * jnp.repeat(draws, extent[position] // parts).reshape([-1 if axis == position else 1 for axis in range(len(extent))])
    return loudness


def assign_block(rng, own, number, rows, count, top, most, lean):
    sequence = jax.random.permutation(rng, count)
    crowded, common = shares(count, rows * top, most, lean, True), shares(count, rows * top, most, lean, False)
    places = jnp.arange(count)

    def named(sizes, rotation):
        used = int((sizes > 0).sum())
        fixed = max(1, used // 4)
        moved = fixed + (places - fixed + rotation * (used - fixed)) % max(1, count - fixed)
        return jnp.zeros((count,), jnp.int32).at[sequence[jnp.where(places < fixed, places, moved)]].set(jnp.asarray(sizes, jnp.int32))

    sizes = jnp.where(number % 4 == 0, named(crowded, number // 4), named(common, number - number // 4 - 1))
    mixed = jax.random.permutation(jax.random.fold_in(own, 3), count)
    source_of, taker = mixed[0:count // 2 * 2:2], mixed[1:count // 2 * 2:2]
    slack = jnp.minimum(sizes[source_of] - 1, most - sizes[taker]) // 2
    slack = jnp.where((source_of == sequence[0]) | (taker == sequence[0]) | (sizes[taker] == 0), 0, jnp.maximum(slack, 0))
    moved = jax.random.randint(jax.random.fold_in(own, 4), (count // 2,), 0, 1 << 20) % (slack + 1)
    sizes = sizes.at[source_of].add(-moved).at[taker].add(moved)
    labels = jnp.searchsorted(jnp.cumsum(sizes), jnp.arange(rows * top), side="right").astype(jnp.int32)
    table = labels.reshape(top, rows).T
    table = table[jax.random.permutation(jax.random.fold_in(own, 1), rows)]
    rotation = jax.random.randint(jax.random.fold_in(own, 2), (rows, 1), 0, top)
    return jnp.take_along_axis(table, (jnp.arange(top)[None, :] + rotation) % top, axis=1)


def shares(number_of, total, reach, skew, full):
    weights = [(1 << 20) // math.isqrt(standing ** skew) + 1 for standing in range(1, number_of + 1)]
    largest = reach if full else min(reach, max(-(-total // number_of), total * weights[0] // sum(weights)))
    least = 1 if total - largest >= number_of - 1 else 0
    counts, surplus = [largest] + [least] * (number_of - 1), total - largest - least * (number_of - 1)
    while surplus > 0:
        free = [i for i in range(1, number_of) if counts[i] < largest] or [i for i in range(1, number_of) if counts[i] < reach]
        pool, remaining = sum([weights[i] for i in free]), surplus
        for i in free:
            extra = min(reach - counts[i], max(1, remaining * weights[i] // pool), surplus)
            counts[i] = counts[i] + extra
            surplus = surplus - extra
    return np.array(counts)


def normal_values(key, dims, spread, most, pieces=(), kind=jnp.bfloat16):
    values = spread * jax.random.normal(key, dims, jnp.float32)
    if pieces:
        values = values * shard_levels(key, dims, pieces, -0.22, 0.18)
    return jnp.clip(values, -most, most).astype(kind)


def setup_inputs(seed: int = 0) -> dict:
    key_of = jax.random.split(jax.random.key(seed), 11)
    comp_type = place_ends(jax.random.randint(key_of[0], (COMPONENTS,), 0, TYPES), jax.random.fold_in(key_of[0], 1), 0, TYPES - 1).astype(jnp.int32)
    stiffness = jnp.clip(jnp.exp(math.log(3.0) - 2.3025851 * jax.random.uniform(key_of[1], (COMPONENTS,), jnp.float32) ** shard_levels(key_of[1], (COMPONENTS,), ((0, 64),), -0.2, 0.2)), 0.3, 3.0)
    near_port = place_ends(jax.random.randint(key_of[2], (COMPONENTS,), 0, PORT_DEV), jax.random.fold_in(key_of[2], 1), 0, PORT_DEV - 1).astype(jnp.int32)
    far_owner_keys = jax.random.split(jax.random.fold_in(key_of[3], 1), COMPONENTS // COMP_DEV)
    far_owner_turns = jax.random.permutation(jax.random.fold_in(key_of[3], 3), COMPONENTS // COMP_DEV)
    far_owner = jax.vmap(lambda own, number: assign_block(jax.random.fold_in(key_of[3], 2), own, number, COMP_DEV, NPART, 1, CAP, 2))(far_owner_keys, far_owner_turns).reshape((COMPONENTS, 1))
    far_port = place_ends(jax.random.randint(key_of[4], (COMPONENTS,), 0, PORT_DEV), jax.random.fold_in(key_of[4], 1), 0, PORT_DEV - 1).astype(jnp.int32)
    bubble_load = normal_values(key_of[5], (MODES, CASES, COMPONENTS), 1.0, 6.0, ((1, 4), (2, 64)), jnp.float32)
    port_load = normal_values(key_of[6], (PD, CASES, PORTS), 0.5, 3.0, ((1, 4), (2, 64)), jnp.float32)
    bubble_inverse = draw_bubble_inverse(jax.random.fold_in(key_of[10], 71), 0)
    coupling = jnp.clip(jax.random.uniform(key_of[8], (TYPES, 2 * PD, MODES), jnp.float32, -0.1, 0.1), -0.1, 0.1)
    port_block = draw_port_block(jax.random.fold_in(key_of[10], 71), 0)
    return {"comp_type": comp_type, "stiffness": stiffness, "near_port": near_port, "far_owner": far_owner, "far_port": far_port, "bubble_load": bubble_load, "port_load": port_load, "bubble_inverse": bubble_inverse, "coupling": coupling, "port_block": port_block}


HIGH = lax.Precision.HIGHEST

def type_tables(bubble_inverse, coupling, port_block):
    reduced = jnp.einsum('tpm,tmn->tpn', coupling, bubble_inverse, precision=HIGH)
    schur_table = port_block - jnp.einsum('tpm,tqm->tpq', reduced, coupling, precision=HIGH)
    return (reduced, schur_table)

def apply_tables(table, comp_type, factor, vectors):
    in_rows = vectors.shape[0]
    case_count = vectors.shape[1]
    part_count = N_PX * N_PY
    vector_blocks = vectors.reshape(in_rows, case_count, part_count, COMP_DEV).transpose(2, 0, 1, 3)
    kind_blocks = comp_type.reshape(part_count, COMP_DEV)
    factor_blocks = factor.reshape(part_count, COMP_DEV)

    def one_block(packed):
        vector_part, kind_part, factor_part = packed
        matrices = jnp.take(table, kind_part, axis=0)
        result = jnp.einsum('cyx,xkc->ykc', matrices, vector_part, precision=HIGH)
        return result * factor_part[None, None, :]
    results = lax.map(one_block, (vector_blocks, kind_blocks, factor_blocks))
    return results.transpose(1, 2, 0, 3).reshape(results.shape[1], case_count, part_count * COMP_DEV)

def port_indices(near_port, far_owner, far_port):
    owners = jnp.arange(COMPONENTS, dtype=jnp.int32) // COMP_DEV
    return (owners * PORT_DEV + near_port, far_owner[:, 0] * PORT_DEV + far_port)

def spread_ports(port_field, near_global, far_global):
    return jnp.concatenate([jnp.take(port_field, near_global, axis=2), jnp.take(port_field, far_global, axis=2)], axis=0)

def assemble(values, near_global, far_global):
    near_sum = jax.ops.segment_sum(jnp.moveaxis(values[:PD], 2, 0), near_global, num_segments=PORTS)
    far_sum = jax.ops.segment_sum(jnp.moveaxis(values[PD:], 2, 0), far_global, num_segments=PORTS)
    return jnp.moveaxis(near_sum + far_sum, 0, 2)

def port_gram(lhs_field, rhs_field):
    product = jnp.einsum('dkp,djp->kj', lhs_field, rhs_field, precision=HIGH)
    return 0.5 * (product + product.T)

def combine_columns(port_field, weights):
    return jnp.einsum('djp,jk->dkp', port_field, weights, precision=HIGH)

def spd_solve(matrix, target):
    factor = jnp.linalg.cholesky(matrix)
    middle = lax.linalg.triangular_solve(factor, target, left_side=True, lower=True)
    return lax.linalg.triangular_solve(factor, middle, left_side=True, lower=True, transpose_a=True)

def reference(comp_type, stiffness, near_port, far_owner, far_port, bubble_load, port_load, bubble_inverse, coupling, port_block):
    reduced, schur_table = type_tables(bubble_inverse, coupling, port_block)
    near_global, far_global = port_indices(near_port, far_owner, far_port)
    unit_scale = jnp.ones_like(stiffness)
    condensed = -apply_tables(reduced, comp_type, unit_scale, bubble_load)
    rhs_field = port_load + assemble(condensed, near_global, far_global)

    def operate(port_field):
        local_field = spread_ports(port_field, near_global, far_global)
        return assemble(apply_tables(schur_table, comp_type, stiffness, local_field), near_global, far_global)
    solution = jnp.zeros_like(rhs_field)
    residual = rhs_field
    direction = rhs_field
    residual_gram = port_gram(residual, residual)
    for iteration in range(ITERS):
        image_field = operate(direction)
        curvature = port_gram(direction, image_field)
        step_coef = spd_solve(curvature, residual_gram)
        solution = solution + combine_columns(direction, step_coef)
        residual = residual - combine_columns(image_field, step_coef)
        if iteration + 1 < ITERS:
            next_gram = port_gram(residual, residual)
            update_coef = spd_solve(residual_gram, next_gram)
            direction = residual + combine_columns(direction, update_coef)
            residual_gram = next_gram
    port_values = spread_ports(solution, near_global, far_global)
    transposed = jnp.transpose(reduced, (0, 2, 1))
    bubble_solution = apply_tables(bubble_inverse, comp_type, 1.0 / stiffness, bubble_load) - apply_tables(transposed, comp_type, unit_scale, port_values)
    return (solution, residual, bubble_solution)
```

```python
import functools

import jax
import jax.numpy as jnp
from jax import lax
from jax.experimental import pallas as pl
from jax.experimental.pallas import tpu as pltpu
from jax.sharding import PartitionSpec as P

HIGH = lax.Precision.HIGHEST
PLANE = ("px", "py")
F32 = jnp.float32
BF16 = jnp.bfloat16
KINDS = 8
LANES = 128
CASES = 8
SLOTS = 3
NN = (((1,), (0,)), ((), ()))
NT = (((1,), (1,)), ((), ()))
TN = (((0,), (0,)), ((), ()))


def dot(lhs, rhs, dims=NN):
    return lax.dot_general(lhs, rhs, dims, preferred_element_type=F32)


def dot_high(lhs, rhs, dims=NN):
    return lax.dot_general(lhs, rhs, dims, precision=HIGH, preferred_element_type=F32)


def split2(x):
    high = x.astype(BF16)
    return high, (x - high.astype(F32)).astype(BF16)


def split3(x):
    high = x.astype(BF16)
    rest = x - high.astype(F32)
    middle = rest.astype(BF16)
    return high, middle, (rest - middle.astype(F32)).astype(BF16)


def pick_left(onehot, x, dims):
    a, b, c = split3(x)
    return dot(onehot, a, dims) + dot(onehot, b, dims) + dot(onehot, c, dims)


def pick_right(x, onehot, dims):
    a, b, c = split3(x)
    return dot(a, onehot, dims) + dot(b, onehot, dims) + dot(c, onehot, dims)


def iota(shape, dim):
    return lax.broadcasted_iota(jnp.int32, shape, dim)


def column(row):
    return jnp.transpose(jnp.broadcast_to(row, (8, row.shape[1])))[:, :1]


def onehot(mask):
    return mask.astype(F32).astype(BF16)


def owner_slots(owner, parts):
    count = owner.shape[1]
    owner_f = owner.astype(F32)
    same = (column(owner_f) == owner_f) & (iota((count, count), 0) < iota((count, count), 1))
    rank = jnp.sum(same.astype(F32), axis=0, keepdims=True).astype(jnp.int32)
    to = iota((parts, count), 0) == owner
    return [to & (rank == s) for s in range(SLOTS)]


def near_onehot(near):
    count = near.shape[1]
    return onehot(column(near.astype(F32)) == iota((count, LANES), 1).astype(F32))


def stacked_rows(meta, lanes):
    turned = jnp.transpose(meta)
    return jnp.concatenate([turned[lanes + s : lanes + s + 1, :] for s in range(SLOTS)], axis=1)


def port_onehot(meta):
    parts = meta.shape[0]
    ports = (iota((parts, LANES), 1) + 1).astype(F32)
    return onehot(jnp.concatenate([meta[:, s : s + 1] == ports for s in range(SLOTS)], axis=0))


def pad_lanes(x, spare):
    if not spare:
        return x
    return jnp.concatenate([x, jnp.zeros((x.shape[0], spare), x.dtype)], axis=1)


def put(pay_ref, rows, first, pitch):
    parts = pay_ref.shape[0] // pitch
    tiles = rows.shape[1] // LANES
    for g in range(rows.shape[0] // parts):
        for t in range(tiles):
            pay_ref[pl.ds(first + g * tiles + t, parts, stride=pitch), :] = rows[
                g * parts : (g + 1) * parts, t * LANES : (t + 1) * LANES
            ]


def get(pay_ref, first, pitch, tiles):
    parts = pay_ref.shape[0] // pitch
    return jnp.concatenate(
        [
            jnp.concatenate(
                [pay_ref[pl.ds(first + s * tiles + t, parts, stride=pitch), :] for t in range(tiles)],
                axis=1,
            )
            for s in range(SLOTS)
        ],
        axis=0,
    )


def by_kind(products, kind, rows):
    chosen = products[:rows]
    for t in range(1, KINDS):
        chosen = jnp.where(kind == t, products[t * rows : (t + 1) * rows], chosen)
    return chosen


def table_product(high, low, x):
    a, b = split2(x)
    return dot(high, a) + (dot(high, b) + dot(low, a))


def condense_kernel(
    parts, kind_ref, stiff_ref, near_ref, owner_ref, far_ref, load_ref, inverse_ref, coupling_ref,
    pay_ref, near_sum_ref, meta_ref, near_part, far_part,
):
    modes = load_ref.shape[0] // CASES
    dofs = near_sum_ref.shape[0] // CASES
    table = jnp.concatenate(
        [dot_high(coupling_ref[t], inverse_ref[t]) for t in range(KINDS)], axis=0
    )
    high, low = split2(table)
    left = jnp.concatenate([high, high, low], axis=1)
    kind = kind_ref[...]
    kind2 = jnp.concatenate([kind, kind], axis=1)
    for k in range(0, CASES, 2):
        loads = jnp.concatenate(
            [load_ref[pl.ds(k + i, modes, stride=CASES), :] for i in range(2)], axis=1
        )
        a, b = split2(loads)
        condensed = -by_kind(dot(left, jnp.concatenate([a, b, a], axis=0)), kind2, 2 * dofs)
        for i in range(2):
            lanes = slice(i * LANES, (i + 1) * LANES)
            near_part[pl.ds(k + i, dofs, stride=CASES), :] = condensed[:dofs, lanes]
            far_part[pl.ds(k + i, dofs, stride=CASES), :] = condensed[dofs:, lanes]
    near = near_ref[...]
    slots = owner_slots(owner_ref[...], parts)
    near_sum_ref[...] = pick_right(near_part[...], near_onehot(near), NN)
    chosen = onehot(jnp.concatenate(slots, axis=0))
    put(pay_ref, pick_left(chosen, far_part[...], NT), 0, 10)
    lane = iota((parts, LANES), 1)
    far_row = (far_ref[...] + 1).astype(F32)
    near_row = (near + 1).astype(F32)
    message = jnp.zeros((parts, LANES), F32)
    own = jnp.zeros((parts, LANES), F32)
    for s in range(SLOTS):
        for at, row in ((0, far_row), (SLOTS, kind.astype(F32)), (2 * SLOTS, stiff_ref[...])):
            value = jnp.sum(jnp.where(slots[s], row, 0.0), axis=1, keepdims=True)
            message = jnp.where(lane == at + s, value, message)
        value = jnp.sum(jnp.where(slots[s], near_row, 0.0), axis=1, keepdims=True)
        own = jnp.where(lane == s, value, own)
    pay_ref[pl.ds(9, parts, stride=10), :] = message
    meta_ref[...] = own


def tables_kernel(
    kind_ref, stiff_ref, load_ref, inverse_ref, coupling_ref, block_ref,
    near_high, near_low, far_high, far_low, turned_high, turned_low, base_ref,
):
    dofs = block_ref.shape[1] // 2
    modes = inverse_ref.shape[1]
    inverses = []
    for t in range(KINDS):
        reduced = dot_high(coupling_ref[t], inverse_ref[t])
        schur = block_ref[t] - dot_high(reduced, coupling_ref[t], NT)
        near_high[t * dofs : (t + 1) * dofs, :], near_low[t * dofs : (t + 1) * dofs, :] = split2(schur[:dofs])
        far_high[t * dofs : (t + 1) * dofs, :], far_low[t * dofs : (t + 1) * dofs, :] = split2(schur[dofs:])
        turned = jnp.transpose(reduced)
        turned_high[t * modes : (t + 1) * modes, :], turned_low[t * modes : (t + 1) * modes, :] = split2(turned)
        inverses.append(inverse_ref[t])
    high, low = split2(jnp.concatenate(inverses, axis=0))
    kind = kind_ref[...]
    stiff = stiff_ref[...]
    for k in range(CASES):
        loads = load_ref[pl.ds(k, modes, stride=CASES), :]
        base_ref[pl.ds(k, modes, stride=CASES), :] = by_kind(table_product(high, low, loads), kind, modes) / stiff


def send_ports(field, asked, own, pay_ref):
    put(pay_ref, pick_left(jnp.concatenate([asked, own], axis=0), field, NT), 0, 18)


def rhs_kernel(parts, arrived_ref, near_sum_ref, load_ref, meta_ref, field_ref, pay_ref, asked_ref):
    asked = arrived_ref[pl.ds(9, parts, stride=10), :]
    asked_ref[...] = asked
    asked_hot = port_onehot(asked)
    arrived = get(arrived_ref, 0, 10, 3)
    field = load_ref[...] + (near_sum_ref[...] + pick_right(arrived, asked_hot, TN))
    field_ref[...] = field
    send_ports(field, asked_hot, port_onehot(meta_ref[...]), pay_ref)


def apply_kernel(
    parts, last, arrived_ref, field_ref, meta_ref, asked_ref, kind_ref, stiff_ref, near_ref, owner_ref,
    near_high, near_low, far_high, far_low, *rest,
):
    if last:
        image_ref, spread_ref, slot_ref, near_part, far_part = rest
    else:
        image_ref, spread_ref, pay_ref, slot_ref, near_part, far_part = rest
    rows = field_ref.shape[0]
    dofs = rows // CASES
    field = field_ref[...]
    asked = asked_ref[...]
    asked_hot = port_onehot(asked)
    near_hot = near_onehot(near_ref[...])
    slots = onehot(jnp.concatenate(owner_slots(owner_ref[...], parts), axis=0))
    spread_ref[:rows, :] = pick_right(field, near_hot, NT)
    spread_ref[rows:, :] = pick_right(get(arrived_ref, 0, 18, 3), slots, TN)
    groups = slot_ref.shape[0]
    spare = groups * LANES - SLOTS * parts
    wide_hot = asked_hot
    if spare:
        wide_hot = jnp.concatenate([asked_hot, jnp.zeros((spare, LANES), BF16)], axis=0)
    from_near = pad_lanes(jnp.transpose(get(arrived_ref, 9, 18, 3)), spare)
    from_far = pick_right(field, wide_hot, NT)
    for g in range(groups):
        lanes = slice(g * LANES, (g + 1) * LANES)
        slot_ref[g, :rows, :] = from_near[:, lanes]
        slot_ref[g, rows:, :] = from_far[:, lanes]
    kind = kind_ref[...]
    stiff = stiff_ref[...]
    kind2 = jnp.concatenate([kind, kind], axis=1)
    stiff2 = jnp.concatenate([stiff, stiff], axis=1)
    asked_kind = pad_lanes(stacked_rows(asked, SLOTS), spare).astype(jnp.int32)
    asked_stiff = pad_lanes(stacked_rows(asked, 2 * SLOTS), spare)
    for k in range(0, CASES, 2):
        values = jnp.concatenate(
            [spread_ref[pl.ds(k + i, 2 * dofs, stride=CASES), :] for i in range(2)], axis=1
        )
        result = by_kind(table_product(near_high[...], near_low[...], values), kind2, dofs) * stiff2
        for i in range(2):
            near_part[pl.ds(k + i, dofs, stride=CASES), :] = result[:, i * LANES : (i + 1) * LANES]
    for k in range(CASES):
        values = jnp.concatenate(
            [slot_ref[g, pl.ds(k, 2 * dofs, stride=CASES), :] for g in range(groups)], axis=1
        )
        result = by_kind(table_product(far_high[...], far_low[...], values), asked_kind, dofs) * asked_stiff
        for g in range(groups):
            far_part[g, pl.ds(k, dofs, stride=CASES), :] = result[:, g * LANES : (g + 1) * LANES]
    image = pick_right(near_part[...], near_hot, NN)
    for g in range(groups):
        image = image + pick_right(far_part[g], wide_hot[g * LANES : (g + 1) * LANES], NN)
    image_ref[...] = image
    if not last:
        send_ports(image, asked_hot, port_onehot(meta_ref[...]), pay_ref)


def turned_kernel(spread_ref, kind_ref, high_ref, low_ref, out_ref):
    dofs2 = spread_ref.shape[0] // CASES
    modes = out_ref.shape[0] // CASES
    kind = kind_ref[...]
    kind2 = jnp.concatenate([kind, kind], axis=1)
    for k in range(0, CASES, 2):
        values = jnp.concatenate(
            [spread_ref[pl.ds(k + i, dofs2, stride=CASES), :] for i in range(2)], axis=1
        )
        result = by_kind(table_product(high_ref[...], low_ref[...], values), kind2, modes)
        for i in range(2):
            out_ref[pl.ds(k + i, modes, stride=CASES), :] = result[:, i * LANES : (i + 1) * LANES]


def gram_kernel(base_all, image_all, base_ref, image_ref, second_ref, out_ref):
    groups, dofs = base_all.shape[:2]
    total = groups * CASES
    lane = iota((CASES, LANES), 1)
    out = jnp.zeros((CASES, LANES), F32)
    for j0 in range(0, total, 8):
        def step(d, sums):
            own = pl.ds(pl.multiple_of(d * CASES, CASES), CASES)
            base, image, second = base_ref[own, :], image_ref[own, :], second_ref[own, :]
            new = []
            for j in range(8):
                q, i = divmod(j0 + j, CASES)
                bj = base_all[q, d, i : i + 1, :]
                aj = image_all[q, d, i : i + 1, :]
                s = sums[j]
                new.append((s[0] + bj * base, s[1] + bj * image, s[2] + aj * image, s[3] + aj * second))
            return tuple(new)

        zero = jnp.zeros((CASES, LANES), F32)
        sums = lax.fori_loop(0, dofs, step, tuple((zero,) * 4 for _ in range(8)))
        for j in range(8):
            for g in range(4):
                value = jnp.sum(sums[j][g], axis=1, keepdims=True)
                out = jnp.where(lane == g * total + j0 + j, value, out)
    for p in range(out_ref.shape[0]):
        out_ref[p] = out


def sum_kernel(in_ref, out_ref):
    total = in_ref[0]
    for p in range(1, in_ref.shape[0]):
        total = total + in_ref[p]
    for p in range(out_ref.shape[0]):
        out_ref[p] = total


def spd_solve(pairs):
    n = pairs[0][0].shape[0]
    row_of = iota((n, 2 * n), 0)
    work = [jnp.concatenate(pair, axis=1) for pair in pairs]
    for k in range(n):
        nxt = []
        for a in work:
            pivot = a[k : k + 1, :] / a[k : k + 1, k : k + 1]
            nxt.append(jnp.where(row_of == k, pivot, a - a[:, k : k + 1] * pivot))
        work = nxt
    return [a[:, n:] for a in work]


def symmetric(m):
    return 0.5 * (m + jnp.transpose(m))


def finish_kernel(
    case_ref, gram_ref, base_all, image_all, second_all, turned0_all, turned1_all, base_ref, bubble_ref,
    x_ref, residual_ref, bubble_out, turned_coef, coef,
):
    groups, dofs = base_all.shape[:2]
    modes = turned0_all.shape[1]
    n = groups * CASES
    rows = jnp.concatenate([gram_ref[q] for q in range(groups)], axis=0)
    g00, g01, g11, g12 = [symmetric(rows[:, g * n : (g + 1) * n]) for g in range(4)]
    eye = (iota((n, n), 0) == iota((n, n), 1)).astype(F32)
    step0, inverse00 = spd_solve([(g01, g00), (g00, eye)])
    step0_t = jnp.transpose(step0)
    gram1 = g00 - dot_high(g01, step0)
    gram1 = gram1 + jnp.transpose(dot_high(dot_high(g11, step0) - g01, step0, TN))
    gram1 = symmetric(gram1)
    update = eye + dot_high(inverse00, gram1)
    update_t = jnp.transpose(update)
    left = dot_high(update_t, g01) - dot_high(step0_t, g11)
    right = dot_high(update_t, g11) - dot_high(step0_t, g12)
    curvature = symmetric(dot_high(left, update) - dot_high(right, step0))
    (step1,) = spd_solve([(curvature, gram1)])
    first = step0 + dot_high(update, step1)
    second = -dot_high(step0, step1)
    turned_coef[:n, :n] = jnp.transpose(first)
    turned_coef[n:, :n] = jnp.transpose(second)
    at = pl.multiple_of(case_ref[0] * CASES, CASES)
    for h in range(2):
        mine = turned_coef[pl.ds(h * n + at, CASES), :]
        for j in range(n):
            coef[h * n + j] = jnp.broadcast_to(mine[:, j : j + 1], (CASES, LANES))

    def ports(block, carry):
        d0 = block * 4
        for i in range(4):
            d = d0 + i
            own = pl.ds(pl.multiple_of(d * CASES, CASES), CASES)
            x = jnp.zeros((CASES, LANES), F32)
            r = base_ref[own, :]
            for j in range(n):
                q, c = divmod(j, CASES)
                a = image_all[q, d, c : c + 1, :]
                c0, c1 = coef[j], coef[n + j]
                x = x + (c0 * base_all[q, d, c : c + 1, :] + c1 * a)
                r = r - (c0 * a + c1 * second_all[q, d, c : c + 1, :])
            x_ref[own, :] = x
            residual_ref[own, :] = r
        return carry

    lax.fori_loop(0, dofs // 4, ports, 0)

    def bubbles(block, carry):
        for i in range(4):
            d = block * 4 + i
            own = pl.ds(pl.multiple_of(d * CASES, CASES), CASES)
            w = bubble_ref[own, :]
            for j in range(n):
                q, c = divmod(j, CASES)
                w = w - (coef[j] * turned0_all[q, d, c : c + 1, :] + coef[n + j] * turned1_all[q, d, c : c + 1, :])
            bubble_out[own, :] = w
        return carry

    lax.fori_loop(0, modes // 4, bubbles, 0)


def call(kernel, outs, scratch=(), name=None, flops=0, smem=0):
    outs = [jax.ShapeDtypeStruct(shape, dtype) for shape, dtype in outs]
    vmem = pl.BlockSpec(memory_space=pltpu.VMEM)

    def run(*args):
        specs = [pl.BlockSpec(memory_space=pltpu.SMEM)] * smem + [vmem] * (len(args) - smem)
        moved = sum(a.size * a.dtype.itemsize for a in args) + sum(o.size * o.dtype.itemsize for o in outs)
        return pl.pallas_call(
            kernel,
            out_shape=outs,
            in_specs=specs,
            out_specs=[vmem] * len(outs),
            scratch_shapes=[pltpu.VMEM(shape, F32) for shape in scratch],
            compiler_params=pltpu.CompilerParams(vmem_limit_bytes=40 << 20),
            cost_estimate=pl.CostEstimate(flops=flops, bytes_accessed=moved, transcendentals=0),
            name=name,
        )(*args)

    return run


def exchange(rows, parts):
    moved = lax.all_to_all(rows.reshape(parts, 1, -1), PLANE, split_axis=0, concat_axis=0)
    return moved.reshape(rows.shape)


def local(
    comp_type, stiffness, near_port, far_owner, far_port, bubble_load, port_load,
    bubble_inverse, coupling, port_block,
):
    parts = lax.axis_size("px") * lax.axis_size("py")
    groups = lax.axis_size("case")
    modes, cases, comps = bubble_load.shape
    dofs, _, ports = port_load.shape
    rows, bubbles = dofs * cases, modes * cases
    slot_tiles = -(-SLOTS * parts // LANES)
    kind = comp_type.reshape(1, comps)
    stiff = stiffness.reshape(1, comps)
    near = near_port.reshape(1, comps)
    owner = far_owner.reshape(1, comps)
    far = far_port.reshape(1, comps)
    loads = bubble_load.reshape(bubbles, comps)
    field_of = ((rows, ports), F32)
    meta_of = ((parts, LANES), F32)
    pay, near_sum, meta = call(
        functools.partial(condense_kernel, parts),
        [((parts * 10, LANES), F32), field_of, meta_of],
        [(rows, comps)] * 2,
        "condense",
    )(kind, stiff, near, owner, far, loads, bubble_inverse, coupling)
    tables = call(
        tables_kernel,
        [((KINDS * dofs, 2 * dofs), BF16)] * 4 + [((KINDS * modes, 2 * dofs), BF16)] * 2 + [((bubbles, comps), F32)],
        name="tables",
        flops=10**9,
    )(kind, stiff, loads, bubble_inverse, coupling, port_block)
    schur, turned_tables, bubble_base = tables[:4], tables[4:6], tables[6]
    base, pay, asked = call(
        functools.partial(rhs_kernel, parts),
        [field_of, ((parts * 18, LANES), F32), meta_of],
        name="rhs",
    )(exchange(pay, parts), near_sum, port_load.reshape(rows, ports), meta)

    def operator(field, pay, last):
        spread_of = ((2 * rows, comps), F32)
        return call(
            functools.partial(apply_kernel, parts, last),
            [field_of, spread_of] + ([] if last else [((parts * 18, LANES), F32)]),
            [(slot_tiles, 2 * rows, LANES), (rows, comps), (slot_tiles, rows, LANES)],
            "apply",
        )(exchange(pay, parts), field, meta, asked, kind, stiff, near, owner, *schur)

    def turned(spread):
        return call(turned_kernel, [((bubbles, comps), F32)], name="turned", flops=10**9)(
            spread, kind, *turned_tables
        )[0]

    def all_cases(field):
        return lax.all_gather(field.reshape(-1, cases, LANES), "case")

    base_all = all_cases(base)
    image, spread, pay = operator(base, pay, False)
    image_all = all_cases(image)
    turned0_all = all_cases(turned(spread))
    second, spread = operator(image, pay, True)
    second_all = all_cases(second)
    turned1_all = all_cases(turned(spread))
    (copies,) = call(gram_kernel, [((parts, cases, LANES), F32)], name="gram")(
        base_all, image_all, base, image, second
    )
    (copies,) = call(sum_kernel, [((groups, cases, LANES), F32)], name="sum")(
        lax.all_to_all(copies, PLANE, split_axis=0, concat_axis=0)
    )
    gram = lax.all_to_all(copies, "case", split_axis=0, concat_axis=0)
    x, residual, bubble = call(
        finish_kernel,
        [field_of, field_of, ((bubbles, comps), F32)],
        [(2 * groups * cases, LANES), (2 * groups * cases, cases, LANES)],
        "finish",
        smem=1,
    )(
        lax.axis_index("case").reshape(1), gram, base_all, image_all, second_all,
        turned0_all, turned1_all, base, bubble_base,
    )
    return (
        x.reshape(port_load.shape),
        residual.reshape(port_load.shape),
        bubble.reshape(bubble_load.shape),
    )


def solution(mesh):
    placed = (
        P(PLANE),
        P(PLANE),
        P(PLANE),
        P(PLANE, None),
        P(PLANE),
        P(None, "case", PLANE),
        P(None, "case", PLANE),
        P(),
        P(),
        P(),
    )
    out = P(None, "case", PLANE)
    return jax.shard_map(
        local, mesh=mesh, in_specs=placed, out_specs=(out, out, out), check_vma=False
    )
```

```python
import functools

import jax
import jax.numpy as jnp
from jax import lax
from jax.experimental import pallas as pl
from jax.experimental.pallas import tpu as pltpu
from jax.sharding import PartitionSpec as P

HIGH = lax.Precision.HIGHEST
PLANE = ("px", "py")
F32 = jnp.float32
BF16 = jnp.bfloat16
KINDS = 8
LANES = 128
CASES = 8
SLOTS = 3
NN = (((1,), (0,)), ((), ()))
NT = (((1,), (1,)), ((), ()))
TN = (((0,), (0,)), ((), ()))


def dot(lhs, rhs, dims=NN):
    return lax.dot_general(lhs, rhs, dims, preferred_element_type=F32)


def dot_high(lhs, rhs, dims=NN):
    return lax.dot_general(lhs, rhs, dims, precision=HIGH, preferred_element_type=F32)


def split2(x):
    high = x.astype(BF16)
    return high, (x - high.astype(F32)).astype(BF16)


def split3(x):
    high = x.astype(BF16)
    rest = x - high.astype(F32)
    middle = rest.astype(BF16)
    return high, middle, (rest - middle.astype(F32)).astype(BF16)


def pick_left(onehot, x, dims):
    a, b, c = split3(x)
    return dot(onehot, a, dims) + dot(onehot, b, dims) + dot(onehot, c, dims)


def pick_right(x, onehot, dims):
    a, b, c = split3(x)
    return dot(a, onehot, dims) + dot(b, onehot, dims) + dot(c, onehot, dims)


def iota(shape, dim):
    return lax.broadcasted_iota(jnp.int32, shape, dim)


def column(row):
    return jnp.transpose(jnp.broadcast_to(row, (8, row.shape[1])))[:, :1]


def onehot(mask):
    return mask.astype(F32).astype(BF16)


def owner_slots(owner, parts):
    count = owner.shape[1]
    owner_f = owner.astype(F32)
    same = (column(owner_f) == owner_f) & (iota((count, count), 0) < iota((count, count), 1))
    rank = jnp.sum(same.astype(F32), axis=0, keepdims=True).astype(jnp.int32)
    to = iota((parts, count), 0) == owner
    return [to & (rank == s) for s in range(SLOTS)]


def near_onehot(near):
    count = near.shape[1]
    return onehot(column(near.astype(F32)) == iota((count, LANES), 1).astype(F32))


def stacked_rows(meta, lanes):
    turned = jnp.transpose(meta)
    return jnp.concatenate([turned[lanes + s : lanes + s + 1, :] for s in range(SLOTS)], axis=1)


def port_onehot(meta):
    parts = meta.shape[0]
    ports = (iota((parts, LANES), 1) + 1).astype(F32)
    return onehot(jnp.concatenate([meta[:, s : s + 1] == ports for s in range(SLOTS)], axis=0))


def pad_lanes(x, spare):
    if not spare:
        return x
    return jnp.concatenate([x, jnp.zeros((x.shape[0], spare), x.dtype)], axis=1)


def put(pay_ref, rows, first, pitch):
    parts = pay_ref.shape[0] // pitch
    tiles = rows.shape[1] // LANES
    for g in range(rows.shape[0] // parts):
        for t in range(tiles):
            pay_ref[pl.ds(first + g * tiles + t, parts, stride=pitch), :] = rows[
                g * parts : (g + 1) * parts, t * LANES : (t + 1) * LANES
            ]


def get(pay_ref, first, pitch, tiles):
    parts = pay_ref.shape[0] // pitch
    return jnp.concatenate(
        [
            jnp.concatenate(
                [pay_ref[pl.ds(first + s * tiles + t, parts, stride=pitch), :] for t in range(tiles)],
                axis=1,
            )
            for s in range(SLOTS)
        ],
        axis=0,
    )


def by_kind(products, kind, rows):
    chosen = products[:rows]
    for t in range(1, KINDS):
        chosen = jnp.where(kind == t, products[t * rows : (t + 1) * rows], chosen)
    return chosen


def table_product(high, low, x):
    a, b = split2(x)
    return dot(high, a) + (dot(high, b) + dot(low, a))


def condense_kernel(
    parts, kind_ref, stiff_ref, near_ref, owner_ref, far_ref, load_ref, inverse_ref, coupling_ref,
    pay_ref, near_sum_ref, meta_ref, near_part, far_part,
):
    modes = load_ref.shape[0] // CASES
    dofs = near_sum_ref.shape[0] // CASES
    table = jnp.concatenate(
        [dot_high(coupling_ref[t], inverse_ref[t]) for t in range(KINDS)], axis=0
    )
    high, low = split2(table)
    left = jnp.concatenate([high, high, low], axis=1)
    kind = kind_ref[...]
    kind2 = jnp.concatenate([kind, kind], axis=1)
    for k in range(0, CASES, 2):
        loads = jnp.concatenate(
            [load_ref[pl.ds(k + i, modes, stride=CASES), :] for i in range(2)], axis=1
        )
        a, b = split2(loads)
        condensed = -by_kind(dot(left, jnp.concatenate([a, b, a], axis=0)), kind2, 2 * dofs)
        for i in range(2):
            lanes = slice(i * LANES, (i + 1) * LANES)
            near_part[pl.ds(k + i, dofs, stride=CASES), :] = condensed[:dofs, lanes]
            far_part[pl.ds(k + i, dofs, stride=CASES), :] = condensed[dofs:, lanes]
    near = near_ref[...]
    slots = owner_slots(owner_ref[...], parts)
    near_sum_ref[...] = pick_right(near_part[...], near_onehot(near), NN)
    chosen = onehot(jnp.concatenate(slots, axis=0))
    put(pay_ref, pick_left(chosen, far_part[...], NT), 0, 10)
    lane = iota((parts, LANES), 1)
    far_row = (far_ref[...] + 1).astype(F32)
    near_row = (near + 1).astype(F32)
    message = jnp.zeros((parts, LANES), F32)
    own = jnp.zeros((parts, LANES), F32)
    for s in range(SLOTS):
        for at, row in ((0, far_row), (SLOTS, kind.astype(F32)), (2 * SLOTS, stiff_ref[...])):
            value = jnp.sum(jnp.where(slots[s], row, 0.0), axis=1, keepdims=True)
            message = jnp.where(lane == at + s, value, message)
        value = jnp.sum(jnp.where(slots[s], near_row, 0.0), axis=1, keepdims=True)
        own = jnp.where(lane == s, value, own)
    pay_ref[pl.ds(9, parts, stride=10), :] = message
    meta_ref[...] = own


def tables_kernel(
    kind_ref, stiff_ref, load_ref, inverse_ref, coupling_ref, block_ref,
    near_high, near_low, far_high, far_low, turned_high, turned_low, base_ref,
):
    dofs = block_ref.shape[1] // 2
    modes = inverse_ref.shape[1]
    inverses = []
    for t in range(KINDS):
        reduced = dot_high(coupling_ref[t], inverse_ref[t])
        schur = block_ref[t] - dot_high(reduced, coupling_ref[t], NT)
        near_high[t * dofs : (t + 1) * dofs, :], near_low[t * dofs : (t + 1) * dofs, :] = split2(schur[:dofs])
        far_high[t * dofs : (t + 1) * dofs, :], far_low[t * dofs : (t + 1) * dofs, :] = split2(schur[dofs:])
        turned = jnp.transpose(reduced)
        turned_high[t * modes : (t + 1) * modes, :], turned_low[t * modes : (t + 1) * modes, :] = split2(turned)
        inverses.append(inverse_ref[t])
    high, low = split2(jnp.concatenate(inverses, axis=0))
    kind = kind_ref[...]
    stiff = stiff_ref[...]
    for k in range(CASES):
        loads = load_ref[pl.ds(k, modes, stride=CASES), :]
        base_ref[pl.ds(k, modes, stride=CASES), :] = by_kind(table_product(high, low, loads), kind, modes) / stiff


def send_ports(field, asked, own, pay_ref):
    put(pay_ref, pick_left(jnp.concatenate([asked, own], axis=0), field, NT), 0, 18)


def rhs_kernel(parts, arrived_ref, near_sum_ref, load_ref, meta_ref, field_ref, pay_ref, asked_ref):
    asked = arrived_ref[pl.ds(9, parts, stride=10), :]
    asked_ref[...] = asked
    asked_hot = port_onehot(asked)
    arrived = get(arrived_ref, 0, 10, 3)
    field = load_ref[...] + (near_sum_ref[...] + pick_right(arrived, asked_hot, TN))
    field_ref[...] = field
    send_ports(field, asked_hot, port_onehot(meta_ref[...]), pay_ref)


def apply_kernel(
    parts, groups, last, arrived_ref, meta_ref, asked_ref, kind_ref, stiff_ref, near_ref, owner_ref,
    near_high, near_low, far_high, far_low, field_ref, *rest,
):
    if last:
        others, rest = rest[: groups - 1], rest[groups - 1 :]
        gram_ref, case_ref, image_ref, spread_ref, copies_ref, slot_ref, near_part, far_part = rest
    else:
        image_ref, spread_ref, pay_ref, slot_ref, near_part, far_part = rest
    rows = field_ref.shape[0]
    dofs = rows // CASES
    field = field_ref[...]
    asked = asked_ref[...]
    asked_hot = port_onehot(asked)
    near_hot = near_onehot(near_ref[...])
    slots = onehot(jnp.concatenate(owner_slots(owner_ref[...], parts), axis=0))
    spread_ref[:rows, :] = pick_right(field, near_hot, NT)
    spread_ref[rows:, :] = pick_right(get(arrived_ref, 0, 18, 3), slots, TN)
    tiles = slot_ref.shape[0]
    spare = tiles * LANES - SLOTS * parts
    wide_hot = asked_hot
    if spare:
        wide_hot = jnp.concatenate([asked_hot, jnp.zeros((spare, LANES), BF16)], axis=0)
    from_near = pad_lanes(jnp.transpose(get(arrived_ref, 9, 18, 3)), spare)
    from_far = pick_right(field, wide_hot, NT)
    for g in range(tiles):
        lanes = slice(g * LANES, (g + 1) * LANES)
        slot_ref[g, :rows, :] = from_near[:, lanes]
        slot_ref[g, rows:, :] = from_far[:, lanes]
    kind = kind_ref[...]
    stiff = stiff_ref[...]
    kind2 = jnp.concatenate([kind, kind], axis=1)
    stiff2 = jnp.concatenate([stiff, stiff], axis=1)
    asked_kind = pad_lanes(stacked_rows(asked, SLOTS), spare).astype(jnp.int32)
    asked_stiff = pad_lanes(stacked_rows(asked, 2 * SLOTS), spare)
    for k in range(0, CASES, 2):
        values = jnp.concatenate(
            [spread_ref[pl.ds(k + i, 2 * dofs, stride=CASES), :] for i in range(2)], axis=1
        )
        result = by_kind(table_product(near_high[...], near_low[...], values), kind2, dofs) * stiff2
        for i in range(2):
            near_part[pl.ds(k + i, dofs, stride=CASES), :] = result[:, i * LANES : (i + 1) * LANES]
    for k in range(CASES):
        values = jnp.concatenate(
            [slot_ref[g, pl.ds(k, 2 * dofs, stride=CASES), :] for g in range(tiles)], axis=1
        )
        result = by_kind(table_product(far_high[...], far_low[...], values), asked_kind, dofs) * asked_stiff
        for g in range(tiles):
            far_part[g, pl.ds(k, dofs, stride=CASES), :] = result[:, g * LANES : (g + 1) * LANES]
    image = pick_right(near_part[...], near_hot, NN)
    for g in range(tiles):
        image = image + pick_right(far_part[g], wide_hot[g * LANES : (g + 1) * LANES], NN)
    image_ref[...] = image
    if last:
        gram = add_products(
            LANES, [field_ref, *others], [image_ref], [3 * groups * CASES], case_ref[0], gram_ref[...]
        )
        for p in range(parts):
            copies_ref[p] = gram
    else:
        send_ports(image, asked_hot, port_onehot(meta_ref[...]), pay_ref)


def turned_kernel(spread_ref, kind_ref, high_ref, low_ref, out_ref):
    dofs2 = spread_ref.shape[0] // CASES
    modes = out_ref.shape[0] // CASES
    kind = kind_ref[...]
    kind2 = jnp.concatenate([kind, kind], axis=1)
    for k in range(0, CASES, 2):
        values = jnp.concatenate(
            [spread_ref[pl.ds(k + i, dofs2, stride=CASES), :] for i in range(2)], axis=1
        )
        result = by_kind(table_product(high_ref[...], low_ref[...], values), kind2, modes)
        for i in range(2):
            out_ref[pl.ds(k + i, modes, stride=CASES), :] = result[:, i * LANES : (i + 1) * LANES]


def add_products(lanes, lefts, rights, first, case, out):
    groups = len(lefts)
    total = groups * CASES
    dofs = lefts[0].shape[0] // CASES
    lane = iota((CASES, LANES), 1)
    for h in range(groups):
        def step(d, sums):
            own = pl.ds(pl.multiple_of(d * CASES, CASES), CASES)
            values = [ref[own, :] for ref in rights]
            new = []
            for i in range(CASES):
                row = lefts[h][pl.ds(d * CASES + i, 1), :]
                new.append(tuple(s + row * v for s, v in zip(sums[i], values)))
            return tuple(new)

        zero = jnp.zeros((CASES, LANES), F32)
        sums = lax.fori_loop(0, dofs, step, ((zero,) * len(rights),) * CASES)
        at = lax.rem(case + h, groups) * CASES
        for i in range(CASES):
            for g in range(len(rights)):
                value = jnp.sum(sums[i][g], axis=1, keepdims=True)
                out = jnp.where(lane == first[g] + at + i, value, out)
    return out


def gram_kernel(groups, case_ref, *refs):
    base, image, out_ref = refs[:groups], refs[groups : 2 * groups], refs[2 * groups]
    total = groups * CASES
    out = jnp.zeros((CASES, LANES), F32)
    out = add_products(LANES, base, [base[0], image[0]], [0, total], case_ref[0], out)
    out_ref[...] = add_products(LANES, image, [image[0]], [2 * total], case_ref[0], out)


def sum_kernel(in_ref, out_ref):
    total = in_ref[0]
    for p in range(1, in_ref.shape[0]):
        total = total + in_ref[p]
    out_ref[...] = total


def spd_solve(pairs):
    n = pairs[0][0].shape[0]
    row_of = iota((n, 2 * n), 0)
    work = [jnp.concatenate(pair, axis=1) for pair in pairs]
    for k in range(n):
        nxt = []
        for a in work:
            pivot = a[k : k + 1, :] / a[k : k + 1, k : k + 1]
            nxt.append(jnp.where(row_of == k, pivot, a - a[:, k : k + 1] * pivot))
        work = nxt
    return [a[:, n:] for a in work]


def symmetric(m):
    return 0.5 * (m + jnp.transpose(m))


def solve_kernel(groups, case_ref, *refs):
    grams, coef, rows_ref, turned_coef = refs[:groups], refs[groups], refs[groups + 1], refs[groups + 2]
    n = groups * CASES
    for h in range(groups):
        at = pl.multiple_of(lax.rem(case_ref[0] + h, groups) * CASES, CASES)
        rows_ref[pl.ds(at, CASES), :] = grams[h][...]
    g00, g01, g11, g12 = [symmetric(rows_ref[:, g * n : (g + 1) * n]) for g in range(4)]
    eye = (iota((n, n), 0) == iota((n, n), 1)).astype(F32)
    step0, inverse00 = spd_solve([(g01, g00), (g00, eye)])
    step0_t = jnp.transpose(step0)
    gram1 = g00 - dot_high(g01, step0)
    gram1 = gram1 + jnp.transpose(dot_high(dot_high(g11, step0) - g01, step0, TN))
    gram1 = symmetric(gram1)
    update = eye + dot_high(inverse00, gram1)
    update_t = jnp.transpose(update)
    left = dot_high(update_t, g01) - dot_high(step0_t, g11)
    right = dot_high(update_t, g11) - dot_high(step0_t, g12)
    curvature = symmetric(dot_high(left, update) - dot_high(right, step0))
    (step1,) = spd_solve([(curvature, gram1)])
    first = jnp.transpose(step0 + dot_high(update, step1))
    second = jnp.transpose(-dot_high(step0, step1))
    turned_coef[:n, :] = jnp.concatenate([first] * (LANES // n), axis=1)
    turned_coef[n:, :] = jnp.concatenate([second] * (LANES // n), axis=1)
    at = pl.multiple_of(case_ref[0] * CASES, CASES)
    for h in range(2):
        mine = pltpu.roll(turned_coef[pl.ds(h * n + at, CASES), :], LANES - case_ref[0] * CASES, 1)
        for j in range(n):
            coef[h * n + j] = jnp.broadcast_to(mine[:, j : j + 1], (CASES, LANES))


def finish_kernel(groups, coef, bubble_ref, *refs):
    base, image, second, turned0, turned1 = [refs[g * groups : (g + 1) * groups] for g in range(5)]
    x_ref, residual_ref, bubble_out = refs[5 * groups :]
    n = groups * CASES
    dofs = x_ref.shape[0] // CASES
    modes = bubble_out.shape[0] // CASES

    def ports(block, carry):
        for i in range(4):
            d = block * 4 + i
            own = pl.ds(pl.multiple_of(d * CASES, CASES), CASES)
            x = jnp.zeros((CASES, LANES), F32)
            r = base[0][own, :]
            for j in range(n):
                q, c = divmod(j, CASES)
                row = pl.ds(d * CASES + c, 1)
                a = image[q][row, :]
                c0, c1 = coef[j], coef[n + j]
                x = x + (c0 * base[q][row, :] + c1 * a)
                r = r - (c0 * a + c1 * second[q][row, :])
            x_ref[own, :] = x
            residual_ref[own, :] = r
        return carry

    lax.fori_loop(0, dofs // 4, ports, 0)

    def bubbles(block, carry):
        for i in range(4):
            d = block * 4 + i
            own = pl.ds(pl.multiple_of(d * CASES, CASES), CASES)
            w = bubble_ref[own, :]
            for j in range(n):
                q, c = divmod(j, CASES)
                row = pl.ds(d * CASES + c, 1)
                w = w - (coef[j] * turned0[q][row, :] + coef[n + j] * turned1[q][row, :])
            bubble_out[own, :] = w
        return carry

    lax.fori_loop(0, modes // 4, bubbles, 0)


def call(kernel, outs, scratch=(), name=None, flops=0, smem=()):
    outs = [jax.ShapeDtypeStruct(shape, dtype) for shape, dtype in outs]
    vmem = pl.BlockSpec(memory_space=pltpu.VMEM)

    def run(*args):
        specs = [pl.BlockSpec(memory_space=pltpu.SMEM) if i in smem else vmem for i in range(len(args))]
        moved = sum(a.size * a.dtype.itemsize for a in args) + sum(o.size * o.dtype.itemsize for o in outs)
        return pl.pallas_call(
            kernel,
            out_shape=outs,
            in_specs=specs,
            out_specs=[vmem] * len(outs),
            scratch_shapes=[pltpu.VMEM(shape, F32) for shape in scratch],
            compiler_params=pltpu.CompilerParams(vmem_limit_bytes=40 << 20),
            cost_estimate=pl.CostEstimate(flops=flops, bytes_accessed=moved, transcendentals=0),
            name=name,
        )(*args)

    return run


def exchange(rows, parts):
    moved = lax.all_to_all(rows.reshape(parts, 1, -1), PLANE, split_axis=0, concat_axis=0)
    return moved.reshape(rows.shape)


def local(
    comp_type, stiffness, near_port, far_owner, far_port, bubble_load, port_load,
    bubble_inverse, coupling, port_block,
):
    parts = lax.axis_size("px") * lax.axis_size("py")
    groups = lax.axis_size("case")
    modes, cases, comps = bubble_load.shape
    dofs, _, ports = port_load.shape
    rows, bubbles = dofs * cases, modes * cases
    slot_tiles = -(-SLOTS * parts // LANES)
    kind = comp_type.reshape(1, comps)
    stiff = stiffness.reshape(1, comps)
    near = near_port.reshape(1, comps)
    owner = far_owner.reshape(1, comps)
    far = far_port.reshape(1, comps)
    loads = bubble_load.reshape(bubbles, comps)
    field_of = ((rows, ports), F32)
    meta_of = ((parts, LANES), F32)
    pay, near_sum, meta = call(
        functools.partial(condense_kernel, parts),
        [((parts * 10, LANES), F32), field_of, meta_of],
        [(rows, comps)] * 2,
        "condense",
    )(kind, stiff, near, owner, far, loads, bubble_inverse, coupling)
    tables = call(
        tables_kernel,
        [((KINDS * dofs, 2 * dofs), BF16)] * 4 + [((KINDS * modes, 2 * dofs), BF16)] * 2 + [((bubbles, comps), F32)],
        name="tables",
        flops=10**9,
    )(kind, stiff, loads, bubble_inverse, coupling, port_block)
    schur, turned_tables, bubble_base = tables[:4], tables[4:6], tables[6]
    base, pay, asked = call(
        functools.partial(rhs_kernel, parts),
        [field_of, ((parts * 18, LANES), F32), meta_of],
        name="rhs",
    )(exchange(pay, parts), near_sum, port_load.reshape(rows, ports), meta)

    case = lax.axis_index("case").reshape(1)
    spread_of = ((2 * rows, comps), F32)
    scratch = [(slot_tiles, 2 * rows, LANES), (rows, comps), (slot_tiles, rows, LANES)]

    def turned(spread):
        return call(turned_kernel, [((bubbles, comps), F32)], name="turned", flops=10**9)(
            spread, kind, *turned_tables
        )[0]

    def all_cases(field):
        return [field] + [
            lax.ppermute(field, "case", [((k + h) % groups, k) for k in range(groups)])
            for h in range(1, groups)
        ]

    arrived = exchange(pay, parts)
    base_all = all_cases(base)
    arrived, *base_all = lax.optimization_barrier((arrived, *base_all))
    shared = (meta, asked, kind, stiff, near, owner, *schur)
    image, spread, pay = call(
        functools.partial(apply_kernel, parts, groups, False),
        [field_of, spread_of, ((parts * 18, LANES), F32)],
        scratch,
        "apply",
    )(arrived, *shared, base_all[0])
    arrived = exchange(pay, parts)
    image_all = all_cases(image)
    turned0_all = all_cases(turned(spread))
    (gram,) = call(functools.partial(gram_kernel, groups), [((cases, LANES), F32)], name="gram", smem=(0,))(
        case, *base_all, *image_all
    )
    arrived, *turned0_all = lax.optimization_barrier((arrived, *turned0_all))
    second, spread, copies = call(
        functools.partial(apply_kernel, parts, groups, True),
        [field_of, spread_of, ((parts, cases, LANES), F32)],
        scratch,
        "apply_last",
        smem=(12 + groups,),
    )(arrived, *shared, *image_all, gram, case)
    copies = lax.all_to_all(copies, PLANE, split_axis=0, concat_axis=0)
    second_all = all_cases(second)
    turned1_all = all_cases(turned(spread))
    copies, *rest = lax.optimization_barrier((copies, *second_all, *turned1_all))
    second_all, turned1_all = rest[:groups], rest[groups:]
    (gram,) = call(sum_kernel, [((cases, LANES), F32)], name="sum")(copies)
    (coef,) = call(
        functools.partial(solve_kernel, groups),
        [((2 * groups * cases, cases, LANES), F32)],
        [(groups * cases, LANES), (2 * groups * cases, LANES)],
        "solve",
        smem=(0,),
    )(case, *all_cases(gram))
    x, residual, bubble = call(
        functools.partial(finish_kernel, groups),
        [field_of, field_of, ((bubbles, comps), F32)],
        name="finish",
    )(coef, bubble_base, *base_all, *image_all, *second_all, *turned0_all, *turned1_all)
    return (
        x.reshape(port_load.shape),
        residual.reshape(port_load.shape),
        bubble.reshape(bubble_load.shape),
    )


def solution(mesh):
    placed = (
        P(PLANE),
        P(PLANE),
        P(PLANE),
        P(PLANE, None),
        P(PLANE),
        P(None, "case", PLANE),
        P(None, "case", PLANE),
        P(),
        P(),
        P(),
    )
    out = P(None, "case", PLANE)
    return jax.shard_map(
        local, mesh=mesh, in_specs=placed, out_specs=(out, out, out), check_vma=False
    )
```

```python
import functools

import jax
import jax.numpy as jnp
from jax import lax
from jax.experimental import pallas as pl
from jax.experimental.pallas import tpu as pltpu
from jax.sharding import PartitionSpec as P

HIGH = lax.Precision.HIGHEST
PLANE = ("px", "py")
F32 = jnp.float32
BF16 = jnp.bfloat16
KINDS = 8
LANES = 128
CASES = 8
SLOTS = 3
NN = (((1,), (0,)), ((), ()))
NT = (((1,), (1,)), ((), ()))
TN = (((0,), (0,)), ((), ()))


def dot(lhs, rhs, dims=NN):
    return lax.dot_general(lhs, rhs, dims, preferred_element_type=F32)


def dot_high(lhs, rhs, dims=NN):
    return lax.dot_general(lhs, rhs, dims, precision=HIGH, preferred_element_type=F32)


def split2(x):
    high = x.astype(BF16)
    return high, (x - high.astype(F32)).astype(BF16)


def split3(x):
    high = x.astype(BF16)
    rest = x - high.astype(F32)
    middle = rest.astype(BF16)
    return high, middle, (rest - middle.astype(F32)).astype(BF16)


def pick_left(onehot, x, dims):
    a, b, c = split3(x)
    return dot(onehot, a, dims) + dot(onehot, b, dims) + dot(onehot, c, dims)


def pick_right(x, onehot, dims):
    a, b, c = split3(x)
    return dot(a, onehot, dims) + dot(b, onehot, dims) + dot(c, onehot, dims)


def iota(shape, dim):
    return lax.broadcasted_iota(jnp.int32, shape, dim)


def column(row):
    return jnp.transpose(jnp.broadcast_to(row, (8, row.shape[1])))[:, :1]


def onehot(mask):
    return mask.astype(F32).astype(BF16)


def owner_slots(owner, parts):
    count = owner.shape[1]
    owner_f = owner.astype(F32)
    same = (column(owner_f) == owner_f) & (iota((count, count), 0) < iota((count, count), 1))
    rank = jnp.sum(same.astype(F32), axis=0, keepdims=True).astype(jnp.int32)
    to = iota((parts, count), 0) == owner
    return [to & (rank == s) for s in range(SLOTS)]


def near_onehot(near):
    count = near.shape[1]
    return onehot(column(near.astype(F32)) == iota((count, LANES), 1).astype(F32))


def stacked_rows(meta, lanes):
    turned = jnp.transpose(meta)
    return jnp.concatenate([turned[lanes + s : lanes + s + 1, :] for s in range(SLOTS)], axis=1)


def port_onehot(meta):
    parts = meta.shape[0]
    ports = (iota((parts, LANES), 1) + 1).astype(F32)
    return onehot(jnp.concatenate([meta[:, s : s + 1] == ports for s in range(SLOTS)], axis=0))


def pad_lanes(x, spare):
    if not spare:
        return x
    return jnp.concatenate([x, jnp.zeros((x.shape[0], spare), x.dtype)], axis=1)


def put(pay_ref, rows, first, pitch):
    parts = pay_ref.shape[0] // pitch
    tiles = rows.shape[1] // LANES
    for g in range(rows.shape[0] // parts):
        for t in range(tiles):
            pay_ref[pl.ds(first + g * tiles + t, parts, stride=pitch), :] = rows[
                g * parts : (g + 1) * parts, t * LANES : (t + 1) * LANES
            ]


def get(pay_ref, first, pitch, tiles):
    parts = pay_ref.shape[0] // pitch
    return jnp.concatenate(
        [
            jnp.concatenate(
                [pay_ref[pl.ds(first + s * tiles + t, parts, stride=pitch), :] for t in range(tiles)],
                axis=1,
            )
            for s in range(SLOTS)
        ],
        axis=0,
    )


def by_kind(products, kind, rows):
    chosen = products[:rows]
    for t in range(1, KINDS):
        chosen = jnp.where(kind == t, products[t * rows : (t + 1) * rows], chosen)
    return chosen


def table_product(high, low, x):
    a, b = split2(x)
    return dot(high, a) + (dot(high, b) + dot(low, a))


def condense_kernel(
    parts, kind_ref, stiff_ref, near_ref, owner_ref, far_ref, load_ref, inverse_ref, coupling_ref,
    pay_ref, near_sum_ref, meta_ref, near_part, far_part,
):
    modes = load_ref.shape[0] // CASES
    dofs = near_sum_ref.shape[0] // CASES
    table = jnp.concatenate(
        [jnp.transpose(dot_high(inverse_ref[t], coupling_ref[t], TN)) for t in range(KINDS)], axis=0
    )
    high, low = split2(table)
    left = jnp.concatenate([high, high, low], axis=1)
    kind = kind_ref[...]
    kind2 = jnp.concatenate([kind, kind], axis=1)
    for k in range(0, CASES, 2):
        loads = jnp.concatenate(
            [load_ref[pl.ds(k + i, modes, stride=CASES), :] for i in range(2)], axis=1
        )
        a, b = split2(loads)
        condensed = -by_kind(dot(left, jnp.concatenate([a, b, a], axis=0)), kind2, 2 * dofs)
        for i in range(2):
            lanes = slice(i * LANES, (i + 1) * LANES)
            near_part[pl.ds(k + i, dofs, stride=CASES), :] = condensed[:dofs, lanes]
            far_part[pl.ds(k + i, dofs, stride=CASES), :] = condensed[dofs:, lanes]
    near = near_ref[...]
    slots = owner_slots(owner_ref[...], parts)
    near_sum_ref[...] = pick_right(near_part[...], near_onehot(near), NN)
    chosen = onehot(jnp.concatenate(slots, axis=0))
    put(pay_ref, pick_left(chosen, far_part[...], NT), 0, 10)
    lane = iota((parts, LANES), 1)
    far_row = (far_ref[...] + 1).astype(F32)
    near_row = (near + 1).astype(F32)
    message = jnp.zeros((parts, LANES), F32)
    own = jnp.zeros((parts, LANES), F32)
    for s in range(SLOTS):
        for at, row in ((0, far_row), (SLOTS, kind.astype(F32)), (2 * SLOTS, stiff_ref[...])):
            value = jnp.sum(jnp.where(slots[s], row, 0.0), axis=1, keepdims=True)
            message = jnp.where(lane == at + s, value, message)
        value = jnp.sum(jnp.where(slots[s], near_row, 0.0), axis=1, keepdims=True)
        own = jnp.where(lane == s, value, own)
    pay_ref[pl.ds(9, parts, stride=10), :] = message
    meta_ref[...] = own


def tables_kernel(
    kind_ref, stiff_ref, load_ref, inverse_ref, coupling_ref, block_ref,
    near_high, near_low, far_high, far_low, turned_high, turned_low, base_ref,
):
    dofs = block_ref.shape[1] // 2
    modes = inverse_ref.shape[1]
    inverses = []
    for t in range(KINDS):
        turned = dot_high(inverse_ref[t], coupling_ref[t], TN)
        schur = block_ref[t] - dot_high(turned, coupling_ref[t], TN)
        near_high[t * dofs : (t + 1) * dofs, :], near_low[t * dofs : (t + 1) * dofs, :] = split2(schur[:dofs])
        far_high[t * dofs : (t + 1) * dofs, :], far_low[t * dofs : (t + 1) * dofs, :] = split2(schur[dofs:])
        turned_high[t * modes : (t + 1) * modes, :], turned_low[t * modes : (t + 1) * modes, :] = split2(turned)
        inverses.append(inverse_ref[t])
    high, low = split2(jnp.concatenate(inverses, axis=0))
    kind = kind_ref[...]
    stiff = stiff_ref[...]
    for k in range(CASES):
        loads = load_ref[pl.ds(k, modes, stride=CASES), :]
        base_ref[pl.ds(k, modes, stride=CASES), :] = by_kind(table_product(high, low, loads), kind, modes) / stiff


def send_ports(field, asked, own, pay_ref):
    put(pay_ref, pick_left(jnp.concatenate([asked, own], axis=0), field, NT), 0, 18)


def rhs_kernel(parts, arrived_ref, near_sum_ref, load_ref, meta_ref, field_ref, pay_ref, asked_ref):
    asked = arrived_ref[pl.ds(9, parts, stride=10), :]
    asked_ref[...] = asked
    asked_hot = port_onehot(asked)
    arrived = get(arrived_ref, 0, 10, 3)
    field = load_ref[...] + (near_sum_ref[...] + pick_right(arrived, asked_hot, TN))
    field_ref[...] = field
    send_ports(field, asked_hot, port_onehot(meta_ref[...]), pay_ref)


def apply_kernel(
    parts, groups, last, arrived_ref, meta_ref, asked_ref, kind_ref, stiff_ref, near_ref, owner_ref,
    near_high, near_low, far_high, far_low, field_ref, *rest,
):
    if last:
        others, rest = rest[: groups - 1], rest[groups - 1 :]
        gram_ref, case_ref, image_ref, spread_ref, copies_ref, slot_ref, near_part, far_part = rest
    else:
        image_ref, spread_ref, pay_ref, slot_ref, near_part, far_part = rest
    rows = field_ref.shape[0]
    dofs = rows // CASES
    field = field_ref[...]
    asked = asked_ref[...]
    asked_hot = port_onehot(asked)
    near_hot = near_onehot(near_ref[...])
    slots = onehot(jnp.concatenate(owner_slots(owner_ref[...], parts), axis=0))
    spread_ref[:rows, :] = pick_right(field, near_hot, NT)
    spread_ref[rows:, :] = pick_right(get(arrived_ref, 0, 18, 3), slots, TN)
    tiles = slot_ref.shape[0]
    spare = tiles * LANES - SLOTS * parts
    wide_hot = asked_hot
    if spare:
        wide_hot = jnp.concatenate([asked_hot, jnp.zeros((spare, LANES), BF16)], axis=0)
    from_near = pad_lanes(jnp.transpose(get(arrived_ref, 9, 18, 3)), spare)
    from_far = pick_right(field, wide_hot, NT)
    for g in range(tiles):
        lanes = slice(g * LANES, (g + 1) * LANES)
        slot_ref[g, :rows, :] = from_near[:, lanes]
        slot_ref[g, rows:, :] = from_far[:, lanes]
    kind = kind_ref[...]
    stiff = stiff_ref[...]
    kind2 = jnp.concatenate([kind, kind], axis=1)
    stiff2 = jnp.concatenate([stiff, stiff], axis=1)
    asked_kind = pad_lanes(stacked_rows(asked, SLOTS), spare).astype(jnp.int32)
    asked_stiff = pad_lanes(stacked_rows(asked, 2 * SLOTS), spare)
    for k in range(0, CASES, 2):
        values = jnp.concatenate(
            [spread_ref[pl.ds(k + i, 2 * dofs, stride=CASES), :] for i in range(2)], axis=1
        )
        result = by_kind(table_product(near_high[...], near_low[...], values), kind2, dofs) * stiff2
        for i in range(2):
            near_part[pl.ds(k + i, dofs, stride=CASES), :] = result[:, i * LANES : (i + 1) * LANES]
    for k in range(CASES):
        values = jnp.concatenate(
            [slot_ref[g, pl.ds(k, 2 * dofs, stride=CASES), :] for g in range(tiles)], axis=1
        )
        result = by_kind(table_product(far_high[...], far_low[...], values), asked_kind, dofs) * asked_stiff
        for g in range(tiles):
            far_part[g, pl.ds(k, dofs, stride=CASES), :] = result[:, g * LANES : (g + 1) * LANES]
    image = pick_right(near_part[...], near_hot, NN)
    for g in range(tiles):
        image = image + pick_right(far_part[g], wide_hot[g * LANES : (g + 1) * LANES], NN)
    image_ref[...] = image
    if last:
        gram = add_products(
            LANES, [field_ref, *others], [image_ref], [3 * groups * CASES], case_ref[0], gram_ref[...]
        )
        for p in range(copies_ref.shape[0]):
            copies_ref[p] = gram
    else:
        send_ports(image, asked_hot, port_onehot(meta_ref[...]), pay_ref)


def turned_kernel(groups, case_ref, spread_ref, field_ref, kind_ref, high_ref, low_ref, *rest):
    own_ref, messages, out_ref = rest[0], rest[1:groups], rest[groups]
    dofs2 = spread_ref.shape[0] // CASES
    rows = field_ref.shape[0]
    modes = out_ref.shape[0] // CASES
    part = out_ref.shape[0] // groups
    kind = kind_ref[...]
    kind2 = jnp.concatenate([kind, kind], axis=1)
    for k in range(0, CASES, 2):
        values = jnp.concatenate(
            [spread_ref[pl.ds(k + i, dofs2, stride=CASES), :] for i in range(2)], axis=1
        )
        result = by_kind(table_product(high_ref[...], low_ref[...], values), kind2, modes)
        for i in range(2):
            out_ref[pl.ds(k + i, modes, stride=CASES), :] = result[:, i * LANES : (i + 1) * LANES]
    own_ref[...] = out_ref[pl.ds(pl.multiple_of(case_ref[0] * part, part), part), :]
    for h in range(1, groups):
        at = lax.rem(case_ref[0] + h, groups)
        messages[h - 1][:rows, :] = field_ref[...]
        messages[h - 1][rows:, :] = out_ref[pl.ds(pl.multiple_of(at * part, part), part), :]


def add_products(lanes, lefts, rights, first, case, out):
    groups = len(lefts)
    total = groups * CASES
    dofs = lefts[0].shape[0] // CASES
    lane = iota((CASES, LANES), 1)
    for h in range(groups):
        def step(d, sums):
            own = pl.ds(pl.multiple_of(d * CASES, CASES), CASES)
            values = [ref[own, :] for ref in rights]
            new = []
            for i in range(CASES):
                row = lefts[h][pl.ds(d * CASES + i, 1), :]
                new.append(tuple(s + row * v for s, v in zip(sums[i], values)))
            return tuple(new)

        zero = jnp.zeros((CASES, LANES), F32)
        sums = lax.fori_loop(0, dofs, step, ((zero,) * len(rights),) * CASES)
        at = lax.rem(case + h, groups) * CASES
        for i in range(CASES):
            for g in range(len(rights)):
                value = jnp.sum(sums[i][g], axis=1, keepdims=True)
                out = jnp.where(lane == first[g] + at + i, value, out)
    return out


def gram_kernel(groups, case_ref, *refs):
    base, image, out_ref = refs[:groups], refs[groups : 2 * groups], refs[2 * groups]
    total = groups * CASES
    out = jnp.zeros((CASES, LANES), F32)
    out = add_products(LANES, base, [base[0], image[0]], [0, total], case_ref[0], out)
    out_ref[...] = add_products(LANES, image, [image[0]], [2 * total], case_ref[0], out)


def sum_kernel(in_ref, out_ref):
    for q in range(in_ref.shape[0]):
        total = in_ref[q, 0]
        for p in range(1, in_ref.shape[1]):
            total = total + in_ref[q, p]
        for p in range(out_ref.shape[0]):
            out_ref[p, q * CASES : (q + 1) * CASES, :] = total


def spd_solve(matrix, target):
    n = matrix.shape[0]
    a = jnp.concatenate([matrix, target], axis=1)
    row_of = iota(a.shape, 0)
    for k in range(0, n, 2):
        r0, r1 = a[k : k + 1, :], a[k + 1 : k + 2, :]
        c0, c1 = a[:, k : k + 1], a[:, k + 1 : k + 2]
        p00, p01, p10, p11 = c0[k : k + 1], c1[k : k + 1], c0[k + 1 : k + 2], c1[k + 1 : k + 2]
        scale = 1.0 / (p00 * p11 - p01 * p10)
        u0 = (r0 * p11 - r1 * p01) * scale
        u1 = (r1 * p00 - r0 * p10) * scale
        a = a - (c0 * u0 + c1 * u1)
        a = jnp.where(row_of == k, u0, jnp.where(row_of == k + 1, u1, a))
    return a[:, n:]


def symmetric(m):
    return 0.5 * (m + jnp.transpose(m))


def solve_kernel(groups, case_ref, gram_ref, coef, coef_rows, turned_coef):
    n = groups * CASES
    total = gram_ref[0]
    for p in range(1, gram_ref.shape[0]):
        total = total + gram_ref[p]
    g00, g01, g11, g12 = [symmetric(total[:, g * n : (g + 1) * n]) for g in range(4)]
    steps = spd_solve(g01, jnp.concatenate([g00, g11], axis=1))
    step0, step1 = steps[:, :n], steps[:, n:]
    both = dot_high(g11, steps)
    second = spd_solve(symmetric(g12 - both[:, n:]), g01 - both[:, :n])
    first = step0 - dot_high(step1, second)
    first, second = jnp.transpose(first), jnp.transpose(second)
    turned_coef[0] = jnp.concatenate([first] * (LANES // n), axis=1)
    turned_coef[1] = jnp.concatenate([second] * (LANES // n), axis=1)
    shift = LANES - case_ref[0] * CASES
    for q in range(groups):
        at = pl.multiple_of(lax.rem(case_ref[0] + q, groups) * CASES, CASES)
        for h in range(2):
            mine = pltpu.roll(turned_coef[h, pl.ds(at, CASES), :], shift, 1)
            coef_rows[q * CASES : (q + 1) * CASES, h * LANES : (h + 1) * LANES] = mine
            if q == 0:
                for j in range(n):
                    coef[h * n + j] = jnp.broadcast_to(mine[:, j : j + 1], (CASES, LANES))


def bubble_kernel(groups, rows, coef_ref, *refs):
    turned0, turned1, outs = refs[:groups], refs[groups : 2 * groups], refs[2 * groups :]
    n = groups * CASES
    part = turned0[0].shape[0]
    coef = jnp.concatenate([coef_ref[:, :n], coef_ref[:, LANES : LANES + n]], axis=1)
    high, low = split2(coef)
    left = jnp.concatenate([high, high, low], axis=1)
    for m in range(0, part // CASES, 2):
        values = []
        for i in range(2):
            at = (m + i) * CASES
            pieces = [
                ref[at + (0 if h == 0 else rows) : at + (0 if h == 0 else rows) + CASES, :]
                for refs_ in (turned0, turned1)
                for h, ref in enumerate(refs_)
            ]
            values.append(jnp.concatenate(pieces, axis=0))
        a, b = split2(jnp.concatenate(values, axis=1))
        result = dot(left, jnp.concatenate([a, b, a], axis=0))
        for i in range(2):
            for h in range(groups):
                outs[h][(m + i) * CASES : (m + i + 1) * CASES, :] = result[
                    h * CASES : (h + 1) * CASES, i * LANES : (i + 1) * LANES
                ]


def ports_kernel(groups, coef, *refs):
    base, image, second = [refs[g * groups : (g + 1) * groups] for g in range(3)]
    x_ref, residual_ref = refs[3 * groups :]
    n = groups * CASES
    dofs = x_ref.shape[0] // CASES
    wide = 4

    def ports(block, carry):
        d0 = block * wide
        own = [pl.ds(pl.multiple_of((d0 + i) * CASES, CASES), CASES) for i in range(wide)]
        x = [jnp.zeros((CASES, LANES), F32)] * wide
        r = [base[0][own[i], :] for i in range(wide)]
        for j in range(n):
            q, c = divmod(j, CASES)
            c0, c1 = coef[j], coef[n + j]
            for i in range(wide):
                row = pl.ds((d0 + i) * CASES + c, 1)
                a = image[q][row, :]
                x[i] = x[i] + (c0 * base[q][row, :] + c1 * a)
                r[i] = r[i] - (c0 * a + c1 * second[q][row, :])
        for i in range(wide):
            x_ref[own[i], :] = x[i]
            residual_ref[own[i], :] = r[i]
        return carry

    lax.fori_loop(0, dofs // wide, ports, 0)


def join_kernel(groups, case_ref, bubble_ref, *refs):
    parts, out_ref = refs[:groups], refs[groups]
    part = parts[0].shape[0]
    for h in range(groups):
        at = pl.ds(pl.multiple_of(lax.rem(case_ref[0] + h, groups) * part, part), part)
        out_ref[at, :] = bubble_ref[at, :] - parts[h][...]


def call(kernel, outs, scratch=(), name=None, flops=0, smem=(), limit=12):
    outs = [jax.ShapeDtypeStruct(shape, dtype) for shape, dtype in outs]
    vmem = pl.BlockSpec(memory_space=pltpu.VMEM)

    def run(*args):
        specs = [pl.BlockSpec(memory_space=pltpu.SMEM) if i in smem else vmem for i in range(len(args))]
        moved = sum(a.size * a.dtype.itemsize for a in args) + sum(o.size * o.dtype.itemsize for o in outs)
        return pl.pallas_call(
            kernel,
            out_shape=outs,
            in_specs=specs,
            out_specs=[vmem] * len(outs),
            scratch_shapes=[pltpu.VMEM(shape, F32) for shape in scratch],
            compiler_params=pltpu.CompilerParams(vmem_limit_bytes=limit << 20),
            cost_estimate=pl.CostEstimate(flops=flops, bytes_accessed=moved, transcendentals=0),
            name=name,
        )(*args)

    return run


def exchange(rows, parts):
    moved = lax.all_to_all(rows.reshape(parts, 1, -1), PLANE, split_axis=0, concat_axis=0)
    return moved.reshape(rows.shape)


def local(
    comp_type, stiffness, near_port, far_owner, far_port, bubble_load, port_load,
    bubble_inverse, coupling, port_block,
):
    parts = lax.axis_size("px") * lax.axis_size("py")
    groups = lax.axis_size("case")
    modes, cases, comps = bubble_load.shape
    dofs, _, ports = port_load.shape
    rows, bubbles = dofs * cases, modes * cases
    slot_tiles = -(-SLOTS * parts // LANES)
    coupling = jnp.swapaxes(coupling, 1, 2)
    kind = comp_type.reshape(1, comps)
    stiff = stiffness.reshape(1, comps)
    near = near_port.reshape(1, comps)
    owner = far_owner.reshape(1, comps)
    far = far_port.reshape(1, comps)
    loads = bubble_load.reshape(bubbles, comps)
    field_of = ((rows, ports), F32)
    meta_of = ((parts, LANES), F32)
    pay, near_sum, meta = call(
        functools.partial(condense_kernel, parts),
        [((parts * 10, LANES), F32), field_of, meta_of],
        [(rows, comps)] * 2,
        "condense",
    )(kind, stiff, near, owner, far, loads, bubble_inverse, coupling)
    tables = call(
        tables_kernel,
        [((KINDS * dofs, 2 * dofs), BF16)] * 4 + [((KINDS * modes, 2 * dofs), BF16)] * 2 + [((bubbles, comps), F32)],
        name="tables",
        flops=10**9,
    )(kind, stiff, loads, bubble_inverse, coupling, port_block)
    schur, turned_tables, bubble_base = tables[:4], tables[4:6], tables[6]
    base, pay, asked = call(
        functools.partial(rhs_kernel, parts),
        [field_of, ((parts * 18, LANES), F32), meta_of],
        name="rhs",
    )(exchange(pay, parts), near_sum, port_load.reshape(rows, ports), meta)

    case = lax.axis_index("case").reshape(1)
    spread_of = ((2 * rows, comps), F32)
    scratch = [(slot_tiles, 2 * rows, LANES), (rows, comps), (slot_tiles, rows, LANES)]

    part = bubbles // groups

    def turned(spread, field):
        own, *messages = call(
            functools.partial(turned_kernel, groups),
            [((part, comps), F32)] + [((rows + part, comps), F32)] * (groups - 1),
            [(bubbles, comps)],
            name="turned",
            flops=10**9,
            smem=(0,),
        )(case, spread, field, kind, *turned_tables)
        return own, messages

    def to_cases(messages):
        backward = [
            lax.ppermute(message, "case", [(k, (k + h) % groups) for k in range(groups)])
            for h, message in enumerate(messages, 1)
        ]
        return backward[::-1]

    arrived = exchange(pay, parts)
    base_all = [base, *to_cases([base] * (groups - 1))]
    arrived, *base_all = lax.optimization_barrier((arrived, *base_all))
    shared = (meta, asked, kind, stiff, near, owner, *schur)
    image, spread, pay = call(
        functools.partial(apply_kernel, parts, groups, False),
        [field_of, spread_of, ((parts * 18, LANES), F32)],
        scratch,
        "apply",
    )(arrived, *shared, base_all[0])
    arrived = exchange(pay, parts)
    turned0, messages = turned(spread, image)
    both0 = to_cases(messages)
    (gram,) = call(functools.partial(gram_kernel, groups), [((cases, LANES), F32)], name="gram", smem=(0,))(
        case, *base_all, image, *both0
    )
    minor = lax.axis_size("py")
    second, spread, copies = call(
        functools.partial(apply_kernel, parts, groups, True),
        [field_of, spread_of, ((groups * minor, cases, LANES), F32)],
        scratch,
        "apply_last",
        smem=(12 + groups,),
    )(arrived, *shared, image, *both0, gram, case)
    copies = lax.all_to_all(copies, ("case", "py"), split_axis=0, concat_axis=0)
    turned1, messages = turned(spread, second)
    both1 = to_cases(messages)
    (copies,) = call(sum_kernel, [((parts // minor, groups * cases, LANES), F32)], name="sum")(
        copies.reshape(groups, minor, cases, LANES)
    )
    copies = lax.all_to_all(copies, "px", split_axis=0, concat_axis=0)
    copies, *both1 = lax.optimization_barrier((copies, *both1))
    coef, coef_rows = call(
        functools.partial(solve_kernel, groups),
        [((2 * groups * cases, cases, LANES), F32), ((groups * cases, 2 * LANES), F32)],
        [(2, groups * cases, LANES)],
        "solve",
        smem=(0,),
    )(case, copies)
    own, *messages = call(
        functools.partial(bubble_kernel, groups, rows), [((part, comps), F32)] * groups, name="bubble"
    )(coef_rows, turned0, *both0, turned1, *both1)
    back = to_cases(messages)
    x, residual = call(
        functools.partial(ports_kernel, groups), [field_of, field_of], name="ports", flops=10**9
    )(coef, *base_all, image, *both0, second, *both1)
    (bubble,) = call(functools.partial(join_kernel, groups), [((bubbles, comps), F32)], name="join", smem=(0,))(
        case, bubble_base, own, *back
    )
    return (
        x.reshape(port_load.shape),
        residual.reshape(port_load.shape),
        bubble.reshape(bubble_load.shape),
    )


def solution(mesh):
    placed = (
        P(PLANE),
        P(PLANE),
        P(PLANE),
        P(PLANE, None),
        P(PLANE),
        P(None, "case", PLANE),
        P(None, "case", PLANE),
        P(),
        P(),
        P(),
    )
    out = P(None, "case", PLANE)
    return jax.shard_map(
        local, mesh=mesh, in_specs=placed, out_specs=(out, out, out), check_vma=False
    )
```

```python
import functools

import jax
import jax.numpy as jnp
from jax import lax
from jax.experimental import pallas as pl
from jax.experimental.pallas import tpu as pltpu
from jax.sharding import PartitionSpec as P

HIGH = lax.Precision.HIGHEST
PLANE = ("px", "py")
F32 = jnp.float32
BF16 = jnp.bfloat16
KINDS = 8
LANES = 128
CASES = 8
SLOTS = 3
NN = (((1,), (0,)), ((), ()))
NT = (((1,), (1,)), ((), ()))
TN = (((0,), (0,)), ((), ()))


def dot(lhs, rhs, dims=NN):
    return lax.dot_general(lhs, rhs, dims, preferred_element_type=F32)


def dot_high(lhs, rhs, dims=NN):
    return lax.dot_general(lhs, rhs, dims, precision=HIGH, preferred_element_type=F32)


def split2(x):
    high = x.astype(BF16)
    return high, (x - high.astype(F32)).astype(BF16)


def pick_right(x, onehot, dims):
    (left,), (right,) = dims[0]
    return dot(jnp.concatenate(split2(x), axis=left), jnp.concatenate([onehot, onehot], axis=right), dims)


def pick_left(onehot, x, dims):
    (left,), (right,) = dims[0]
    return dot(jnp.concatenate([onehot, onehot], axis=left), jnp.concatenate(split2(x), axis=right), dims)


def stacked_table(table):
    high, low = split2(table)
    return jnp.concatenate([high, high, low], axis=1)


def stacked_values(x):
    high, low = split2(x)
    return jnp.concatenate([high, low, high], axis=0)


def iota(shape, dim):
    return lax.broadcasted_iota(jnp.int32, shape, dim)


def column(row):
    return jnp.transpose(jnp.broadcast_to(row, (8, row.shape[1])))[:, :1]


def onehot(mask):
    return mask.astype(F32).astype(BF16)


def owner_slots(owner, parts):
    count = owner.shape[1]
    owner_f = owner.astype(F32)
    same = (column(owner_f) == owner_f) & (iota((count, count), 0) < iota((count, count), 1))
    rank = jnp.sum(same.astype(F32), axis=0, keepdims=True).astype(jnp.int32)
    to = iota((parts, count), 0) == owner
    return [to & (rank == s) for s in range(SLOTS)]


def near_onehot(near):
    count = near.shape[1]
    return onehot(column(near.astype(F32)) == iota((count, LANES), 1).astype(F32))


def stacked_rows(meta, lanes):
    turned = jnp.transpose(meta)
    return jnp.concatenate([turned[lanes + s : lanes + s + 1, :] for s in range(SLOTS)], axis=1)


def port_onehot(meta):
    parts = meta.shape[0]
    ports = (iota((parts, LANES), 1) + 1).astype(F32)
    return onehot(jnp.concatenate([meta[:, s : s + 1] == ports for s in range(SLOTS)], axis=0))


def pad_lanes(x, spare):
    if not spare:
        return x
    return jnp.concatenate([x, jnp.zeros((x.shape[0], spare), x.dtype)], axis=1)


def put(pay_ref, rows, first, pitch):
    parts = pay_ref.shape[0] // pitch
    tiles = rows.shape[1] // LANES
    for g in range(rows.shape[0] // parts):
        for t in range(tiles):
            pay_ref[pl.ds(first + g * tiles + t, parts, stride=pitch), :] = rows[
                g * parts : (g + 1) * parts, t * LANES : (t + 1) * LANES
            ]


def get(pay_ref, first, pitch, tiles):
    parts = pay_ref.shape[0] // pitch
    return jnp.concatenate(
        [
            jnp.concatenate(
                [pay_ref[pl.ds(first + s * tiles + t, parts, stride=pitch), :] for t in range(tiles)],
                axis=1,
            )
            for s in range(SLOTS)
        ],
        axis=0,
    )


def by_kind(products, kind, rows):
    chosen = products[:rows]
    for t in range(1, KINDS):
        chosen = jnp.where(kind == t, products[t * rows : (t + 1) * rows], chosen)
    return chosen


def condense_kernel(
    parts, kind_hbm, stiff_hbm, near_hbm, owner_hbm, far_hbm, load_hbm, inverse_hbm, coupling_hbm,
    pay_ref, near_sum_ref, meta_ref,
    kind_ref, stiff_ref, near_ref, owner_ref, far_ref, load_ref, inverse_ref, coupling_ref, near_part, far_part, sems,
):
    copies = [
        pltpu.make_async_copy(source, target, sems.at[i])
        for i, (source, target) in enumerate((
            (inverse_hbm, inverse_ref), (coupling_hbm, coupling_ref), (load_hbm, load_ref), (kind_hbm, kind_ref),
            (stiff_hbm, stiff_ref), (near_hbm, near_ref), (owner_hbm, owner_ref), (far_hbm, far_ref),
        ))
    ]
    for copy in copies:
        copy.start()
    for copy in copies:
        copy.wait()
    modes = load_ref.shape[0] // CASES
    dofs = near_sum_ref.shape[0] // CASES
    left = stacked_table(
        jnp.concatenate(
            [jnp.transpose(dot_high(inverse_ref[t], coupling_ref[t], TN)) for t in range(KINDS)], axis=0
        )
    )
    kind = kind_ref[...]
    kind2 = jnp.concatenate([kind, kind], axis=1)
    for k in range(0, CASES, 2):
        loads = jnp.concatenate(
            [load_ref[pl.ds(k + i, modes, stride=CASES), :] for i in range(2)], axis=1
        )
        condensed = -by_kind(dot(left, stacked_values(loads)), kind2, 2 * dofs)
        for i in range(2):
            lanes = slice(i * LANES, (i + 1) * LANES)
            near_part[pl.ds(k + i, dofs, stride=CASES), :] = condensed[:dofs, lanes]
            far_part[pl.ds(k + i, dofs, stride=CASES), :] = condensed[dofs:, lanes]
    near = near_ref[...]
    slots = owner_slots(owner_ref[...], parts)
    near_sum_ref[...] = pick_right(near_part[...], near_onehot(near), NN)
    chosen = onehot(jnp.concatenate(slots, axis=0))
    put(pay_ref, pick_left(chosen, far_part[...], NT), 0, 10)
    lane = iota((parts, LANES), 1)
    far_row = (far_ref[...] + 1).astype(F32)
    near_row = (near + 1).astype(F32)
    message = jnp.zeros((parts, LANES), F32)
    own = jnp.zeros((parts, LANES), F32)
    for s in range(SLOTS):
        for at, row in ((0, far_row), (SLOTS, kind.astype(F32)), (2 * SLOTS, stiff_ref[...])):
            value = jnp.sum(jnp.where(slots[s], row, 0.0), axis=1, keepdims=True)
            message = jnp.where(lane == at + s, value, message)
        value = jnp.sum(jnp.where(slots[s], near_row, 0.0), axis=1, keepdims=True)
        own = jnp.where(lane == s, value, own)
    pay_ref[pl.ds(9, parts, stride=10), :] = message
    meta_ref[...] = own


def tables_kernel(
    kind_ref, stiff_ref, load_ref, inverse_ref, coupling_ref, block_ref,
    near_near, near_far, far_near, far_far, turned_near, turned_far, base_ref,
):
    dofs = block_ref.shape[1] // 2
    modes = inverse_ref.shape[1]
    inverses = []
    for t in range(KINDS):
        turned = dot_high(inverse_ref[t], coupling_ref[t], TN)
        schur = block_ref[t] - dot_high(turned, coupling_ref[t], TN)
        at = slice(t * dofs, (t + 1) * dofs)
        near_near[at, :] = stacked_table(schur[:dofs, :dofs])
        near_far[at, :] = stacked_table(schur[:dofs, dofs:])
        far_near[at, :] = stacked_table(schur[dofs:, :dofs])
        far_far[at, :] = stacked_table(schur[dofs:, dofs:])
        at = slice(t * modes, (t + 1) * modes)
        turned_near[at, :] = stacked_table(turned[:, :dofs])
        turned_far[at, :] = stacked_table(turned[:, dofs:])
        inverses.append(inverse_ref[t])
    left = stacked_table(jnp.concatenate(inverses, axis=0))
    kind = kind_ref[...]
    stiff = stiff_ref[...]
    kind2 = jnp.concatenate([kind, kind], axis=1)
    stiff2 = jnp.concatenate([stiff, stiff], axis=1)
    for k in range(0, CASES, 2):
        loads = jnp.concatenate(
            [load_ref[pl.ds(k + i, modes, stride=CASES), :] for i in range(2)], axis=1
        )
        result = by_kind(dot(left, stacked_values(loads)), kind2, modes) / stiff2
        for i in range(2):
            base_ref[pl.ds(k + i, modes, stride=CASES), :] = result[:, i * LANES : (i + 1) * LANES]


def send_ports(field, asked, own, pay_ref):
    put(pay_ref, pick_left(jnp.concatenate([asked, own], axis=0), field, NT), 0, 18)


def rhs_kernel(parts, arrived_ref, near_sum_ref, load_ref, meta_ref, field_ref, pay_ref, asked_ref):
    asked = arrived_ref[pl.ds(9, parts, stride=10), :]
    asked_ref[...] = asked
    asked_hot = port_onehot(asked)
    arrived = get(arrived_ref, 0, 10, 3)
    field = load_ref[...] + (near_sum_ref[...] + pick_right(arrived, asked_hot, TN))
    field_ref[...] = field
    send_ports(field, asked_hot, port_onehot(meta_ref[...]), pay_ref)


def component_products(table_ref, part_ref, kind_ref, stiff_ref, out_ref):
    dofs = part_ref.shape[0] // CASES
    kind, stiff = kind_ref[...], stiff_ref[...]
    kind2 = jnp.concatenate([kind, kind], axis=1)
    stiff2 = jnp.concatenate([stiff, stiff], axis=1)
    for k in range(0, CASES, 2):
        values = jnp.concatenate(
            [part_ref[pl.ds(k + i, dofs, stride=CASES), :] for i in range(2)], axis=1
        )
        result = by_kind(dot(table_ref[...], stacked_values(values)), kind2, dofs) * stiff2
        for i in range(2):
            out_ref[pl.ds(k + i, dofs, stride=CASES), :] = result[:, i * LANES : (i + 1) * LANES]


def slot_products(table_ref, slot_ref, asked, out_ref):
    tiles = slot_ref.shape[0]
    dofs = slot_ref.shape[1] // CASES
    spare = tiles * LANES - SLOTS * asked.shape[0]
    kind = pad_lanes(stacked_rows(asked, SLOTS), spare).astype(jnp.int32)
    stiff = pad_lanes(stacked_rows(asked, 2 * SLOTS), spare)
    for k in range(CASES):
        values = jnp.concatenate(
            [slot_ref[g, pl.ds(k, dofs, stride=CASES), :] for g in range(tiles)], axis=1
        )
        result = by_kind(dot(table_ref[...], stacked_values(values)), kind, dofs) * stiff
        for g in range(tiles):
            out_ref[g, pl.ds(k, dofs, stride=CASES), :] = result[:, g * LANES : (g + 1) * LANES]


def wide_onehot(asked_hot, tiles):
    spare = tiles * LANES - asked_hot.shape[0]
    if not spare:
        return asked_hot
    return jnp.concatenate([asked_hot, jnp.zeros((spare, LANES), BF16)], axis=0)


def slots_to_ports(part_ref, asked_hot):
    tiles = part_ref.shape[0]
    hot = wide_onehot(asked_hot, tiles)
    total = pick_right(part_ref[0], hot[:LANES], NN)
    for g in range(1, tiles):
        total = total + pick_right(part_ref[g], hot[g * LANES : (g + 1) * LANES], NN)
    return total


def inner_kernel(
    field_ref, asked_ref, kind_ref, stiff_ref, near_ref, near_near, far_far,
    inner_ref, near_values, near_part, slot_ref, slot_part,
):
    field, asked = field_ref[...], asked_ref[...]
    near_hot, asked_hot = near_onehot(near_ref[...]), port_onehot(asked)
    tiles = slot_ref.shape[0]
    near_values[...] = pick_right(field, near_hot, NT)
    values = pick_right(field, wide_onehot(asked_hot, tiles), NT)
    for g in range(tiles):
        slot_ref[g] = values[:, g * LANES : (g + 1) * LANES]
    component_products(near_near, near_values, kind_ref, stiff_ref, near_part)
    slot_products(far_far, slot_ref, asked, slot_part)
    inner_ref[...] = pick_right(near_part[...], near_hot, NN) + slots_to_ports(slot_part, asked_hot)


def near_cross(parts, arrived_ref, pitch, kind_ref, stiff_ref, near_ref, owner_ref, near_far, far_values, near_part):
    slots = onehot(jnp.concatenate(owner_slots(owner_ref[...], parts), axis=0))
    far_values[...] = pick_right(get(arrived_ref, 0, pitch, 3), slots, TN)
    component_products(near_far, far_values, kind_ref, stiff_ref, near_part)
    return pick_right(near_part[...], near_onehot(near_ref[...]), NN)


def far_cross(arrived_ref, first, pitch, asked, asked_hot, far_near, slot_ref, slot_part):
    tiles = slot_ref.shape[0]
    values = jnp.transpose(get(arrived_ref, first, pitch, 3))
    values = pad_lanes(values, tiles * LANES - values.shape[1])
    for g in range(tiles):
        slot_ref[g] = values[:, g * LANES : (g + 1) * LANES]
    slot_products(far_near, slot_ref, asked, slot_part)
    return slots_to_ports(slot_part, asked_hot)


def image_kernel(
    parts, groups, last, arrived_ref, inner_ref, asked_ref, kind_ref, stiff_ref, near_ref, owner_ref,
    near_far, far_near, *rest,
):
    if last:
        case_ref, gram_ref, rest = rest[0], rest[1], rest[2:]
        images, (image_ref, far_values, copies_ref, near_part, slot_ref, slot_part) = rest[:groups], rest[groups:]
    else:
        meta_ref, image_ref, far_values, pay_ref, near_part, slot_ref, slot_part = rest
    asked = asked_ref[...]
    asked_hot = port_onehot(asked)
    slots = onehot(jnp.concatenate(owner_slots(owner_ref[...], parts), axis=0))
    far_values[...] = pick_right(get(arrived_ref, 0, 18, 3), slots, TN)
    component_products(near_far, far_values, kind_ref, stiff_ref, near_part)
    tiles = slot_ref.shape[0]
    values = jnp.transpose(get(arrived_ref, 9, 18, 3))
    values = pad_lanes(values, tiles * LANES - values.shape[1])
    for g in range(tiles):
        slot_ref[g] = values[:, g * LANES : (g + 1) * LANES]
    slot_products(far_near, slot_ref, asked, slot_part)
    image = inner_ref[...] + pick_right(near_part[...], near_onehot(near_ref[...]), NN)
    image = image + slots_to_ports(slot_part, asked_hot)
    image_ref[...] = image
    if last:
        gram = add_products(LANES, images, [image_ref], [3 * groups * CASES], case_ref[0], gram_ref[...])
        for p in range(copies_ref.shape[0]):
            copies_ref[p] = gram
    else:
        send_ports(image, asked_hot, port_onehot(meta_ref[...]), pay_ref)


def turned_rows(near_values, far_values, kind_ref, turned_near, turned_far, out_ref):
    dofs = near_values.shape[0] // CASES
    modes = out_ref.shape[0] // CASES
    kind = kind_ref[...]
    kind2 = jnp.concatenate([kind, kind], axis=1)
    for k in range(0, CASES, 2):
        sums = 0.0
        for table, part in ((turned_near, near_values), (turned_far, far_values)):
            values = jnp.concatenate(
                [part[pl.ds(k + i, dofs, stride=CASES), :] for i in range(2)], axis=1
            )
            sums = sums + dot(table[...], stacked_values(values))
        result = by_kind(sums, kind2, modes)
        for i in range(2):
            out_ref[pl.ds(k + i, modes, stride=CASES), :] = result[:, i * LANES : (i + 1) * LANES]


def quarter(ref, case_ref, h, groups):
    part = ref.shape[0] // groups
    return ref[pl.ds(pl.multiple_of(lax.rem(case_ref[0] + h, groups) * part, part), part), :]


def turned_kernel(groups, first, case_ref, near_values, far_values, kind_ref, turned_near, turned_far, *rest):
    if not first:
        field_ref, rest = rest[0], rest[1:]
    outs, out_ref = rest[:groups], rest[groups]
    turned_rows(near_values, far_values, kind_ref, turned_near, turned_far, out_ref)
    for h in range(groups):
        at = 0
        if h and not first:
            at = field_ref.shape[0]
            outs[h][:at, :] = field_ref[...]
        outs[h][at:, :] = quarter(out_ref, case_ref, h, groups)


def add_products(lanes, lefts, rights, first, case, out):
    groups = len(lefts)
    total = groups * CASES
    dofs = lefts[0].shape[0] // CASES
    lane = iota((CASES, LANES), 1)
    for h in range(groups):
        def step(d, sums):
            own = pl.ds(pl.multiple_of(d * CASES, CASES), CASES)
            values = [ref[own, :] for ref in rights]
            new = []
            for i in range(CASES):
                row = lefts[h][pl.ds(d * CASES + i, 1), :]
                new.append(tuple(s + row * v for s, v in zip(sums[i], values)))
            return tuple(new)

        zero = jnp.zeros((CASES, LANES), F32)
        sums = lax.fori_loop(0, dofs, step, ((zero,) * len(rights),) * CASES)
        at = lax.rem(case + h, groups) * CASES
        for i in range(CASES):
            for g in range(len(rights)):
                value = jnp.sum(sums[i][g], axis=1, keepdims=True)
                out = jnp.where(lane == first[g] + at + i, value, out)
    return out


def gram_kernel(groups, case_ref, *refs):
    base, image, out_ref = refs[:groups], refs[groups : 2 * groups], refs[2 * groups]
    total = groups * CASES
    out = jnp.zeros((CASES, LANES), F32)
    out = add_products(LANES, base, [base[0], image[0]], [0, total], case_ref[0], out)
    out_ref[...] = add_products(LANES, image, [image[0]], [2 * total], case_ref[0], out)


def sum_kernel(in_ref, out_ref):
    for q in range(in_ref.shape[0]):
        total = in_ref[q, 0]
        for p in range(1, in_ref.shape[1]):
            total = total + in_ref[q, p]
        for p in range(out_ref.shape[0]):
            out_ref[p, q * CASES : (q + 1) * CASES, :] = total


def inverse2(p, q, r, s):
    scale = 1.0 / (p * s - q * r)
    return s * scale, -q * scale, -r * scale, p * scale


def spd_solve(matrix, target):
    n = matrix.shape[0]
    a = jnp.concatenate([matrix, target], axis=1)
    row_of = iota(a.shape, 0)
    for k in range(0, n, 4):
        c = [jnp.broadcast_to(a[:, k + i : k + i + 1], a.shape) for i in range(4)]
        r = [a[k + i : k + i + 1] for i in range(4)]
        p = [[c[j][k + i : k + i + 1] for j in range(4)] for i in range(4)]
        a00, a01, a10, a11 = inverse2(p[0][0], p[0][1], p[1][0], p[1][1])
        e00, e01 = p[2][0] * a00 + p[2][1] * a10, p[2][0] * a01 + p[2][1] * a11
        e10, e11 = p[3][0] * a00 + p[3][1] * a10, p[3][0] * a01 + p[3][1] * a11
        i00, i01, i10, i11 = inverse2(
            p[2][2] - (e00 * p[0][2] + e01 * p[1][2]),
            p[2][3] - (e00 * p[0][3] + e01 * p[1][3]),
            p[3][2] - (e10 * p[0][2] + e11 * p[1][2]),
            p[3][3] - (e10 * p[0][3] + e11 * p[1][3]),
        )
        t2 = r[2] - (e00 * r[0] + e01 * r[1])
        t3 = r[3] - (e10 * r[0] + e11 * r[1])
        u2, u3 = i00 * t2 + i01 * t3, i10 * t2 + i11 * t3
        w0 = r[0] - (p[0][2] * u2 + p[0][3] * u3)
        w1 = r[1] - (p[1][2] * u2 + p[1][3] * u3)
        u = [a00 * w0 + a01 * w1, a10 * w0 + a11 * w1, u2, u3]
        a = a - ((c[0] * u[0] + c[1] * u[1]) + (c[2] * u[2] + c[3] * u[3]))
        for i in range(4):
            a = jnp.where(row_of == k + i, u[i], a)
    return a[:, n:]


def symmetric(m):
    return 0.5 * (m + jnp.transpose(m))


def solve_kernel(groups, case_ref, gram_ref, coef, coef_rows, turned_coef):
    n = groups * CASES
    total = gram_ref[0]
    for p in range(1, gram_ref.shape[0]):
        total = total + gram_ref[p]
    g00, g01, g11, g12 = [symmetric(total[:, g * n : (g + 1) * n]) for g in range(4)]
    steps = spd_solve(g01, jnp.concatenate([g00, g11], axis=1))
    step0, step1 = steps[:, :n], steps[:, n:]
    both = dot_high(g11, steps)
    second = spd_solve(symmetric(g12 - both[:, n:]), g01 - both[:, :n])
    first = step0 - dot_high(step1, second)
    first, second = jnp.transpose(first), jnp.transpose(second)
    turned_coef[0] = jnp.concatenate([first] * (LANES // n), axis=1)
    turned_coef[1] = jnp.concatenate([second] * (LANES // n), axis=1)
    shift = LANES - case_ref[0] * CASES
    for q in range(groups):
        at = pl.multiple_of(lax.rem(case_ref[0] + q, groups) * CASES, CASES)
        for h in range(2):
            mine = pltpu.roll(turned_coef[h, pl.ds(at, CASES), :], shift, 1)
            coef_rows[q * CASES : (q + 1) * CASES, h * LANES : (h + 1) * LANES] = mine
            if q == 0:
                for j in range(n):
                    coef[h * n + j] = jnp.broadcast_to(mine[:, j : j + 1], (CASES, LANES))


def bubble_kernel(groups, rows, coef_ref, *refs):
    turned0, turned1, outs = refs[:groups], refs[groups : 2 * groups], refs[2 * groups :]
    n = groups * CASES
    part = turned0[0].shape[0]
    coef = jnp.concatenate([coef_ref[:, :n], coef_ref[:, LANES : LANES + n]], axis=1)
    left = stacked_table(coef)
    for m in range(0, part // CASES, 2):
        values = []
        for i in range(2):
            at = (m + i) * CASES
            pieces = [ref[at : at + CASES, :] for ref in turned0]
            pieces += [ref[at + shift : at + shift + CASES, :] for ref, shift in zip(turned1, [0] + [rows] * (groups - 1))]
            values.append(jnp.concatenate(pieces, axis=0))
        result = dot(left, stacked_values(jnp.concatenate(values, axis=1)))
        for i in range(2):
            for h in range(groups):
                outs[h][(m + i) * CASES : (m + i + 1) * CASES, :] = result[
                    h * CASES : (h + 1) * CASES, i * LANES : (i + 1) * LANES
                ]


def ports_kernel(groups, coef, *refs):
    base, image, second = [refs[g * groups : (g + 1) * groups] for g in range(3)]
    x_ref, residual_ref = refs[3 * groups :]
    n = groups * CASES
    dofs = x_ref.shape[0] // CASES
    wide = 4

    def ports(block, carry):
        d0 = block * wide
        own = [pl.ds(pl.multiple_of((d0 + i) * CASES, CASES), CASES) for i in range(wide)]
        x = [jnp.zeros((CASES, LANES), F32)] * wide
        r = [base[0][own[i], :] for i in range(wide)]
        for j in range(n):
            q, c = divmod(j, CASES)
            c0, c1 = coef[j], coef[n + j]
            for i in range(wide):
                row = pl.ds((d0 + i) * CASES + c, 1)
                a = image[q][row, :]
                x[i] = x[i] + (c0 * base[q][row, :] + c1 * a)
                r[i] = r[i] - (c0 * a + c1 * second[q][row, :])
        for i in range(wide):
            x_ref[own[i], :] = x[i]
            residual_ref[own[i], :] = r[i]
        return carry

    lax.fori_loop(0, dofs // wide, ports, 0)


def join_kernel(groups, case_ref, bubble_ref, *refs):
    parts, out_ref = refs[:groups], refs[groups]
    part = parts[0].shape[0]
    for h in range(groups):
        at = pl.ds(pl.multiple_of(lax.rem(case_ref[0] + h, groups) * part, part), part)
        out_ref[at, :] = bubble_ref[at, :] - parts[h][...]


def call(kernel, outs, scratch=(), name=None, flops=0, smem=(), hbm=False):
    outs = [jax.ShapeDtypeStruct(shape, dtype) for shape, dtype in outs]
    vmem = pl.BlockSpec(memory_space=pltpu.VMEM)

    def run(*args):
        usual = pl.BlockSpec(memory_space=pltpu.HBM) if hbm else vmem
        specs = [pl.BlockSpec(memory_space=pltpu.SMEM) if i in smem else usual for i in range(len(args))]
        moved = sum(a.size * a.dtype.itemsize for a in args) + sum(o.size * o.dtype.itemsize for o in outs)
        fetched = [pltpu.VMEM(a.shape, a.dtype) for a in args] if hbm else []
        sems = [pltpu.SemaphoreType.DMA((len(args),))] if hbm else []
        return pl.pallas_call(
            kernel,
            out_shape=outs,
            in_specs=specs,
            out_specs=[vmem] * len(outs),
            scratch_shapes=fetched + [pltpu.VMEM(shape, F32) for shape in scratch] + sems,
            compiler_params=pltpu.CompilerParams(vmem_limit_bytes=12 << 20),
            cost_estimate=pl.CostEstimate(flops=flops, bytes_accessed=moved, transcendentals=0),
            name=name,
        )(*args)

    return run


def exchange(rows, parts):
    moved = lax.all_to_all(rows.reshape(parts, 1, -1), PLANE, split_axis=0, concat_axis=0)
    return moved.reshape(rows.shape)


def local(
    comp_type, stiffness, near_port, far_owner, far_port, bubble_load, port_load,
    bubble_inverse, coupling, port_block,
):
    parts = lax.axis_size("px") * lax.axis_size("py")
    groups = lax.axis_size("case")
    modes, cases, comps = bubble_load.shape
    dofs, _, ports = port_load.shape
    rows, bubbles = dofs * cases, modes * cases
    slot_tiles = -(-SLOTS * parts // LANES)
    coupling = jnp.swapaxes(coupling, 1, 2)
    kind = comp_type.reshape(1, comps)
    stiff = stiffness.reshape(1, comps)
    near = near_port.reshape(1, comps)
    owner = far_owner.reshape(1, comps)
    far = far_port.reshape(1, comps)
    loads = bubble_load.reshape(bubbles, comps)
    field_of = ((rows, ports), F32)
    meta_of = ((parts, LANES), F32)
    pay, near_sum, meta = call(
        functools.partial(condense_kernel, parts),
        [((parts * 10, LANES), F32), field_of, meta_of],
        [(rows, comps)] * 2,
        "condense",
        hbm=True,
    )(kind, stiff, near, owner, far, loads, bubble_inverse, coupling)
    near_near, near_far, far_near, far_far, turned_near, turned_far, bubble_base = call(
        tables_kernel,
        [((KINDS * dofs, 3 * dofs), BF16)] * 4 + [((KINDS * modes, 3 * dofs), BF16)] * 2 + [((bubbles, comps), F32)],
        name="tables",
        flops=10**9,
    )(kind, stiff, loads, bubble_inverse, coupling, port_block)
    base, pay, asked = call(
        functools.partial(rhs_kernel, parts),
        [field_of, ((parts * 18, LANES), F32), meta_of],
        name="rhs",
    )(exchange(pay, parts), near_sum, port_load.reshape(rows, ports), meta)

    case = lax.axis_index("case").reshape(1)
    part = bubbles // groups
    part_of = ((part, comps), F32)
    slot_scratch = [(slot_tiles, rows, LANES)] * 2
    where = (kind, stiff, near, owner)

    def to_cases(messages):
        backward = [
            lax.ppermute(message, "case", [(k, (k + h) % groups) for k in range(groups)])
            for h, message in enumerate(messages, 1)
        ]
        return backward[::-1]

    def inner(field):
        return call(inner_kernel, [field_of] * 2, [(rows, comps)] + slot_scratch, "inner", flops=10**9)(
            field, asked, kind, stiff, near, near_near, far_far
        )

    arrived = exchange(pay, parts)
    base_all = to_cases([base] * (groups - 1))
    base_inner, base_near = inner(base)
    arrived, *base_all = lax.optimization_barrier((arrived, *base_all))
    image, base_far, pay = call(
        functools.partial(image_kernel, parts, groups, False),
        [field_of] * 2 + [((parts * 18, LANES), F32)],
        [(rows, comps)] + slot_scratch,
        "image",
    )(arrived, base_inner, asked, *where, near_far, far_near, meta)
    arrived = exchange(pay, parts)
    image_all = to_cases([image] * (groups - 1))
    image_inner, image_near = inner(image)
    turned0, *messages = call(
        functools.partial(turned_kernel, groups, True),
        [part_of] * groups,
        [(bubbles, comps)],
        name="turned",
        flops=10**9,
        smem=(0,),
    )(case, base_near, base_far, kind, turned_near, turned_far)
    turned0_all = to_cases(messages)
    (gram,) = call(functools.partial(gram_kernel, groups), [((cases, LANES), F32)], name="gram", smem=(0,))(
        case, base, *base_all, image, *image_all
    )
    arrived, *turned0_all = lax.optimization_barrier((arrived, *turned0_all))
    minor = lax.axis_size("py")
    second, image_far, copies = call(
        functools.partial(image_kernel, parts, groups, True),
        [field_of] * 2 + [((groups * minor, cases, LANES), F32)],
        [(rows, comps)] + slot_scratch,
        "second",
        smem=(9,),
    )(arrived, image_inner, asked, *where, near_far, far_near, case, gram, image, *image_all)
    copies = lax.all_to_all(copies, ("case", "py"), split_axis=0, concat_axis=0)
    turned1, *messages = call(
        functools.partial(turned_kernel, groups, False),
        [part_of] + [((rows + part, comps), F32)] * (groups - 1),
        [(bubbles, comps)],
        "turned_second",
        flops=10**9,
        smem=(0,),
    )(case, image_near, image_far, kind, turned_near, turned_far, second)
    both1 = to_cases(messages)
    (copies,) = call(sum_kernel, [((parts // minor, groups * cases, LANES), F32)], name="sum")(
        copies.reshape(groups, minor, cases, LANES)
    )
    copies = lax.all_to_all(copies, "px", split_axis=0, concat_axis=0)
    coef, coef_rows = call(
        functools.partial(solve_kernel, groups),
        [((2 * groups * cases, cases, LANES), F32), ((groups * cases, 2 * LANES), F32)],
        [(2, groups * cases, LANES)],
        "solve",
        smem=(0,),
    )(case, copies)
    own, *messages = call(
        functools.partial(bubble_kernel, groups, rows), [part_of] * groups, name="bubble"
    )(coef_rows, turned0, *turned0_all, turned1, *both1)
    back = to_cases(messages)
    x, residual = call(
        functools.partial(ports_kernel, groups), [field_of, field_of], name="ports", flops=10**9
    )(coef, base, *base_all, image, *image_all, second, *both1)
    (bubble,) = call(functools.partial(join_kernel, groups), [((bubbles, comps), F32)], name="join", smem=(0,))(
        case, bubble_base, own, *back
    )
    return (
        x.reshape(port_load.shape),
        residual.reshape(port_load.shape),
        bubble.reshape(bubble_load.shape),
    )


def solution(mesh):
    placed = (
        P(PLANE),
        P(PLANE),
        P(PLANE),
        P(PLANE, None),
        P(PLANE),
        P(None, "case", PLANE),
        P(None, "case", PLANE),
        P(),
        P(),
        P(),
    )
    out = P(None, "case", PLANE)
    return jax.shard_map(
        local, mesh=mesh, in_specs=placed, out_specs=(out, out, out), check_vma=False
    )
```

```python
import functools

import jax
import jax.numpy as jnp
from jax import lax
from jax.experimental import pallas as pl
from jax.experimental.pallas import tpu as pltpu
from jax.sharding import PartitionSpec as P

HIGH = lax.Precision.HIGHEST
PLANE = ("px", "py")
EVERY = ("px", "py", "case")
F32 = jnp.float32
BF16 = jnp.bfloat16
KINDS = 8
LANES = 128
CASES = 8
SLOTS = 3
NN = (((1,), (0,)), ((), ()))
NT = (((1,), (1,)), ((), ()))
TN = (((0,), (0,)), ((), ()))


def dot(lhs, rhs, dims=NN):
    return lax.dot_general(lhs, rhs, dims, preferred_element_type=F32)


def dot_high(lhs, rhs, dims=NN):
    return lax.dot_general(lhs, rhs, dims, precision=HIGH, preferred_element_type=F32)


def split2(x):
    high = x.astype(BF16)
    return high, (x - high.astype(F32)).astype(BF16)


def pick_right(x, onehot, dims):
    (left,), (right,) = dims[0]
    return dot(jnp.concatenate(split2(x), axis=left), jnp.concatenate([onehot, onehot], axis=right), dims)


def pick_left(onehot, x, dims):
    (left,), (right,) = dims[0]
    return dot(jnp.concatenate([onehot, onehot], axis=left), jnp.concatenate(split2(x), axis=right), dims)


def stacked_table(table):
    high, low = split2(table)
    return jnp.concatenate([high, high, low], axis=1)


def stacked_values(x):
    high, low = split2(x)
    return jnp.concatenate([high, low, high], axis=0)


def iota(shape, dim):
    return lax.broadcasted_iota(jnp.int32, shape, dim)


def column(row):
    return jnp.transpose(jnp.broadcast_to(row, (8, row.shape[1])))[:, :1]


def onehot(mask):
    return mask.astype(F32).astype(BF16)


def owner_slots(owner, parts):
    count = owner.shape[1]
    owner_f = owner.astype(F32)
    same = (column(owner_f) == owner_f) & (iota((count, count), 0) < iota((count, count), 1))
    rank = jnp.sum(same.astype(F32), axis=0, keepdims=True).astype(jnp.int32)
    to = iota((parts, count), 0) == owner
    return [to & (rank == s) for s in range(SLOTS)]


def near_onehot(near):
    count = near.shape[1]
    return onehot(column(near.astype(F32)) == iota((count, LANES), 1).astype(F32))


def stacked_rows(meta, lanes):
    turned = jnp.transpose(meta)
    return jnp.concatenate([turned[lanes + s : lanes + s + 1, :] for s in range(SLOTS)], axis=1)


def port_onehot(meta):
    parts = meta.shape[0]
    ports = (iota((parts, LANES), 1) + 1).astype(F32)
    return onehot(jnp.concatenate([meta[:, s : s + 1] == ports for s in range(SLOTS)], axis=0))


def pad_lanes(x, spare):
    if not spare:
        return x
    return jnp.concatenate([x, jnp.zeros((x.shape[0], spare), x.dtype)], axis=1)


def put(pay_ref, rows, first, pitch):
    parts = pay_ref.shape[0] // pitch
    tiles = rows.shape[1] // LANES
    for g in range(rows.shape[0] // parts):
        for t in range(tiles):
            pay_ref[pl.ds(first + g * tiles + t, parts, stride=pitch), :] = rows[
                g * parts : (g + 1) * parts, t * LANES : (t + 1) * LANES
            ]


def get(pay_ref, first, pitch, tiles):
    parts = pay_ref.shape[0] // pitch
    return jnp.concatenate(
        [
            jnp.concatenate(
                [pay_ref[pl.ds(first + s * tiles + t, parts, stride=pitch), :] for t in range(tiles)],
                axis=1,
            )
            for s in range(SLOTS)
        ],
        axis=0,
    )


def by_kind(products, kind, rows):
    chosen = products[:rows]
    for t in range(1, KINDS):
        chosen = jnp.where(kind == t, products[t * rows : (t + 1) * rows], chosen)
    return chosen


def condense_kernel(
    parts, kind_hbm, stiff_hbm, near_hbm, owner_hbm, far_hbm, load_hbm, inverse_hbm, coupling_hbm,
    pay_ref, near_sum_ref, meta_ref,
    kind_ref, stiff_ref, near_ref, owner_ref, far_ref, load_ref, inverse_ref, coupling_ref, near_part, far_part, sems,
):
    copies = [
        pltpu.make_async_copy(source, target, sems.at[i])
        for i, (source, target) in enumerate((
            (inverse_hbm, inverse_ref), (coupling_hbm, coupling_ref), (load_hbm, load_ref), (kind_hbm, kind_ref),
            (stiff_hbm, stiff_ref), (near_hbm, near_ref), (owner_hbm, owner_ref), (far_hbm, far_ref),
        ))
    ]
    for copy in copies:
        copy.start()
    for copy in copies:
        copy.wait()
    modes = load_ref.shape[0] // CASES
    dofs = near_sum_ref.shape[0] // CASES
    left = stacked_table(
        jnp.concatenate(
            [jnp.transpose(dot_high(inverse_ref[t], coupling_ref[t], TN)) for t in range(KINDS)], axis=0
        )
    )
    kind = kind_ref[...]
    kind2 = jnp.concatenate([kind, kind], axis=1)
    for k in range(0, CASES, 2):
        loads = jnp.concatenate(
            [load_ref[pl.ds(k + i, modes, stride=CASES), :] for i in range(2)], axis=1
        )
        condensed = -by_kind(dot(left, stacked_values(loads)), kind2, 2 * dofs)
        for i in range(2):
            lanes = slice(i * LANES, (i + 1) * LANES)
            near_part[pl.ds(k + i, dofs, stride=CASES), :] = condensed[:dofs, lanes]
            far_part[pl.ds(k + i, dofs, stride=CASES), :] = condensed[dofs:, lanes]
    near = near_ref[...]
    slots = owner_slots(owner_ref[...], parts)
    near_sum_ref[...] = pick_right(near_part[...], near_onehot(near), NN)
    chosen = onehot(jnp.concatenate(slots, axis=0))
    put(pay_ref, pick_left(chosen, far_part[...], NT), 0, 10)
    lane = iota((parts, LANES), 1)
    far_row = (far_ref[...] + 1).astype(F32)
    near_row = (near + 1).astype(F32)
    message = jnp.zeros((parts, LANES), F32)
    own = jnp.zeros((parts, LANES), F32)
    for s in range(SLOTS):
        for at, row in ((0, far_row), (SLOTS, kind.astype(F32)), (2 * SLOTS, stiff_ref[...])):
            value = jnp.sum(jnp.where(slots[s], row, 0.0), axis=1, keepdims=True)
            message = jnp.where(lane == at + s, value, message)
        value = jnp.sum(jnp.where(slots[s], near_row, 0.0), axis=1, keepdims=True)
        own = jnp.where(lane == s, value, own)
    pay_ref[pl.ds(9, parts, stride=10), :] = message
    meta_ref[...] = own


def tables_kernel(
    kind_ref, stiff_ref, load_ref, inverse_ref, coupling_ref, block_ref,
    near_near, near_far, far_near, far_far, turned_near, turned_far, base_ref,
):
    dofs = block_ref.shape[1] // 2
    modes = inverse_ref.shape[1]
    inverses = []
    for t in range(KINDS):
        turned = dot_high(inverse_ref[t], coupling_ref[t], TN)
        schur = block_ref[t] - dot_high(turned, coupling_ref[t], TN)
        at = slice(t * dofs, (t + 1) * dofs)
        near_near[at, :] = stacked_table(schur[:dofs, :dofs])
        near_far[at, :] = stacked_table(schur[:dofs, dofs:])
        far_near[at, :] = stacked_table(schur[dofs:, :dofs])
        far_far[at, :] = stacked_table(schur[dofs:, dofs:])
        at = slice(t * modes, (t + 1) * modes)
        turned_near[at, :] = stacked_table(turned[:, :dofs])
        turned_far[at, :] = stacked_table(turned[:, dofs:])
        inverses.append(inverse_ref[t])
    left = stacked_table(jnp.concatenate(inverses, axis=0))
    kind = kind_ref[...]
    stiff = stiff_ref[...]
    kind2 = jnp.concatenate([kind, kind], axis=1)
    stiff2 = jnp.concatenate([stiff, stiff], axis=1)
    for k in range(0, CASES, 2):
        loads = jnp.concatenate(
            [load_ref[pl.ds(k + i, modes, stride=CASES), :] for i in range(2)], axis=1
        )
        result = by_kind(dot(left, stacked_values(loads)), kind2, modes) / stiff2
        for i in range(2):
            base_ref[pl.ds(k + i, modes, stride=CASES), :] = result[:, i * LANES : (i + 1) * LANES]


def send_ports(field, asked, own, pay_ref):
    put(pay_ref, pick_left(jnp.concatenate([asked, own], axis=0), field, NT), 0, 18)


def rhs_kernel(parts, arrived_ref, near_sum_ref, load_ref, meta_ref, field_ref, pay_ref, asked_ref):
    asked = arrived_ref[pl.ds(9, parts, stride=10), :]
    asked_ref[...] = asked
    asked_hot = port_onehot(asked)
    arrived = get(arrived_ref, 0, 10, 3)
    field = load_ref[...] + (near_sum_ref[...] + pick_right(arrived, asked_hot, TN))
    field_ref[...] = field
    send_ports(field, asked_hot, port_onehot(meta_ref[...]), pay_ref)


def component_products(table_ref, part_ref, kind_ref, stiff_ref, out_ref):
    dofs = part_ref.shape[0] // CASES
    kind, stiff = kind_ref[...], stiff_ref[...]
    kind2 = jnp.concatenate([kind, kind], axis=1)
    stiff2 = jnp.concatenate([stiff, stiff], axis=1)
    for k in range(0, CASES, 2):
        values = jnp.concatenate(
            [part_ref[pl.ds(k + i, dofs, stride=CASES), :] for i in range(2)], axis=1
        )
        result = by_kind(dot(table_ref[...], stacked_values(values)), kind2, dofs) * stiff2
        for i in range(2):
            out_ref[pl.ds(k + i, dofs, stride=CASES), :] = result[:, i * LANES : (i + 1) * LANES]


def slot_products(table_ref, slot_ref, asked, out_ref):
    tiles = slot_ref.shape[0]
    dofs = slot_ref.shape[1] // CASES
    spare = tiles * LANES - SLOTS * asked.shape[0]
    kind = pad_lanes(stacked_rows(asked, SLOTS), spare).astype(jnp.int32)
    stiff = pad_lanes(stacked_rows(asked, 2 * SLOTS), spare)
    for k in range(CASES):
        values = jnp.concatenate(
            [slot_ref[g, pl.ds(k, dofs, stride=CASES), :] for g in range(tiles)], axis=1
        )
        result = by_kind(dot(table_ref[...], stacked_values(values)), kind, dofs) * stiff
        for g in range(tiles):
            out_ref[g, pl.ds(k, dofs, stride=CASES), :] = result[:, g * LANES : (g + 1) * LANES]


def wide_onehot(asked_hot, tiles):
    spare = tiles * LANES - asked_hot.shape[0]
    if not spare:
        return asked_hot
    return jnp.concatenate([asked_hot, jnp.zeros((spare, LANES), BF16)], axis=0)


def slots_to_ports(part_ref, asked_hot):
    tiles = part_ref.shape[0]
    hot = wide_onehot(asked_hot, tiles)
    total = pick_right(part_ref[0], hot[:LANES], NN)
    for g in range(1, tiles):
        total = total + pick_right(part_ref[g], hot[g * LANES : (g + 1) * LANES], NN)
    return total


def inner_kernel(
    field_ref, asked_ref, kind_ref, stiff_ref, near_ref, near_near, far_far,
    inner_ref, near_values, near_part, slot_ref, slot_part,
):
    field, asked = field_ref[...], asked_ref[...]
    near_hot, asked_hot = near_onehot(near_ref[...]), port_onehot(asked)
    tiles = slot_ref.shape[0]
    near_values[...] = pick_right(field, near_hot, NT)
    values = pick_right(field, wide_onehot(asked_hot, tiles), NT)
    for g in range(tiles):
        slot_ref[g] = values[:, g * LANES : (g + 1) * LANES]
    component_products(near_near, near_values, kind_ref, stiff_ref, near_part)
    slot_products(far_far, slot_ref, asked, slot_part)
    inner_ref[...] = pick_right(near_part[...], near_hot, NN) + slots_to_ports(slot_part, asked_hot)


def near_cross(parts, arrived_ref, pitch, kind_ref, stiff_ref, near_ref, owner_ref, near_far, far_values, near_part):
    slots = onehot(jnp.concatenate(owner_slots(owner_ref[...], parts), axis=0))
    far_values[...] = pick_right(get(arrived_ref, 0, pitch, 3), slots, TN)
    component_products(near_far, far_values, kind_ref, stiff_ref, near_part)
    return pick_right(near_part[...], near_onehot(near_ref[...]), NN)


def far_cross(arrived_ref, first, pitch, asked, asked_hot, far_near, slot_ref, slot_part):
    tiles = slot_ref.shape[0]
    values = jnp.transpose(get(arrived_ref, first, pitch, 3))
    values = pad_lanes(values, tiles * LANES - values.shape[1])
    for g in range(tiles):
        slot_ref[g] = values[:, g * LANES : (g + 1) * LANES]
    slot_products(far_near, slot_ref, asked, slot_part)
    return slots_to_ports(slot_part, asked_hot)


def image_kernel(
    parts, groups, last, arrived_ref, inner_ref, asked_ref, kind_ref, stiff_ref, near_ref, owner_ref,
    near_far, far_near, *rest,
):
    if last:
        case_ref, gram_ref, near_values, turned_near, turned_far = rest[:5]
        images, rest = rest[5 : 5 + groups], rest[5 + groups :]
        image_ref, copies_ref, turned_ref, near_part, slot_ref, slot_part, far_values = rest
    else:
        meta_ref, image_ref, far_values, pay_ref, near_part, slot_ref, slot_part = rest
    asked = asked_ref[...]
    asked_hot = port_onehot(asked)
    slots = onehot(jnp.concatenate(owner_slots(owner_ref[...], parts), axis=0))
    far_values[...] = pick_right(get(arrived_ref, 0, 18, 3), slots, TN)
    component_products(near_far, far_values, kind_ref, stiff_ref, near_part)
    tiles = slot_ref.shape[0]
    values = jnp.transpose(get(arrived_ref, 9, 18, 3))
    values = pad_lanes(values, tiles * LANES - values.shape[1])
    for g in range(tiles):
        slot_ref[g] = values[:, g * LANES : (g + 1) * LANES]
    slot_products(far_near, slot_ref, asked, slot_part)
    image = inner_ref[...] + pick_right(near_part[...], near_onehot(near_ref[...]), NN)
    image = image + slots_to_ports(slot_part, asked_hot)
    image_ref[...] = image
    if last:
        gram = add_products(LANES, images, [image_ref], [3 * groups * CASES], case_ref[0], gram_ref[...])
        for p in range(copies_ref.shape[0]):
            copies_ref[p] = gram
        turned_rows(near_values, far_values, kind_ref, turned_near, turned_far, turned_ref)
    else:
        send_ports(image, asked_hot, port_onehot(meta_ref[...]), pay_ref)


def turned_rows(near_values, far_values, kind_ref, turned_near, turned_far, out_ref):
    dofs = near_values.shape[0] // CASES
    modes = out_ref.shape[0] // CASES
    kind = kind_ref[...]
    kind2 = jnp.concatenate([kind, kind], axis=1)
    for k in range(0, CASES, 2):
        sums = 0.0
        for table, part in ((turned_near, near_values), (turned_far, far_values)):
            values = jnp.concatenate(
                [part[pl.ds(k + i, dofs, stride=CASES), :] for i in range(2)], axis=1
            )
            sums = sums + dot(table[...], stacked_values(values))
        result = by_kind(sums, kind2, modes)
        for i in range(2):
            out_ref[pl.ds(k + i, modes, stride=CASES), :] = result[:, i * LANES : (i + 1) * LANES]


def quarter(ref, case_ref, h, groups):
    part = ref.shape[0] // groups
    return ref[pl.ds(pl.multiple_of(lax.rem(case_ref[0] + h, groups) * part, part), part), :]


def turned_kernel(groups, case_ref, near_values, far_values, kind_ref, turned_near, turned_far, *rest):
    outs, out_ref = rest[:groups], rest[groups]
    turned_rows(near_values, far_values, kind_ref, turned_near, turned_far, out_ref)
    for h in range(groups):
        outs[h][...] = quarter(out_ref, case_ref, h, groups)


def messages_kernel(groups, case_ref, field_ref, turned_ref, own_ref, *messages):
    rows = field_ref.shape[0]
    own_ref[...] = quarter(turned_ref, case_ref, 0, groups)
    for h in range(1, groups):
        messages[h - 1][:rows, :] = field_ref[...]
        messages[h - 1][rows:, :] = quarter(turned_ref, case_ref, h, groups)


def add_products(lanes, lefts, rights, first, case, out):
    groups = len(lefts)
    total = groups * CASES
    dofs = lefts[0].shape[0] // CASES
    lane = iota((CASES, LANES), 1)
    for h in range(groups):
        def step(d, sums):
            own = pl.ds(pl.multiple_of(d * CASES, CASES), CASES)
            values = [ref[own, :] for ref in rights]
            new = []
            for i in range(CASES):
                row = lefts[h][pl.ds(d * CASES + i, 1), :]
                new.append(tuple(s + row * v for s, v in zip(sums[i], values)))
            return tuple(new)

        zero = jnp.zeros((CASES, LANES), F32)
        sums = lax.fori_loop(0, dofs, step, ((zero,) * len(rights),) * CASES)
        at = lax.rem(case + h, groups) * CASES
        for i in range(CASES):
            for g in range(len(rights)):
                value = jnp.sum(sums[i][g], axis=1, keepdims=True)
                out = jnp.where(lane == first[g] + at + i, value, out)
    return out


def gram_kernel(groups, case_ref, *refs):
    base, image, out_ref = refs[:groups], refs[groups : 2 * groups], refs[2 * groups]
    total = groups * CASES
    out = jnp.zeros((CASES, LANES), F32)
    out = add_products(LANES, base, [base[0], image[0]], [0, total], case_ref[0], out)
    out_ref[...] = add_products(LANES, image, [image[0]], [2 * total], case_ref[0], out)


def sum_kernel(in_ref, out_ref):
    total = in_ref[0]
    for p in range(1, in_ref.shape[0]):
        total = total + in_ref[p]
    for p in range(out_ref.shape[0]):
        out_ref[p] = total


def inverse2(p, q, r, s):
    scale = 1.0 / (p * s - q * r)
    return s * scale, -q * scale, -r * scale, p * scale


def spd_solve(matrix, target):
    n = matrix.shape[0]
    a = jnp.concatenate([matrix, target], axis=1)
    row_of = iota(a.shape, 0)
    for k in range(0, n, 4):
        c = [jnp.broadcast_to(a[:, k + i : k + i + 1], a.shape) for i in range(4)]
        r = [a[k + i : k + i + 1] for i in range(4)]
        p = [[c[j][k + i : k + i + 1] for j in range(4)] for i in range(4)]
        a00, a01, a10, a11 = inverse2(p[0][0], p[0][1], p[1][0], p[1][1])
        e00, e01 = p[2][0] * a00 + p[2][1] * a10, p[2][0] * a01 + p[2][1] * a11
        e10, e11 = p[3][0] * a00 + p[3][1] * a10, p[3][0] * a01 + p[3][1] * a11
        i00, i01, i10, i11 = inverse2(
            p[2][2] - (e00 * p[0][2] + e01 * p[1][2]),
            p[2][3] - (e00 * p[0][3] + e01 * p[1][3]),
            p[3][2] - (e10 * p[0][2] + e11 * p[1][2]),
            p[3][3] - (e10 * p[0][3] + e11 * p[1][3]),
        )
        t2 = r[2] - (e00 * r[0] + e01 * r[1])
        t3 = r[3] - (e10 * r[0] + e11 * r[1])
        u2, u3 = i00 * t2 + i01 * t3, i10 * t2 + i11 * t3
        w0 = r[0] - (p[0][2] * u2 + p[0][3] * u3)
        w1 = r[1] - (p[1][2] * u2 + p[1][3] * u3)
        u = [a00 * w0 + a01 * w1, a10 * w0 + a11 * w1, u2, u3]
        a = a - ((c[0] * u[0] + c[1] * u[1]) + (c[2] * u[2] + c[3] * u[3]))
        for i in range(4):
            a = jnp.where(row_of == k + i, u[i], a)
    return a[:, n:]


def symmetric(m):
    return 0.5 * (m + jnp.transpose(m))


def solve_kernel(groups, case_ref, gram_ref, coef, coef_rows, turned_coef):
    n = groups * CASES
    each = gram_ref.shape[0] // groups
    rows = []
    for q in range(groups):
        rows.append(gram_ref[q * each])
        for p in range(1, each):
            rows[q] = rows[q] + gram_ref[q * each + p]
    total = jnp.concatenate(rows, axis=0)
    g00, g01, g11, g12 = [symmetric(total[:, g * n : (g + 1) * n]) for g in range(4)]
    steps = spd_solve(g01, jnp.concatenate([g00, g11], axis=1))
    step0, step1 = steps[:, :n], steps[:, n:]
    both = dot_high(g11, steps)
    second = spd_solve(symmetric(g12 - both[:, n:]), g01 - both[:, :n])
    first = step0 - dot_high(step1, second)
    first, second = jnp.transpose(first), jnp.transpose(second)
    turned_coef[0] = jnp.concatenate([first] * (LANES // n), axis=1)
    turned_coef[1] = jnp.concatenate([second] * (LANES // n), axis=1)
    shift = LANES - case_ref[0] * CASES
    for q in range(groups):
        at = pl.multiple_of(lax.rem(case_ref[0] + q, groups) * CASES, CASES)
        for h in range(2):
            mine = pltpu.roll(turned_coef[h, pl.ds(at, CASES), :], shift, 1)
            coef_rows[q * CASES : (q + 1) * CASES, h * LANES : (h + 1) * LANES] = mine
            if q == 0:
                for j in range(n):
                    coef[h * n + j] = jnp.broadcast_to(mine[:, j : j + 1], (CASES, LANES))


def bubble_kernel(groups, rows, coef_ref, *refs):
    turned0, turned1, outs = refs[:groups], refs[groups : 2 * groups], refs[2 * groups :]
    n = groups * CASES
    part = turned0[0].shape[0]
    coef = jnp.concatenate([coef_ref[:, :n], coef_ref[:, LANES : LANES + n]], axis=1)
    left = stacked_table(coef)
    for m in range(0, part // CASES, 2):
        values = []
        for i in range(2):
            at = (m + i) * CASES
            pieces = [ref[at : at + CASES, :] for ref in turned0]
            pieces += [ref[at + shift : at + shift + CASES, :] for ref, shift in zip(turned1, [0] + [rows] * (groups - 1))]
            values.append(jnp.concatenate(pieces, axis=0))
        result = dot(left, stacked_values(jnp.concatenate(values, axis=1)))
        for i in range(2):
            for h in range(groups):
                outs[h][(m + i) * CASES : (m + i + 1) * CASES, :] = result[
                    h * CASES : (h + 1) * CASES, i * LANES : (i + 1) * LANES
                ]


def ports_kernel(groups, coef, *refs):
    base, image, second = [refs[g * groups : (g + 1) * groups] for g in range(3)]
    x_ref, residual_ref = refs[3 * groups :]
    n = groups * CASES
    dofs = x_ref.shape[0] // CASES
    wide = 4

    def ports(block, carry):
        d0 = block * wide
        own = [pl.ds(pl.multiple_of((d0 + i) * CASES, CASES), CASES) for i in range(wide)]
        x = [jnp.zeros((CASES, LANES), F32)] * wide
        r = [base[0][own[i], :] for i in range(wide)]
        for j in range(n):
            q, c = divmod(j, CASES)
            c0, c1 = coef[j], coef[n + j]
            for i in range(wide):
                row = pl.ds((d0 + i) * CASES + c, 1)
                a = image[q][row, :]
                x[i] = x[i] + (c0 * base[q][row, :] + c1 * a)
                r[i] = r[i] - (c0 * a + c1 * second[q][row, :])
        for i in range(wide):
            x_ref[own[i], :] = x[i]
            residual_ref[own[i], :] = r[i]
        return carry

    lax.fori_loop(0, dofs // wide, ports, 0)


def join_kernel(groups, case_ref, bubble_ref, *refs):
    parts, out_ref = refs[:groups], refs[groups]
    part = parts[0].shape[0]
    for h in range(groups):
        at = pl.ds(pl.multiple_of(lax.rem(case_ref[0] + h, groups) * part, part), part)
        out_ref[at, :] = bubble_ref[at, :] - parts[h][...]


def call(kernel, outs, scratch=(), name=None, flops=0, smem=(), hbm=False):
    outs = [jax.ShapeDtypeStruct(shape, dtype) for shape, dtype in outs]
    vmem = pl.BlockSpec(memory_space=pltpu.VMEM)

    def run(*args):
        usual = pl.BlockSpec(memory_space=pltpu.HBM) if hbm else vmem
        specs = [pl.BlockSpec(memory_space=pltpu.SMEM) if i in smem else usual for i in range(len(args))]
        moved = sum(a.size * a.dtype.itemsize for a in args) + sum(o.size * o.dtype.itemsize for o in outs)
        fetched = [pltpu.VMEM(a.shape, a.dtype) for a in args] if hbm else []
        sems = [pltpu.SemaphoreType.DMA((len(args),))] if hbm else []
        return pl.pallas_call(
            kernel,
            out_shape=outs,
            in_specs=specs,
            out_specs=[vmem] * len(outs),
            scratch_shapes=fetched + [pltpu.VMEM(shape, F32) for shape in scratch] + sems,
            compiler_params=pltpu.CompilerParams(vmem_limit_bytes=(60 if hbm else 12) << 20),
            cost_estimate=pl.CostEstimate(flops=flops, bytes_accessed=moved, transcendentals=0),
            name=name,
        )(*args)

    return run


def reduction_groups():
    majors, minors, cases = [lax.axis_size(axis) for axis in EVERY]

    def at(half, odd, minor, case):
        return ((half * 2 + odd) * minors + minor) * cases + case

    within = [
        [at(half, odd, minor, case) for odd in range(2) for minor in range(minors)]
        for half in range(majors // 2)
        for case in range(cases)
    ]
    across = [
        [at(half, odd, minor, case) for case in range(cases) for half in range(majors // 2)]
        for odd in range(2)
        for minor in range(minors)
    ]
    return within, across


def exchange(rows, parts):
    moved = lax.all_to_all(rows.reshape(parts, 1, -1), PLANE, split_axis=0, concat_axis=0)
    return moved.reshape(rows.shape)


def local(
    comp_type, stiffness, near_port, far_owner, far_port, bubble_load, port_load,
    bubble_inverse, coupling, port_block,
):
    parts = lax.axis_size("px") * lax.axis_size("py")
    groups = lax.axis_size("case")
    modes, cases, comps = bubble_load.shape
    dofs, _, ports = port_load.shape
    rows, bubbles = dofs * cases, modes * cases
    slot_tiles = -(-SLOTS * parts // LANES)
    coupling = jnp.swapaxes(coupling, 1, 2)
    kind = comp_type.reshape(1, comps)
    stiff = stiffness.reshape(1, comps)
    near = near_port.reshape(1, comps)
    owner = far_owner.reshape(1, comps)
    far = far_port.reshape(1, comps)
    loads = bubble_load.reshape(bubbles, comps)
    field_of = ((rows, ports), F32)
    meta_of = ((parts, LANES), F32)
    pay, near_sum, meta = call(
        functools.partial(condense_kernel, parts),
        [((parts * 10, LANES), F32), field_of, meta_of],
        [(rows, comps)] * 2,
        "condense",
        hbm=True,
    )(kind, stiff, near, owner, far, loads, bubble_inverse, coupling)
    near_near, near_far, far_near, far_far, turned_near, turned_far, bubble_base = call(
        tables_kernel,
        [((KINDS * dofs, 3 * dofs), BF16)] * 4 + [((KINDS * modes, 3 * dofs), BF16)] * 2 + [((bubbles, comps), F32)],
        name="tables",
        flops=10**9,
    )(kind, stiff, loads, bubble_inverse, coupling, port_block)
    base, pay, asked = call(
        functools.partial(rhs_kernel, parts),
        [field_of, ((parts * 18, LANES), F32), meta_of],
        name="rhs",
    )(exchange(pay, parts), near_sum, port_load.reshape(rows, ports), meta)

    case = lax.axis_index("case").reshape(1)
    part = bubbles // groups
    part_of = ((part, comps), F32)
    slot_scratch = [(slot_tiles, rows, LANES)] * 2
    where = (kind, stiff, near, owner)

    def to_cases(messages):
        backward = [
            lax.ppermute(message, "case", [(k, (k + h) % groups) for k in range(groups)])
            for h, message in enumerate(messages, 1)
        ]
        return backward[::-1]

    def inner(field):
        return call(inner_kernel, [field_of] * 2, [(rows, comps)] + slot_scratch, "inner", flops=10**9)(
            field, asked, kind, stiff, near, near_near, far_far
        )

    arrived = exchange(pay, parts)
    base_all = to_cases([base] * (groups - 1))
    base_inner, base_near = inner(base)
    arrived, *base_all = lax.optimization_barrier((arrived, *base_all))
    image, base_far, pay = call(
        functools.partial(image_kernel, parts, groups, False),
        [field_of] * 2 + [((parts * 18, LANES), F32)],
        [(rows, comps)] + slot_scratch,
        "image",
    )(arrived, base_inner, asked, *where, near_far, far_near, meta)
    arrived = exchange(pay, parts)
    image_all = to_cases([image] * (groups - 1))
    image_inner, image_near = inner(image)
    turned0, *messages = call(
        functools.partial(turned_kernel, groups),
        [part_of] * groups,
        [(bubbles, comps)],
        name="turned",
        flops=10**9,
        smem=(0,),
    )(case, base_near, base_far, kind, turned_near, turned_far)
    turned0_all = to_cases(messages)
    (gram,) = call(functools.partial(gram_kernel, groups), [((cases, LANES), F32)], name="gram", smem=(0,))(
        case, base, *base_all, image, *image_all
    )
    arrived, *turned0_all = lax.optimization_barrier((arrived, *turned0_all))
    within, across = reduction_groups()
    second, copies, turned1 = call(
        functools.partial(image_kernel, parts, groups, True),
        [field_of, ((len(within[0]), cases, LANES), F32), ((bubbles, comps), F32)],
        [(rows, comps)] + slot_scratch + [(rows, comps)],
        "second",
        smem=(9,),
    )(
        arrived, image_inner, asked, *where, near_far, far_near, case, gram, image_near, turned_near, turned_far,
        image, *image_all,
    )
    copies = lax.all_to_all(copies, EVERY, split_axis=0, concat_axis=0, axis_index_groups=within)
    turned1, *messages = call(
        functools.partial(messages_kernel, groups),
        [part_of] + [((rows + part, comps), F32)] * (groups - 1),
        name="messages",
        flops=10**9,
        smem=(0,),
    )(case, second, turned1)
    both1 = to_cases(messages)
    (copies,) = call(sum_kernel, [((len(across[0]), cases, LANES), F32)], name="sum")(copies)
    copies = lax.all_to_all(copies, EVERY, split_axis=0, concat_axis=0, axis_index_groups=across)
    coef, coef_rows = call(
        functools.partial(solve_kernel, groups),
        [((2 * groups * cases, cases, LANES), F32), ((groups * cases, 2 * LANES), F32)],
        [(2, groups * cases, LANES)],
        "solve",
        smem=(0,),
    )(case, copies)
    own, *messages = call(
        functools.partial(bubble_kernel, groups, rows), [part_of] * groups, name="bubble"
    )(coef_rows, turned0, *turned0_all, turned1, *both1)
    back = to_cases(messages)
    x, residual = call(
        functools.partial(ports_kernel, groups), [field_of, field_of], name="ports", flops=10**9
    )(coef, base, *base_all, image, *image_all, second, *both1)
    (bubble,) = call(functools.partial(join_kernel, groups), [((bubbles, comps), F32)], name="join", smem=(0,))(
        case, bubble_base, own, *back
    )
    return (
        x.reshape(port_load.shape),
        residual.reshape(port_load.shape),
        bubble.reshape(bubble_load.shape),
    )


def solution(mesh):
    placed = (
        P(PLANE),
        P(PLANE),
        P(PLANE),
        P(PLANE, None),
        P(PLANE),
        P(None, "case", PLANE),
        P(None, "case", PLANE),
        P(),
        P(),
        P(),
    )
    out = P(None, "case", PLANE)
    return jax.shard_map(
        local, mesh=mesh, in_specs=placed, out_specs=(out, out, out), check_vma=False
    )
```

```python
import functools

import jax
import jax.numpy as jnp
from jax import lax
from jax.experimental import pallas as pl
from jax.experimental.pallas import tpu as pltpu
from jax.sharding import PartitionSpec as P

HIGH = lax.Precision.HIGHEST
PLANE = ("px", "py")
F32 = jnp.float32
BF16 = jnp.bfloat16
KINDS = 8
LANES = 128
CASES = 8
SLOTS = 3
NN = (((1,), (0,)), ((), ()))
NT = (((1,), (1,)), ((), ()))
TN = (((0,), (0,)), ((), ()))


def dot(lhs, rhs, dims=NN):
    return lax.dot_general(lhs, rhs, dims, preferred_element_type=F32)


def dot_high(lhs, rhs, dims=NN):
    return lax.dot_general(lhs, rhs, dims, precision=HIGH, preferred_element_type=F32)


def split2(x):
    high = x.astype(BF16)
    return high, (x - high.astype(F32)).astype(BF16)


def pick_right(x, onehot, dims):
    (left,), (right,) = dims[0]
    return dot(jnp.concatenate(split2(x), axis=left), jnp.concatenate([onehot, onehot], axis=right), dims)


def pick_left(onehot, x, dims):
    (left,), (right,) = dims[0]
    return dot(jnp.concatenate([onehot, onehot], axis=left), jnp.concatenate(split2(x), axis=right), dims)


def stacked_table(table):
    high, low = split2(table)
    return jnp.concatenate([high, high, low], axis=1)


def stacked_values(x):
    high, low = split2(x)
    return jnp.concatenate([high, low, high], axis=0)


def iota(shape, dim):
    return lax.broadcasted_iota(jnp.int32, shape, dim)


def column(row):
    return jnp.transpose(jnp.broadcast_to(row, (8, row.shape[1])))[:, :1]


def onehot(mask):
    return mask.astype(F32).astype(BF16)


def owner_slots(owner, parts):
    count = owner.shape[1]
    owner_f = owner.astype(F32)
    same = (column(owner_f) == owner_f) & (iota((count, count), 0) < iota((count, count), 1))
    rank = jnp.sum(same.astype(F32), axis=0, keepdims=True).astype(jnp.int32)
    to = iota((parts, count), 0) == owner
    return [to & (rank == s) for s in range(SLOTS)]


def near_onehot(near):
    count = near.shape[1]
    return onehot(column(near.astype(F32)) == iota((count, LANES), 1).astype(F32))


def stacked_rows(meta, lanes):
    turned = jnp.transpose(meta)
    return jnp.concatenate([turned[lanes + s : lanes + s + 1, :] for s in range(SLOTS)], axis=1)


def port_onehot(meta):
    parts = meta.shape[0]
    ports = (iota((parts, LANES), 1) + 1).astype(F32)
    return onehot(jnp.concatenate([meta[:, s : s + 1] == ports for s in range(SLOTS)], axis=0))


def pad_lanes(x, spare):
    if not spare:
        return x
    return jnp.concatenate([x, jnp.zeros((x.shape[0], spare), x.dtype)], axis=1)


def put(pay_ref, rows, first, pitch):
    parts = pay_ref.shape[0] // pitch
    tiles = rows.shape[1] // LANES
    for g in range(rows.shape[0] // parts):
        for t in range(tiles):
            pay_ref[pl.ds(first + g * tiles + t, parts, stride=pitch), :] = rows[
                g * parts : (g + 1) * parts, t * LANES : (t + 1) * LANES
            ]


def get(pay_ref, first, pitch, tiles):
    parts = pay_ref.shape[0] // pitch
    return jnp.concatenate(
        [
            jnp.concatenate(
                [pay_ref[pl.ds(first + s * tiles + t, parts, stride=pitch), :] for t in range(tiles)],
                axis=1,
            )
            for s in range(SLOTS)
        ],
        axis=0,
    )


def by_kind(products, kind, rows):
    chosen = products[:rows]
    for t in range(1, KINDS):
        chosen = jnp.where(kind == t, products[t * rows : (t + 1) * rows], chosen)
    return chosen


def condense_kernel(
    parts, kind_hbm, stiff_hbm, near_hbm, owner_hbm, far_hbm, load_hbm, inverse_hbm, coupling_hbm,
    pay_ref, near_sum_ref, meta_ref,
    kind_ref, stiff_ref, near_ref, owner_ref, far_ref, load_ref, inverse_ref, coupling_ref, near_part, far_part, sems,
):
    copies = [
        pltpu.make_async_copy(source, target, sems.at[i])
        for i, (source, target) in enumerate((
            (inverse_hbm, inverse_ref), (coupling_hbm, coupling_ref), (load_hbm, load_ref), (kind_hbm, kind_ref),
            (stiff_hbm, stiff_ref), (near_hbm, near_ref), (owner_hbm, owner_ref), (far_hbm, far_ref),
        ))
    ]
    for copy in copies:
        copy.start()
    for copy in copies:
        copy.wait()
    modes = load_ref.shape[0] // CASES
    dofs = near_sum_ref.shape[0] // CASES
    left = stacked_table(
        jnp.concatenate(
            [jnp.transpose(dot_high(inverse_ref[t], coupling_ref[t], TN)) for t in range(KINDS)], axis=0
        )
    )
    kind = kind_ref[...]
    kind2 = jnp.concatenate([kind, kind], axis=1)
    for k in range(0, CASES, 2):
        loads = jnp.concatenate(
            [load_ref[pl.ds(k + i, modes, stride=CASES), :] for i in range(2)], axis=1
        )
        condensed = -by_kind(dot(left, stacked_values(loads)), kind2, 2 * dofs)
        for i in range(2):
            lanes = slice(i * LANES, (i + 1) * LANES)
            near_part[pl.ds(k + i, dofs, stride=CASES), :] = condensed[:dofs, lanes]
            far_part[pl.ds(k + i, dofs, stride=CASES), :] = condensed[dofs:, lanes]
    near = near_ref[...]
    slots = owner_slots(owner_ref[...], parts)
    near_sum_ref[...] = pick_right(near_part[...], near_onehot(near), NN)
    chosen = onehot(jnp.concatenate(slots, axis=0))
    put(pay_ref, pick_left(chosen, far_part[...], NT), 0, 10)
    lane = iota((parts, LANES), 1)
    far_row = (far_ref[...] + 1).astype(F32)
    near_row = (near + 1).astype(F32)
    message = jnp.zeros((parts, LANES), F32)
    own = jnp.zeros((parts, LANES), F32)
    for s in range(SLOTS):
        for at, row in ((0, far_row), (SLOTS, kind.astype(F32)), (2 * SLOTS, stiff_ref[...])):
            value = jnp.sum(jnp.where(slots[s], row, 0.0), axis=1, keepdims=True)
            message = jnp.where(lane == at + s, value, message)
        value = jnp.sum(jnp.where(slots[s], near_row, 0.0), axis=1, keepdims=True)
        own = jnp.where(lane == s, value, own)
    pay_ref[pl.ds(9, parts, stride=10), :] = message
    meta_ref[...] = own


def tables_kernel(
    kind_ref, stiff_ref, load_ref, inverse_ref, coupling_ref, block_ref,
    near_near, near_far, far_near, far_far, turned_near, turned_far, base_ref,
):
    dofs = block_ref.shape[1] // 2
    modes = inverse_ref.shape[1]
    inverses = []
    for t in range(KINDS):
        turned = dot_high(inverse_ref[t], coupling_ref[t], TN)
        schur = block_ref[t] - dot_high(turned, coupling_ref[t], TN)
        at = slice(t * dofs, (t + 1) * dofs)
        near_near[at, :] = stacked_table(schur[:dofs, :dofs])
        near_far[at, :] = stacked_table(schur[:dofs, dofs:])
        far_near[at, :] = stacked_table(schur[dofs:, :dofs])
        far_far[at, :] = stacked_table(schur[dofs:, dofs:])
        at = slice(t * modes, (t + 1) * modes)
        turned_near[at, :] = stacked_table(turned[:, :dofs])
        turned_far[at, :] = stacked_table(turned[:, dofs:])
        inverses.append(inverse_ref[t])
    left = stacked_table(jnp.concatenate(inverses, axis=0))
    kind = kind_ref[...]
    stiff = stiff_ref[...]
    kind2 = jnp.concatenate([kind, kind], axis=1)
    stiff2 = jnp.concatenate([stiff, stiff], axis=1)
    for k in range(0, CASES, 2):
        loads = jnp.concatenate(
            [load_ref[pl.ds(k + i, modes, stride=CASES), :] for i in range(2)], axis=1
        )
        result = by_kind(dot(left, stacked_values(loads)), kind2, modes) / stiff2
        for i in range(2):
            base_ref[pl.ds(k + i, modes, stride=CASES), :] = result[:, i * LANES : (i + 1) * LANES]


def send_ports(field, asked, own, pay_ref):
    put(pay_ref, pick_left(jnp.concatenate([asked, own], axis=0), field, NT), 0, 18)


def rhs_kernel(parts, arrived_ref, near_sum_ref, load_ref, meta_ref, field_ref, pay_ref, asked_ref):
    asked = arrived_ref[pl.ds(9, parts, stride=10), :]
    asked_ref[...] = asked
    asked_hot = port_onehot(asked)
    arrived = get(arrived_ref, 0, 10, 3)
    field = load_ref[...] + (near_sum_ref[...] + pick_right(arrived, asked_hot, TN))
    field_ref[...] = field
    send_ports(field, asked_hot, port_onehot(meta_ref[...]), pay_ref)


def component_products(table_ref, part_ref, kind_ref, stiff_ref, out_ref):
    dofs = part_ref.shape[0] // CASES
    kind, stiff = kind_ref[...], stiff_ref[...]
    kind2 = jnp.concatenate([kind, kind], axis=1)
    stiff2 = jnp.concatenate([stiff, stiff], axis=1)
    for k in range(0, CASES, 2):
        values = jnp.concatenate(
            [part_ref[pl.ds(k + i, dofs, stride=CASES), :] for i in range(2)], axis=1
        )
        result = by_kind(dot(table_ref[...], stacked_values(values)), kind2, dofs) * stiff2
        for i in range(2):
            out_ref[pl.ds(k + i, dofs, stride=CASES), :] = result[:, i * LANES : (i + 1) * LANES]


def slot_products(table_ref, slot_ref, asked, out_ref):
    tiles = slot_ref.shape[0]
    dofs = slot_ref.shape[1] // CASES
    spare = tiles * LANES - SLOTS * asked.shape[0]
    kind = pad_lanes(stacked_rows(asked, SLOTS), spare).astype(jnp.int32)
    stiff = pad_lanes(stacked_rows(asked, 2 * SLOTS), spare)
    for k in range(CASES):
        values = jnp.concatenate(
            [slot_ref[g, pl.ds(k, dofs, stride=CASES), :] for g in range(tiles)], axis=1
        )
        result = by_kind(dot(table_ref[...], stacked_values(values)), kind, dofs) * stiff
        for g in range(tiles):
            out_ref[g, pl.ds(k, dofs, stride=CASES), :] = result[:, g * LANES : (g + 1) * LANES]


def wide_onehot(asked_hot, tiles):
    spare = tiles * LANES - asked_hot.shape[0]
    if not spare:
        return asked_hot
    return jnp.concatenate([asked_hot, jnp.zeros((spare, LANES), BF16)], axis=0)


def slots_to_ports(part_ref, asked_hot):
    tiles = part_ref.shape[0]
    hot = wide_onehot(asked_hot, tiles)
    total = pick_right(part_ref[0], hot[:LANES], NN)
    for g in range(1, tiles):
        total = total + pick_right(part_ref[g], hot[g * LANES : (g + 1) * LANES], NN)
    return total


def inner_kernel(
    field_ref, asked_ref, kind_ref, stiff_ref, near_ref, near_near, far_far,
    inner_ref, near_values, near_part, slot_ref, slot_part,
):
    field, asked = field_ref[...], asked_ref[...]
    near_hot, asked_hot = near_onehot(near_ref[...]), port_onehot(asked)
    tiles = slot_ref.shape[0]
    near_values[...] = pick_right(field, near_hot, NT)
    values = pick_right(field, wide_onehot(asked_hot, tiles), NT)
    for g in range(tiles):
        slot_ref[g] = values[:, g * LANES : (g + 1) * LANES]
    component_products(near_near, near_values, kind_ref, stiff_ref, near_part)
    slot_products(far_far, slot_ref, asked, slot_part)
    inner_ref[...] = pick_right(near_part[...], near_hot, NN) + slots_to_ports(slot_part, asked_hot)


def near_cross(parts, arrived_ref, pitch, kind_ref, stiff_ref, near_ref, owner_ref, near_far, far_values, near_part):
    slots = onehot(jnp.concatenate(owner_slots(owner_ref[...], parts), axis=0))
    far_values[...] = pick_right(get(arrived_ref, 0, pitch, 3), slots, TN)
    component_products(near_far, far_values, kind_ref, stiff_ref, near_part)
    return pick_right(near_part[...], near_onehot(near_ref[...]), NN)


def far_cross(arrived_ref, first, pitch, asked, asked_hot, far_near, slot_ref, slot_part):
    tiles = slot_ref.shape[0]
    values = jnp.transpose(get(arrived_ref, first, pitch, 3))
    values = pad_lanes(values, tiles * LANES - values.shape[1])
    for g in range(tiles):
        slot_ref[g] = values[:, g * LANES : (g + 1) * LANES]
    slot_products(far_near, slot_ref, asked, slot_part)
    return slots_to_ports(slot_part, asked_hot)


def image_kernel(
    parts, groups, last, arrived_ref, inner_hbm, asked_ref, kind_ref, stiff_ref, near_ref, owner_ref,
    near_far, far_near, *rest,
):
    if last:
        case_ref, gram_ref, near_values, turned_near, turned_far = rest[:5]
        images, rest = rest[5 : 5 + groups], rest[5 + groups :]
        image_ref, copies_ref, turned_ref, near_part, slot_ref, slot_part, far_values, inner_ref, sem = rest
    else:
        meta_ref, image_ref, far_values, pay_ref, near_part, slot_ref, slot_part, inner_ref, sem = rest
    fetch = pltpu.make_async_copy(inner_hbm, inner_ref, sem)
    fetch.start()
    asked = asked_ref[...]
    asked_hot = port_onehot(asked)
    slots = onehot(jnp.concatenate(owner_slots(owner_ref[...], parts), axis=0))
    far_values[...] = pick_right(get(arrived_ref, 0, 18, 3), slots, TN)
    component_products(near_far, far_values, kind_ref, stiff_ref, near_part)
    tiles = slot_ref.shape[0]
    values = jnp.transpose(get(arrived_ref, 9, 18, 3))
    values = pad_lanes(values, tiles * LANES - values.shape[1])
    for g in range(tiles):
        slot_ref[g] = values[:, g * LANES : (g + 1) * LANES]
    slot_products(far_near, slot_ref, asked, slot_part)
    fetch.wait()
    image = inner_ref[...] + pick_right(near_part[...], near_onehot(near_ref[...]), NN)
    image = image + slots_to_ports(slot_part, asked_hot)
    image_ref[...] = image
    if last:
        gram = add_products(LANES, images, [image_ref], [3 * groups * CASES], case_ref[0], gram_ref[...])
        for p in range(copies_ref.shape[0]):
            copies_ref[p] = gram
        turned_rows(near_values, far_values, kind_ref, turned_near, turned_far, turned_ref)
    else:
        send_ports(image, asked_hot, port_onehot(meta_ref[...]), pay_ref)


def turned_rows(near_values, far_values, kind_ref, turned_near, turned_far, out_ref):
    dofs = near_values.shape[0] // CASES
    modes = out_ref.shape[0] // CASES
    kind = kind_ref[...]
    kind2 = jnp.concatenate([kind, kind], axis=1)
    for k in range(0, CASES, 2):
        sums = 0.0
        for table, part in ((turned_near, near_values), (turned_far, far_values)):
            values = jnp.concatenate(
                [part[pl.ds(k + i, dofs, stride=CASES), :] for i in range(2)], axis=1
            )
            sums = sums + dot(table[...], stacked_values(values))
        result = by_kind(sums, kind2, modes)
        for i in range(2):
            out_ref[pl.ds(k + i, modes, stride=CASES), :] = result[:, i * LANES : (i + 1) * LANES]


def messages_kernel(groups, case_ref, field_ref, turned_ref, own_ref, *rest):
    messages, sems = rest[: groups - 1], rest[groups - 1]
    rows = field_ref.shape[0]
    part = own_ref.shape[0]
    copies = []
    for h in range(groups):
        at = pl.multiple_of(lax.rem(case_ref[0] + h, groups) * part, part)
        target = messages[h - 1].at[pl.ds(rows, part), :] if h else own_ref
        copies.append(pltpu.make_async_copy(turned_ref.at[pl.ds(at, part), :], target, sems.at[h]))
        if h:
            copies.append(
                pltpu.make_async_copy(field_ref, messages[h - 1].at[pl.ds(0, rows), :], sems.at[groups + h])
            )
    for copy in copies:
        copy.start()
    for copy in copies:
        copy.wait()


def add_products(lanes, lefts, rights, first, case, out):
    groups = len(lefts)
    total = groups * CASES
    dofs = lefts[0].shape[0] // CASES
    lane = iota((CASES, LANES), 1)
    for h in range(groups):
        def step(d, sums):
            own = pl.ds(pl.multiple_of(d * CASES, CASES), CASES)
            values = [ref[own, :] for ref in rights]
            new = []
            for i in range(CASES):
                row = lefts[h][pl.ds(d * CASES + i, 1), :]
                new.append(tuple(s + row * v for s, v in zip(sums[i], values)))
            return tuple(new)

        zero = jnp.zeros((CASES, LANES), F32)
        sums = lax.fori_loop(0, dofs, step, ((zero,) * len(rights),) * CASES)
        at = lax.rem(case + h, groups) * CASES
        for i in range(CASES):
            for g in range(len(rights)):
                value = jnp.sum(sums[i][g], axis=1, keepdims=True)
                out = jnp.where(lane == first[g] + at + i, value, out)
    return out


def gram_kernel(groups, case_ref, *refs):
    base, image, out_ref = refs[:groups], refs[groups : 2 * groups], refs[2 * groups]
    total = groups * CASES
    out = jnp.zeros((CASES, LANES), F32)
    out = add_products(LANES, base, [base[0], image[0]], [0, total], case_ref[0], out)
    out_ref[...] = add_products(LANES, image, [image[0]], [2 * total], case_ref[0], out)


def sum_kernel(in_ref, out_ref):
    for q in range(in_ref.shape[0]):
        total = in_ref[q, 0]
        for p in range(1, in_ref.shape[1]):
            total = total + in_ref[q, p]
        for p in range(out_ref.shape[0]):
            out_ref[p, q * CASES : (q + 1) * CASES, :] = total


def inverse2(p, q, r, s):
    scale = 1.0 / (p * s - q * r)
    return s * scale, -q * scale, -r * scale, p * scale


def spd_solve(matrix, target):
    n = matrix.shape[0]
    a = jnp.concatenate([matrix, target], axis=1)
    row_of = iota(a.shape, 0)
    for k in range(0, n, 4):
        c = [jnp.broadcast_to(a[:, k + i : k + i + 1], a.shape) for i in range(4)]
        r = [a[k + i : k + i + 1] for i in range(4)]
        p = [[c[j][k + i : k + i + 1] for j in range(4)] for i in range(4)]
        a00, a01, a10, a11 = inverse2(p[0][0], p[0][1], p[1][0], p[1][1])
        e00, e01 = p[2][0] * a00 + p[2][1] * a10, p[2][0] * a01 + p[2][1] * a11
        e10, e11 = p[3][0] * a00 + p[3][1] * a10, p[3][0] * a01 + p[3][1] * a11
        i00, i01, i10, i11 = inverse2(
            p[2][2] - (e00 * p[0][2] + e01 * p[1][2]),
            p[2][3] - (e00 * p[0][3] + e01 * p[1][3]),
            p[3][2] - (e10 * p[0][2] + e11 * p[1][2]),
            p[3][3] - (e10 * p[0][3] + e11 * p[1][3]),
        )
        t2 = r[2] - (e00 * r[0] + e01 * r[1])
        t3 = r[3] - (e10 * r[0] + e11 * r[1])
        u2, u3 = i00 * t2 + i01 * t3, i10 * t2 + i11 * t3
        w0 = r[0] - (p[0][2] * u2 + p[0][3] * u3)
        w1 = r[1] - (p[1][2] * u2 + p[1][3] * u3)
        u = [a00 * w0 + a01 * w1, a10 * w0 + a11 * w1, u2, u3]
        a = a - ((c[0] * u[0] + c[1] * u[1]) + (c[2] * u[2] + c[3] * u[3]))
        for i in range(4):
            a = jnp.where(row_of == k + i, u[i], a)
    return a[:, n:]


def symmetric(m):
    return 0.5 * (m + jnp.transpose(m))


def solve_kernel(groups, case_ref, gram_ref, coef, coef_rows, turned_coef):
    n = groups * CASES
    total = gram_ref[0]
    for p in range(1, gram_ref.shape[0]):
        total = total + gram_ref[p]
    g00, g01, g11, g12 = [symmetric(total[:, g * n : (g + 1) * n]) for g in range(4)]
    steps = spd_solve(g01, jnp.concatenate([g00, g11], axis=1))
    step0, step1 = steps[:, :n], steps[:, n:]
    both = dot_high(g11, steps)
    second = spd_solve(symmetric(g12 - both[:, n:]), g01 - both[:, :n])
    first = step0 - dot_high(step1, second)
    first, second = jnp.transpose(first), jnp.transpose(second)
    turned_coef[0] = jnp.concatenate([first] * (LANES // n), axis=1)
    turned_coef[1] = jnp.concatenate([second] * (LANES // n), axis=1)
    shift = LANES - case_ref[0] * CASES
    for q in range(groups):
        at = pl.multiple_of(lax.rem(case_ref[0] + q, groups) * CASES, CASES)
        for h in range(2):
            mine = pltpu.roll(turned_coef[h, pl.ds(at, CASES), :], shift, 1)
            coef_rows[q * CASES : (q + 1) * CASES, h * LANES : (h + 1) * LANES] = mine
            if q == 0:
                for j in range(n):
                    coef[h * n + j] = jnp.broadcast_to(mine[:, j : j + 1], (CASES, LANES))


def bubble_kernel(groups, rows, coef_ref, *refs):
    turned0, turned1, outs = refs[:groups], refs[groups : 2 * groups], refs[2 * groups :]
    n = groups * CASES
    part = turned0[0].shape[0]
    coef = jnp.concatenate([coef_ref[:, :n], coef_ref[:, LANES : LANES + n]], axis=1)
    left = stacked_table(coef)
    for m in range(0, part // CASES, 2):
        values = []
        for i in range(2):
            at = (m + i) * CASES
            pieces = [
                ref[at + shift : at + shift + CASES, :]
                for turned in (turned0, turned1)
                for ref, shift in zip(turned, [0] + [rows] * (groups - 1))
            ]
            values.append(jnp.concatenate(pieces, axis=0))
        result = dot(left, stacked_values(jnp.concatenate(values, axis=1)))
        for i in range(2):
            for h in range(groups):
                outs[h][(m + i) * CASES : (m + i + 1) * CASES, :] = result[
                    h * CASES : (h + 1) * CASES, i * LANES : (i + 1) * LANES
                ]


def ports_kernel(groups, coef, *refs):
    base, image, second = [refs[g * groups : (g + 1) * groups] for g in range(3)]
    x_ref, residual_ref = refs[3 * groups :]
    n = groups * CASES
    dofs = x_ref.shape[0] // CASES
    wide = 4

    def ports(block, carry):
        d0 = block * wide
        own = [pl.ds(pl.multiple_of((d0 + i) * CASES, CASES), CASES) for i in range(wide)]
        x = [jnp.zeros((CASES, LANES), F32)] * wide
        r = [base[0][own[i], :] for i in range(wide)]
        for j in range(n):
            q, c = divmod(j, CASES)
            c0, c1 = coef[j], coef[n + j]
            for i in range(wide):
                row = pl.ds((d0 + i) * CASES + c, 1)
                a = image[q][row, :]
                x[i] = x[i] + (c0 * base[q][row, :] + c1 * a)
                r[i] = r[i] - (c0 * a + c1 * second[q][row, :])
        for i in range(wide):
            x_ref[own[i], :] = x[i]
            residual_ref[own[i], :] = r[i]
        return carry

    lax.fori_loop(0, dofs // wide, ports, 0)


def join_kernel(groups, case_ref, bubble_ref, *refs):
    parts, out_ref = refs[:groups], refs[groups]
    part = parts[0].shape[0]
    for h in range(groups):
        at = pl.ds(pl.multiple_of(lax.rem(case_ref[0] + h, groups) * part, part), part)
        out_ref[at, :] = bubble_ref[at, :] - parts[h][...]


def call(kernel, outs, scratch=(), name=None, flops=0, smem=(), hbm=(), sems=0, limit=12):
    results = [(pltpu.HBM if far else jax.ShapeDtypeStruct)(shape, dtype) for shape, dtype, far in outs]
    vmem = pl.BlockSpec(memory_space=pltpu.VMEM)
    far_spec = pl.BlockSpec(memory_space=pltpu.HBM)
    copies_only = name == "messages"

    def run(*args):
        specs = [
            pl.BlockSpec(memory_space=pltpu.SMEM) if i in smem else far_spec if i in hbm else vmem
            for i in range(len(args))
        ]
        moved = sum(a.size * a.dtype.itemsize for a in args)
        args = [pltpu.with_memory_space_constraint(a, pltpu.HBM) if i in hbm else a for i, a in enumerate(args)]
        return pl.pallas_call(
            kernel,
            out_shape=results,
            in_specs=specs,
            out_specs=[far_spec if copies_only else vmem] * len(outs),
            scratch_shapes=[pltpu.VMEM(*shape) if isinstance(shape[0], tuple) else pltpu.VMEM(shape, F32) for shape in scratch]
            + ([pltpu.SemaphoreType.DMA((sems,) if sems > 1 else ())] if sems else []),
            compiler_params=pltpu.CompilerParams(vmem_limit_bytes=limit << 20),
            cost_estimate=pl.CostEstimate(flops=flops, bytes_accessed=moved, transcendentals=0),
            name=name,
        )(*args)

    return run


def exchange(rows, parts):
    moved = lax.all_to_all(rows.reshape(parts, 1, -1), PLANE, split_axis=0, concat_axis=0)
    return moved.reshape(rows.shape)


def local(
    comp_type, stiffness, near_port, far_owner, far_port, bubble_load, port_load,
    bubble_inverse, coupling, port_block,
):
    parts = lax.axis_size("px") * lax.axis_size("py")
    groups = lax.axis_size("case")
    modes, cases, comps = bubble_load.shape
    dofs, _, ports = port_load.shape
    rows, bubbles = dofs * cases, modes * cases
    slot_tiles = -(-SLOTS * parts // LANES)
    coupling = jnp.swapaxes(coupling, 1, 2)
    kind = comp_type.reshape(1, comps)
    stiff = stiffness.reshape(1, comps)
    near = near_port.reshape(1, comps)
    owner = far_owner.reshape(1, comps)
    far = far_port.reshape(1, comps)
    loads = bubble_load.reshape(bubbles, comps)
    field_of = ((rows, ports), F32, True)
    meta_of = ((parts, LANES), F32, False)
    bubble_of = ((bubbles, comps), F32, True)
    given = (kind, stiff, near, owner, far, loads, bubble_inverse, coupling)
    pay, near_sum, meta = call(
        functools.partial(condense_kernel, parts),
        [((parts * 10, LANES), F32, False), field_of, meta_of],
        [(a.shape, a.dtype) for a in given] + [(rows, comps)] * 2,
        "condense",
        hbm=range(len(given)),
        sems=len(given),
    )(*given)
    near_near, near_far, far_near, far_far, turned_near, turned_far, bubble_base = call(
        tables_kernel,
        [((KINDS * dofs, 3 * dofs), BF16, False)] * 4 + [((KINDS * modes, 3 * dofs), BF16, True)] * 2 + [bubble_of],
        name="tables",
        flops=10**9,
    )(kind, stiff, loads, bubble_inverse, coupling, port_block)
    base, pay, asked = call(
        functools.partial(rhs_kernel, parts),
        [field_of, ((parts * 18, LANES), F32, False), meta_of],
        name="rhs",
    )(exchange(pay, parts), near_sum, port_load.reshape(rows, ports), meta)

    case = lax.axis_index("case").reshape(1)
    part = bubbles // groups
    part_of = ((part, comps), F32, True)
    slot_scratch = [(slot_tiles, rows, LANES)] * 2
    where = (kind, stiff, near, owner)

    def to_cases(messages):
        backward = [
            lax.ppermute(message, "case", [(k, (k + h) % groups) for k in range(groups)])
            for h, message in enumerate(messages, 1)
        ]
        return backward[::-1]

    def inner(field):
        return call(inner_kernel, [field_of] * 2, [(rows, comps)] + slot_scratch, "inner", flops=10**9)(
            field, asked, kind, stiff, near, near_near, far_far
        )

    arrived = exchange(pay, parts)
    base_all = to_cases([base] * (groups - 1))
    base_inner, base_near = inner(base)
    arrived, *base_all = lax.optimization_barrier((arrived, *base_all))
    image, base_far, pay = call(
        functools.partial(image_kernel, parts, groups, False),
        [field_of] * 2 + [((parts * 18, LANES), F32, False)],
        [(rows, comps)] + slot_scratch + [(rows, ports)],
        "image",
        hbm=(1,),
        sems=1,
    )(arrived, base_inner, asked, *where, near_far, far_near, meta)
    arrived = exchange(pay, parts)
    def messages(field, turned):
        own, *others = call(
            functools.partial(messages_kernel, groups),
            [part_of] + [((rows + part, comps), F32, True)] * (groups - 1),
            name="messages",
            flops=10**9,
            smem=(0,),
            hbm=(1, 2),
            sems=2 * groups,
        )(case, field, turned)
        return own, to_cases(others)

    (turned0,) = call(turned_rows, [bubble_of], name="turned", flops=10**9)(
        base_near, base_far, kind, turned_near, turned_far
    )
    turned0, both0 = messages(image, turned0)
    image_inner, image_near = inner(image)
    (gram,) = call(functools.partial(gram_kernel, groups), [((cases, LANES), F32, False)], name="gram", smem=(0,))(
        case, base, *base_all, image, *both0
    )
    minor = lax.axis_size("py")
    second, copies, turned1 = call(
        functools.partial(image_kernel, parts, groups, True),
        [field_of, ((groups * minor, cases, LANES), F32, True), bubble_of],
        [(rows, comps)] + slot_scratch + [(rows, comps), (rows, ports)],
        "second",
        smem=(9,),
        hbm=(1,),
        sems=1,
    )(
        arrived, image_inner, asked, *where, near_far, far_near, case, gram, image_near, turned_near, turned_far,
        image, *both0,
    )
    copies = lax.all_to_all(copies, ("case", "py"), split_axis=0, concat_axis=0)
    turned1, both1 = messages(second, turned1)
    (copies,) = call(sum_kernel, [((parts // minor, groups * cases, LANES), F32, False)], name="sum")(
        copies.reshape(groups, minor, cases, LANES)
    )
    copies = lax.all_to_all(copies, "px", split_axis=0, concat_axis=0)
    coef, coef_rows = call(
        functools.partial(solve_kernel, groups),
        [((2 * groups * cases, cases, LANES), F32, False), ((groups * cases, 2 * LANES), F32, False)],
        [(2, groups * cases, LANES)],
        "solve",
        smem=(0,),
    )(case, copies)
    own, *messages = call(
        functools.partial(bubble_kernel, groups, rows), [part_of] * groups, name="bubble"
    )(coef_rows, turned0, *both0, turned1, *both1)
    back = to_cases(messages)
    x, residual = call(
        functools.partial(ports_kernel, groups), [field_of, field_of], name="ports", flops=10**9
    )(coef, base, *base_all, image, *both0, second, *both1)
    (bubble,) = call(functools.partial(join_kernel, groups), [bubble_of], name="join", smem=(0,))(
        case, bubble_base, own, *back
    )
    return (
        x.reshape(port_load.shape),
        residual.reshape(port_load.shape),
        bubble.reshape(bubble_load.shape),
    )


def solution(mesh):
    placed = (
        P(PLANE),
        P(PLANE),
        P(PLANE),
        P(PLANE, None),
        P(PLANE),
        P(None, "case", PLANE),
        P(None, "case", PLANE),
        P(),
        P(),
        P(),
    )
    out = P(None, "case", PLANE)
    return jax.shard_map(
        local, mesh=mesh, in_specs=placed, out_specs=(out, out, out), check_vma=False
    )
```

```python
import functools

import jax
import jax.numpy as jnp
from jax import lax
from jax.experimental import pallas as pl
from jax.experimental.pallas import tpu as pltpu
from jax.sharding import PartitionSpec as P

HIGH = lax.Precision.HIGHEST
PLANE = ("px", "py")
F32 = jnp.float32
BF16 = jnp.bfloat16
KINDS = 8
LANES = 128
CASES = 8
SLOTS = 3
NN = (((1,), (0,)), ((), ()))
NT = (((1,), (1,)), ((), ()))
TN = (((0,), (0,)), ((), ()))


def dot(lhs, rhs, dims=NN):
    return lax.dot_general(lhs, rhs, dims, preferred_element_type=F32)


def dot_high(lhs, rhs, dims=NN):
    return lax.dot_general(lhs, rhs, dims, precision=HIGH, preferred_element_type=F32)


def split2(x):
    high = x.astype(BF16)
    return high, (x - high.astype(F32)).astype(BF16)


def pick_right(x, onehot, dims):
    (left,), (right,) = dims[0]
    return dot(jnp.concatenate(split2(x), axis=left), jnp.concatenate([onehot, onehot], axis=right), dims)


def pick_left(onehot, x, dims):
    (left,), (right,) = dims[0]
    return dot(jnp.concatenate([onehot, onehot], axis=left), jnp.concatenate(split2(x), axis=right), dims)


def stacked_table(table):
    high, low = split2(table)
    return jnp.concatenate([high, high, low], axis=1)


def stacked_values(x):
    high, low = split2(x)
    return jnp.concatenate([high, low, high], axis=0)


def iota(shape, dim):
    return lax.broadcasted_iota(jnp.int32, shape, dim)


def column(row):
    return jnp.transpose(jnp.broadcast_to(row, (8, row.shape[1])))[:, :1]


def onehot(mask):
    return mask.astype(F32).astype(BF16)


KIND, STIFF, NEAR, OWNER = [slice(i, i + 1) for i in range(4)]


def owner_slots(owner, parts):
    count = owner.shape[1]
    owner_f = owner.astype(F32)
    same = (column(owner_f) == owner_f) & (iota((count, count), 0) < iota((count, count), 1))
    rank = jnp.sum(same.astype(F32), axis=0, keepdims=True).astype(jnp.int32)
    to = iota((parts, count), 0).astype(F32) == owner_f
    return [to & (rank == s) for s in range(SLOTS)]


def near_onehot(near):
    count = near.shape[1]
    return onehot(column(near.astype(F32)) == iota((count, LANES), 1).astype(F32))


def stacked_rows(meta, lanes):
    turned = jnp.transpose(meta)
    return jnp.concatenate([turned[lanes + s : lanes + s + 1, :] for s in range(SLOTS)], axis=1)


def port_onehot(meta):
    parts = meta.shape[0]
    ports = (iota((parts, LANES), 1) + 1).astype(F32)
    return onehot(jnp.concatenate([meta[:, s : s + 1] == ports for s in range(SLOTS)], axis=0))


def pad_lanes(x, spare):
    if not spare:
        return x
    return jnp.concatenate([x, jnp.zeros((x.shape[0], spare), x.dtype)], axis=1)


def put(pay_ref, rows, first, pitch):
    parts = pay_ref.shape[0] // pitch
    tiles = rows.shape[1] // LANES
    for g in range(rows.shape[0] // parts):
        for t in range(tiles):
            pay_ref[pl.ds(first + g * tiles + t, parts, stride=pitch), :] = rows[
                g * parts : (g + 1) * parts, t * LANES : (t + 1) * LANES
            ]


def get(pay_ref, first, pitch, tiles):
    parts = pay_ref.shape[0] // pitch
    return jnp.concatenate(
        [
            jnp.concatenate(
                [pay_ref[pl.ds(first + s * tiles + t, parts, stride=pitch), :] for t in range(tiles)],
                axis=1,
            )
            for s in range(SLOTS)
        ],
        axis=0,
    )


def by_kind(products, kind, rows):
    chosen = products[:rows]
    for t in range(1, KINDS):
        chosen = jnp.where(kind == t, products[t * rows : (t + 1) * rows], chosen)
    return chosen


def condense_kernel(
    parts, kind_hbm, stiff_hbm, near_hbm, owner_hbm, far_hbm, load_hbm, inverse_hbm, coupling_hbm,
    pay_ref, near_sum_ref, meta_ref, where_ref,
    kind_ref, stiff_ref, near_ref, owner_ref, far_ref, load_ref, inverse_ref, coupling_ref, near_part, far_part, sems,
):
    copies = [
        pltpu.make_async_copy(source, target, sems.at[i])
        for i, (source, target) in enumerate((
            (inverse_hbm, inverse_ref), (coupling_hbm, coupling_ref), (load_hbm, load_ref), (kind_hbm, kind_ref),
            (stiff_hbm, stiff_ref), (near_hbm, near_ref), (owner_hbm, owner_ref), (far_hbm, far_ref),
        ))
    ]
    for copy in copies:
        copy.start()
    for copy in copies:
        copy.wait()
    modes = load_ref.shape[0] // CASES
    dofs = near_sum_ref.shape[0] // CASES
    left = stacked_table(
        jnp.concatenate(
            [jnp.transpose(dot_high(inverse_ref[t], coupling_ref[t], TN)) for t in range(KINDS)], axis=0
        )
    )
    kind = kind_ref[...]
    kind2 = jnp.concatenate([kind, kind], axis=1)
    for k in range(0, CASES, 2):
        loads = jnp.concatenate(
            [load_ref[pl.ds(k + i, modes, stride=CASES), :] for i in range(2)], axis=1
        )
        condensed = -by_kind(dot(left, stacked_values(loads)), kind2, 2 * dofs)
        for i in range(2):
            lanes = slice(i * LANES, (i + 1) * LANES)
            near_part[pl.ds(k + i, dofs, stride=CASES), :] = condensed[:dofs, lanes]
            far_part[pl.ds(k + i, dofs, stride=CASES), :] = condensed[dofs:, lanes]
    near = near_ref[...]
    slots = owner_slots(owner_ref[...], parts)
    near_sum_ref[...] = pick_right(near_part[...], near_onehot(near), NN)
    chosen = onehot(jnp.concatenate(slots, axis=0))
    put(pay_ref, pick_left(chosen, far_part[...], NT), 0, 10)
    lane = iota((parts, LANES), 1)
    far_row = (far_ref[...] + 1).astype(F32)
    near_row = (near + 1).astype(F32)
    message = jnp.zeros((parts, LANES), F32)
    own = jnp.zeros((parts, LANES), F32)
    for s in range(SLOTS):
        for at, row in ((0, far_row), (SLOTS, kind.astype(F32)), (2 * SLOTS, stiff_ref[...])):
            value = jnp.sum(jnp.where(slots[s], row, 0.0), axis=1, keepdims=True)
            message = jnp.where(lane == at + s, value, message)
        value = jnp.sum(jnp.where(slots[s], near_row, 0.0), axis=1, keepdims=True)
        own = jnp.where(lane == s, value, own)
    pay_ref[pl.ds(9, parts, stride=10), :] = message
    packed = [kind.astype(F32), stiff_ref[...], near.astype(F32), owner_ref[...].astype(F32)]
    where_ref[...] = jnp.concatenate(packed + packed, axis=0)
    meta_ref[...] = own


def tables_kernel(
    where_ref, load_ref, inverse_ref, coupling_ref, block_ref,
    near_near, near_far, far_near, far_far, turned_near, turned_far, base_ref,
):
    dofs = block_ref.shape[1] // 2
    modes = inverse_ref.shape[1]
    inverses = []
    for t in range(KINDS):
        turned = dot_high(inverse_ref[t], coupling_ref[t], TN)
        schur = block_ref[t] - dot_high(turned, coupling_ref[t], TN)
        at = slice(t * dofs, (t + 1) * dofs)
        near_near[at, :] = stacked_table(schur[:dofs, :dofs])
        near_far[at, :] = stacked_table(schur[:dofs, dofs:])
        far_near[at, :] = stacked_table(schur[dofs:, :dofs])
        far_far[at, :] = stacked_table(schur[dofs:, dofs:])
        at = slice(t * modes, (t + 1) * modes)
        turned_near[at, :] = stacked_table(turned[:, :dofs])
        turned_far[at, :] = stacked_table(turned[:, dofs:])
        inverses.append(inverse_ref[t])
    left = stacked_table(jnp.concatenate(inverses, axis=0))
    kind = where_ref[KIND]
    stiff = where_ref[STIFF]
    kind2 = jnp.concatenate([kind, kind], axis=1)
    stiff2 = jnp.concatenate([stiff, stiff], axis=1)
    for k in range(0, CASES, 2):
        loads = jnp.concatenate(
            [load_ref[pl.ds(k + i, modes, stride=CASES), :] for i in range(2)], axis=1
        )
        result = by_kind(dot(left, stacked_values(loads)), kind2, modes) / stiff2
        for i in range(2):
            base_ref[pl.ds(k + i, modes, stride=CASES), :] = result[:, i * LANES : (i + 1) * LANES]


def send_ports(field, asked, own, pay_ref):
    put(pay_ref, pick_left(jnp.concatenate([asked, own], axis=0), field, NT), 0, 18)


def rhs_kernel(parts, arrived_ref, near_sum_ref, load_ref, meta_ref, field_ref, pay_ref, asked_ref):
    asked = arrived_ref[pl.ds(9, parts, stride=10), :]
    asked_ref[...] = asked
    asked_hot = port_onehot(asked)
    arrived = get(arrived_ref, 0, 10, 3)
    field = load_ref[...] + (near_sum_ref[...] + pick_right(arrived, asked_hot, TN))
    field_ref[...] = field
    send_ports(field, asked_hot, port_onehot(meta_ref[...]), pay_ref)


def component_products(table_ref, part_ref, where_ref, out_ref):
    dofs = part_ref.shape[0] // CASES
    kind, stiff = where_ref[KIND], where_ref[STIFF]
    kind2 = jnp.concatenate([kind, kind], axis=1)
    stiff2 = jnp.concatenate([stiff, stiff], axis=1)
    for k in range(0, CASES, 2):
        values = jnp.concatenate(
            [part_ref[pl.ds(k + i, dofs, stride=CASES), :] for i in range(2)], axis=1
        )
        result = by_kind(dot(table_ref[...], stacked_values(values)), kind2, dofs) * stiff2
        for i in range(2):
            out_ref[pl.ds(k + i, dofs, stride=CASES), :] = result[:, i * LANES : (i + 1) * LANES]


def slot_products(table_ref, slot_ref, asked, out_ref):
    tiles = slot_ref.shape[0]
    dofs = slot_ref.shape[1] // CASES
    spare = tiles * LANES - SLOTS * asked.shape[0]
    kind = pad_lanes(stacked_rows(asked, SLOTS), spare)
    stiff = pad_lanes(stacked_rows(asked, 2 * SLOTS), spare)
    for k in range(CASES):
        values = jnp.concatenate(
            [slot_ref[g, pl.ds(k, dofs, stride=CASES), :] for g in range(tiles)], axis=1
        )
        result = by_kind(dot(table_ref[...], stacked_values(values)), kind, dofs) * stiff
        for g in range(tiles):
            out_ref[g, pl.ds(k, dofs, stride=CASES), :] = result[:, g * LANES : (g + 1) * LANES]


def wide_onehot(asked_hot, tiles):
    spare = tiles * LANES - asked_hot.shape[0]
    if not spare:
        return asked_hot
    return jnp.concatenate([asked_hot, jnp.zeros((spare, LANES), BF16)], axis=0)


def slots_to_ports(part_ref, asked_hot):
    tiles = part_ref.shape[0]
    hot = wide_onehot(asked_hot, tiles)
    total = pick_right(part_ref[0], hot[:LANES], NN)
    for g in range(1, tiles):
        total = total + pick_right(part_ref[g], hot[g * LANES : (g + 1) * LANES], NN)
    return total


def inner_kernel(
    field_ref, asked_ref, where_ref, near_near, far_far,
    inner_ref, near_values, near_part, slot_ref, slot_part,
):
    field, asked = field_ref[...], asked_ref[...]
    near_hot, asked_hot = near_onehot(where_ref[NEAR]), port_onehot(asked)
    tiles = slot_ref.shape[0]
    near_values[...] = pick_right(field, near_hot, NT)
    values = pick_right(field, wide_onehot(asked_hot, tiles), NT)
    for g in range(tiles):
        slot_ref[g] = values[:, g * LANES : (g + 1) * LANES]
    component_products(near_near, near_values, where_ref, near_part)
    slot_products(far_far, slot_ref, asked, slot_part)
    inner_ref[...] = pick_right(near_part[...], near_hot, NN) + slots_to_ports(slot_part, asked_hot)


def near_cross(parts, arrived_ref, pitch, kind_ref, stiff_ref, near_ref, owner_ref, near_far, far_values, near_part):
    slots = onehot(jnp.concatenate(owner_slots(where_ref[OWNER], parts), axis=0))
    far_values[...] = pick_right(get(arrived_ref, 0, pitch, 3), slots, TN)
    component_products(near_far, far_values, where_ref, near_part)
    return pick_right(near_part[...], near_onehot(near_ref[...]), NN)


def far_cross(arrived_ref, first, pitch, asked, asked_hot, far_near, slot_ref, slot_part):
    tiles = slot_ref.shape[0]
    values = jnp.transpose(get(arrived_ref, first, pitch, 3))
    values = pad_lanes(values, tiles * LANES - values.shape[1])
    for g in range(tiles):
        slot_ref[g] = values[:, g * LANES : (g + 1) * LANES]
    slot_products(far_near, slot_ref, asked, slot_part)
    return slots_to_ports(slot_part, asked_hot)


def image_kernel(
    parts, groups, last, arrived_ref, inner_hbm, asked_ref, where_ref,
    near_far, far_near, *rest,
):
    if last:
        case_ref, gram_ref, near_values, turned_near, turned_far = rest[:5]
        images, rest = rest[5 : 5 + groups], rest[5 + groups :]
        image_ref, copies_ref, turned_ref, near_part, slot_ref, slot_part, far_values, inner_ref, sem = rest
    else:
        meta_ref, image_ref, far_values, pay_ref, near_part, slot_ref, slot_part, inner_ref, sem = rest
    fetch = pltpu.make_async_copy(inner_hbm, inner_ref, sem)
    fetch.start()
    asked = asked_ref[...]
    asked_hot = port_onehot(asked)
    slots = onehot(jnp.concatenate(owner_slots(where_ref[OWNER], parts), axis=0))
    far_values[...] = pick_right(get(arrived_ref, 0, 18, 3), slots, TN)
    component_products(near_far, far_values, where_ref, near_part)
    tiles = slot_ref.shape[0]
    values = jnp.transpose(get(arrived_ref, 9, 18, 3))
    values = pad_lanes(values, tiles * LANES - values.shape[1])
    for g in range(tiles):
        slot_ref[g] = values[:, g * LANES : (g + 1) * LANES]
    slot_products(far_near, slot_ref, asked, slot_part)
    fetch.wait()
    image = inner_ref[...] + pick_right(near_part[...], near_onehot(where_ref[NEAR]), NN)
    image = image + slots_to_ports(slot_part, asked_hot)
    image_ref[...] = image
    if last:
        gram = add_products(LANES, images, [image_ref], [3 * groups * CASES], case_ref[0], gram_ref[...])
        for p in range(copies_ref.shape[0]):
            copies_ref[p] = gram
        turned_rows(near_values, far_values, where_ref, turned_near, turned_far, turned_ref)
    else:
        send_ports(image, asked_hot, port_onehot(meta_ref[...]), pay_ref)


def turned_rows(near_values, far_values, where_ref, turned_near, turned_far, out_ref):
    dofs = near_values.shape[0] // CASES
    modes = out_ref.shape[0] // CASES
    kind = where_ref[KIND]
    kind2 = jnp.concatenate([kind, kind], axis=1)
    for k in range(0, CASES, 2):
        sums = 0.0
        for table, part in ((turned_near, near_values), (turned_far, far_values)):
            values = jnp.concatenate(
                [part[pl.ds(k + i, dofs, stride=CASES), :] for i in range(2)], axis=1
            )
            sums = sums + dot(table[...], stacked_values(values))
        result = by_kind(sums, kind2, modes)
        for i in range(2):
            out_ref[pl.ds(k + i, modes, stride=CASES), :] = result[:, i * LANES : (i + 1) * LANES]


def turned_kernel(groups, case_ref, near_values, far_values, where_ref, turned_near, turned_far, *rest):
    outs, out_ref = rest[:groups], rest[groups]
    turned_rows(near_values, far_values, where_ref, turned_near, turned_far, out_ref)
    part = outs[0].shape[0]
    for h in range(groups):
        at = pl.multiple_of(lax.rem(case_ref[0] + h, groups) * part, part)
        outs[h][...] = out_ref[pl.ds(at, part), :]


def messages_kernel(groups, case_ref, field_ref, turned_ref, own_ref, *rest):
    messages, (field, turned, sems) = rest[: groups - 1], rest[groups - 1 :]
    rows = field_ref.shape[0]
    part = own_ref.shape[0]
    fetches = [
        pltpu.make_async_copy(turned_ref, turned, sems.at[0]),
        pltpu.make_async_copy(field_ref, field, sems.at[groups]),
    ]
    for fetch in fetches:
        fetch.start()
    for fetch in fetches:
        fetch.wait()
    copies = []
    for h in range(groups):
        at = pl.multiple_of(lax.rem(case_ref[0] + h, groups) * part, part)
        target = messages[h - 1].at[pl.ds(rows, part), :] if h else own_ref
        copies.append(pltpu.make_async_copy(turned.at[pl.ds(at, part), :], target, sems.at[h]))
        if h:
            copies.append(pltpu.make_async_copy(field, messages[h - 1].at[pl.ds(0, rows), :], sems.at[groups + h]))
    for copy in copies:
        copy.start()
    for copy in copies:
        copy.wait()


def add_products(lanes, lefts, rights, first, case, out):
    groups = len(lefts)
    total = groups * CASES
    dofs = lefts[0].shape[0] // CASES
    lane = iota((CASES, LANES), 1)
    for h in range(groups):
        def step(d, sums):
            own = pl.ds(pl.multiple_of(d * CASES, CASES), CASES)
            values = [ref[own, :] for ref in rights]
            new = []
            for i in range(CASES):
                row = lefts[h][pl.ds(d * CASES + i, 1), :]
                new.append(tuple(s + row * v for s, v in zip(sums[i], values)))
            return tuple(new)

        zero = jnp.zeros((CASES, LANES), F32)
        sums = lax.fori_loop(0, dofs, step, ((zero,) * len(rights),) * CASES)
        at = lax.rem(case + h, groups) * CASES
        for i in range(CASES):
            for g in range(len(rights)):
                value = jnp.sum(sums[i][g], axis=1, keepdims=True)
                out = jnp.where(lane == first[g] + at + i, value, out)
    return out


def gram_kernel(groups, case_ref, *refs):
    base, image, out_ref = refs[:groups], refs[groups : 2 * groups], refs[2 * groups]
    total = groups * CASES
    out = jnp.zeros((CASES, LANES), F32)
    out = add_products(LANES, base, [base[0], image[0]], [0, total], case_ref[0], out)
    out_ref[...] = add_products(LANES, image, [image[0]], [2 * total], case_ref[0], out)


def sum_kernel(in_ref, out_ref):
    for q in range(in_ref.shape[0]):
        total = in_ref[q, 0]
        for p in range(1, in_ref.shape[1]):
            total = total + in_ref[q, p]
        for p in range(out_ref.shape[0]):
            out_ref[p, q * CASES : (q + 1) * CASES, :] = total


def inverse2(p, q, r, s):
    scale = 1.0 / (p * s - q * r)
    return s * scale, -q * scale, -r * scale, p * scale


def spd_solve(matrix, target):
    n = matrix.shape[0]
    a = jnp.concatenate([matrix, target], axis=1)
    row_of = iota(a.shape, 0)
    for k in range(0, n, 4):
        c = [jnp.broadcast_to(a[:, k + i : k + i + 1], a.shape) for i in range(4)]
        r = [a[k + i : k + i + 1] for i in range(4)]
        p = [[c[j][k + i : k + i + 1] for j in range(4)] for i in range(4)]
        a00, a01, a10, a11 = inverse2(p[0][0], p[0][1], p[1][0], p[1][1])
        e00, e01 = p[2][0] * a00 + p[2][1] * a10, p[2][0] * a01 + p[2][1] * a11
        e10, e11 = p[3][0] * a00 + p[3][1] * a10, p[3][0] * a01 + p[3][1] * a11
        i00, i01, i10, i11 = inverse2(
            p[2][2] - (e00 * p[0][2] + e01 * p[1][2]),
            p[2][3] - (e00 * p[0][3] + e01 * p[1][3]),
            p[3][2] - (e10 * p[0][2] + e11 * p[1][2]),
            p[3][3] - (e10 * p[0][3] + e11 * p[1][3]),
        )
        t2 = r[2] - (e00 * r[0] + e01 * r[1])
        t3 = r[3] - (e10 * r[0] + e11 * r[1])
        u2, u3 = i00 * t2 + i01 * t3, i10 * t2 + i11 * t3
        w0 = r[0] - (p[0][2] * u2 + p[0][3] * u3)
        w1 = r[1] - (p[1][2] * u2 + p[1][3] * u3)
        u = [a00 * w0 + a01 * w1, a10 * w0 + a11 * w1, u2, u3]
        a = a - ((c[0] * u[0] + c[1] * u[1]) + (c[2] * u[2] + c[3] * u[3]))
        for i in range(4):
            a = jnp.where(row_of == k + i, u[i], a)
    return a[:, n:]


def symmetric(m):
    return 0.5 * (m + jnp.transpose(m))


def solve_kernel(groups, case_ref, gram_ref, *rest):
    pieces, (coef, *outs), (held, coef_rows, turned_coef, sems) = (
        rest[: 2 * groups], rest[2 * groups : 3 * groups + 1], rest[3 * groups + 1 :]
    )
    part = held.shape[1]
    fetches = [
        pltpu.make_async_copy(piece.at[pl.ds(piece.shape[0] - part, part), :], held.at[i], sems.at[i])
        for i, piece in enumerate(pieces)
    ]
    for fetch in fetches:
        fetch.start()
    n = groups * CASES
    total = gram_ref[0]
    for p in range(1, gram_ref.shape[0]):
        total = total + gram_ref[p]
    g00, g01, g11, g12 = [symmetric(total[:, g * n : (g + 1) * n]) for g in range(4)]
    steps = spd_solve(g01, jnp.concatenate([g00, g11], axis=1))
    step0, step1 = steps[:, :n], steps[:, n:]
    both = dot_high(g11, steps)
    second = spd_solve(symmetric(g12 - both[:, n:]), g01 - both[:, :n])
    first = step0 - dot_high(step1, second)
    first, second = jnp.transpose(first), jnp.transpose(second)
    turned_coef[0] = jnp.concatenate([first] * (LANES // n), axis=1)
    turned_coef[1] = jnp.concatenate([second] * (LANES // n), axis=1)
    shift = LANES - case_ref[0] * CASES
    for q in range(groups):
        at = pl.multiple_of(lax.rem(case_ref[0] + q, groups) * CASES, CASES)
        for h in range(2):
            mine = pltpu.roll(turned_coef[h, pl.ds(at, CASES), :], shift, 1)
            coef_rows[q * CASES : (q + 1) * CASES, h * LANES : (h + 1) * LANES] = mine
            if q == 0:
                for j in range(n):
                    coef[h * n + j] = jnp.broadcast_to(mine[:, j : j + 1], (CASES, LANES))
    for fetch in fetches:
        fetch.wait()
    left = stacked_table(jnp.concatenate([coef_rows[:, :n], coef_rows[:, LANES : LANES + n]], axis=1))
    for m in range(0, part // CASES, 2):
        values = [
            jnp.concatenate([held[i, at : at + CASES, :] for i in range(2 * groups)], axis=0)
            for at in (m * CASES, (m + 1) * CASES)
        ]
        result = dot(left, stacked_values(jnp.concatenate(values, axis=1)))
        for i in range(2):
            for h in range(groups):
                outs[h][(m + i) * CASES : (m + i + 1) * CASES, :] = result[
                    h * CASES : (h + 1) * CASES, i * LANES : (i + 1) * LANES
                ]


def ports_kernel(groups, coef, *refs):
    base, image, second = [refs[g * groups : (g + 1) * groups] for g in range(3)]
    x_ref, residual_ref = refs[3 * groups :]
    n = groups * CASES
    dofs = x_ref.shape[0] // CASES
    wide = 4

    def ports(block, carry):
        d0 = block * wide
        own = [pl.ds(pl.multiple_of((d0 + i) * CASES, CASES), CASES) for i in range(wide)]
        x = [jnp.zeros((CASES, LANES), F32)] * wide
        r = [base[0][own[i], :] for i in range(wide)]
        for j in range(n):
            q, c = divmod(j, CASES)
            c0, c1 = coef[j], coef[n + j]
            for i in range(wide):
                row = pl.ds((d0 + i) * CASES + c, 1)
                a = image[q][row, :]
                x[i] = x[i] + (c0 * base[q][row, :] + c1 * a)
                r[i] = r[i] - (c0 * a + c1 * second[q][row, :])
        for i in range(wide):
            x_ref[own[i], :] = x[i]
            residual_ref[own[i], :] = r[i]
        return carry

    lax.fori_loop(0, dofs // wide, ports, 0)


def join_kernel(groups, case_ref, bubble_ref, *refs):
    parts, out_ref = refs[:groups], refs[groups]
    part = parts[0].shape[0]
    for h in range(groups):
        at = pl.ds(pl.multiple_of(lax.rem(case_ref[0] + h, groups) * part, part), part)
        out_ref[at, :] = bubble_ref[at, :] - parts[h][...]


def call(kernel, outs, scratch=(), name=None, flops=0, smem=(), hbm=(), anywhere=(), sems=0, limit=12):
    results = [(pltpu.HBM if far else jax.ShapeDtypeStruct)(shape, dtype) for shape, dtype, far in outs]
    vmem = pl.BlockSpec(memory_space=pltpu.VMEM)
    far_spec = pl.BlockSpec(memory_space=pltpu.HBM)
    copies_only = name == "messages"

    def run(*args):
        specs = [
            pl.BlockSpec(memory_space=pltpu.SMEM) if i in smem else far_spec if i in hbm else pl.BlockSpec(memory_space=pl.ANY) if i in anywhere else vmem
            for i in range(len(args))
        ]
        moved = sum(a.size * a.dtype.itemsize for a in args)
        args = [pltpu.with_memory_space_constraint(a, pltpu.HBM) if i in hbm else a for i, a in enumerate(args)]
        return pl.pallas_call(
            kernel,
            out_shape=results,
            in_specs=specs,
            out_specs=[far_spec if copies_only else vmem] * len(outs),
            scratch_shapes=[pltpu.VMEM(*shape) if isinstance(shape[0], tuple) else pltpu.VMEM(shape, F32) for shape in scratch]
            + ([pltpu.SemaphoreType.DMA((sems,) if sems > 1 else ())] if sems else []),
            compiler_params=pltpu.CompilerParams(vmem_limit_bytes=limit << 20),
            cost_estimate=pl.CostEstimate(flops=flops, bytes_accessed=moved, transcendentals=0),
            name=name,
        )(*args)

    return run


def exchange(rows, parts):
    moved = lax.all_to_all(rows.reshape(parts, 1, -1), PLANE, split_axis=0, concat_axis=0)
    return moved.reshape(rows.shape)


def local(
    comp_type, stiffness, near_port, far_owner, far_port, bubble_load, port_load,
    bubble_inverse, coupling, port_block,
):
    parts = lax.axis_size("px") * lax.axis_size("py")
    groups = lax.axis_size("case")
    modes, cases, comps = bubble_load.shape
    dofs, _, ports = port_load.shape
    rows, bubbles = dofs * cases, modes * cases
    slot_tiles = -(-SLOTS * parts // LANES)
    coupling = jnp.swapaxes(coupling, 1, 2)
    kind = comp_type.reshape(1, comps)
    stiff = stiffness.reshape(1, comps)
    near = near_port.reshape(1, comps)
    owner = far_owner.reshape(1, comps)
    far = far_port.reshape(1, comps)
    loads = bubble_load.reshape(bubbles, comps)
    field_of = ((rows, ports), F32, True)
    meta_of = ((parts, LANES), F32, False)
    bubble_of = ((bubbles, comps), F32, True)
    given = (kind, stiff, near, owner, far, loads, bubble_inverse, coupling)
    pay, near_sum, meta, where = call(
        functools.partial(condense_kernel, parts),
        [((parts * 10, LANES), F32, False), field_of, meta_of, ((8, LANES), F32, False)],
        [(a.shape, a.dtype) for a in given] + [(rows, comps)] * 2,
        "condense",
        hbm=range(len(given)),
        sems=len(given),
    )(*given)
    near_near, near_far, far_near, far_far, turned_near, turned_far, bubble_base = call(
        tables_kernel,
        [((KINDS * dofs, 3 * dofs), BF16, False)] * 4 + [((KINDS * modes, 3 * dofs), BF16, True)] * 2 + [bubble_of],
        name="tables",
        flops=10**9,
    )(where, loads, bubble_inverse, coupling, port_block)
    base, pay, asked = call(
        functools.partial(rhs_kernel, parts),
        [field_of, ((parts * 18, LANES), F32, False), meta_of],
        name="rhs",
    )(exchange(pay, parts), near_sum, port_load.reshape(rows, ports), meta)

    case = lax.axis_index("case").reshape(1)
    part = bubbles // groups
    part_of = ((part, comps), F32, True)
    slot_scratch = [(slot_tiles, rows, LANES)] * 2

    def to_cases(messages):
        backward = [
            lax.ppermute(message, "case", [(k, (k + h) % groups) for k in range(groups)])
            for h, message in enumerate(messages, 1)
        ]
        return backward[::-1]

    def inner(field):
        return call(inner_kernel, [field_of] * 2, [(rows, comps)] + slot_scratch, "inner", flops=10**9)(
            field, asked, where, near_near, far_far
        )

    arrived = exchange(pay, parts)
    base_all = to_cases([base] * (groups - 1))
    base_inner, base_near = inner(base)
    arrived, *base_all = lax.optimization_barrier((arrived, *base_all))
    image, base_far, pay = call(
        functools.partial(image_kernel, parts, groups, False),
        [((rows, ports), F32, False)] * 2 + [((parts * 18, LANES), F32, False)],
        [(rows, comps)] + slot_scratch + [(rows, ports)],
        "image",
        hbm=(1,),
        sems=1,
    )(arrived, base_inner, asked, where, near_far, far_near, meta)
    arrived = exchange(pay, parts)
    image_all = to_cases([image] * (groups - 1))
    turned0, *messages = call(
        functools.partial(turned_kernel, groups),
        [part_of] * groups,
        [(bubbles, comps)],
        "turned",
        flops=10**9,
        smem=(0,),
    )(case, base_near, base_far, where, turned_near, turned_far)
    turned0_all = to_cases(messages)
    image_inner, image_near = inner(image)
    (gram,) = call(functools.partial(gram_kernel, groups), [((cases, LANES), F32, False)], name="gram", smem=(0,))(
        case, base, *base_all, image, *image_all
    )
    arrived, *turned0_all = lax.optimization_barrier((arrived, *turned0_all))
    minor = lax.axis_size("py")
    second, copies, turned1 = call(
        functools.partial(image_kernel, parts, groups, True),
        [field_of, ((groups * minor, cases, LANES), F32, True), bubble_of],
        [(rows, comps)] + slot_scratch + [(rows, comps), (rows, ports)],
        "second",
        smem=(6,),
        hbm=(1,),
        sems=1,
    )(
        arrived, image_inner, asked, where, near_far, far_near, case, gram, image_near, turned_near, turned_far,
        image, *image_all,
    )
    copies = lax.all_to_all(copies, ("case", "py"), split_axis=0, concat_axis=0)
    turned1, *messages = call(
        functools.partial(messages_kernel, groups),
        [part_of] + [((rows + part, comps), F32, True)] * (groups - 1),
        [(rows, ports), (bubbles, comps)],
        "messages",
        flops=10**9,
        smem=(0,),
        hbm=(1, 2),
        sems=2 * groups,
    )(case, second, turned1)
    both1 = to_cases(messages)
    (copies,) = call(sum_kernel, [((parts // minor, groups * cases, LANES), F32, False)], name="sum")(
        copies.reshape(groups, minor, cases, LANES)
    )
    copies = lax.all_to_all(copies, "px", split_axis=0, concat_axis=0)
    pieces = [turned0, *turned0_all, turned1, *both1]
    coef, own, *messages = call(
        functools.partial(solve_kernel, groups),
        [((2 * groups * cases, cases, LANES), F32, False)] + [((part, comps), F32, False)] * groups,
        [(2 * groups, part, comps), (groups * cases, 2 * LANES), (2, groups * cases, LANES)],
        "solve",
        smem=(0,),
        anywhere=range(2, 2 + len(pieces)),
        sems=len(pieces),
    )(case, copies, *pieces)
    back = to_cases(messages)
    x, residual = call(
        functools.partial(ports_kernel, groups), [field_of, field_of], name="ports", flops=10**9
    )(coef, base, *base_all, image, *image_all, second, *both1)
    (bubble,) = call(functools.partial(join_kernel, groups), [bubble_of], name="join", smem=(0,))(
        case, bubble_base, own, *back
    )
    return (
        x.reshape(port_load.shape),
        residual.reshape(port_load.shape),
        bubble.reshape(bubble_load.shape),
    )


def solution(mesh):
    placed = (
        P(PLANE),
        P(PLANE),
        P(PLANE),
        P(PLANE, None),
        P(PLANE),
        P(None, "case", PLANE),
        P(None, "case", PLANE),
        P(),
        P(),
        P(),
    )
    out = P(None, "case", PLANE)
    return jax.shard_map(
        local, mesh=mesh, in_specs=placed, out_specs=(out, out, out), check_vma=False
    )
```

```python
import functools

import jax
import jax.numpy as jnp
from jax import lax
from jax.experimental import pallas as pl
from jax.experimental.pallas import tpu as pltpu
from jax.sharding import PartitionSpec as P

HIGH = lax.Precision.HIGHEST
PLANE = ("px", "py")
F32 = jnp.float32
BF16 = jnp.bfloat16
KINDS = 8
LANES = 128
CASES = 8
SLOTS = 3
NN = (((1,), (0,)), ((), ()))
NT = (((1,), (1,)), ((), ()))
TN = (((0,), (0,)), ((), ()))


def dot(lhs, rhs, dims=NN):
    return lax.dot_general(lhs, rhs, dims, preferred_element_type=F32)


def dot_high(lhs, rhs, dims=NN):
    return lax.dot_general(lhs, rhs, dims, precision=HIGH, preferred_element_type=F32)


def split2(x):
    high = x.astype(BF16)
    return high, (x - high.astype(F32)).astype(BF16)


def pick_right(x, onehot, dims):
    (left,), (right,) = dims[0]
    return dot(jnp.concatenate(split2(x), axis=left), jnp.concatenate([onehot, onehot], axis=right), dims)


def pick_left(onehot, x, dims):
    (left,), (right,) = dims[0]
    return dot(jnp.concatenate([onehot, onehot], axis=left), jnp.concatenate(split2(x), axis=right), dims)


def stacked_table(table):
    high, low = split2(table)
    return jnp.concatenate([high, high, low], axis=1)


def stacked_values(x):
    high, low = split2(x)
    return jnp.concatenate([high, low, high], axis=0)


def iota(shape, dim):
    return lax.broadcasted_iota(jnp.int32, shape, dim)


def column(row):
    return jnp.transpose(jnp.broadcast_to(row, (8, row.shape[1])))[:, :1]


def onehot(mask):
    return mask.astype(F32).astype(BF16)


KIND, STIFF, NEAR, OWNER = [slice(i, i + 1) for i in range(4)]


def owner_slots(owner, parts):
    count = owner.shape[1]
    owner_f = owner.astype(F32)
    same = (column(owner_f) == owner_f) & (iota((count, count), 0) < iota((count, count), 1))
    rank = jnp.sum(same.astype(F32), axis=0, keepdims=True).astype(jnp.int32)
    to = iota((parts, count), 0).astype(F32) == owner_f
    return [to & (rank == s) for s in range(SLOTS)]


def near_onehot(near):
    count = near.shape[1]
    return onehot(column(near.astype(F32)) == iota((count, LANES), 1).astype(F32))


def stacked_rows(meta, lanes):
    turned = jnp.transpose(meta)
    return jnp.concatenate([turned[lanes + s : lanes + s + 1, :] for s in range(SLOTS)], axis=1)


def port_onehot(meta):
    parts = meta.shape[0]
    ports = (iota((parts, LANES), 1) + 1).astype(F32)
    return onehot(jnp.concatenate([meta[:, s : s + 1] == ports for s in range(SLOTS)], axis=0))


def pad_lanes(x, spare):
    if not spare:
        return x
    return jnp.concatenate([x, jnp.zeros((x.shape[0], spare), x.dtype)], axis=1)


def put(pay_ref, rows, first, pitch):
    parts = pay_ref.shape[0] // pitch
    tiles = rows.shape[1] // LANES
    for g in range(rows.shape[0] // parts):
        for t in range(tiles):
            pay_ref[pl.ds(first + g * tiles + t, parts, stride=pitch), :] = rows[
                g * parts : (g + 1) * parts, t * LANES : (t + 1) * LANES
            ]


def get(pay_ref, first, pitch, tiles):
    parts = pay_ref.shape[0] // pitch
    return jnp.concatenate(
        [
            jnp.concatenate(
                [pay_ref[pl.ds(first + s * tiles + t, parts, stride=pitch), :] for t in range(tiles)],
                axis=1,
            )
            for s in range(SLOTS)
        ],
        axis=0,
    )


def by_kind(products, kind, rows):
    chosen = products[:rows]
    for t in range(1, KINDS):
        chosen = jnp.where(kind == t, products[t * rows : (t + 1) * rows], chosen)
    return chosen


def condense_kernel(
    parts, kind_hbm, stiff_hbm, near_hbm, owner_hbm, far_hbm, load_hbm, inverse_hbm, coupling_hbm,
    pay_ref, near_sum_ref, meta_ref, where_ref,
    kind_ref, stiff_ref, near_ref, owner_ref, far_ref, load_ref, inverse_ref, coupling_ref, near_part, far_part, sems,
):
    copies = [
        pltpu.make_async_copy(source, target, sems.at[i])
        for i, (source, target) in enumerate((
            (inverse_hbm, inverse_ref), (coupling_hbm, coupling_ref), (load_hbm, load_ref), (kind_hbm, kind_ref),
            (stiff_hbm, stiff_ref), (near_hbm, near_ref), (owner_hbm, owner_ref), (far_hbm, far_ref),
        ))
    ]
    for copy in copies:
        copy.start()
    for copy in copies:
        copy.wait()
    modes = load_ref.shape[0] // CASES
    dofs = near_sum_ref.shape[0] // CASES
    left = stacked_table(
        jnp.concatenate(
            [jnp.transpose(dot_high(inverse_ref[t], coupling_ref[t], TN)) for t in range(KINDS)], axis=0
        )
    )
    kind = kind_ref[...]
    kind2 = jnp.concatenate([kind, kind], axis=1)
    for k in range(0, CASES, 2):
        loads = jnp.concatenate(
            [load_ref[pl.ds(k + i, modes, stride=CASES), :] for i in range(2)], axis=1
        )
        condensed = -by_kind(dot(left, stacked_values(loads)), kind2, 2 * dofs)
        for i in range(2):
            lanes = slice(i * LANES, (i + 1) * LANES)
            near_part[pl.ds(k + i, dofs, stride=CASES), :] = condensed[:dofs, lanes]
            far_part[pl.ds(k + i, dofs, stride=CASES), :] = condensed[dofs:, lanes]
    near = near_ref[...]
    slots = owner_slots(owner_ref[...], parts)
    near_sum_ref[...] = pick_right(near_part[...], near_onehot(near), NN)
    chosen = onehot(jnp.concatenate(slots, axis=0))
    put(pay_ref, pick_left(chosen, far_part[...], NT), 0, 10)
    lane = iota((parts, LANES), 1)
    far_row = (far_ref[...] + 1).astype(F32)
    near_row = (near + 1).astype(F32)
    message = jnp.zeros((parts, LANES), F32)
    own = jnp.zeros((parts, LANES), F32)
    for s in range(SLOTS):
        for at, row in ((0, far_row), (SLOTS, kind.astype(F32)), (2 * SLOTS, stiff_ref[...])):
            value = jnp.sum(jnp.where(slots[s], row, 0.0), axis=1, keepdims=True)
            message = jnp.where(lane == at + s, value, message)
        value = jnp.sum(jnp.where(slots[s], near_row, 0.0), axis=1, keepdims=True)
        own = jnp.where(lane == s, value, own)
    pay_ref[pl.ds(9, parts, stride=10), :] = message
    packed = [kind.astype(F32), stiff_ref[...], near.astype(F32), owner_ref[...].astype(F32)]
    where_ref[...] = jnp.concatenate(packed + packed, axis=0)
    meta_ref[...] = own


def tables_kernel(
    where_ref, load_ref, inverse_ref, coupling_ref, block_ref,
    near_near, near_far, far_near, far_far, turned_near, turned_far, base_ref,
):
    dofs = block_ref.shape[1] // 2
    modes = inverse_ref.shape[1]
    inverses = []
    for t in range(KINDS):
        turned = dot_high(inverse_ref[t], coupling_ref[t], TN)
        schur = block_ref[t] - dot_high(turned, coupling_ref[t], TN)
        at = slice(t * dofs, (t + 1) * dofs)
        near_near[at, :] = stacked_table(schur[:dofs, :dofs])
        near_far[at, :] = stacked_table(schur[:dofs, dofs:])
        far_near[at, :] = stacked_table(schur[dofs:, :dofs])
        far_far[at, :] = stacked_table(schur[dofs:, dofs:])
        at = slice(t * modes, (t + 1) * modes)
        turned_near[at, :] = stacked_table(turned[:, :dofs])
        turned_far[at, :] = stacked_table(turned[:, dofs:])
        inverses.append(inverse_ref[t])
    left = stacked_table(jnp.concatenate(inverses, axis=0))
    kind = where_ref[KIND]
    stiff = where_ref[STIFF]
    kind2 = jnp.concatenate([kind, kind], axis=1)
    stiff2 = jnp.concatenate([stiff, stiff], axis=1)
    for k in range(0, CASES, 2):
        loads = jnp.concatenate(
            [load_ref[pl.ds(k + i, modes, stride=CASES), :] for i in range(2)], axis=1
        )
        result = by_kind(dot(left, stacked_values(loads)), kind2, modes) / stiff2
        for i in range(2):
            base_ref[pl.ds(k + i, modes, stride=CASES), :] = result[:, i * LANES : (i + 1) * LANES]


def send_ports(field, asked, own, pay_ref):
    put(pay_ref, pick_left(jnp.concatenate([asked, own], axis=0), field, NT), 0, 18)


def rhs_kernel(parts, arrived_ref, near_sum_ref, load_ref, meta_ref, field_ref, pay_ref, asked_ref):
    asked = arrived_ref[pl.ds(9, parts, stride=10), :]
    asked_ref[...] = asked
    asked_hot = port_onehot(asked)
    arrived = get(arrived_ref, 0, 10, 3)
    field = load_ref[...] + (near_sum_ref[...] + pick_right(arrived, asked_hot, TN))
    field_ref[...] = field
    send_ports(field, asked_hot, port_onehot(meta_ref[...]), pay_ref)


def component_products(table_ref, part_ref, where_ref, out_ref):
    dofs = part_ref.shape[0] // CASES
    kind, stiff = where_ref[KIND], where_ref[STIFF]
    kind2 = jnp.concatenate([kind, kind], axis=1)
    stiff2 = jnp.concatenate([stiff, stiff], axis=1)
    for k in range(0, CASES, 2):
        values = jnp.concatenate(
            [part_ref[pl.ds(k + i, dofs, stride=CASES), :] for i in range(2)], axis=1
        )
        result = by_kind(dot(table_ref[...], stacked_values(values)), kind2, dofs) * stiff2
        for i in range(2):
            out_ref[pl.ds(k + i, dofs, stride=CASES), :] = result[:, i * LANES : (i + 1) * LANES]


def slot_products(table_ref, slot_ref, asked, out_ref):
    tiles = slot_ref.shape[0]
    dofs = slot_ref.shape[1] // CASES
    spare = tiles * LANES - SLOTS * asked.shape[0]
    kind = pad_lanes(stacked_rows(asked, SLOTS), spare)
    stiff = pad_lanes(stacked_rows(asked, 2 * SLOTS), spare)
    for k in range(CASES):
        values = jnp.concatenate(
            [slot_ref[g, pl.ds(k, dofs, stride=CASES), :] for g in range(tiles)], axis=1
        )
        result = by_kind(dot(table_ref[...], stacked_values(values)), kind, dofs) * stiff
        for g in range(tiles):
            out_ref[g, pl.ds(k, dofs, stride=CASES), :] = result[:, g * LANES : (g + 1) * LANES]


def wide_onehot(asked_hot, tiles):
    spare = tiles * LANES - asked_hot.shape[0]
    if not spare:
        return asked_hot
    return jnp.concatenate([asked_hot, jnp.zeros((spare, LANES), BF16)], axis=0)


def slots_to_ports(part_ref, asked_hot):
    tiles = part_ref.shape[0]
    hot = wide_onehot(asked_hot, tiles)
    total = pick_right(part_ref[0], hot[:LANES], NN)
    for g in range(1, tiles):
        total = total + pick_right(part_ref[g], hot[g * LANES : (g + 1) * LANES], NN)
    return total


def inner_kernel(
    field_ref, asked_ref, where_ref, near_near, far_far,
    inner_ref, near_values, near_part, slot_ref, slot_part,
):
    field, asked = field_ref[...], asked_ref[...]
    near_hot, asked_hot = near_onehot(where_ref[NEAR]), port_onehot(asked)
    tiles = slot_ref.shape[0]
    near_values[...] = pick_right(field, near_hot, NT)
    values = pick_right(field, wide_onehot(asked_hot, tiles), NT)
    for g in range(tiles):
        slot_ref[g] = values[:, g * LANES : (g + 1) * LANES]
    component_products(near_near, near_values, where_ref, near_part)
    slot_products(far_far, slot_ref, asked, slot_part)
    inner_ref[...] = pick_right(near_part[...], near_hot, NN) + slots_to_ports(slot_part, asked_hot)


def near_cross(parts, arrived_ref, pitch, kind_ref, stiff_ref, near_ref, owner_ref, near_far, far_values, near_part):
    slots = onehot(jnp.concatenate(owner_slots(where_ref[OWNER], parts), axis=0))
    far_values[...] = pick_right(get(arrived_ref, 0, pitch, 3), slots, TN)
    component_products(near_far, far_values, where_ref, near_part)
    return pick_right(near_part[...], near_onehot(near_ref[...]), NN)


def far_cross(arrived_ref, first, pitch, asked, asked_hot, far_near, slot_ref, slot_part):
    tiles = slot_ref.shape[0]
    values = jnp.transpose(get(arrived_ref, first, pitch, 3))
    values = pad_lanes(values, tiles * LANES - values.shape[1])
    for g in range(tiles):
        slot_ref[g] = values[:, g * LANES : (g + 1) * LANES]
    slot_products(far_near, slot_ref, asked, slot_part)
    return slots_to_ports(slot_part, asked_hot)


def image_kernel(
    parts, groups, last, arrived_ref, inner_ref, asked_ref, where_ref,
    near_far, far_near, *rest,
):
    if last:
        case_ref, gram_ref, near_values, turned_near, turned_far = rest[:5]
        images, rest = rest[5 : 5 + groups], rest[5 + groups :]
        image_ref, copies_ref, turned_ref, near_part, slot_ref, slot_part, far_values = rest
    else:
        meta_ref, image_ref, far_values, pay_ref, near_part, slot_ref, slot_part = rest
    asked = asked_ref[...]
    asked_hot = port_onehot(asked)
    slots = onehot(jnp.concatenate(owner_slots(where_ref[OWNER], parts), axis=0))
    far_values[...] = pick_right(get(arrived_ref, 0, 18, 3), slots, TN)
    component_products(near_far, far_values, where_ref, near_part)
    tiles = slot_ref.shape[0]
    values = jnp.transpose(get(arrived_ref, 9, 18, 3))
    values = pad_lanes(values, tiles * LANES - values.shape[1])
    for g in range(tiles):
        slot_ref[g] = values[:, g * LANES : (g + 1) * LANES]
    slot_products(far_near, slot_ref, asked, slot_part)
    image = inner_ref[...] + pick_right(near_part[...], near_onehot(where_ref[NEAR]), NN)
    image = image + slots_to_ports(slot_part, asked_hot)
    image_ref[...] = image
    if last:
        gram = add_products(LANES, images, [image_ref], [3 * groups * CASES], case_ref[0], gram_ref[...])
        for p in range(copies_ref.shape[0]):
            copies_ref[p] = gram
        turned_rows(near_values, far_values, where_ref, turned_near, turned_far, turned_ref)
    else:
        send_ports(image, asked_hot, port_onehot(meta_ref[...]), pay_ref)


def turned_rows(near_values, far_values, where_ref, turned_near, turned_far, out_ref):
    dofs = near_values.shape[0] // CASES
    modes = out_ref.shape[0] // CASES
    kind = where_ref[KIND]
    kind2 = jnp.concatenate([kind, kind], axis=1)
    for k in range(0, CASES, 2):
        sums = 0.0
        for table, part in ((turned_near, near_values), (turned_far, far_values)):
            values = jnp.concatenate(
                [part[pl.ds(k + i, dofs, stride=CASES), :] for i in range(2)], axis=1
            )
            sums = sums + dot(table[...], stacked_values(values))
        result = by_kind(sums, kind2, modes)
        for i in range(2):
            out_ref[pl.ds(k + i, modes, stride=CASES), :] = result[:, i * LANES : (i + 1) * LANES]


def turned_kernel(groups, case_ref, near_values, far_values, where_ref, turned_near, turned_far, *rest):
    outs, out_ref = rest[:groups], rest[groups]
    turned_rows(near_values, far_values, where_ref, turned_near, turned_far, out_ref)
    part = outs[0].shape[0]
    for h in range(groups):
        at = pl.multiple_of(lax.rem(case_ref[0] + h, groups) * part, part)
        outs[h][...] = out_ref[pl.ds(at, part), :]


def messages_kernel(groups, case_ref, field_ref, turned_ref, own_ref, *rest):
    messages, (field, turned, sems) = rest[: groups - 1], rest[groups - 1 :]
    rows = field_ref.shape[0]
    part = own_ref.shape[0]
    fetches = [
        pltpu.make_async_copy(turned_ref, turned, sems.at[0]),
        pltpu.make_async_copy(field_ref, field, sems.at[groups]),
    ]
    for fetch in fetches:
        fetch.start()
    for fetch in fetches:
        fetch.wait()
    copies = []
    for h in range(groups):
        at = pl.multiple_of(lax.rem(case_ref[0] + h, groups) * part, part)
        target = messages[h - 1].at[pl.ds(rows, part), :] if h else own_ref
        copies.append(pltpu.make_async_copy(turned.at[pl.ds(at, part), :], target, sems.at[h]))
        if h:
            copies.append(pltpu.make_async_copy(field, messages[h - 1].at[pl.ds(0, rows), :], sems.at[groups + h]))
    for copy in copies:
        copy.start()
    for copy in copies:
        copy.wait()


def add_products(lanes, lefts, rights, first, case, out):
    groups = len(lefts)
    total = groups * CASES
    dofs = lefts[0].shape[0] // CASES
    lane = iota((CASES, LANES), 1)
    for h in range(groups):
        def step(d, sums):
            own = pl.ds(pl.multiple_of(d * CASES, CASES), CASES)
            values = [ref[own, :] for ref in rights]
            new = []
            for i in range(CASES):
                row = lefts[h][pl.ds(d * CASES + i, 1), :]
                new.append(tuple(s + row * v for s, v in zip(sums[i], values)))
            return tuple(new)

        zero = jnp.zeros((CASES, LANES), F32)
        sums = lax.fori_loop(0, dofs, step, ((zero,) * len(rights),) * CASES)
        at = lax.rem(case + h, groups) * CASES
        for i in range(CASES):
            for g in range(len(rights)):
                value = jnp.sum(sums[i][g], axis=1, keepdims=True)
                out = jnp.where(lane == first[g] + at + i, value, out)
    return out


def base_gram_kernel(groups, case_ref, *refs):
    base, out_ref = refs[:groups], refs[groups]
    out_ref[...] = add_products(LANES, base, [base[0]], [0], case_ref[0], jnp.zeros((CASES, LANES), F32))


def gram_kernel(groups, case_ref, gram_ref, *refs):
    base, image, out_ref = refs[:groups], refs[groups : 2 * groups], refs[2 * groups]
    total = groups * CASES
    out = add_products(LANES, base, [image[0]], [total], case_ref[0], gram_ref[...])
    out_ref[...] = add_products(LANES, image, [image[0]], [2 * total], case_ref[0], out)


def sum_kernel(in_ref, out_ref):
    for q in range(in_ref.shape[0]):
        total = in_ref[q, 0]
        for p in range(1, in_ref.shape[1]):
            total = total + in_ref[q, p]
        for p in range(out_ref.shape[0]):
            out_ref[p, q * CASES : (q + 1) * CASES, :] = total


def inverse2(p, q, r, s):
    scale = 1.0 / (p * s - q * r)
    return s * scale, -q * scale, -r * scale, p * scale


def spd_solve(matrix, target):
    n = matrix.shape[0]
    a = jnp.concatenate([matrix, target], axis=1)
    row_of = iota(a.shape, 0)
    for k in range(0, n, 4):
        c = [jnp.broadcast_to(a[:, k + i : k + i + 1], a.shape) for i in range(4)]
        r = [a[k + i : k + i + 1] for i in range(4)]
        p = [[c[j][k + i : k + i + 1] for j in range(4)] for i in range(4)]
        a00, a01, a10, a11 = inverse2(p[0][0], p[0][1], p[1][0], p[1][1])
        e00, e01 = p[2][0] * a00 + p[2][1] * a10, p[2][0] * a01 + p[2][1] * a11
        e10, e11 = p[3][0] * a00 + p[3][1] * a10, p[3][0] * a01 + p[3][1] * a11
        i00, i01, i10, i11 = inverse2(
            p[2][2] - (e00 * p[0][2] + e01 * p[1][2]),
            p[2][3] - (e00 * p[0][3] + e01 * p[1][3]),
            p[3][2] - (e10 * p[0][2] + e11 * p[1][2]),
            p[3][3] - (e10 * p[0][3] + e11 * p[1][3]),
        )
        t2 = r[2] - (e00 * r[0] + e01 * r[1])
        t3 = r[3] - (e10 * r[0] + e11 * r[1])
        u2, u3 = i00 * t2 + i01 * t3, i10 * t2 + i11 * t3
        w0 = r[0] - (p[0][2] * u2 + p[0][3] * u3)
        w1 = r[1] - (p[1][2] * u2 + p[1][3] * u3)
        u = [a00 * w0 + a01 * w1, a10 * w0 + a11 * w1, u2, u3]
        a = a - ((c[0] * u[0] + c[1] * u[1]) + (c[2] * u[2] + c[3] * u[3]))
        for i in range(4):
            a = jnp.where(row_of == k + i, u[i], a)
    return a[:, n:]


def symmetric(m):
    return 0.5 * (m + jnp.transpose(m))


def solve_kernel(groups, case_ref, gram_ref, *rest):
    pieces, (coef, *outs), (held, coef_rows, turned_coef, sems) = (
        rest[: 2 * groups], rest[2 * groups : 3 * groups + 1], rest[3 * groups + 1 :]
    )
    part = held.shape[1]
    fetches = [
        pltpu.make_async_copy(piece.at[pl.ds(piece.shape[0] - part, part), :], held.at[i], sems.at[i])
        for i, piece in enumerate(pieces)
    ]
    for fetch in fetches:
        fetch.start()
    n = groups * CASES
    total = gram_ref[0]
    for p in range(1, gram_ref.shape[0]):
        total = total + gram_ref[p]
    g00, g01, g11, g12 = [symmetric(total[:, g * n : (g + 1) * n]) for g in range(4)]
    steps = spd_solve(g01, jnp.concatenate([g00, g11], axis=1))
    step0, step1 = steps[:, :n], steps[:, n:]
    both = dot_high(g11, steps)
    second = spd_solve(symmetric(g12 - both[:, n:]), g01 - both[:, :n])
    first = step0 - dot_high(step1, second)
    first, second = jnp.transpose(first), jnp.transpose(second)
    turned_coef[0] = jnp.concatenate([first] * (LANES // n), axis=1)
    turned_coef[1] = jnp.concatenate([second] * (LANES // n), axis=1)
    shift = LANES - case_ref[0] * CASES
    for q in range(groups):
        at = pl.multiple_of(lax.rem(case_ref[0] + q, groups) * CASES, CASES)
        for h in range(2):
            mine = pltpu.roll(turned_coef[h, pl.ds(at, CASES), :], shift, 1)
            coef_rows[q * CASES : (q + 1) * CASES, h * LANES : (h + 1) * LANES] = mine
            if q == 0:
                for j in range(n):
                    coef[h * n + j] = jnp.broadcast_to(mine[:, j : j + 1], (CASES, LANES))
    for fetch in fetches:
        fetch.wait()
    left = stacked_table(jnp.concatenate([coef_rows[:, :n], coef_rows[:, LANES : LANES + n]], axis=1))
    for m in range(0, part // CASES, 2):
        values = [
            jnp.concatenate([held[i, at : at + CASES, :] for i in range(2 * groups)], axis=0)
            for at in (m * CASES, (m + 1) * CASES)
        ]
        result = dot(left, stacked_values(jnp.concatenate(values, axis=1)))
        for i in range(2):
            for h in range(groups):
                outs[h][(m + i) * CASES : (m + i + 1) * CASES, :] = result[
                    h * CASES : (h + 1) * CASES, i * LANES : (i + 1) * LANES
                ]


def ports_kernel(groups, coef, *refs):
    base, image, second = [refs[g * groups : (g + 1) * groups] for g in range(3)]
    x_ref, residual_ref = refs[3 * groups :]
    n = groups * CASES
    dofs = x_ref.shape[0] // CASES
    wide = 4

    def ports(block, carry):
        d0 = block * wide
        own = [pl.ds(pl.multiple_of((d0 + i) * CASES, CASES), CASES) for i in range(wide)]
        x = [jnp.zeros((CASES, LANES), F32)] * wide
        r = [base[0][own[i], :] for i in range(wide)]
        for j in range(n):
            q, c = divmod(j, CASES)
            c0, c1 = coef[j], coef[n + j]
            for i in range(wide):
                row = pl.ds((d0 + i) * CASES + c, 1)
                a = image[q][row, :]
                x[i] = x[i] + (c0 * base[q][row, :] + c1 * a)
                r[i] = r[i] - (c0 * a + c1 * second[q][row, :])
        for i in range(wide):
            x_ref[own[i], :] = x[i]
            residual_ref[own[i], :] = r[i]
        return carry

    lax.fori_loop(0, dofs // wide, ports, 0)


def join_kernel(groups, case_ref, bubble_ref, *refs):
    parts, out_ref = refs[:groups], refs[groups]
    part = parts[0].shape[0]
    for h in range(groups):
        at = pl.ds(pl.multiple_of(lax.rem(case_ref[0] + h, groups) * part, part), part)
        out_ref[at, :] = bubble_ref[at, :] - parts[h][...]


def call(kernel, outs, scratch=(), name=None, flops=0, smem=(), hbm=(), anywhere=(), sems=0, limit=12):
    results = [(pltpu.HBM if far else jax.ShapeDtypeStruct)(shape, dtype) for shape, dtype, far in outs]
    vmem = pl.BlockSpec(memory_space=pltpu.VMEM)
    far_spec = pl.BlockSpec(memory_space=pltpu.HBM)
    copies_only = name == "messages"

    def run(*args):
        specs = [
            pl.BlockSpec(memory_space=pltpu.SMEM) if i in smem else far_spec if i in hbm else pl.BlockSpec(memory_space=pl.ANY) if i in anywhere else vmem
            for i in range(len(args))
        ]
        moved = sum(a.size * a.dtype.itemsize for a in args)
        args = [pltpu.with_memory_space_constraint(a, pltpu.HBM) if i in hbm else a for i, a in enumerate(args)]
        return pl.pallas_call(
            kernel,
            out_shape=results,
            in_specs=specs,
            out_specs=[far_spec if copies_only else vmem] * len(outs),
            scratch_shapes=[pltpu.VMEM(*shape) if isinstance(shape[0], tuple) else pltpu.VMEM(shape, F32) for shape in scratch]
            + ([pltpu.SemaphoreType.DMA((sems,) if sems > 1 else ())] if sems else []),
            compiler_params=pltpu.CompilerParams(vmem_limit_bytes=limit << 20),
            cost_estimate=pl.CostEstimate(flops=flops, bytes_accessed=moved, transcendentals=0),
            name=name,
        )(*args)

    return run


def exchange(rows, parts):
    moved = lax.all_to_all(rows.reshape(parts, 1, -1), PLANE, split_axis=0, concat_axis=0)
    return moved.reshape(rows.shape)


def local(
    comp_type, stiffness, near_port, far_owner, far_port, bubble_load, port_load,
    bubble_inverse, coupling, port_block,
):
    parts = lax.axis_size("px") * lax.axis_size("py")
    groups = lax.axis_size("case")
    modes, cases, comps = bubble_load.shape
    dofs, _, ports = port_load.shape
    rows, bubbles = dofs * cases, modes * cases
    slot_tiles = -(-SLOTS * parts // LANES)
    coupling = jnp.swapaxes(coupling, 1, 2)
    kind = comp_type.reshape(1, comps)
    stiff = stiffness.reshape(1, comps)
    near = near_port.reshape(1, comps)
    owner = far_owner.reshape(1, comps)
    far = far_port.reshape(1, comps)
    loads = bubble_load.reshape(bubbles, comps)
    field_of = ((rows, ports), F32, True)
    meta_of = ((parts, LANES), F32, False)
    bubble_of = ((bubbles, comps), F32, True)
    given = (kind, stiff, near, owner, far, loads, bubble_inverse, coupling)
    pay, near_sum, meta, where = call(
        functools.partial(condense_kernel, parts),
        [((parts * 10, LANES), F32, False), field_of, meta_of, ((8, LANES), F32, False)],
        [(a.shape, a.dtype) for a in given] + [(rows, comps)] * 2,
        "condense",
        hbm=range(len(given)),
        sems=len(given),
    )(*given)
    near_near, near_far, far_near, far_far, turned_near, turned_far, bubble_base = call(
        tables_kernel,
        [((KINDS * dofs, 3 * dofs), BF16, False)] * 4 + [((KINDS * modes, 3 * dofs), BF16, True)] * 2 + [bubble_of],
        name="tables",
        flops=10**9,
    )(where, loads, bubble_inverse, coupling, port_block)
    base, pay, asked = call(
        functools.partial(rhs_kernel, parts),
        [field_of, ((parts * 18, LANES), F32, False), meta_of],
        name="rhs",
    )(exchange(pay, parts), near_sum, port_load.reshape(rows, ports), meta)

    case = lax.axis_index("case").reshape(1)
    part = bubbles // groups
    part_of = ((part, comps), F32, True)
    slot_scratch = [(slot_tiles, rows, LANES)] * 2

    def to_cases(messages):
        backward = [
            lax.ppermute(message, "case", [(k, (k + h) % groups) for k in range(groups)])
            for h, message in enumerate(messages, 1)
        ]
        return backward[::-1]

    def inner(field):
        return call(inner_kernel, [((rows, ports), F32, False)] * 2, [(rows, comps)] + slot_scratch, "inner", flops=10**9)(
            field, asked, where, near_near, far_far
        )

    arrived = exchange(pay, parts)
    base_all = to_cases([base] * (groups - 1))
    base_inner, base_near = inner(base)
    gram_of = [((cases, LANES), F32, False)]
    (gram,) = call(functools.partial(base_gram_kernel, groups), gram_of, name="base_gram", smem=(0,))(
        case, base, *base_all
    )
    arrived, gram = lax.optimization_barrier((arrived, gram))
    image, base_far, pay = call(
        functools.partial(image_kernel, parts, groups, False),
        [((rows, ports), F32, False)] * 2 + [((parts * 18, LANES), F32, False)],
        [(rows, comps)] + slot_scratch,
        "image",
    )(arrived, base_inner, asked, where, near_far, far_near, meta)
    arrived = exchange(pay, parts)
    image_all = to_cases([image] * (groups - 1))
    turned0, *messages = call(
        functools.partial(turned_kernel, groups),
        [part_of] * groups,
        [(bubbles, comps)],
        "turned",
        flops=10**9,
        smem=(0,),
    )(case, base_near, base_far, where, turned_near, turned_far)
    turned0_all = to_cases(messages)
    image_inner, image_near = inner(image)
    (gram,) = call(functools.partial(gram_kernel, groups), gram_of, name="gram", smem=(0,))(
        case, gram, base, *base_all, image, *image_all
    )
    arrived, *turned0_all = lax.optimization_barrier((arrived, *turned0_all))
    minor = lax.axis_size("py")
    second, copies, turned1 = call(
        functools.partial(image_kernel, parts, groups, True),
        [field_of, ((groups * minor, cases, LANES), F32, True), bubble_of],
        [(rows, comps)] + slot_scratch + [(rows, comps)],
        "second",
        smem=(6,),
    )(
        arrived, image_inner, asked, where, near_far, far_near, case, gram, image_near, turned_near, turned_far,
        image, *image_all,
    )
    copies = lax.all_to_all(copies, ("case", "py"), split_axis=0, concat_axis=0)
    turned1, *messages = call(
        functools.partial(messages_kernel, groups),
        [part_of] + [((rows + part, comps), F32, True)] * (groups - 1),
        [(rows, ports), (bubbles, comps)],
        "messages",
        flops=10**9,
        smem=(0,),
        hbm=(1, 2),
        sems=2 * groups,
    )(case, second, turned1)
    both1 = to_cases(messages)
    (copies,) = call(sum_kernel, [((parts // minor, groups * cases, LANES), F32, False)], name="sum")(
        copies.reshape(groups, minor, cases, LANES)
    )
    copies = lax.all_to_all(copies, "px", split_axis=0, concat_axis=0)
    pieces = [turned0, *turned0_all, turned1, *both1]
    coef, own, *messages = call(
        functools.partial(solve_kernel, groups),
        [((2 * groups * cases, cases, LANES), F32, False)] + [((part, comps), F32, False)] * groups,
        [(2 * groups, part, comps), (groups * cases, 2 * LANES), (2, groups * cases, LANES)],
        "solve",
        smem=(0,),
        anywhere=range(2, 2 + len(pieces)),
        sems=len(pieces),
    )(case, copies, *pieces)
    back = to_cases(messages)
    x, residual = call(
        functools.partial(ports_kernel, groups), [field_of, field_of], name="ports", flops=10**9
    )(coef, base, *base_all, image, *image_all, second, *both1)
    (bubble,) = call(functools.partial(join_kernel, groups), [bubble_of], name="join", smem=(0,))(
        case, bubble_base, own, *back
    )
    return (
        x.reshape(port_load.shape),
        residual.reshape(port_load.shape),
        bubble.reshape(bubble_load.shape),
    )


def solution(mesh):
    placed = (
        P(PLANE),
        P(PLANE),
        P(PLANE),
        P(PLANE, None),
        P(PLANE),
        P(None, "case", PLANE),
        P(None, "case", PLANE),
        P(),
        P(),
        P(),
    )
    out = P(None, "case", PLANE)
    return jax.shard_map(
        local, mesh=mesh, in_specs=placed, out_specs=(out, out, out), check_vma=False
    )
```

```python
import functools

import jax
import jax.numpy as jnp
from jax import lax
from jax.experimental import pallas as pl
from jax.experimental.pallas import tpu as pltpu
from jax.sharding import PartitionSpec as P

HIGH = lax.Precision.HIGHEST
PLANE = ("px", "py")
F32 = jnp.float32
BF16 = jnp.bfloat16
KINDS = 8
LANES = 128
CASES = 8
SLOTS = 3
NN = (((1,), (0,)), ((), ()))
NT = (((1,), (1,)), ((), ()))
TN = (((0,), (0,)), ((), ()))


def dot(lhs, rhs, dims=NN):
    return lax.dot_general(lhs, rhs, dims, preferred_element_type=F32)


def dot_high(lhs, rhs, dims=NN):
    return lax.dot_general(lhs, rhs, dims, precision=HIGH, preferred_element_type=F32)


def split2(x):
    high = x.astype(BF16)
    return high, (x - high.astype(F32)).astype(BF16)


def pick_right(x, onehot, dims):
    (left,), (right,) = dims[0]
    return dot(jnp.concatenate(split2(x), axis=left), jnp.concatenate([onehot, onehot], axis=right), dims)


def pick_left(onehot, x, dims):
    (left,), (right,) = dims[0]
    return dot(jnp.concatenate([onehot, onehot], axis=left), jnp.concatenate(split2(x), axis=right), dims)


def stacked_table(table):
    high, low = split2(table)
    return jnp.concatenate([high, high, low], axis=1)


def stacked_values(x):
    high, low = split2(x)
    return jnp.concatenate([high, low, high], axis=0)


def iota(shape, dim):
    return lax.broadcasted_iota(jnp.int32, shape, dim)


def column(row):
    return jnp.transpose(jnp.broadcast_to(row, (8, row.shape[1])))[:, :1]


def onehot(mask):
    return mask.astype(F32).astype(BF16)


KIND, STIFF, NEAR, OWNER = [slice(i, i + 1) for i in range(4)]


def owner_slots(owner, parts):
    count = owner.shape[1]
    owner_f = owner.astype(F32)
    same = (column(owner_f) == owner_f) & (iota((count, count), 0) < iota((count, count), 1))
    rank = jnp.sum(same.astype(F32), axis=0, keepdims=True).astype(jnp.int32)
    to = iota((parts, count), 0).astype(F32) == owner_f
    return [to & (rank == s) for s in range(SLOTS)]


def near_onehot(near):
    count = near.shape[1]
    return onehot(column(near.astype(F32)) == iota((count, LANES), 1).astype(F32))


def stacked_rows(meta, lanes):
    turned = jnp.transpose(meta)
    return jnp.concatenate([turned[lanes + s : lanes + s + 1, :] for s in range(SLOTS)], axis=1)


def port_onehot(meta):
    parts = meta.shape[0]
    ports = (iota((parts, LANES), 1) + 1).astype(F32)
    return onehot(jnp.concatenate([meta[:, s : s + 1] == ports for s in range(SLOTS)], axis=0))


def pad_lanes(x, spare):
    if not spare:
        return x
    return jnp.concatenate([x, jnp.zeros((x.shape[0], spare), x.dtype)], axis=1)


def put(pay_ref, rows, first, pitch):
    parts = pay_ref.shape[0] // pitch
    tiles = rows.shape[1] // LANES
    for g in range(rows.shape[0] // parts):
        for t in range(tiles):
            pay_ref[pl.ds(first + g * tiles + t, parts, stride=pitch), :] = rows[
                g * parts : (g + 1) * parts, t * LANES : (t + 1) * LANES
            ]


def get(pay_ref, first, pitch, tiles):
    parts = pay_ref.shape[0] // pitch
    return jnp.concatenate(
        [
            jnp.concatenate(
                [pay_ref[pl.ds(first + s * tiles + t, parts, stride=pitch), :] for t in range(tiles)],
                axis=1,
            )
            for s in range(SLOTS)
        ],
        axis=0,
    )


def by_kind(products, kind, rows):
    chosen = products[:rows]
    for t in range(1, KINDS):
        chosen = jnp.where(kind == t, products[t * rows : (t + 1) * rows], chosen)
    return chosen


def condense_kernel(
    parts, kind_hbm, stiff_hbm, near_hbm, owner_hbm, far_hbm, load_hbm, inverse_hbm, coupling_hbm,
    pay_ref, near_sum_ref, meta_ref, where_ref,
    kind_ref, stiff_ref, near_ref, owner_ref, far_ref, load_ref, inverse_ref, coupling_ref, near_part, far_part, sems,
):
    copies = [
        pltpu.make_async_copy(source, target, sems.at[i])
        for i, (source, target) in enumerate((
            (inverse_hbm, inverse_ref), (coupling_hbm, coupling_ref), (load_hbm, load_ref), (kind_hbm, kind_ref),
            (stiff_hbm, stiff_ref), (near_hbm, near_ref), (owner_hbm, owner_ref), (far_hbm, far_ref),
        ))
    ]
    for copy in copies:
        copy.start()
    for copy in copies[:2]:
        copy.wait()
    modes = load_ref.shape[0] // CASES
    dofs = near_sum_ref.shape[0] // CASES
    left = stacked_table(
        jnp.concatenate(
            [jnp.transpose(dot_high(inverse_ref[t], coupling_ref[t], TN)) for t in range(KINDS)], axis=0
        )
    )
    for copy in copies[2:]:
        copy.wait()
    kind = kind_ref[...]
    kind2 = jnp.concatenate([kind, kind], axis=1)
    for k in range(0, CASES, 2):
        loads = jnp.concatenate(
            [load_ref[pl.ds(k + i, modes, stride=CASES), :] for i in range(2)], axis=1
        )
        condensed = -by_kind(dot(left, stacked_values(loads)), kind2, 2 * dofs)
        for i in range(2):
            lanes = slice(i * LANES, (i + 1) * LANES)
            near_part[pl.ds(k + i, dofs, stride=CASES), :] = condensed[:dofs, lanes]
            far_part[pl.ds(k + i, dofs, stride=CASES), :] = condensed[dofs:, lanes]
    near = near_ref[...]
    slots = owner_slots(owner_ref[...], parts)
    near_sum_ref[...] = pick_right(near_part[...], near_onehot(near), NN)
    chosen = onehot(jnp.concatenate(slots, axis=0))
    put(pay_ref, pick_left(chosen, far_part[...], NT), 0, 10)
    lane = iota((parts, LANES), 1)
    far_row = (far_ref[...] + 1).astype(F32)
    near_row = (near + 1).astype(F32)
    message = jnp.zeros((parts, LANES), F32)
    own = jnp.zeros((parts, LANES), F32)
    for s in range(SLOTS):
        for at, row in ((0, far_row), (SLOTS, kind.astype(F32)), (2 * SLOTS, stiff_ref[...])):
            value = jnp.sum(jnp.where(slots[s], row, 0.0), axis=1, keepdims=True)
            message = jnp.where(lane == at + s, value, message)
        value = jnp.sum(jnp.where(slots[s], near_row, 0.0), axis=1, keepdims=True)
        own = jnp.where(lane == s, value, own)
    pay_ref[pl.ds(9, parts, stride=10), :] = message
    packed = [kind.astype(F32), stiff_ref[...], near.astype(F32), owner_ref[...].astype(F32)]
    where_ref[...] = jnp.concatenate(packed + packed, axis=0)
    meta_ref[...] = own


def tables_kernel(
    where_ref, load_ref, inverse_ref, coupling_ref, block_ref,
    near_near, near_far, far_near, far_far, turned_near, turned_far, base_ref,
):
    dofs = block_ref.shape[1] // 2
    modes = inverse_ref.shape[1]
    inverses = []
    for t in range(KINDS):
        turned = dot_high(inverse_ref[t], coupling_ref[t], TN)
        schur = block_ref[t] - dot_high(turned, coupling_ref[t], TN)
        at = slice(t * dofs, (t + 1) * dofs)
        near_near[at, :] = stacked_table(schur[:dofs, :dofs])
        near_far[at, :] = stacked_table(schur[:dofs, dofs:])
        far_near[at, :] = stacked_table(schur[dofs:, :dofs])
        far_far[at, :] = stacked_table(schur[dofs:, dofs:])
        at = slice(t * modes, (t + 1) * modes)
        turned_near[at, :] = stacked_table(turned[:, :dofs])
        turned_far[at, :] = stacked_table(turned[:, dofs:])
        inverses.append(inverse_ref[t])
    left = stacked_table(jnp.concatenate(inverses, axis=0))
    kind = where_ref[KIND]
    stiff = where_ref[STIFF]
    kind2 = jnp.concatenate([kind, kind], axis=1)
    stiff2 = jnp.concatenate([stiff, stiff], axis=1)
    for k in range(0, CASES, 2):
        loads = jnp.concatenate(
            [load_ref[pl.ds(k + i, modes, stride=CASES), :] for i in range(2)], axis=1
        )
        result = by_kind(dot(left, stacked_values(loads)), kind2, modes) / stiff2
        for i in range(2):
            base_ref[pl.ds(k + i, modes, stride=CASES), :] = result[:, i * LANES : (i + 1) * LANES]


def send_ports(field, asked, own, pay_ref):
    put(pay_ref, pick_left(jnp.concatenate([asked, own], axis=0), field, NT), 0, 18)


def rhs_kernel(parts, arrived_ref, near_sum_ref, load_ref, meta_ref, field_ref, pay_ref, asked_ref):
    asked = arrived_ref[pl.ds(9, parts, stride=10), :]
    asked_ref[...] = asked
    asked_hot = port_onehot(asked)
    arrived = get(arrived_ref, 0, 10, 3)
    field = load_ref[...] + (near_sum_ref[...] + pick_right(arrived, asked_hot, TN))
    field_ref[...] = field
    send_ports(field, asked_hot, port_onehot(meta_ref[...]), pay_ref)


def component_products(table_ref, part_ref, where_ref, out_ref):
    dofs = part_ref.shape[0] // CASES
    kind, stiff = where_ref[KIND], where_ref[STIFF]
    kind2 = jnp.concatenate([kind, kind], axis=1)
    stiff2 = jnp.concatenate([stiff, stiff], axis=1)
    for k in range(0, CASES, 2):
        values = jnp.concatenate(
            [part_ref[pl.ds(k + i, dofs, stride=CASES), :] for i in range(2)], axis=1
        )
        result = by_kind(dot(table_ref[...], stacked_values(values)), kind2, dofs) * stiff2
        for i in range(2):
            out_ref[pl.ds(k + i, dofs, stride=CASES), :] = result[:, i * LANES : (i + 1) * LANES]


def slot_products(table_ref, slot_ref, asked, out_ref):
    tiles = slot_ref.shape[0]
    dofs = slot_ref.shape[1] // CASES
    spare = tiles * LANES - SLOTS * asked.shape[0]
    kind = pad_lanes(stacked_rows(asked, SLOTS), spare)
    stiff = pad_lanes(stacked_rows(asked, 2 * SLOTS), spare)
    for k in range(CASES):
        values = jnp.concatenate(
            [slot_ref[g, pl.ds(k, dofs, stride=CASES), :] for g in range(tiles)], axis=1
        )
        result = by_kind(dot(table_ref[...], stacked_values(values)), kind, dofs) * stiff
        for g in range(tiles):
            out_ref[g, pl.ds(k, dofs, stride=CASES), :] = result[:, g * LANES : (g + 1) * LANES]


def wide_onehot(asked_hot, tiles):
    spare = tiles * LANES - asked_hot.shape[0]
    if not spare:
        return asked_hot
    return jnp.concatenate([asked_hot, jnp.zeros((spare, LANES), BF16)], axis=0)


def slots_to_ports(part_ref, asked_hot):
    tiles = part_ref.shape[0]
    hot = wide_onehot(asked_hot, tiles)
    total = pick_right(part_ref[0], hot[:LANES], NN)
    for g in range(1, tiles):
        total = total + pick_right(part_ref[g], hot[g * LANES : (g + 1) * LANES], NN)
    return total


def inner_kernel(
    field_ref, asked_ref, where_ref, near_near, far_far,
    inner_ref, near_values, near_part, slot_ref, slot_part,
):
    field, asked = field_ref[...], asked_ref[...]
    near_hot, asked_hot = near_onehot(where_ref[NEAR]), port_onehot(asked)
    tiles = slot_ref.shape[0]
    near_values[...] = pick_right(field, near_hot, NT)
    values = pick_right(field, wide_onehot(asked_hot, tiles), NT)
    for g in range(tiles):
        slot_ref[g] = values[:, g * LANES : (g + 1) * LANES]
    component_products(near_near, near_values, where_ref, near_part)
    slot_products(far_far, slot_ref, asked, slot_part)
    inner_ref[...] = pick_right(near_part[...], near_hot, NN) + slots_to_ports(slot_part, asked_hot)


def near_cross(parts, arrived_ref, pitch, kind_ref, stiff_ref, near_ref, owner_ref, near_far, far_values, near_part):
    slots = onehot(jnp.concatenate(owner_slots(where_ref[OWNER], parts), axis=0))
    far_values[...] = pick_right(get(arrived_ref, 0, pitch, 3), slots, TN)
    component_products(near_far, far_values, where_ref, near_part)
    return pick_right(near_part[...], near_onehot(near_ref[...]), NN)


def far_cross(arrived_ref, first, pitch, asked, asked_hot, far_near, slot_ref, slot_part):
    tiles = slot_ref.shape[0]
    values = jnp.transpose(get(arrived_ref, first, pitch, 3))
    values = pad_lanes(values, tiles * LANES - values.shape[1])
    for g in range(tiles):
        slot_ref[g] = values[:, g * LANES : (g + 1) * LANES]
    slot_products(far_near, slot_ref, asked, slot_part)
    return slots_to_ports(slot_part, asked_hot)


def image_kernel(
    parts, groups, last, arrived_ref, inner_ref, asked_ref, where_ref,
    near_far, far_near, *rest,
):
    if last:
        case_ref, gram_ref, near_values, turned_near, turned_far = rest[:5]
        images, rest = rest[5 : 5 + groups], rest[5 + groups :]
        image_ref, copies_ref, own_ref = rest[:3]
        messages, (near_part, slot_ref, slot_part, far_values, turned_ref) = rest[3 : 2 + groups], rest[2 + groups :]
    else:
        meta_ref, image_ref, far_values, pay_ref, near_part, slot_ref, slot_part = rest
    asked = asked_ref[...]
    asked_hot = port_onehot(asked)
    slots = onehot(jnp.concatenate(owner_slots(where_ref[OWNER], parts), axis=0))
    far_values[...] = pick_right(get(arrived_ref, 0, 18, 3), slots, TN)
    component_products(near_far, far_values, where_ref, near_part)
    tiles = slot_ref.shape[0]
    values = jnp.transpose(get(arrived_ref, 9, 18, 3))
    values = pad_lanes(values, tiles * LANES - values.shape[1])
    for g in range(tiles):
        slot_ref[g] = values[:, g * LANES : (g + 1) * LANES]
    slot_products(far_near, slot_ref, asked, slot_part)
    image = inner_ref[...] + pick_right(near_part[...], near_onehot(where_ref[NEAR]), NN)
    image = image + slots_to_ports(slot_part, asked_hot)
    image_ref[...] = image
    if last:
        total = groups * CASES
        gram = add_products(
            LANES, images, [images[0], image_ref], [2 * total, 3 * total], case_ref[0], gram_ref[...]
        )
        for p in range(copies_ref.shape[0]):
            copies_ref[p] = gram
        turned_rows(near_values, far_values, where_ref, turned_near, turned_far, turned_ref)
        rows, part = image.shape[0], own_ref.shape[0]
        for h in range(groups):
            at = pl.multiple_of(lax.rem(case_ref[0] + h, groups) * part, part)
            if h:
                messages[h - 1][:rows, :] = image
                messages[h - 1][rows:, :] = turned_ref[pl.ds(at, part), :]
            else:
                own_ref[...] = turned_ref[pl.ds(at, part), :]
    else:
        send_ports(image, asked_hot, port_onehot(meta_ref[...]), pay_ref)


def turned_rows(near_values, far_values, where_ref, turned_near, turned_far, out_ref):
    dofs = near_values.shape[0] // CASES
    modes = out_ref.shape[0] // CASES
    kind = where_ref[KIND]
    kind2 = jnp.concatenate([kind, kind], axis=1)
    for k in range(0, CASES, 2):
        sums = 0.0
        for table, part in ((turned_near, near_values), (turned_far, far_values)):
            values = jnp.concatenate(
                [part[pl.ds(k + i, dofs, stride=CASES), :] for i in range(2)], axis=1
            )
            sums = sums + dot(table[...], stacked_values(values))
        result = by_kind(sums, kind2, modes)
        for i in range(2):
            out_ref[pl.ds(k + i, modes, stride=CASES), :] = result[:, i * LANES : (i + 1) * LANES]


def turned_kernel(groups, case_ref, near_values, far_values, where_ref, turned_near, turned_far, *rest):
    outs, out_ref = rest[:groups], rest[groups]
    turned_rows(near_values, far_values, where_ref, turned_near, turned_far, out_ref)
    part = outs[0].shape[0]
    for h in range(groups):
        at = pl.multiple_of(lax.rem(case_ref[0] + h, groups) * part, part)
        outs[h][...] = out_ref[pl.ds(at, part), :]


def pass_kernel(*refs):
    pass


def add_products(lanes, lefts, rights, first, case, out):
    groups = len(lefts)
    total = groups * CASES
    dofs = lefts[0].shape[0] // CASES
    lane = iota((CASES, LANES), 1)
    for h in range(groups):
        def step(d, sums):
            own = pl.ds(pl.multiple_of(d * CASES, CASES), CASES)
            values = [ref[own, :] for ref in rights]
            new = []
            for i in range(CASES):
                row = lefts[h][pl.ds(d * CASES + i, 1), :]
                new.append(tuple(s + row * v for s, v in zip(sums[i], values)))
            return tuple(new)

        zero = jnp.zeros((CASES, LANES), F32)
        sums = lax.fori_loop(0, dofs, step, ((zero,) * len(rights),) * CASES)
        at = lax.rem(case + h, groups) * CASES
        for i in range(CASES):
            for g in range(len(rights)):
                value = jnp.sum(sums[i][g], axis=1, keepdims=True)
                out = jnp.where(lane == first[g] + at + i, value, out)
    return out


def base_gram_kernel(groups, case_ref, *refs):
    base, out_ref = refs[:groups], refs[groups]
    out_ref[...] = add_products(LANES, base, [base[0]], [0], case_ref[0], jnp.zeros((CASES, LANES), F32))


def gram_kernel(groups, case_ref, gram_ref, *refs):
    base, image_ref, out_ref = refs[:groups], refs[groups], refs[groups + 1]
    out_ref[...] = add_products(LANES, base, [image_ref], [groups * CASES], case_ref[0], gram_ref[...])


def sum_kernel(in_ref, out_ref):
    for q in range(in_ref.shape[0]):
        total = in_ref[q, 0]
        for p in range(1, in_ref.shape[1]):
            total = total + in_ref[q, p]
        for p in range(out_ref.shape[0]):
            out_ref[p, q * CASES : (q + 1) * CASES, :] = total


def inverse2(p, q, r, s):
    scale = 1.0 / (p * s - q * r)
    return s * scale, -q * scale, -r * scale, p * scale


def spd_solve(matrix, target):
    n = matrix.shape[0]
    a = jnp.concatenate([matrix, target], axis=1)
    row_of = iota(a.shape, 0)
    for k in range(0, n, 4):
        c = [jnp.broadcast_to(a[:, k + i : k + i + 1], a.shape) for i in range(4)]
        r = [a[k + i : k + i + 1] for i in range(4)]
        p = [[c[j][k + i : k + i + 1] for j in range(4)] for i in range(4)]
        a00, a01, a10, a11 = inverse2(p[0][0], p[0][1], p[1][0], p[1][1])
        e00, e01 = p[2][0] * a00 + p[2][1] * a10, p[2][0] * a01 + p[2][1] * a11
        e10, e11 = p[3][0] * a00 + p[3][1] * a10, p[3][0] * a01 + p[3][1] * a11
        i00, i01, i10, i11 = inverse2(
            p[2][2] - (e00 * p[0][2] + e01 * p[1][2]),
            p[2][3] - (e00 * p[0][3] + e01 * p[1][3]),
            p[3][2] - (e10 * p[0][2] + e11 * p[1][2]),
            p[3][3] - (e10 * p[0][3] + e11 * p[1][3]),
        )
        t2 = r[2] - (e00 * r[0] + e01 * r[1])
        t3 = r[3] - (e10 * r[0] + e11 * r[1])
        u2, u3 = i00 * t2 + i01 * t3, i10 * t2 + i11 * t3
        w0 = r[0] - (p[0][2] * u2 + p[0][3] * u3)
        w1 = r[1] - (p[1][2] * u2 + p[1][3] * u3)
        u = [a00 * w0 + a01 * w1, a10 * w0 + a11 * w1, u2, u3]
        a = a - ((c[0] * u[0] + c[1] * u[1]) + (c[2] * u[2] + c[3] * u[3]))
        for i in range(4):
            a = jnp.where(row_of == k + i, u[i], a)
    return a[:, n:]


def symmetric(m):
    return 0.5 * (m + jnp.transpose(m))


def solve_kernel(groups, case_ref, gram_ref, *rest):
    pieces, (coef, *outs), (held, coef_rows, turned_coef, sems) = (
        rest[: 2 * groups], rest[2 * groups : 3 * groups + 1], rest[3 * groups + 1 :]
    )
    part = held.shape[1]
    fetches = [
        pltpu.make_async_copy(piece.at[pl.ds(piece.shape[0] - part, part), :], held.at[i], sems.at[i])
        for i, piece in enumerate(pieces)
    ]
    for fetch in fetches:
        fetch.start()
    n = groups * CASES
    total = gram_ref[0]
    for p in range(1, gram_ref.shape[0]):
        total = total + gram_ref[p]
    g00, g01, g11, g12 = [symmetric(total[:, g * n : (g + 1) * n]) for g in range(4)]
    steps = spd_solve(g01, jnp.concatenate([g00, g11], axis=1))
    step0, step1 = steps[:, :n], steps[:, n:]
    both = dot_high(g11, steps)
    second = spd_solve(symmetric(g12 - both[:, n:]), g01 - both[:, :n])
    first = step0 - dot_high(step1, second)
    first, second = jnp.transpose(first), jnp.transpose(second)
    turned_coef[0] = jnp.concatenate([first] * (LANES // n), axis=1)
    turned_coef[1] = jnp.concatenate([second] * (LANES // n), axis=1)
    shift = LANES - case_ref[0] * CASES
    for q in range(groups):
        at = pl.multiple_of(lax.rem(case_ref[0] + q, groups) * CASES, CASES)
        for h in range(2):
            mine = pltpu.roll(turned_coef[h, pl.ds(at, CASES), :], shift, 1)
            coef_rows[q * CASES : (q + 1) * CASES, h * LANES : (h + 1) * LANES] = mine
            if q == 0:
                for j in range(n):
                    coef[h * n + j] = jnp.broadcast_to(mine[:, j : j + 1], (CASES, LANES))
    for fetch in fetches:
        fetch.wait()
    left = stacked_table(jnp.concatenate([coef_rows[:, :n], coef_rows[:, LANES : LANES + n]], axis=1))
    for m in range(0, part // CASES, 2):
        values = [
            jnp.concatenate([held[i, at : at + CASES, :] for i in range(2 * groups)], axis=0)
            for at in (m * CASES, (m + 1) * CASES)
        ]
        result = dot(left, stacked_values(jnp.concatenate(values, axis=1)))
        for i in range(2):
            for h in range(groups):
                outs[h][(m + i) * CASES : (m + i + 1) * CASES, :] = result[
                    h * CASES : (h + 1) * CASES, i * LANES : (i + 1) * LANES
                ]


def ports_kernel(groups, coef, *refs):
    base, image, second = [refs[g * groups : (g + 1) * groups] for g in range(3)]
    x_ref, residual_ref = refs[3 * groups :]
    n = groups * CASES
    dofs = x_ref.shape[0] // CASES
    wide = 4

    def ports(block, carry):
        d0 = block * wide
        own = [pl.ds(pl.multiple_of((d0 + i) * CASES, CASES), CASES) for i in range(wide)]
        x = [jnp.zeros((CASES, LANES), F32)] * wide
        r = [base[0][own[i], :] for i in range(wide)]
        for j in range(n):
            q, c = divmod(j, CASES)
            c0, c1 = coef[j], coef[n + j]
            for i in range(wide):
                row = pl.ds((d0 + i) * CASES + c, 1)
                a = image[q][row, :]
                x[i] = x[i] + (c0 * base[q][row, :] + c1 * a)
                r[i] = r[i] - (c0 * a + c1 * second[q][row, :])
        for i in range(wide):
            x_ref[own[i], :] = x[i]
            residual_ref[own[i], :] = r[i]
        return carry

    lax.fori_loop(0, dofs // wide, ports, 0)


def join_kernel(groups, case_ref, bubble_ref, *refs):
    parts, out_ref = refs[:groups], refs[groups]
    part = parts[0].shape[0]
    for h in range(groups):
        at = pl.ds(pl.multiple_of(lax.rem(case_ref[0] + h, groups) * part, part), part)
        out_ref[at, :] = bubble_ref[at, :] - parts[h][...]


def call(kernel, outs, scratch=(), name=None, flops=0, smem=(), hbm=(), anywhere=(), sems=0, limit=12):
    results = [(pltpu.HBM if far else jax.ShapeDtypeStruct)(shape, dtype) for shape, dtype, far in outs]
    vmem = pl.BlockSpec(memory_space=pltpu.VMEM)
    far_spec = pl.BlockSpec(memory_space=pltpu.HBM)

    def run(*args):
        specs = [
            pl.BlockSpec(memory_space=pltpu.SMEM) if i in smem else far_spec if i in hbm else pl.BlockSpec(memory_space=pl.ANY) if i in anywhere else vmem
            for i in range(len(args))
        ]
        moved = sum(a.size * a.dtype.itemsize for a in args)
        args = [pltpu.with_memory_space_constraint(a, pltpu.HBM) if i in hbm else a for i, a in enumerate(args)]
        return pl.pallas_call(
            kernel,
            out_shape=results,
            in_specs=specs,
            out_specs=[vmem] * len(outs),
            scratch_shapes=[pltpu.VMEM(*shape) if isinstance(shape[0], tuple) else pltpu.VMEM(shape, F32) for shape in scratch]
            + ([pltpu.SemaphoreType.DMA((sems,) if sems > 1 else ())] if sems else []),
            compiler_params=pltpu.CompilerParams(vmem_limit_bytes=limit << 20),
            cost_estimate=pl.CostEstimate(flops=flops, bytes_accessed=moved, transcendentals=0),
            name=name,
        )(*args)

    return run


def exchange(rows, parts):
    moved = lax.all_to_all(rows.reshape(parts, 1, -1), PLANE, split_axis=0, concat_axis=0)
    return moved.reshape(rows.shape)


def local(
    comp_type, stiffness, near_port, far_owner, far_port, bubble_load, port_load,
    bubble_inverse, coupling, port_block,
):
    parts = lax.axis_size("px") * lax.axis_size("py")
    groups = lax.axis_size("case")
    modes, cases, comps = bubble_load.shape
    dofs, _, ports = port_load.shape
    rows, bubbles = dofs * cases, modes * cases
    slot_tiles = -(-SLOTS * parts // LANES)
    coupling = jnp.swapaxes(coupling, 1, 2)
    kind = comp_type.reshape(1, comps)
    stiff = stiffness.reshape(1, comps)
    near = near_port.reshape(1, comps)
    owner = far_owner.reshape(1, comps)
    far = far_port.reshape(1, comps)
    loads = bubble_load.reshape(bubbles, comps)
    field_of = ((rows, ports), F32, True)
    meta_of = ((parts, LANES), F32, False)
    bubble_of = ((bubbles, comps), F32, True)
    given = (kind, stiff, near, owner, far, loads, bubble_inverse, coupling)
    pay, near_sum, meta, where = call(
        functools.partial(condense_kernel, parts),
        [((parts * 10, LANES), F32, False), field_of, meta_of, ((8, LANES), F32, False)],
        [(a.shape, a.dtype) for a in given] + [(rows, comps)] * 2,
        "condense",
        hbm=range(len(given)),
        sems=len(given),
    )(*given)
    near_near, near_far, far_near, far_far, turned_near, turned_far, bubble_base = call(
        tables_kernel,
        [((KINDS * dofs, 3 * dofs), BF16, False)] * 4 + [((KINDS * modes, 3 * dofs), BF16, True)] * 2 + [bubble_of],
        name="tables",
        flops=10**9,
    )(where, loads, bubble_inverse, coupling, port_block)
    base, pay, asked = call(
        functools.partial(rhs_kernel, parts),
        [field_of, ((parts * 18, LANES), F32, False), meta_of],
        name="rhs",
    )(exchange(pay, parts), near_sum, port_load.reshape(rows, ports), meta)

    case = lax.axis_index("case").reshape(1)
    part = bubbles // groups
    part_of = ((part, comps), F32, True)
    slot_scratch = [(slot_tiles, rows, LANES)] * 2

    def to_cases(messages):
        backward = [
            lax.ppermute(message, "case", [(k, (k + h) % groups) for k in range(groups)])
            for h, message in enumerate(messages, 1)
        ]
        return backward[::-1]

    def inner(field):
        return call(inner_kernel, [((rows, ports), F32, False)] * 2, [(rows, comps)] + slot_scratch, "inner", flops=10**9)(
            field, asked, where, near_near, far_far
        )

    arrived = exchange(pay, parts)
    base_all = to_cases([base] * (groups - 1))
    base_inner, base_near = inner(base)
    gram_of = [((cases, LANES), F32, False)]
    (gram,) = call(functools.partial(base_gram_kernel, groups), gram_of, name="base_gram", smem=(0,))(
        case, base, *base_all
    )
    arrived, gram = lax.optimization_barrier((arrived, gram))
    image, base_far, pay = call(
        functools.partial(image_kernel, parts, groups, False),
        [((rows, ports), F32, False)] * 2 + [((parts * 18, LANES), F32, False)],
        [(rows, comps)] + slot_scratch,
        "image",
    )(arrived, base_inner, asked, where, near_far, far_near, meta)
    arrived = exchange(pay, parts)
    image_all = to_cases([image] * (groups - 1))
    turned0, *messages = call(
        functools.partial(turned_kernel, groups),
        [part_of] * groups,
        [(bubbles, comps)],
        "turned",
        flops=10**9,
        smem=(0,),
    )(case, base_near, base_far, where, turned_near, turned_far)
    turned0_all = to_cases(messages)
    image_inner, image_near = inner(image)
    (gram,) = call(functools.partial(gram_kernel, groups), gram_of, name="gram", smem=(0,))(
        case, gram, base, *base_all, image
    )
    arrived, *turned0_all = lax.optimization_barrier((arrived, *turned0_all))
    minor = lax.axis_size("py")
    second, copies, turned1, *messages = call(
        functools.partial(image_kernel, parts, groups, True),
        [field_of, ((groups * minor, cases, LANES), F32, True), part_of]
        + [((rows + part, comps), F32, True)] * (groups - 1),
        [(rows, comps)] + slot_scratch + [(rows, comps), (bubbles, comps)],
        "second",
        smem=(6,),
    )(
        arrived, image_inner, asked, where, near_far, far_near, case, gram, image_near, turned_near, turned_far,
        image, *image_all,
    )
    copies = lax.all_to_all(copies, ("case", "py"), split_axis=0, concat_axis=0)
    messages = pl.pallas_call(
        pass_kernel,
        out_shape=[pltpu.HBM(m.shape, m.dtype) for m in messages],
        in_specs=[pl.BlockSpec(memory_space=pltpu.HBM)] * len(messages),
        out_specs=[pl.BlockSpec(memory_space=pltpu.HBM)] * len(messages),
        input_output_aliases={i: i for i in range(len(messages))},
        cost_estimate=pl.CostEstimate(flops=10**9, bytes_accessed=1 << 20, transcendentals=0),
        name="pass_on",
    )(*messages)
    both1 = to_cases(messages)
    (copies,) = call(sum_kernel, [((parts // minor, groups * cases, LANES), F32, False)], name="sum")(
        copies.reshape(groups, minor, cases, LANES)
    )
    copies = lax.all_to_all(copies, "px", split_axis=0, concat_axis=0)
    pieces = [turned0, *turned0_all, turned1, *both1]
    coef, own, *messages = call(
        functools.partial(solve_kernel, groups),
        [((2 * groups * cases, cases, LANES), F32, False)] + [((part, comps), F32, False)] * groups,
        [(2 * groups, part, comps), (groups * cases, 2 * LANES), (2, groups * cases, LANES)],
        "solve",
        smem=(0,),
        anywhere=range(2, 2 + len(pieces)),
        sems=len(pieces),
    )(case, copies, *pieces)
    back = to_cases(messages)
    x, residual = call(
        functools.partial(ports_kernel, groups), [field_of, field_of], name="ports", flops=10**9
    )(coef, base, *base_all, image, *image_all, second, *both1)
    (bubble,) = call(functools.partial(join_kernel, groups), [bubble_of], name="join", smem=(0,))(
        case, bubble_base, own, *back
    )
    return (
        x.reshape(port_load.shape),
        residual.reshape(port_load.shape),
        bubble.reshape(bubble_load.shape),
    )


def solution(mesh):
    placed = (
        P(PLANE),
        P(PLANE),
        P(PLANE),
        P(PLANE, None),
        P(PLANE),
        P(None, "case", PLANE),
        P(None, "case", PLANE),
        P(),
        P(),
        P(),
    )
    out = P(None, "case", PLANE)
    return jax.shard_map(
        local, mesh=mesh, in_specs=placed, out_specs=(out, out, out), check_vma=False
    )
```

```python
import functools

import jax
import jax.numpy as jnp
from jax import lax
from jax.experimental import pallas as pl
from jax.experimental.pallas import tpu as pltpu
from jax.sharding import PartitionSpec as P

HIGH = lax.Precision.HIGHEST
PLANE = ("px", "py")
F32 = jnp.float32
BF16 = jnp.bfloat16
KINDS = 8
LANES = 128
CASES = 8
SLOTS = 3
NN = (((1,), (0,)), ((), ()))
NT = (((1,), (1,)), ((), ()))
TN = (((0,), (0,)), ((), ()))


def dot(lhs, rhs, dims=NN):
    return lax.dot_general(lhs, rhs, dims, preferred_element_type=F32)


def dot_high(lhs, rhs, dims=NN):
    return lax.dot_general(lhs, rhs, dims, precision=HIGH, preferred_element_type=F32)


def split2(x):
    high = x.astype(BF16)
    return high, (x - high.astype(F32)).astype(BF16)


def pick_right(x, onehot, dims):
    (left,), (right,) = dims[0]
    return dot(jnp.concatenate(split2(x), axis=left), jnp.concatenate([onehot, onehot], axis=right), dims)


def pick_left(onehot, x, dims):
    (left,), (right,) = dims[0]
    return dot(jnp.concatenate([onehot, onehot], axis=left), jnp.concatenate(split2(x), axis=right), dims)


def stacked_table(table):
    high, low = split2(table)
    return jnp.concatenate([high, high, low], axis=1)


def stacked_values(x):
    high, low = split2(x)
    return jnp.concatenate([high, low, high], axis=0)


def iota(shape, dim):
    return lax.broadcasted_iota(jnp.int32, shape, dim)


def column(row):
    return jnp.transpose(jnp.broadcast_to(row, (8, row.shape[1])))[:, :1]


def onehot(mask):
    return mask.astype(F32).astype(BF16)


KIND, STIFF, NEAR, OWNER = [slice(i, i + 1) for i in range(4)]


def owner_slots(owner, parts):
    count = owner.shape[1]
    owner_f = owner.astype(F32)
    same = (column(owner_f) == owner_f) & (iota((count, count), 0) < iota((count, count), 1))
    rank = jnp.sum(same.astype(F32), axis=0, keepdims=True).astype(jnp.int32)
    to = iota((parts, count), 0).astype(F32) == owner_f
    return [to & (rank == s) for s in range(SLOTS)]


def near_onehot(near):
    count = near.shape[1]
    return onehot(column(near.astype(F32)) == iota((count, LANES), 1).astype(F32))


def stacked_rows(meta, lanes):
    turned = jnp.transpose(meta)
    return jnp.concatenate([turned[lanes + s : lanes + s + 1, :] for s in range(SLOTS)], axis=1)


def port_onehot(meta):
    parts = meta.shape[0]
    ports = (iota((parts, LANES), 1) + 1).astype(F32)
    return onehot(jnp.concatenate([meta[:, s : s + 1] == ports for s in range(SLOTS)], axis=0))


def pad_lanes(x, spare):
    if not spare:
        return x
    return jnp.concatenate([x, jnp.zeros((x.shape[0], spare), x.dtype)], axis=1)


def put(pay_ref, rows, first, pitch):
    parts = pay_ref.shape[0] // pitch
    tiles = rows.shape[1] // LANES
    for g in range(rows.shape[0] // parts):
        for t in range(tiles):
            pay_ref[pl.ds(first + g * tiles + t, parts, stride=pitch), :] = rows[
                g * parts : (g + 1) * parts, t * LANES : (t + 1) * LANES
            ]


def get(pay_ref, first, pitch, tiles):
    parts = pay_ref.shape[0] // pitch
    return jnp.concatenate(
        [
            jnp.concatenate(
                [pay_ref[pl.ds(first + s * tiles + t, parts, stride=pitch), :] for t in range(tiles)],
                axis=1,
            )
            for s in range(SLOTS)
        ],
        axis=0,
    )


def by_kind(products, kind, rows):
    chosen = products[:rows]
    for t in range(1, KINDS):
        chosen = jnp.where(kind == t, products[t * rows : (t + 1) * rows], chosen)
    return chosen


def condense_kernel(
    parts, kind_hbm, stiff_hbm, near_hbm, owner_hbm, far_hbm, load_hbm, inverse_hbm, coupling_hbm,
    pay_ref, near_sum_ref, meta_ref, where_ref,
    kind_ref, stiff_ref, near_ref, owner_ref, far_ref, load_ref, inverse_ref, coupling_ref, near_part, far_part, sems,
):
    copies = [
        pltpu.make_async_copy(source, target, sems.at[i])
        for i, (source, target) in enumerate((
            (inverse_hbm, inverse_ref), (coupling_hbm, coupling_ref), (load_hbm, load_ref), (kind_hbm, kind_ref),
            (stiff_hbm, stiff_ref), (near_hbm, near_ref), (owner_hbm, owner_ref), (far_hbm, far_ref),
        ))
    ]
    for copy in copies:
        copy.start()
    for copy in copies[:2]:
        copy.wait()
    modes = load_ref.shape[0] // CASES
    dofs = near_sum_ref.shape[0] // CASES
    left = stacked_table(
        jnp.concatenate(
            [jnp.transpose(dot_high(inverse_ref[t], coupling_ref[t], TN)) for t in range(KINDS)], axis=0
        )
    )
    for copy in copies[2:]:
        copy.wait()
    kind = kind_ref[...]
    kind2 = jnp.concatenate([kind, kind], axis=1)
    for k in range(0, CASES, 2):
        loads = jnp.concatenate(
            [load_ref[pl.ds(k + i, modes, stride=CASES), :] for i in range(2)], axis=1
        )
        condensed = -by_kind(dot(left, stacked_values(loads)), kind2, 2 * dofs)
        for i in range(2):
            lanes = slice(i * LANES, (i + 1) * LANES)
            near_part[pl.ds(k + i, dofs, stride=CASES), :] = condensed[:dofs, lanes]
            far_part[pl.ds(k + i, dofs, stride=CASES), :] = condensed[dofs:, lanes]
    near = near_ref[...]
    slots = owner_slots(owner_ref[...], parts)
    near_sum_ref[...] = pick_right(near_part[...], near_onehot(near), NN)
    chosen = onehot(jnp.concatenate(slots, axis=0))
    put(pay_ref, pick_left(chosen, far_part[...], NT), 0, 10)
    lane = iota((parts, LANES), 1)
    far_row = (far_ref[...] + 1).astype(F32)
    near_row = (near + 1).astype(F32)
    message = jnp.zeros((parts, LANES), F32)
    own = jnp.zeros((parts, LANES), F32)
    for s in range(SLOTS):
        for at, row in ((0, far_row), (SLOTS, kind.astype(F32)), (2 * SLOTS, stiff_ref[...])):
            value = jnp.sum(jnp.where(slots[s], row, 0.0), axis=1, keepdims=True)
            message = jnp.where(lane == at + s, value, message)
        value = jnp.sum(jnp.where(slots[s], near_row, 0.0), axis=1, keepdims=True)
        own = jnp.where(lane == s, value, own)
    pay_ref[pl.ds(9, parts, stride=10), :] = message
    packed = [kind.astype(F32), stiff_ref[...], near.astype(F32), owner_ref[...].astype(F32)]
    where_ref[...] = jnp.concatenate(packed + packed, axis=0)
    meta_ref[...] = own


def tables_kernel(
    where_ref, load_ref, inverse_ref, coupling_ref, block_ref,
    near_near, near_far, far_near, far_far, turned_near, turned_far, base_ref,
):
    dofs = block_ref.shape[1] // 2
    modes = inverse_ref.shape[1]
    inverses = []
    for t in range(KINDS):
        turned = dot_high(inverse_ref[t], coupling_ref[t], TN)
        schur = block_ref[t] - dot_high(turned, coupling_ref[t], TN)
        at = slice(t * dofs, (t + 1) * dofs)
        near_near[at, :] = stacked_table(schur[:dofs, :dofs])
        near_far[at, :] = stacked_table(schur[:dofs, dofs:])
        far_near[at, :] = stacked_table(schur[dofs:, :dofs])
        far_far[at, :] = stacked_table(schur[dofs:, dofs:])
        at = slice(t * modes, (t + 1) * modes)
        turned_near[at, :] = stacked_table(turned[:, :dofs])
        turned_far[at, :] = stacked_table(turned[:, dofs:])
        inverses.append(inverse_ref[t])
    left = stacked_table(jnp.concatenate(inverses, axis=0))
    kind = where_ref[KIND]
    stiff = where_ref[STIFF]
    kind2 = jnp.concatenate([kind, kind], axis=1)
    stiff2 = jnp.concatenate([stiff, stiff], axis=1)
    for k in range(0, CASES, 2):
        loads = jnp.concatenate(
            [load_ref[pl.ds(k + i, modes, stride=CASES), :] for i in range(2)], axis=1
        )
        result = by_kind(dot(left, stacked_values(loads)), kind2, modes) / stiff2
        for i in range(2):
            base_ref[pl.ds(k + i, modes, stride=CASES), :] = result[:, i * LANES : (i + 1) * LANES]


def send_ports(field, asked, own, pay_ref):
    put(pay_ref, pick_left(jnp.concatenate([asked, own], axis=0), field, NT), 0, 18)


def rhs_kernel(parts, arrived_ref, near_sum_ref, load_ref, meta_ref, field_ref, pay_ref, asked_ref):
    asked = arrived_ref[pl.ds(9, parts, stride=10), :]
    asked_ref[...] = asked
    asked_hot = port_onehot(asked)
    arrived = get(arrived_ref, 0, 10, 3)
    field = load_ref[...] + (near_sum_ref[...] + pick_right(arrived, asked_hot, TN))
    field_ref[...] = field
    send_ports(field, asked_hot, port_onehot(meta_ref[...]), pay_ref)


def component_products(table_ref, part_ref, where_ref, out_ref):
    dofs = part_ref.shape[0] // CASES
    kind, stiff = where_ref[KIND], where_ref[STIFF]
    kind2 = jnp.concatenate([kind, kind], axis=1)
    stiff2 = jnp.concatenate([stiff, stiff], axis=1)
    for k in range(0, CASES, 2):
        values = jnp.concatenate(
            [part_ref[pl.ds(k + i, dofs, stride=CASES), :] for i in range(2)], axis=1
        )
        result = by_kind(dot(table_ref[...], stacked_values(values)), kind2, dofs) * stiff2
        for i in range(2):
            out_ref[pl.ds(k + i, dofs, stride=CASES), :] = result[:, i * LANES : (i + 1) * LANES]


def slot_products(table_ref, slot_ref, asked, out_ref):
    tiles = slot_ref.shape[0]
    dofs = slot_ref.shape[1] // CASES
    spare = tiles * LANES - SLOTS * asked.shape[0]
    kind = pad_lanes(stacked_rows(asked, SLOTS), spare)
    stiff = pad_lanes(stacked_rows(asked, 2 * SLOTS), spare)
    for k in range(CASES):
        values = jnp.concatenate(
            [slot_ref[g, pl.ds(k, dofs, stride=CASES), :] for g in range(tiles)], axis=1
        )
        result = by_kind(dot(table_ref[...], stacked_values(values)), kind, dofs) * stiff
        for g in range(tiles):
            out_ref[g, pl.ds(k, dofs, stride=CASES), :] = result[:, g * LANES : (g + 1) * LANES]


def wide_onehot(asked_hot, tiles):
    spare = tiles * LANES - asked_hot.shape[0]
    if not spare:
        return asked_hot
    return jnp.concatenate([asked_hot, jnp.zeros((spare, LANES), BF16)], axis=0)


def slots_to_ports(part_ref, asked_hot):
    tiles = part_ref.shape[0]
    hot = wide_onehot(asked_hot, tiles)
    total = pick_right(part_ref[0], hot[:LANES], NN)
    for g in range(1, tiles):
        total = total + pick_right(part_ref[g], hot[g * LANES : (g + 1) * LANES], NN)
    return total


def inner_kernel(
    field_ref, asked_ref, where_ref, near_near, far_far,
    inner_ref, near_values, near_part, slot_ref, slot_part,
):
    field, asked = field_ref[...], asked_ref[...]
    near_hot, asked_hot = near_onehot(where_ref[NEAR]), port_onehot(asked)
    tiles = slot_ref.shape[0]
    near_values[...] = pick_right(field, near_hot, NT)
    values = pick_right(field, wide_onehot(asked_hot, tiles), NT)
    for g in range(tiles):
        slot_ref[g] = values[:, g * LANES : (g + 1) * LANES]
    component_products(near_near, near_values, where_ref, near_part)
    slot_products(far_far, slot_ref, asked, slot_part)
    inner_ref[...] = pick_right(near_part[...], near_hot, NN) + slots_to_ports(slot_part, asked_hot)


def near_cross(parts, arrived_ref, pitch, kind_ref, stiff_ref, near_ref, owner_ref, near_far, far_values, near_part):
    slots = onehot(jnp.concatenate(owner_slots(where_ref[OWNER], parts), axis=0))
    far_values[...] = pick_right(get(arrived_ref, 0, pitch, 3), slots, TN)
    component_products(near_far, far_values, where_ref, near_part)
    return pick_right(near_part[...], near_onehot(near_ref[...]), NN)


def far_cross(arrived_ref, first, pitch, asked, asked_hot, far_near, slot_ref, slot_part):
    tiles = slot_ref.shape[0]
    values = jnp.transpose(get(arrived_ref, first, pitch, 3))
    values = pad_lanes(values, tiles * LANES - values.shape[1])
    for g in range(tiles):
        slot_ref[g] = values[:, g * LANES : (g + 1) * LANES]
    slot_products(far_near, slot_ref, asked, slot_part)
    return slots_to_ports(slot_part, asked_hot)


def image_kernel(
    parts, groups, last, arrived_ref, inner_ref, asked_ref, where_ref,
    near_far, far_near, *rest,
):
    if last:
        case_ref, gram_ref, turned_near, turned_far, turned0_hbm = rest[:5]
        images, rest = rest[5 : 5 + groups], rest[5 + groups :]
        image_ref, copies_ref, own_ref = rest[:3]
        messages = rest[3 : 2 + groups]
        near_part, slot_ref, slot_part, far_values, near_values, turned_ref, turned0_ref, sem = rest[2 + groups :]
        fetch = pltpu.make_async_copy(turned0_hbm, turned0_ref, sem)
        fetch.start()
    else:
        meta_ref, image_ref, far_values, pay_ref, near_part, slot_ref, slot_part = rest
    asked = asked_ref[...]
    asked_hot = port_onehot(asked)
    slots = onehot(jnp.concatenate(owner_slots(where_ref[OWNER], parts), axis=0))
    far_values[...] = pick_right(get(arrived_ref, 0, 18, 3), slots, TN)
    component_products(near_far, far_values, where_ref, near_part)
    tiles = slot_ref.shape[0]
    values = jnp.transpose(get(arrived_ref, 9, 18, 3))
    values = pad_lanes(values, tiles * LANES - values.shape[1])
    for g in range(tiles):
        slot_ref[g] = values[:, g * LANES : (g + 1) * LANES]
    slot_products(far_near, slot_ref, asked, slot_part)
    image = inner_ref[...] + pick_right(near_part[...], near_onehot(where_ref[NEAR]), NN)
    image = image + slots_to_ports(slot_part, asked_hot)
    image_ref[...] = image
    if last:
        total = groups * CASES
        gram = add_products(
            LANES, images, [images[0], image_ref], [2 * total, 3 * total], case_ref[0], gram_ref[...]
        )
        for p in range(copies_ref.shape[0]):
            copies_ref[p] = gram
        near_values[...] = pick_right(images[0][...], near_onehot(where_ref[NEAR]), NT)
        turned_rows(near_values, far_values, where_ref, turned_near, turned_far, turned_ref)
        fetch.wait()
        rows, part = image.shape[0], own_ref.shape[0] // 2
        for h in range(groups):
            at = pl.ds(pl.multiple_of(lax.rem(case_ref[0] + h, groups) * part, part), part)
            target, first = (messages[h - 1], rows) if h else (own_ref, 0)
            if h:
                target[:rows, :] = image
            target[first : first + part, :] = turned0_ref[at, :]
            target[first + part :, :] = turned_ref[at, :]
    else:
        send_ports(image, asked_hot, port_onehot(meta_ref[...]), pay_ref)


def turned_rows(near_values, far_values, where_ref, turned_near, turned_far, out_ref):
    dofs = near_values.shape[0] // CASES
    modes = out_ref.shape[0] // CASES
    kind = where_ref[KIND]
    kind2 = jnp.concatenate([kind, kind], axis=1)
    for k in range(0, CASES, 2):
        sums = 0.0
        for table, part in ((turned_near, near_values), (turned_far, far_values)):
            values = jnp.concatenate(
                [part[pl.ds(k + i, dofs, stride=CASES), :] for i in range(2)], axis=1
            )
            sums = sums + dot(table[...], stacked_values(values))
        result = by_kind(sums, kind2, modes)
        for i in range(2):
            out_ref[pl.ds(k + i, modes, stride=CASES), :] = result[:, i * LANES : (i + 1) * LANES]


def pass_kernel(*refs):
    pass


def add_products(lanes, lefts, rights, first, case, out):
    groups = len(lefts)
    total = groups * CASES
    dofs = lefts[0].shape[0] // CASES
    lane = iota((CASES, LANES), 1)
    for h in range(groups):
        def step(d, sums):
            own = pl.ds(pl.multiple_of(d * CASES, CASES), CASES)
            values = [ref[own, :] for ref in rights]
            new = []
            for i in range(CASES):
                row = lefts[h][pl.ds(d * CASES + i, 1), :]
                new.append(tuple(s + row * v for s, v in zip(sums[i], values)))
            return tuple(new)

        zero = jnp.zeros((CASES, LANES), F32)
        sums = lax.fori_loop(0, dofs, step, ((zero,) * len(rights),) * CASES)
        at = lax.rem(case + h, groups) * CASES
        for i in range(CASES):
            for g in range(len(rights)):
                value = jnp.sum(sums[i][g], axis=1, keepdims=True)
                out = jnp.where(lane == first[g] + at + i, value, out)
    return out


def base_gram_kernel(groups, case_ref, *refs):
    base, out_ref = refs[:groups], refs[groups]
    out_ref[...] = add_products(LANES, base, [base[0]], [0], case_ref[0], jnp.zeros((CASES, LANES), F32))


def gram_kernel(groups, case_ref, gram_ref, *refs):
    base, image_ref, out_ref = refs[:groups], refs[groups], refs[groups + 1]
    out_ref[...] = add_products(LANES, base, [image_ref], [groups * CASES], case_ref[0], gram_ref[...])


def sum_kernel(in_ref, out_ref):
    for q in range(in_ref.shape[1]):
        total = in_ref[0, q]
        for p in range(1, in_ref.shape[0]):
            total = total + in_ref[p, q]
        for p in range(out_ref.shape[0]):
            out_ref[p, q * CASES : (q + 1) * CASES, :] = total


def inverse2(p, q, r, s):
    scale = 1.0 / (p * s - q * r)
    return s * scale, -q * scale, -r * scale, p * scale


def spd_solve(matrix, target):
    n = matrix.shape[0]
    a = jnp.concatenate([matrix, target], axis=1)
    row_of = iota(a.shape, 0)
    for k in range(0, n, 4):
        c = [jnp.broadcast_to(a[:, k + i : k + i + 1], a.shape) for i in range(4)]
        r = [a[k + i : k + i + 1] for i in range(4)]
        p = [[c[j][k + i : k + i + 1] for j in range(4)] for i in range(4)]
        a00, a01, a10, a11 = inverse2(p[0][0], p[0][1], p[1][0], p[1][1])
        e00, e01 = p[2][0] * a00 + p[2][1] * a10, p[2][0] * a01 + p[2][1] * a11
        e10, e11 = p[3][0] * a00 + p[3][1] * a10, p[3][0] * a01 + p[3][1] * a11
        i00, i01, i10, i11 = inverse2(
            p[2][2] - (e00 * p[0][2] + e01 * p[1][2]),
            p[2][3] - (e00 * p[0][3] + e01 * p[1][3]),
            p[3][2] - (e10 * p[0][2] + e11 * p[1][2]),
            p[3][3] - (e10 * p[0][3] + e11 * p[1][3]),
        )
        t2 = r[2] - (e00 * r[0] + e01 * r[1])
        t3 = r[3] - (e10 * r[0] + e11 * r[1])
        u2, u3 = i00 * t2 + i01 * t3, i10 * t2 + i11 * t3
        w0 = r[0] - (p[0][2] * u2 + p[0][3] * u3)
        w1 = r[1] - (p[1][2] * u2 + p[1][3] * u3)
        u = [a00 * w0 + a01 * w1, a10 * w0 + a11 * w1, u2, u3]
        a = a - ((c[0] * u[0] + c[1] * u[1]) + (c[2] * u[2] + c[3] * u[3]))
        for i in range(4):
            a = jnp.where(row_of == k + i, u[i], a)
    return a[:, n:]


def symmetric(m):
    return 0.5 * (m + jnp.transpose(m))


def solve_kernel(groups, case_ref, gram_ref, coef, coef_rows, turned_coef):
    n = groups * CASES
    total = gram_ref[0]
    for p in range(1, gram_ref.shape[0]):
        total = total + gram_ref[p]
    g00, g01, g11, g12 = [symmetric(total[:, g * n : (g + 1) * n]) for g in range(4)]
    steps = spd_solve(g01, jnp.concatenate([g00, g11], axis=1))
    step0, step1 = steps[:, :n], steps[:, n:]
    both = dot_high(g11, steps)
    second = spd_solve(symmetric(g12 - both[:, n:]), g01 - both[:, :n])
    first = step0 - dot_high(step1, second)
    first, second = jnp.transpose(first), jnp.transpose(second)
    turned_coef[0] = jnp.concatenate([first] * (LANES // n), axis=1)
    turned_coef[1] = jnp.concatenate([second] * (LANES // n), axis=1)
    shift = LANES - case_ref[0] * CASES
    for q in range(groups):
        at = pl.multiple_of(lax.rem(case_ref[0] + q, groups) * CASES, CASES)
        for h in range(2):
            mine = pltpu.roll(turned_coef[h, pl.ds(at, CASES), :], shift, 1)
            coef_rows[q * CASES : (q + 1) * CASES, h * LANES : (h + 1) * LANES] = mine
            if q == 0:
                for j in range(n):
                    coef[h * n + j] = jnp.broadcast_to(mine[:, j : j + 1], (CASES, LANES))


def bubble_kernel(groups, rows, coef_ref, *refs):
    turned, outs = refs[:groups], refs[groups:]
    n = groups * CASES
    part = outs[0].shape[0]
    firsts = [0] + [rows] * (groups - 1)
    left = stacked_table(jnp.concatenate([coef_ref[:, :n], coef_ref[:, LANES : LANES + n]], axis=1))
    for m in range(0, part // CASES, 2):
        values = [
            jnp.concatenate(
                [
                    ref[first + half * part + at : first + half * part + at + CASES, :]
                    for half in range(2)
                    for ref, first in zip(turned, firsts)
                ],
                axis=0,
            )
            for at in (m * CASES, (m + 1) * CASES)
        ]
        result = dot(left, stacked_values(jnp.concatenate(values, axis=1)))
        for i in range(2):
            for h in range(groups):
                outs[h][(m + i) * CASES : (m + i + 1) * CASES, :] = result[
                    h * CASES : (h + 1) * CASES, i * LANES : (i + 1) * LANES
                ]


def ports_kernel(groups, coef, *refs):
    base, image, second = [refs[g * groups : (g + 1) * groups] for g in range(3)]
    x_ref, residual_ref = refs[3 * groups :]
    n = groups * CASES
    dofs = x_ref.shape[0] // CASES
    wide = 4

    def ports(block, carry):
        d0 = block * wide
        own = [pl.ds(pl.multiple_of((d0 + i) * CASES, CASES), CASES) for i in range(wide)]
        x = [jnp.zeros((CASES, LANES), F32)] * wide
        r = [base[0][own[i], :] for i in range(wide)]
        for j in range(n):
            q, c = divmod(j, CASES)
            c0, c1 = coef[j], coef[n + j]
            for i in range(wide):
                row = pl.ds((d0 + i) * CASES + c, 1)
                a = image[q][row, :]
                x[i] = x[i] + (c0 * base[q][row, :] + c1 * a)
                r[i] = r[i] - (c0 * a + c1 * second[q][row, :])
        for i in range(wide):
            x_ref[own[i], :] = x[i]
            residual_ref[own[i], :] = r[i]
        return carry

    lax.fori_loop(0, dofs // wide, ports, 0)


def join_kernel(groups, case_ref, bubble_ref, *refs):
    parts, out_ref = refs[:groups], refs[groups]
    part = parts[0].shape[0]
    for h in range(groups):
        at = pl.ds(pl.multiple_of(lax.rem(case_ref[0] + h, groups) * part, part), part)
        out_ref[at, :] = bubble_ref[at, :] - parts[h][...]


def call(kernel, outs, scratch=(), name=None, flops=0, smem=(), hbm=(), anywhere=(), sems=0, limit=12):
    results = [(pltpu.HBM if far else jax.ShapeDtypeStruct)(shape, dtype) for shape, dtype, far in outs]
    vmem = pl.BlockSpec(memory_space=pltpu.VMEM)
    far_spec = pl.BlockSpec(memory_space=pltpu.HBM)

    def run(*args):
        specs = [
            pl.BlockSpec(memory_space=pltpu.SMEM) if i in smem else far_spec if i in hbm else pl.BlockSpec(memory_space=pl.ANY) if i in anywhere else vmem
            for i in range(len(args))
        ]
        moved = sum(a.size * a.dtype.itemsize for a in args)
        args = [pltpu.with_memory_space_constraint(a, pltpu.HBM) if i in hbm else a for i, a in enumerate(args)]
        return pl.pallas_call(
            kernel,
            out_shape=results,
            in_specs=specs,
            out_specs=[vmem] * len(outs),
            scratch_shapes=[pltpu.VMEM(*shape) if isinstance(shape[0], tuple) else pltpu.VMEM(shape, F32) for shape in scratch]
            + ([pltpu.SemaphoreType.DMA((sems,) if sems > 1 else ())] if sems else []),
            compiler_params=pltpu.CompilerParams(vmem_limit_bytes=limit << 20),
            cost_estimate=pl.CostEstimate(flops=flops, bytes_accessed=moved, transcendentals=0),
            name=name,
        )(*args)

    return run


def exchange(rows, parts):
    moved = lax.all_to_all(rows.reshape(parts, 1, -1), PLANE, split_axis=0, concat_axis=0)
    return moved.reshape(rows.shape)


def local(
    comp_type, stiffness, near_port, far_owner, far_port, bubble_load, port_load,
    bubble_inverse, coupling, port_block,
):
    parts = lax.axis_size("px") * lax.axis_size("py")
    groups = lax.axis_size("case")
    modes, cases, comps = bubble_load.shape
    dofs, _, ports = port_load.shape
    rows, bubbles = dofs * cases, modes * cases
    slot_tiles = -(-SLOTS * parts // LANES)
    coupling = jnp.swapaxes(coupling, 1, 2)
    kind = comp_type.reshape(1, comps)
    stiff = stiffness.reshape(1, comps)
    near = near_port.reshape(1, comps)
    owner = far_owner.reshape(1, comps)
    far = far_port.reshape(1, comps)
    loads = bubble_load.reshape(bubbles, comps)
    field_of = ((rows, ports), F32, True)
    meta_of = ((parts, LANES), F32, False)
    bubble_of = ((bubbles, comps), F32, True)
    given = (kind, stiff, near, owner, far, loads, bubble_inverse, coupling)
    pay, near_sum, meta, where = call(
        functools.partial(condense_kernel, parts),
        [((parts * 10, LANES), F32, False), field_of, meta_of, ((8, LANES), F32, False)],
        [(a.shape, a.dtype) for a in given] + [(rows, comps)] * 2,
        "condense",
        hbm=range(len(given)),
        sems=len(given),
    )(*given)
    near_near, near_far, far_near, far_far, turned_near, turned_far, bubble_base = call(
        tables_kernel,
        [((KINDS * dofs, 3 * dofs), BF16, False)] * 4 + [((KINDS * modes, 3 * dofs), BF16, True)] * 2 + [bubble_of],
        name="tables",
        flops=10**9,
    )(where, loads, bubble_inverse, coupling, port_block)
    base, pay, asked = call(
        functools.partial(rhs_kernel, parts),
        [field_of, ((parts * 18, LANES), F32, False), meta_of],
        name="rhs",
    )(exchange(pay, parts), near_sum, port_load.reshape(rows, ports), meta)

    case = lax.axis_index("case").reshape(1)
    part = bubbles // groups
    part_of = ((part, comps), F32, True)
    slot_scratch = [(slot_tiles, rows, LANES)] * 2

    def to_cases(messages):
        backward = [
            lax.ppermute(message, "case", [(k, (k + h) % groups) for k in range(groups)])
            for h, message in enumerate(messages, 1)
        ]
        return backward[::-1]

    def inner(field):
        return call(inner_kernel, [((rows, ports), F32, False)] * 2, [(rows, comps)] + slot_scratch, "inner", flops=10**9)(
            field, asked, where, near_near, far_far
        )

    arrived = exchange(pay, parts)
    base_all = to_cases([base] * (groups - 1))
    base_inner, base_near = inner(base)
    gram_of = [((cases, LANES), F32, False)]
    (gram,) = call(functools.partial(base_gram_kernel, groups), gram_of, name="base_gram", smem=(0,))(
        case, base, *base_all
    )
    arrived, gram = lax.optimization_barrier((arrived, gram))
    image, base_far, pay = call(
        functools.partial(image_kernel, parts, groups, False),
        [((rows, ports), F32, False), field_of, ((parts * 18, LANES), F32, False)],
        [(rows, comps)] + slot_scratch,
        "image",
    )(arrived, base_inner, asked, where, near_far, far_near, meta)
    arrived = exchange(pay, parts)
    image_all = to_cases([image] * (groups - 1))
    (turned0,) = call(turned_rows, [bubble_of], name="turned", flops=10**9)(
        base_near, base_far, where, turned_near, turned_far
    )
    image_inner, _ = inner(image)
    (gram,) = call(functools.partial(gram_kernel, groups), gram_of, name="gram", smem=(0,))(
        case, gram, base, *base_all, image
    )
    arrived, turned0 = lax.optimization_barrier((arrived, turned0))
    minor = lax.axis_size("py")
    second, copies, turned_own, *messages = call(
        functools.partial(image_kernel, parts, groups, True),
        [field_of, ((groups * minor, cases, LANES), F32, True), ((2 * part, comps), F32, True)]
        + [((rows + 2 * part, comps), F32, True)] * (groups - 1),
        [(rows, comps)] + slot_scratch + [(rows, comps)] * 2 + [(bubbles, comps)] * 2,
        "second",
        smem=(6,),
        hbm=(10,),
        sems=1,
    )(
        arrived, image_inner, asked, where, near_far, far_near, case, gram, turned_near, turned_far, turned0,
        image, *image_all,
    )
    copies = lax.all_to_all(copies, ("py", "case"), split_axis=0, concat_axis=0)
    messages = pl.pallas_call(
        pass_kernel,
        out_shape=[pltpu.HBM(m.shape, m.dtype) for m in messages],
        in_specs=[pl.BlockSpec(memory_space=pltpu.HBM)] * len(messages),
        out_specs=[pl.BlockSpec(memory_space=pltpu.HBM)] * len(messages),
        input_output_aliases={i: i for i in range(len(messages))},
        cost_estimate=pl.CostEstimate(flops=10**9, bytes_accessed=1 << 20, transcendentals=0),
        name="pass_on",
    )(*messages)
    both1 = to_cases(messages)
    (copies,) = call(sum_kernel, [((parts // minor, groups * cases, LANES), F32, False)], name="sum")(
        copies.reshape(minor, groups, cases, LANES)
    )
    copies = lax.all_to_all(copies, "px", split_axis=0, concat_axis=0)
    coef, coef_rows = call(
        functools.partial(solve_kernel, groups),
        [((2 * groups * cases, cases, LANES), F32, False), ((groups * cases, 2 * LANES), F32, False)],
        [(2, groups * cases, LANES)],
        "solve",
        smem=(0,),
    )(case, copies)
    own, *messages = call(
        functools.partial(bubble_kernel, groups, rows), [((part, comps), F32, False)] * groups, name="bubble"
    )(coef_rows, turned_own, *both1)
    back = to_cases(messages)
    x, residual = call(
        functools.partial(ports_kernel, groups), [field_of, field_of], name="ports", flops=10**9
    )(coef, base, *base_all, image, *image_all, second, *both1)
    (bubble,) = call(functools.partial(join_kernel, groups), [bubble_of], name="join", smem=(0,))(
        case, bubble_base, own, *back
    )
    return (
        x.reshape(port_load.shape),
        residual.reshape(port_load.shape),
        bubble.reshape(bubble_load.shape),
    )


def solution(mesh):
    placed = (
        P(PLANE),
        P(PLANE),
        P(PLANE),
        P(PLANE, None),
        P(PLANE),
        P(None, "case", PLANE),
        P(None, "case", PLANE),
        P(),
        P(),
        P(),
    )
    out = P(None, "case", PLANE)
    return jax.shard_map(
        local, mesh=mesh, in_specs=placed, out_specs=(out, out, out), check_vma=False
    )
```

```python
import functools

import jax
import jax.numpy as jnp
from jax import lax
from jax.experimental import pallas as pl
from jax.experimental.pallas import tpu as pltpu
from jax.sharding import PartitionSpec as P

HIGH = lax.Precision.HIGHEST
PLANE = ("px", "py")
F32 = jnp.float32
BF16 = jnp.bfloat16
KINDS = 8
LANES = 128
CASES = 8
SLOTS = 3
NN = (((1,), (0,)), ((), ()))
NT = (((1,), (1,)), ((), ()))
TN = (((0,), (0,)), ((), ()))


def dot(lhs, rhs, dims=NN):
    return lax.dot_general(lhs, rhs, dims, preferred_element_type=F32)


def dot_high(lhs, rhs, dims=NN):
    return lax.dot_general(lhs, rhs, dims, precision=HIGH, preferred_element_type=F32)


def split2(x):
    high = x.astype(BF16)
    return high, (x - high.astype(F32)).astype(BF16)


def pick_right(x, onehot, dims):
    (left,), (right,) = dims[0]
    return dot(jnp.concatenate(split2(x), axis=left), jnp.concatenate([onehot, onehot], axis=right), dims)


def pick_left(onehot, x, dims):
    (left,), (right,) = dims[0]
    return dot(jnp.concatenate([onehot, onehot], axis=left), jnp.concatenate(split2(x), axis=right), dims)


def stacked_table(table):
    high, low = split2(table)
    return jnp.concatenate([high, high, low], axis=1)


def stacked_values(x):
    high, low = split2(x)
    return jnp.concatenate([high, low, high], axis=0)


def iota(shape, dim):
    return lax.broadcasted_iota(jnp.int32, shape, dim)


def column(row):
    return jnp.transpose(jnp.broadcast_to(row, (8, row.shape[1])))[:, :1]


def onehot(mask):
    return mask.astype(F32).astype(BF16)


KIND, STIFF, NEAR, OWNER = [slice(i, i + 1) for i in range(4)]


def owner_slots(owner, parts):
    count = owner.shape[1]
    owner_f = owner.astype(F32)
    same = (column(owner_f) == owner_f) & (iota((count, count), 0) < iota((count, count), 1))
    rank = jnp.sum(same.astype(F32), axis=0, keepdims=True).astype(jnp.int32)
    to = iota((parts, count), 0).astype(F32) == owner_f
    return [to & (rank == s) for s in range(SLOTS)]


def near_onehot(near):
    count = near.shape[1]
    return onehot(column(near.astype(F32)) == iota((count, LANES), 1).astype(F32))


def stacked_rows(meta, lanes):
    turned = jnp.transpose(meta)
    return jnp.concatenate([turned[lanes + s : lanes + s + 1, :] for s in range(SLOTS)], axis=1)


def port_onehot(meta):
    parts = meta.shape[0]
    ports = (iota((parts, LANES), 1) + 1).astype(F32)
    return onehot(jnp.concatenate([meta[:, s : s + 1] == ports for s in range(SLOTS)], axis=0))


def pad_lanes(x, spare):
    if not spare:
        return x
    return jnp.concatenate([x, jnp.zeros((x.shape[0], spare), x.dtype)], axis=1)


def put(pay_ref, rows, first, pitch):
    parts = pay_ref.shape[0] // pitch
    tiles = rows.shape[1] // LANES
    for g in range(rows.shape[0] // parts):
        for t in range(tiles):
            pay_ref[pl.ds(first + g * tiles + t, parts, stride=pitch), :] = rows[
                g * parts : (g + 1) * parts, t * LANES : (t + 1) * LANES
            ]


def get(pay_ref, first, pitch, tiles):
    parts = pay_ref.shape[0] // pitch
    return jnp.concatenate(
        [
            jnp.concatenate(
                [pay_ref[pl.ds(first + s * tiles + t, parts, stride=pitch), :] for t in range(tiles)],
                axis=1,
            )
            for s in range(SLOTS)
        ],
        axis=0,
    )


def by_kind(products, kind, rows):
    chosen = products[:rows]
    for t in range(1, KINDS):
        chosen = jnp.where(kind == t, products[t * rows : (t + 1) * rows], chosen)
    return chosen


def condense_kernel(
    parts, kind_hbm, stiff_hbm, near_hbm, owner_hbm, far_hbm, load_hbm, inverse_hbm, coupling_hbm,
    pay_ref, near_sum_ref, meta_ref, where_ref,
    kind_ref, stiff_ref, near_ref, owner_ref, far_ref, load_ref, inverse_ref, coupling_ref, near_part, far_part, sems,
):
    copies = [
        pltpu.make_async_copy(source, target, sems.at[i])
        for i, (source, target) in enumerate((
            (inverse_hbm, inverse_ref), (coupling_hbm, coupling_ref), (load_hbm, load_ref), (kind_hbm, kind_ref),
            (stiff_hbm, stiff_ref), (near_hbm, near_ref), (owner_hbm, owner_ref), (far_hbm, far_ref),
        ))
    ]
    for copy in copies:
        copy.start()
    for copy in copies[:2]:
        copy.wait()
    modes = load_ref.shape[0] // CASES
    dofs = near_sum_ref.shape[0] // CASES
    left = stacked_table(
        jnp.concatenate(
            [jnp.transpose(dot_high(inverse_ref[t], coupling_ref[t], TN)) for t in range(KINDS)], axis=0
        )
    )
    for copy in copies[2:]:
        copy.wait()
    kind = kind_ref[...]
    kind2 = jnp.concatenate([kind, kind], axis=1)
    for k in range(0, CASES, 2):
        loads = jnp.concatenate(
            [load_ref[pl.ds(k + i, modes, stride=CASES), :] for i in range(2)], axis=1
        )
        condensed = -by_kind(dot(left, stacked_values(loads)), kind2, 2 * dofs)
        for i in range(2):
            lanes = slice(i * LANES, (i + 1) * LANES)
            near_part[pl.ds(k + i, dofs, stride=CASES), :] = condensed[:dofs, lanes]
            far_part[pl.ds(k + i, dofs, stride=CASES), :] = condensed[dofs:, lanes]
    near = near_ref[...]
    slots = owner_slots(owner_ref[...], parts)
    near_sum_ref[...] = pick_right(near_part[...], near_onehot(near), NN)
    chosen = onehot(jnp.concatenate(slots, axis=0))
    put(pay_ref, pick_left(chosen, far_part[...], NT), 0, 10)
    lane = iota((parts, LANES), 1)
    far_row = (far_ref[...] + 1).astype(F32)
    near_row = (near + 1).astype(F32)
    message = jnp.zeros((parts, LANES), F32)
    own = jnp.zeros((parts, LANES), F32)
    for s in range(SLOTS):
        for at, row in ((0, far_row), (SLOTS, kind.astype(F32)), (2 * SLOTS, stiff_ref[...])):
            value = jnp.sum(jnp.where(slots[s], row, 0.0), axis=1, keepdims=True)
            message = jnp.where(lane == at + s, value, message)
        value = jnp.sum(jnp.where(slots[s], near_row, 0.0), axis=1, keepdims=True)
        own = jnp.where(lane == s, value, own)
    pay_ref[pl.ds(9, parts, stride=10), :] = message
    packed = [kind.astype(F32), stiff_ref[...], near.astype(F32), owner_ref[...].astype(F32)]
    where_ref[...] = jnp.concatenate(packed + packed, axis=0)
    meta_ref[...] = own


def tables_kernel(
    where_ref, load_ref, inverse_ref, coupling_ref, block_ref,
    near_near, near_far, far_near, far_far, turned_near, turned_far, base_ref,
):
    dofs = block_ref.shape[1] // 2
    modes = inverse_ref.shape[1]
    inverses = []
    for t in range(KINDS):
        turned = dot_high(inverse_ref[t], coupling_ref[t], TN)
        schur = block_ref[t] - dot_high(turned, coupling_ref[t], TN)
        at = slice(t * dofs, (t + 1) * dofs)
        near_near[at, :] = stacked_table(schur[:dofs, :dofs])
        near_far[at, :] = stacked_table(schur[:dofs, dofs:])
        far_near[at, :] = stacked_table(schur[dofs:, :dofs])
        far_far[at, :] = stacked_table(schur[dofs:, dofs:])
        at = slice(t * modes, (t + 1) * modes)
        turned_near[at, :] = stacked_table(turned[:, :dofs])
        turned_far[at, :] = stacked_table(turned[:, dofs:])
        inverses.append(inverse_ref[t])
    left = stacked_table(jnp.concatenate(inverses, axis=0))
    kind = where_ref[KIND]
    stiff = where_ref[STIFF]
    kind2 = jnp.concatenate([kind, kind], axis=1)
    stiff2 = jnp.concatenate([stiff, stiff], axis=1)
    for k in range(0, CASES, 2):
        loads = jnp.concatenate(
            [load_ref[pl.ds(k + i, modes, stride=CASES), :] for i in range(2)], axis=1
        )
        result = by_kind(dot(left, stacked_values(loads)), kind2, modes) / stiff2
        for i in range(2):
            base_ref[pl.ds(k + i, modes, stride=CASES), :] = result[:, i * LANES : (i + 1) * LANES]


def send_ports(field, asked, own, pay_ref):
    put(pay_ref, pick_left(jnp.concatenate([asked, own], axis=0), field, NT), 0, 18)


def rhs_kernel(parts, arrived_ref, near_sum_ref, load_ref, meta_ref, field_ref, pay_ref, asked_ref):
    asked = arrived_ref[pl.ds(9, parts, stride=10), :]
    asked_ref[...] = asked
    asked_hot = port_onehot(asked)
    arrived = get(arrived_ref, 0, 10, 3)
    field = load_ref[...] + (near_sum_ref[...] + pick_right(arrived, asked_hot, TN))
    field_ref[...] = field
    send_ports(field, asked_hot, port_onehot(meta_ref[...]), pay_ref)


def component_products(table_ref, part_ref, where_ref, out_ref):
    dofs = part_ref.shape[0] // CASES
    kind, stiff = where_ref[KIND], where_ref[STIFF]
    kind2 = jnp.concatenate([kind, kind], axis=1)
    stiff2 = jnp.concatenate([stiff, stiff], axis=1)
    for k in range(0, CASES, 2):
        values = jnp.concatenate(
            [part_ref[pl.ds(k + i, dofs, stride=CASES), :] for i in range(2)], axis=1
        )
        result = by_kind(dot(table_ref[...], stacked_values(values)), kind2, dofs) * stiff2
        for i in range(2):
            out_ref[pl.ds(k + i, dofs, stride=CASES), :] = result[:, i * LANES : (i + 1) * LANES]


def slot_products(table_ref, slot_ref, asked, out_ref):
    tiles = slot_ref.shape[0]
    dofs = slot_ref.shape[1] // CASES
    spare = tiles * LANES - SLOTS * asked.shape[0]
    kind = pad_lanes(stacked_rows(asked, SLOTS), spare)
    stiff = pad_lanes(stacked_rows(asked, 2 * SLOTS), spare)
    for k in range(CASES):
        values = jnp.concatenate(
            [slot_ref[g, pl.ds(k, dofs, stride=CASES), :] for g in range(tiles)], axis=1
        )
        result = by_kind(dot(table_ref[...], stacked_values(values)), kind, dofs) * stiff
        for g in range(tiles):
            out_ref[g, pl.ds(k, dofs, stride=CASES), :] = result[:, g * LANES : (g + 1) * LANES]


def wide_onehot(asked_hot, tiles):
    spare = tiles * LANES - asked_hot.shape[0]
    if not spare:
        return asked_hot
    return jnp.concatenate([asked_hot, jnp.zeros((spare, LANES), BF16)], axis=0)


def slots_to_ports(part_ref, asked_hot):
    tiles = part_ref.shape[0]
    hot = wide_onehot(asked_hot, tiles)
    total = pick_right(part_ref[0], hot[:LANES], NN)
    for g in range(1, tiles):
        total = total + pick_right(part_ref[g], hot[g * LANES : (g + 1) * LANES], NN)
    return total


def inner_kernel(
    field_ref, asked_ref, where_ref, near_near, far_far,
    inner_ref, near_values, near_part, slot_ref, slot_part,
):
    field, asked = field_ref[...], asked_ref[...]
    near_hot, asked_hot = near_onehot(where_ref[NEAR]), port_onehot(asked)
    tiles = slot_ref.shape[0]
    near_values[...] = pick_right(field, near_hot, NT)
    values = pick_right(field, wide_onehot(asked_hot, tiles), NT)
    for g in range(tiles):
        slot_ref[g] = values[:, g * LANES : (g + 1) * LANES]
    component_products(near_near, near_values, where_ref, near_part)
    slot_products(far_far, slot_ref, asked, slot_part)
    inner_ref[...] = pick_right(near_part[...], near_hot, NN) + slots_to_ports(slot_part, asked_hot)


def near_cross(parts, arrived_ref, pitch, kind_ref, stiff_ref, near_ref, owner_ref, near_far, far_values, near_part):
    slots = onehot(jnp.concatenate(owner_slots(where_ref[OWNER], parts), axis=0))
    far_values[...] = pick_right(get(arrived_ref, 0, pitch, 3), slots, TN)
    component_products(near_far, far_values, where_ref, near_part)
    return pick_right(near_part[...], near_onehot(near_ref[...]), NN)


def far_cross(arrived_ref, first, pitch, asked, asked_hot, far_near, slot_ref, slot_part):
    tiles = slot_ref.shape[0]
    values = jnp.transpose(get(arrived_ref, first, pitch, 3))
    values = pad_lanes(values, tiles * LANES - values.shape[1])
    for g in range(tiles):
        slot_ref[g] = values[:, g * LANES : (g + 1) * LANES]
    slot_products(far_near, slot_ref, asked, slot_part)
    return slots_to_ports(slot_part, asked_hot)


def image_kernel(
    parts, groups, last, arrived_ref, inner_ref, asked_ref, where_ref,
    near_far, far_near, *rest,
):
    if last:
        case_ref, gram_ref, turned_far, turned0_hbm, turned1_hbm = rest[:5]
        images, rest = rest[5 : 5 + groups], rest[5 + groups :]
        image_ref, copies_ref, own_ref = rest[:3]
        messages = rest[3 : 2 + groups]
        near_part, slot_ref, slot_part, far_values, turned_ref, turned0_ref, turned1_ref, sems = rest[2 + groups :]
        fetches = [
            pltpu.make_async_copy(turned1_hbm, turned1_ref, sems.at[0]),
            pltpu.make_async_copy(turned0_hbm, turned0_ref, sems.at[1]),
        ]
        for fetch in fetches:
            fetch.start()
    else:
        meta_ref, image_ref, far_values, pay_ref, near_part, slot_ref, slot_part = rest
    asked = asked_ref[...]
    asked_hot = port_onehot(asked)
    slots = onehot(jnp.concatenate(owner_slots(where_ref[OWNER], parts), axis=0))
    far_values[...] = pick_right(get(arrived_ref, 0, 18, 3), slots, TN)
    component_products(near_far, far_values, where_ref, near_part)
    tiles = slot_ref.shape[0]
    values = jnp.transpose(get(arrived_ref, 9, 18, 3))
    values = pad_lanes(values, tiles * LANES - values.shape[1])
    for g in range(tiles):
        slot_ref[g] = values[:, g * LANES : (g + 1) * LANES]
    slot_products(far_near, slot_ref, asked, slot_part)
    image = inner_ref[...] + pick_right(near_part[...], near_onehot(where_ref[NEAR]), NN)
    image = image + slots_to_ports(slot_part, asked_hot)
    image_ref[...] = image
    if last:
        total = groups * CASES
        gram = add_products(
            LANES, images, [images[0], image_ref], [2 * total, 3 * total], case_ref[0], gram_ref[...]
        )
        for p in range(copies_ref.shape[0]):
            copies_ref[p] = gram
        for fetch in fetches:
            fetch.wait()
        turned_sums([(turned_far, far_values)], where_ref, turned_ref, turned1_ref)
        rows, part = image.shape[0], own_ref.shape[0] // 2
        for h in range(groups):
            at = pl.ds(pl.multiple_of(lax.rem(case_ref[0] + h, groups) * part, part), part)
            target, first = (messages[h - 1], rows) if h else (own_ref, 0)
            if h:
                target[:rows, :] = image
            target[first : first + part, :] = turned0_ref[at, :]
            target[first + part :, :] = turned_ref[at, :]
    else:
        send_ports(image, asked_hot, port_onehot(meta_ref[...]), pay_ref)


def turned_sums(pairs, where_ref, out_ref, first=None):
    dofs = pairs[0][1].shape[0] // CASES
    modes = out_ref.shape[0] // CASES
    kind = where_ref[KIND]
    kind2 = jnp.concatenate([kind, kind], axis=1)
    for k in range(0, CASES, 2):
        sums = 0.0
        for table, part in pairs:
            values = jnp.concatenate(
                [part[pl.ds(k + i, dofs, stride=CASES), :] for i in range(2)], axis=1
            )
            sums = sums + dot(table[...], stacked_values(values))
        result = by_kind(sums, kind2, modes)
        for i in range(2):
            rows = pl.ds(k + i, modes, stride=CASES)
            mine = result[:, i * LANES : (i + 1) * LANES]
            out_ref[rows, :] = mine if first is None else first[rows, :] + mine


def turned_rows(near_values, far_values, where_ref, turned_near, turned_far, out_ref):
    turned_sums([(turned_near, near_values), (turned_far, far_values)], where_ref, out_ref)


def turned_near_rows(near_values, where_ref, turned_near, out_ref):
    turned_sums([(turned_near, near_values)], where_ref, out_ref)


def pass_kernel(*refs):
    pass


def add_products(lanes, lefts, rights, first, case, out):
    groups = len(lefts)
    total = groups * CASES
    dofs = lefts[0].shape[0] // CASES
    lane = iota((CASES, LANES), 1)
    for h in range(groups):
        def step(d, sums):
            own = pl.ds(pl.multiple_of(d * CASES, CASES), CASES)
            values = [ref[own, :] for ref in rights]
            new = []
            for i in range(CASES):
                row = lefts[h][pl.ds(d * CASES + i, 1), :]
                new.append(tuple(s + row * v for s, v in zip(sums[i], values)))
            return tuple(new)

        zero = jnp.zeros((CASES, LANES), F32)
        sums = lax.fori_loop(0, dofs, step, ((zero,) * len(rights),) * CASES)
        at = lax.rem(case + h, groups) * CASES
        for i in range(CASES):
            for g in range(len(rights)):
                value = jnp.sum(sums[i][g], axis=1, keepdims=True)
                out = jnp.where(lane == first[g] + at + i, value, out)
    return out


def base_gram_kernel(groups, case_ref, *refs):
    base, out_ref = refs[:groups], refs[groups]
    out_ref[...] = add_products(LANES, base, [base[0]], [0], case_ref[0], jnp.zeros((CASES, LANES), F32))


def gram_kernel(groups, case_ref, gram_ref, *refs):
    base, image_ref, out_ref = refs[:groups], refs[groups], refs[groups + 1]
    out_ref[...] = add_products(LANES, base, [image_ref], [groups * CASES], case_ref[0], gram_ref[...])


def sum_kernel(in_ref, out_ref):
    for q in range(in_ref.shape[1]):
        total = in_ref[0, q]
        for p in range(1, in_ref.shape[0]):
            total = total + in_ref[p, q]
        for p in range(out_ref.shape[0]):
            out_ref[p, q * CASES : (q + 1) * CASES, :] = total


def inverse2(p, q, r, s):
    scale = 1.0 / (p * s - q * r)
    return s * scale, -q * scale, -r * scale, p * scale


def spd_solve(matrix, target):
    n = matrix.shape[0]
    a = jnp.concatenate([matrix, target], axis=1)
    row_of = iota(a.shape, 0)
    for k in range(0, n, 4):
        c = [jnp.broadcast_to(a[:, k + i : k + i + 1], a.shape) for i in range(4)]
        r = [a[k + i : k + i + 1] for i in range(4)]
        p = [[c[j][k + i : k + i + 1] for j in range(4)] for i in range(4)]
        a00, a01, a10, a11 = inverse2(p[0][0], p[0][1], p[1][0], p[1][1])
        e00, e01 = p[2][0] * a00 + p[2][1] * a10, p[2][0] * a01 + p[2][1] * a11
        e10, e11 = p[3][0] * a00 + p[3][1] * a10, p[3][0] * a01 + p[3][1] * a11
        i00, i01, i10, i11 = inverse2(
            p[2][2] - (e00 * p[0][2] + e01 * p[1][2]),
            p[2][3] - (e00 * p[0][3] + e01 * p[1][3]),
            p[3][2] - (e10 * p[0][2] + e11 * p[1][2]),
            p[3][3] - (e10 * p[0][3] + e11 * p[1][3]),
        )
        t2 = r[2] - (e00 * r[0] + e01 * r[1])
        t3 = r[3] - (e10 * r[0] + e11 * r[1])
        u2, u3 = i00 * t2 + i01 * t3, i10 * t2 + i11 * t3
        w0 = r[0] - (p[0][2] * u2 + p[0][3] * u3)
        w1 = r[1] - (p[1][2] * u2 + p[1][3] * u3)
        u = [a00 * w0 + a01 * w1, a10 * w0 + a11 * w1, u2, u3]
        a = a - ((c[0] * u[0] + c[1] * u[1]) + (c[2] * u[2] + c[3] * u[3]))
        for i in range(4):
            a = jnp.where(row_of == k + i, u[i], a)
    return a[:, n:]


def symmetric(m):
    return 0.5 * (m + jnp.transpose(m))


def solve_kernel(groups, case_ref, gram_ref, coef, coef_rows, turned_coef):
    n = groups * CASES
    total = gram_ref[0]
    for p in range(1, gram_ref.shape[0]):
        total = total + gram_ref[p]
    g00, g01, g11, g12 = [symmetric(total[:, g * n : (g + 1) * n]) for g in range(4)]
    steps = spd_solve(g01, jnp.concatenate([g00, g11], axis=1))
    step0, step1 = steps[:, :n], steps[:, n:]
    both = dot_high(g11, steps)
    second = spd_solve(symmetric(g12 - both[:, n:]), g01 - both[:, :n])
    first = step0 - dot_high(step1, second)
    first, second = jnp.transpose(first), jnp.transpose(second)
    turned_coef[0] = jnp.concatenate([first] * (LANES // n), axis=1)
    turned_coef[1] = jnp.concatenate([second] * (LANES // n), axis=1)
    shift = LANES - case_ref[0] * CASES
    for q in range(groups):
        at = pl.multiple_of(lax.rem(case_ref[0] + q, groups) * CASES, CASES)
        for h in range(2):
            mine = pltpu.roll(turned_coef[h, pl.ds(at, CASES), :], shift, 1)
            coef_rows[q * CASES : (q + 1) * CASES, h * LANES : (h + 1) * LANES] = mine
            if q == 0:
                for j in range(n):
                    coef[h * n + j] = jnp.broadcast_to(mine[:, j : j + 1], (CASES, LANES))


def bubble_kernel(groups, rows, case_ref, coef_ref, *refs):
    turned, out_ref = refs[:groups], refs[groups]
    n = groups * CASES
    part = out_ref.shape[1]
    firsts = [0] + [rows] * (groups - 1)
    left = stacked_table(jnp.concatenate([coef_ref[:, :n], coef_ref[:, LANES : LANES + n]], axis=1))
    for m in range(0, part // CASES, 2):
        values = [
            jnp.concatenate(
                [
                    ref[first + half * part + at : first + half * part + at + CASES, :]
                    for half in range(2)
                    for ref, first in zip(turned, firsts)
                ],
                axis=0,
            )
            for at in (m * CASES, (m + 1) * CASES)
        ]
        result = dot(left, stacked_values(jnp.concatenate(values, axis=1)))
        for i in range(2):
            for h in range(groups):
                out_ref[lax.rem(case_ref[0] + h, groups), (m + i) * CASES : (m + i + 1) * CASES, :] = result[
                    h * CASES : (h + 1) * CASES, i * LANES : (i + 1) * LANES
                ]


def ports_kernel(groups, coef, *refs):
    base, image, second = [refs[g * groups : (g + 1) * groups] for g in range(3)]
    x_ref, residual_ref = refs[3 * groups :]
    n = groups * CASES
    dofs = x_ref.shape[0] // CASES
    wide = 4

    def ports(block, carry):
        d0 = block * wide
        own = [pl.ds(pl.multiple_of((d0 + i) * CASES, CASES), CASES) for i in range(wide)]
        x = [jnp.zeros((CASES, LANES), F32)] * wide
        r = [base[0][own[i], :] for i in range(wide)]
        for j in range(n):
            q, c = divmod(j, CASES)
            c0, c1 = coef[j], coef[n + j]
            for i in range(wide):
                row = pl.ds((d0 + i) * CASES + c, 1)
                a = image[q][row, :]
                x[i] = x[i] + (c0 * base[q][row, :] + c1 * a)
                r[i] = r[i] - (c0 * a + c1 * second[q][row, :])
        for i in range(wide):
            x_ref[own[i], :] = x[i]
            residual_ref[own[i], :] = r[i]
        return carry

    lax.fori_loop(0, dofs // wide, ports, 0)


def join_kernel(bubble_ref, sums_ref, out_ref):
    out_ref[...] = bubble_ref[...] - sums_ref[...]


def call(kernel, outs, scratch=(), name=None, flops=0, smem=(), hbm=(), anywhere=(), sems=0, limit=12):
    results = [(pltpu.HBM if far else jax.ShapeDtypeStruct)(shape, dtype) for shape, dtype, far in outs]
    vmem = pl.BlockSpec(memory_space=pltpu.VMEM)
    far_spec = pl.BlockSpec(memory_space=pltpu.HBM)

    def run(*args):
        specs = [
            pl.BlockSpec(memory_space=pltpu.SMEM) if i in smem else far_spec if i in hbm else pl.BlockSpec(memory_space=pl.ANY) if i in anywhere else vmem
            for i in range(len(args))
        ]
        moved = sum(a.size * a.dtype.itemsize for a in args)
        args = [pltpu.with_memory_space_constraint(a, pltpu.HBM) if i in hbm else a for i, a in enumerate(args)]
        return pl.pallas_call(
            kernel,
            out_shape=results,
            in_specs=specs,
            out_specs=[vmem] * len(outs),
            scratch_shapes=[pltpu.VMEM(*shape) if isinstance(shape[0], tuple) else pltpu.VMEM(shape, F32) for shape in scratch]
            + ([pltpu.SemaphoreType.DMA((sems,) if sems > 1 else ())] if sems else []),
            compiler_params=pltpu.CompilerParams(vmem_limit_bytes=limit << 20),
            cost_estimate=pl.CostEstimate(flops=flops, bytes_accessed=moved, transcendentals=0),
            name=name,
        )(*args)

    return run


def exchange(rows, parts):
    moved = lax.all_to_all(rows.reshape(parts, 1, -1), PLANE, split_axis=0, concat_axis=0)
    return moved.reshape(rows.shape)


def local(
    comp_type, stiffness, near_port, far_owner, far_port, bubble_load, port_load,
    bubble_inverse, coupling, port_block,
):
    parts = lax.axis_size("px") * lax.axis_size("py")
    groups = lax.axis_size("case")
    modes, cases, comps = bubble_load.shape
    dofs, _, ports = port_load.shape
    rows, bubbles = dofs * cases, modes * cases
    slot_tiles = -(-SLOTS * parts // LANES)
    coupling = jnp.swapaxes(coupling, 1, 2)
    kind = comp_type.reshape(1, comps)
    stiff = stiffness.reshape(1, comps)
    near = near_port.reshape(1, comps)
    owner = far_owner.reshape(1, comps)
    far = far_port.reshape(1, comps)
    loads = bubble_load.reshape(bubbles, comps)
    field_of = ((rows, ports), F32, True)
    meta_of = ((parts, LANES), F32, False)
    bubble_of = ((bubbles, comps), F32, True)
    given = (kind, stiff, near, owner, far, loads, bubble_inverse, coupling)
    pay, near_sum, meta, where = call(
        functools.partial(condense_kernel, parts),
        [((parts * 10, LANES), F32, False), field_of, meta_of, ((8, LANES), F32, False)],
        [(a.shape, a.dtype) for a in given] + [(rows, comps)] * 2,
        "condense",
        hbm=range(len(given)),
        sems=len(given),
    )(*given)
    near_near, near_far, far_near, far_far, turned_near, turned_far, bubble_base = call(
        tables_kernel,
        [((KINDS * dofs, 3 * dofs), BF16, False)] * 4 + [((KINDS * modes, 3 * dofs), BF16, True)] * 2 + [bubble_of],
        name="tables",
        flops=10**9,
    )(where, loads, bubble_inverse, coupling, port_block)
    base, pay, asked = call(
        functools.partial(rhs_kernel, parts),
        [field_of, ((parts * 18, LANES), F32, False), meta_of],
        name="rhs",
    )(exchange(pay, parts), near_sum, port_load.reshape(rows, ports), meta)

    case = lax.axis_index("case").reshape(1)
    part = bubbles // groups
    part_of = ((part, comps), F32, True)
    slot_scratch = [(slot_tiles, rows, LANES)] * 2

    def to_cases(messages):
        backward = [
            lax.ppermute(message, "case", [(k, (k + h) % groups) for k in range(groups)])
            for h, message in enumerate(messages, 1)
        ]
        return backward[::-1]

    def inner(field):
        return call(inner_kernel, [((rows, ports), F32, False)] * 2, [(rows, comps)] + slot_scratch, "inner", flops=10**9)(
            field, asked, where, near_near, far_far
        )

    arrived = exchange(pay, parts)
    base_all = to_cases([base] * (groups - 1))
    base_inner, base_near = inner(base)
    gram_of = [((cases, LANES), F32, False)]
    (gram,) = call(functools.partial(base_gram_kernel, groups), gram_of, name="base_gram", smem=(0,))(
        case, base, *base_all
    )
    arrived, gram = lax.optimization_barrier((arrived, gram))
    image, base_far, pay = call(
        functools.partial(image_kernel, parts, groups, False),
        [((rows, ports), F32, False), field_of, ((parts * 18, LANES), F32, False)],
        [(rows, comps)] + slot_scratch,
        "image",
    )(arrived, base_inner, asked, where, near_far, far_near, meta)
    arrived = exchange(pay, parts)
    image_all = to_cases([image] * (groups - 1))
    (turned0,) = call(turned_rows, [bubble_of], name="turned", flops=10**9)(
        base_near, base_far, where, turned_near, turned_far
    )
    image_inner, image_near = inner(image)
    (turned1,) = call(turned_near_rows, [bubble_of], name="turned_near", flops=10**9)(image_near, where, turned_near)
    (gram,) = call(functools.partial(gram_kernel, groups), gram_of, name="gram", smem=(0,))(
        case, gram, base, *base_all, image
    )
    arrived, turned0, turned1 = lax.optimization_barrier((arrived, turned0, turned1))
    minor = lax.axis_size("py")
    second, copies, turned_own, *messages = call(
        functools.partial(image_kernel, parts, groups, True),
        [field_of, ((groups * minor, cases, LANES), F32, True), ((2 * part, comps), F32, True)]
        + [((rows + 2 * part, comps), F32, True)] * (groups - 1),
        [(rows, comps)] + slot_scratch + [(rows, comps)] + [(bubbles, comps)] * 3,
        "second",
        smem=(6,),
        hbm=(9, 10),
        sems=2,
    )(
        arrived, image_inner, asked, where, near_far, far_near, case, gram, turned_far, turned0, turned1,
        image, *image_all,
    )
    copies = lax.all_to_all(copies, ("py", "case"), split_axis=0, concat_axis=0)
    messages = pl.pallas_call(
        pass_kernel,
        out_shape=[pltpu.HBM(m.shape, m.dtype) for m in messages],
        in_specs=[pl.BlockSpec(memory_space=pltpu.HBM)] * len(messages),
        out_specs=[pl.BlockSpec(memory_space=pltpu.HBM)] * len(messages),
        input_output_aliases={i: i for i in range(len(messages))},
        cost_estimate=pl.CostEstimate(flops=10**9, bytes_accessed=1 << 20, transcendentals=0),
        name="pass_on",
    )(*messages)
    both1 = to_cases(messages)
    (copies,) = call(sum_kernel, [((parts // minor, groups * cases, LANES), F32, False)], name="sum")(
        copies.reshape(minor, groups, cases, LANES)
    )
    copies = lax.all_to_all(copies, "px", split_axis=0, concat_axis=0)
    coef, coef_rows = call(
        functools.partial(solve_kernel, groups),
        [((2 * groups * cases, cases, LANES), F32, False), ((groups * cases, 2 * LANES), F32, False)],
        [(2, groups * cases, LANES)],
        "solve",
        smem=(0,),
    )(case, copies)
    (sums,) = call(
        functools.partial(bubble_kernel, groups, rows), [((groups, part, comps), F32, False)], name="bubble", smem=(0,)
    )(case, coef_rows, turned_own, *both1)
    sums = lax.all_to_all(sums, "case", split_axis=0, concat_axis=0)
    x, residual = call(
        functools.partial(ports_kernel, groups), [field_of, field_of], name="ports", flops=10**9
    )(coef, base, *base_all, image, *image_all, second, *both1)
    (bubble,) = call(join_kernel, [bubble_of], name="join")(bubble_base, sums.reshape(bubbles, comps))
    return (
        x.reshape(port_load.shape),
        residual.reshape(port_load.shape),
        bubble.reshape(bubble_load.shape),
    )


def solution(mesh):
    placed = (
        P(PLANE),
        P(PLANE),
        P(PLANE),
        P(PLANE, None),
        P(PLANE),
        P(None, "case", PLANE),
        P(None, "case", PLANE),
        P(),
        P(),
        P(),
    )
    out = P(None, "case", PLANE)
    return jax.shard_map(
        local, mesh=mesh, in_specs=placed, out_specs=(out, out, out), check_vma=False
    )
```

```python
import functools

import jax
import jax.numpy as jnp
from jax import lax
from jax.experimental import pallas as pl
from jax.experimental.pallas import tpu as pltpu
from jax.sharding import PartitionSpec as P

HIGH = lax.Precision.HIGHEST
PLANE = ("px", "py")
F32 = jnp.float32
BF16 = jnp.bfloat16
KINDS = 8
LANES = 128
CASES = 8
SLOTS = 3
NN = (((1,), (0,)), ((), ()))
NT = (((1,), (1,)), ((), ()))
TN = (((0,), (0,)), ((), ()))


def dot(lhs, rhs, dims=NN):
    return lax.dot_general(lhs, rhs, dims, preferred_element_type=F32)


def dot_high(lhs, rhs, dims=NN):
    return lax.dot_general(lhs, rhs, dims, precision=HIGH, preferred_element_type=F32)


def split2(x):
    high = x.astype(BF16)
    return high, (x - high.astype(F32)).astype(BF16)


def pick_right(x, onehot, dims):
    (left,), (right,) = dims[0]
    return dot(jnp.concatenate(split2(x), axis=left), jnp.concatenate([onehot, onehot], axis=right), dims)


def pick_left(onehot, x, dims):
    (left,), (right,) = dims[0]
    return dot(jnp.concatenate([onehot, onehot], axis=left), jnp.concatenate(split2(x), axis=right), dims)


def stacked_table(table):
    high, low = split2(table)
    return jnp.concatenate([high, high, low], axis=1)


def stacked_values(x):
    high, low = split2(x)
    return jnp.concatenate([high, low, high], axis=0)


def iota(shape, dim):
    return lax.broadcasted_iota(jnp.int32, shape, dim)


def column(row):
    return jnp.transpose(jnp.broadcast_to(row, (8, row.shape[1])))[:, :1]


def onehot(mask):
    return mask.astype(F32).astype(BF16)


KIND, STIFF, NEAR, OWNER = [slice(i, i + 1) for i in range(4)]


def owner_slots(owner, parts):
    count = owner.shape[1]
    owner_f = owner.astype(F32)
    same = (column(owner_f) == owner_f) & (iota((count, count), 0) < iota((count, count), 1))
    rank = jnp.sum(same.astype(F32), axis=0, keepdims=True).astype(jnp.int32)
    to = iota((parts, count), 0).astype(F32) == owner_f
    return [to & (rank == s) for s in range(SLOTS)]


def near_onehot(near):
    count = near.shape[1]
    return onehot(column(near.astype(F32)) == iota((count, LANES), 1).astype(F32))


def stacked_rows(meta, lanes):
    turned = jnp.transpose(meta)
    return jnp.concatenate([turned[lanes + s : lanes + s + 1, :] for s in range(SLOTS)], axis=1)


def port_onehot(meta):
    parts = meta.shape[0]
    ports = (iota((parts, LANES), 1) + 1).astype(F32)
    return onehot(jnp.concatenate([meta[:, s : s + 1] == ports for s in range(SLOTS)], axis=0))


def pad_lanes(x, spare):
    if not spare:
        return x
    return jnp.concatenate([x, jnp.zeros((x.shape[0], spare), x.dtype)], axis=1)


def put(pay_ref, rows, first, pitch):
    parts = pay_ref.shape[0] // pitch
    tiles = rows.shape[1] // LANES
    for g in range(rows.shape[0] // parts):
        for t in range(tiles):
            pay_ref[pl.ds(first + g * tiles + t, parts, stride=pitch), :] = rows[
                g * parts : (g + 1) * parts, t * LANES : (t + 1) * LANES
            ]


def get(pay_ref, first, pitch, tiles):
    parts = pay_ref.shape[0] // pitch
    return jnp.concatenate(
        [
            jnp.concatenate(
                [pay_ref[pl.ds(first + s * tiles + t, parts, stride=pitch), :] for t in range(tiles)],
                axis=1,
            )
            for s in range(SLOTS)
        ],
        axis=0,
    )


def by_kind(products, kind, rows):
    chosen = products[:rows]
    for t in range(1, KINDS):
        chosen = jnp.where(kind == t, products[t * rows : (t + 1) * rows], chosen)
    return chosen


def condense_kernel(
    parts, kind_hbm, stiff_hbm, near_hbm, owner_hbm, far_hbm, load_hbm, inverse_hbm, coupling_hbm,
    pay_ref, near_sum_ref, meta_ref, where_ref,
    kind_ref, stiff_ref, near_ref, owner_ref, far_ref, load_ref, inverse_ref, coupling_ref, near_part, far_part, sems,
):
    copies = [
        pltpu.make_async_copy(source, target, sems.at[i])
        for i, (source, target) in enumerate((
            (inverse_hbm, inverse_ref), (coupling_hbm, coupling_ref), (load_hbm, load_ref), (kind_hbm, kind_ref),
            (stiff_hbm, stiff_ref), (near_hbm, near_ref), (owner_hbm, owner_ref), (far_hbm, far_ref),
        ))
    ]
    for copy in copies:
        copy.start()
    for copy in copies[:2]:
        copy.wait()
    modes = load_ref.shape[0] // CASES
    dofs = near_sum_ref.shape[0] // CASES
    left = stacked_table(
        jnp.concatenate(
            [jnp.transpose(dot_high(inverse_ref[t], coupling_ref[t], TN)) for t in range(KINDS)], axis=0
        )
    )
    for copy in copies[2:]:
        copy.wait()
    kind = kind_ref[...]
    kind2 = jnp.concatenate([kind, kind], axis=1)
    for k in range(0, CASES, 2):
        loads = jnp.concatenate(
            [load_ref[pl.ds(k + i, modes, stride=CASES), :] for i in range(2)], axis=1
        )
        condensed = -by_kind(dot(left, stacked_values(loads)), kind2, 2 * dofs)
        for i in range(2):
            lanes = slice(i * LANES, (i + 1) * LANES)
            near_part[pl.ds(k + i, dofs, stride=CASES), :] = condensed[:dofs, lanes]
            far_part[pl.ds(k + i, dofs, stride=CASES), :] = condensed[dofs:, lanes]
    near = near_ref[...]
    slots = owner_slots(owner_ref[...], parts)
    near_sum_ref[...] = pick_right(near_part[...], near_onehot(near), NN)
    chosen = onehot(jnp.concatenate(slots, axis=0))
    put(pay_ref, pick_left(chosen, far_part[...], NT), 0, 10)
    lane = iota((parts, LANES), 1)
    far_row = (far_ref[...] + 1).astype(F32)
    near_row = (near + 1).astype(F32)
    message = jnp.zeros((parts, LANES), F32)
    own = jnp.zeros((parts, LANES), F32)
    for s in range(SLOTS):
        for at, row in ((0, far_row), (SLOTS, kind.astype(F32)), (2 * SLOTS, stiff_ref[...])):
            value = jnp.sum(jnp.where(slots[s], row, 0.0), axis=1, keepdims=True)
            message = jnp.where(lane == at + s, value, message)
        value = jnp.sum(jnp.where(slots[s], near_row, 0.0), axis=1, keepdims=True)
        own = jnp.where(lane == s, value, own)
    pay_ref[pl.ds(9, parts, stride=10), :] = message
    packed = [kind.astype(F32), stiff_ref[...], near.astype(F32), owner_ref[...].astype(F32)]
    where_ref[...] = jnp.concatenate(packed + packed, axis=0)
    meta_ref[...] = own


def tables_kernel(
    where_ref, load_ref, inverse_ref, coupling_ref, block_ref,
    near_near, near_far, far_near, far_far, turned_near, turned_far, base_ref,
):
    dofs = block_ref.shape[1] // 2
    modes = inverse_ref.shape[1]
    inverses = []
    for t in range(KINDS):
        turned = dot_high(inverse_ref[t], coupling_ref[t], TN)
        schur = block_ref[t] - dot_high(turned, coupling_ref[t], TN)
        at = slice(t * dofs, (t + 1) * dofs)
        near_near[at, :] = stacked_table(schur[:dofs, :dofs])
        near_far[at, :] = stacked_table(schur[:dofs, dofs:])
        far_near[at, :] = stacked_table(schur[dofs:, :dofs])
        far_far[at, :] = stacked_table(schur[dofs:, dofs:])
        at = slice(t * modes, (t + 1) * modes)
        turned_near[at, :] = stacked_table(turned[:, :dofs])
        turned_far[at, :] = stacked_table(turned[:, dofs:])
        inverses.append(inverse_ref[t])
    left = stacked_table(jnp.concatenate(inverses, axis=0))
    kind = where_ref[KIND]
    stiff = where_ref[STIFF]
    kind2 = jnp.concatenate([kind, kind], axis=1)
    stiff2 = jnp.concatenate([stiff, stiff], axis=1)
    for k in range(0, CASES, 2):
        loads = jnp.concatenate(
            [load_ref[pl.ds(k + i, modes, stride=CASES), :] for i in range(2)], axis=1
        )
        result = by_kind(dot(left, stacked_values(loads)), kind2, modes) / stiff2
        for i in range(2):
            base_ref[pl.ds(k + i, modes, stride=CASES), :] = result[:, i * LANES : (i + 1) * LANES]


def send_ports(field, asked, own, pay_ref):
    put(pay_ref, pick_left(jnp.concatenate([asked, own], axis=0), field, NT), 0, 18)


def rhs_kernel(parts, arrived_ref, near_sum_ref, load_ref, meta_ref, field_ref, pay_ref, asked_ref):
    asked = arrived_ref[pl.ds(9, parts, stride=10), :]
    asked_ref[...] = asked
    asked_hot = port_onehot(asked)
    arrived = get(arrived_ref, 0, 10, 3)
    field = load_ref[...] + (near_sum_ref[...] + pick_right(arrived, asked_hot, TN))
    field_ref[...] = field
    send_ports(field, asked_hot, port_onehot(meta_ref[...]), pay_ref)


def component_products(table_ref, part_ref, where_ref, out_ref):
    dofs = part_ref.shape[0] // CASES
    kind, stiff = where_ref[KIND], where_ref[STIFF]
    kind2 = jnp.concatenate([kind, kind], axis=1)
    stiff2 = jnp.concatenate([stiff, stiff], axis=1)
    for k in range(0, CASES, 2):
        values = jnp.concatenate(
            [part_ref[pl.ds(k + i, dofs, stride=CASES), :] for i in range(2)], axis=1
        )
        result = by_kind(dot(table_ref[...], stacked_values(values)), kind2, dofs) * stiff2
        for i in range(2):
            out_ref[pl.ds(k + i, dofs, stride=CASES), :] = result[:, i * LANES : (i + 1) * LANES]


def slot_products(table_ref, slot_ref, asked, out_ref):
    tiles = slot_ref.shape[0]
    dofs = slot_ref.shape[1] // CASES
    spare = tiles * LANES - SLOTS * asked.shape[0]
    kind = pad_lanes(stacked_rows(asked, SLOTS), spare)
    stiff = pad_lanes(stacked_rows(asked, 2 * SLOTS), spare)
    for k in range(CASES):
        values = jnp.concatenate(
            [slot_ref[g, pl.ds(k, dofs, stride=CASES), :] for g in range(tiles)], axis=1
        )
        result = by_kind(dot(table_ref[...], stacked_values(values)), kind, dofs) * stiff
        for g in range(tiles):
            out_ref[g, pl.ds(k, dofs, stride=CASES), :] = result[:, g * LANES : (g + 1) * LANES]


def wide_onehot(asked_hot, tiles):
    spare = tiles * LANES - asked_hot.shape[0]
    if not spare:
        return asked_hot
    return jnp.concatenate([asked_hot, jnp.zeros((spare, LANES), BF16)], axis=0)


def slots_to_ports(part_ref, asked_hot):
    tiles = part_ref.shape[0]
    hot = wide_onehot(asked_hot, tiles)
    total = pick_right(part_ref[0], hot[:LANES], NN)
    for g in range(1, tiles):
        total = total + pick_right(part_ref[g], hot[g * LANES : (g + 1) * LANES], NN)
    return total


def inner_kernel(
    field_ref, asked_ref, where_ref, near_near, far_far,
    inner_ref, near_values, near_part, slot_ref, slot_part,
):
    field, asked = field_ref[...], asked_ref[...]
    near_hot, asked_hot = near_onehot(where_ref[NEAR]), port_onehot(asked)
    tiles = slot_ref.shape[0]
    near_values[...] = pick_right(field, near_hot, NT)
    values = pick_right(field, wide_onehot(asked_hot, tiles), NT)
    for g in range(tiles):
        slot_ref[g] = values[:, g * LANES : (g + 1) * LANES]
    component_products(near_near, near_values, where_ref, near_part)
    slot_products(far_far, slot_ref, asked, slot_part)
    inner_ref[...] = pick_right(near_part[...], near_hot, NN) + slots_to_ports(slot_part, asked_hot)


def near_cross(parts, arrived_ref, pitch, kind_ref, stiff_ref, near_ref, owner_ref, near_far, far_values, near_part):
    slots = onehot(jnp.concatenate(owner_slots(where_ref[OWNER], parts), axis=0))
    far_values[...] = pick_right(get(arrived_ref, 0, pitch, 3), slots, TN)
    component_products(near_far, far_values, where_ref, near_part)
    return pick_right(near_part[...], near_onehot(near_ref[...]), NN)


def far_cross(arrived_ref, first, pitch, asked, asked_hot, far_near, slot_ref, slot_part):
    tiles = slot_ref.shape[0]
    values = jnp.transpose(get(arrived_ref, first, pitch, 3))
    values = pad_lanes(values, tiles * LANES - values.shape[1])
    for g in range(tiles):
        slot_ref[g] = values[:, g * LANES : (g + 1) * LANES]
    slot_products(far_near, slot_ref, asked, slot_part)
    return slots_to_ports(slot_part, asked_hot)


def image_kernel(
    parts, groups, last, arrived_ref, inner_ref, asked_ref, where_ref,
    near_far, far_near, *rest,
):
    if last:
        case_ref, gram_ref, turned_far, turned0_hbm, turned1_hbm = rest[:5]
        images, rest = rest[5 : 5 + groups], rest[5 + groups :]
        image_ref, copies_ref, own_ref = rest[:3]
        messages = rest[3 : 2 + groups]
        near_part, slot_ref, slot_part, far_values, turned_ref, turned0_ref, turned1_ref, sems = rest[2 + groups :]
        fetches = [
            pltpu.make_async_copy(turned1_hbm, turned1_ref, sems.at[0]),
            pltpu.make_async_copy(turned0_hbm, turned0_ref, sems.at[1]),
        ]
        for fetch in fetches:
            fetch.start()
    else:
        meta_ref, image_ref, far_values, pay_ref, near_part, slot_ref, slot_part = rest
    asked = asked_ref[...]
    asked_hot = port_onehot(asked)
    slots = onehot(jnp.concatenate(owner_slots(where_ref[OWNER], parts), axis=0))
    far_values[...] = pick_right(get(arrived_ref, 0, 18, 3), slots, TN)
    component_products(near_far, far_values, where_ref, near_part)
    tiles = slot_ref.shape[0]
    values = jnp.transpose(get(arrived_ref, 9, 18, 3))
    values = pad_lanes(values, tiles * LANES - values.shape[1])
    for g in range(tiles):
        slot_ref[g] = values[:, g * LANES : (g + 1) * LANES]
    slot_products(far_near, slot_ref, asked, slot_part)
    image = inner_ref[...] + pick_right(near_part[...], near_onehot(where_ref[NEAR]), NN)
    image = image + slots_to_ports(slot_part, asked_hot)
    image_ref[...] = image
    if last:
        total = groups * CASES
        gram = add_products(
            LANES, images, [images[0], image_ref], [2 * total, 3 * total], case_ref[0], gram_ref[...]
        )
        for p in range(copies_ref.shape[0]):
            copies_ref[p] = gram
        for fetch in fetches:
            fetch.wait()
        turned_sums([(turned_far, far_values)], where_ref, turned_ref, turned1_ref)
        rows, part = image.shape[0], own_ref.shape[0] // 2
        for h in range(groups):
            at = pl.ds(pl.multiple_of(lax.rem(case_ref[0] + h, groups) * part, part), part)
            target, first = (messages[h - 1], rows) if h else (own_ref, 0)
            if h:
                target[:rows, :] = image
            target[first : first + part, :] = turned0_ref[at, :]
            target[first + part :, :] = turned_ref[at, :]
    else:
        send_ports(image, asked_hot, port_onehot(meta_ref[...]), pay_ref)


def turned_sums(pairs, where_ref, out_ref, first=None):
    dofs = pairs[0][1].shape[0] // CASES
    modes = out_ref.shape[0] // CASES
    kind = where_ref[KIND]
    kind2 = jnp.concatenate([kind, kind], axis=1)
    for k in range(0, CASES, 2):
        sums = 0.0
        for table, part in pairs:
            values = jnp.concatenate(
                [part[pl.ds(k + i, dofs, stride=CASES), :] for i in range(2)], axis=1
            )
            sums = sums + dot(table[...], stacked_values(values))
        result = by_kind(sums, kind2, modes)
        for i in range(2):
            rows = pl.ds(k + i, modes, stride=CASES)
            mine = result[:, i * LANES : (i + 1) * LANES]
            out_ref[rows, :] = mine if first is None else first[rows, :] + mine


def turned_rows(near_values, far_values, where_ref, turned_near, turned_far, out_ref):
    turned_sums([(turned_near, near_values), (turned_far, far_values)], where_ref, out_ref)


def turned_near_rows(near_values, where_ref, turned_near, out_ref):
    turned_sums([(turned_near, near_values)], where_ref, out_ref)


def pass_kernel(*refs):
    pass


def add_products(lanes, lefts, rights, first, case, out):
    groups = len(lefts)
    total = groups * CASES
    dofs = lefts[0].shape[0] // CASES
    lane = iota((CASES, LANES), 1)
    for h in range(groups):
        def step(d, sums):
            own = pl.ds(pl.multiple_of(d * CASES, CASES), CASES)
            values = [ref[own, :] for ref in rights]
            new = []
            for i in range(CASES):
                row = lefts[h][pl.ds(d * CASES + i, 1), :]
                new.append(tuple(s + row * v for s, v in zip(sums[i], values)))
            return tuple(new)

        zero = jnp.zeros((CASES, LANES), F32)
        sums = lax.fori_loop(0, dofs, step, ((zero,) * len(rights),) * CASES)
        at = lax.rem(case + h, groups) * CASES
        for i in range(CASES):
            for g in range(len(rights)):
                value = jnp.sum(sums[i][g], axis=1, keepdims=True)
                out = jnp.where(lane == first[g] + at + i, value, out)
    return out


def base_gram_kernel(groups, case_ref, *refs):
    base, out_ref = refs[:groups], refs[groups]
    out_ref[...] = add_products(LANES, base, [base[0]], [0], case_ref[0], jnp.zeros((CASES, LANES), F32))


def gram_kernel(groups, case_ref, gram_ref, *refs):
    base, image_ref, out_ref = refs[:groups], refs[groups], refs[groups + 1]
    out_ref[...] = add_products(LANES, base, [image_ref], [groups * CASES], case_ref[0], gram_ref[...])


def sum_kernel(in_ref, out_ref):
    for q in range(in_ref.shape[1]):
        total = in_ref[0, q]
        for p in range(1, in_ref.shape[0]):
            total = total + in_ref[p, q]
        for p in range(out_ref.shape[0]):
            out_ref[p, q * CASES : (q + 1) * CASES, :] = total


def inverse2(p, q, r, s):
    scale = 1.0 / (p * s - q * r)
    return s * scale, -q * scale, -r * scale, p * scale


def spd_solve(matrix, target):
    n = matrix.shape[0]
    a = jnp.concatenate([matrix, target], axis=1)
    row_of = iota(a.shape, 0)
    for k in range(0, n, 4):
        c = [jnp.broadcast_to(a[:, k + i : k + i + 1], a.shape) for i in range(4)]
        r = [a[k + i : k + i + 1] for i in range(4)]
        p = [[c[j][k + i : k + i + 1] for j in range(4)] for i in range(4)]
        a00, a01, a10, a11 = inverse2(p[0][0], p[0][1], p[1][0], p[1][1])
        e00, e01 = p[2][0] * a00 + p[2][1] * a10, p[2][0] * a01 + p[2][1] * a11
        e10, e11 = p[3][0] * a00 + p[3][1] * a10, p[3][0] * a01 + p[3][1] * a11
        i00, i01, i10, i11 = inverse2(
            p[2][2] - (e00 * p[0][2] + e01 * p[1][2]),
            p[2][3] - (e00 * p[0][3] + e01 * p[1][3]),
            p[3][2] - (e10 * p[0][2] + e11 * p[1][2]),
            p[3][3] - (e10 * p[0][3] + e11 * p[1][3]),
        )
        t2 = r[2] - (e00 * r[0] + e01 * r[1])
        t3 = r[3] - (e10 * r[0] + e11 * r[1])
        u2, u3 = i00 * t2 + i01 * t3, i10 * t2 + i11 * t3
        w0 = r[0] - (p[0][2] * u2 + p[0][3] * u3)
        w1 = r[1] - (p[1][2] * u2 + p[1][3] * u3)
        u = [a00 * w0 + a01 * w1, a10 * w0 + a11 * w1, u2, u3]
        a = a - ((c[0] * u[0] + c[1] * u[1]) + (c[2] * u[2] + c[3] * u[3]))
        for i in range(4):
            a = jnp.where(row_of == k + i, u[i], a)
    return a[:, n:]


def symmetric(m):
    return 0.5 * (m + jnp.transpose(m))


def solve_kernel(groups, case_ref, gram_ref, coef, coef_rows, turned_coef):
    n = groups * CASES
    total = gram_ref[0]
    for p in range(1, gram_ref.shape[0]):
        total = total + gram_ref[p]
    g00, g01, g11, g12 = [symmetric(total[:, g * n : (g + 1) * n]) for g in range(4)]
    steps = spd_solve(g01, jnp.concatenate([g00, g11], axis=1))
    step0, step1 = steps[:, :n], steps[:, n:]
    both = dot_high(g11, steps)
    second = spd_solve(symmetric(g12 - both[:, n:]), g01 - both[:, :n])
    first = step0 - dot_high(step1, second)
    first, second = jnp.transpose(first), jnp.transpose(second)
    turned_coef[0] = jnp.concatenate([first] * (LANES // n), axis=1)
    turned_coef[1] = jnp.concatenate([second] * (LANES // n), axis=1)
    shift = LANES - case_ref[0] * CASES
    for q in range(groups):
        at = pl.multiple_of(lax.rem(case_ref[0] + q, groups) * CASES, CASES)
        for h in range(2):
            mine = pltpu.roll(turned_coef[h, pl.ds(at, CASES), :], shift, 1)
            coef_rows[q * CASES : (q + 1) * CASES, h * LANES : (h + 1) * LANES] = mine
            if q == 0:
                for j in range(n):
                    coef[h * n + j] = jnp.broadcast_to(mine[:, j : j + 1], (CASES, LANES))


def bubble_kernel(groups, rows, coef_ref, *refs):
    turned, outs = refs[:groups], refs[groups:]
    n = groups * CASES
    part = outs[0].shape[0]
    firsts = [0] + [rows] * (groups - 1)
    left = stacked_table(jnp.concatenate([coef_ref[:, :n], coef_ref[:, LANES : LANES + n]], axis=1))
    for m in range(0, part // CASES, 2):
        values = [
            jnp.concatenate(
                [
                    ref[first + half * part + at : first + half * part + at + CASES, :]
                    for half in range(2)
                    for ref, first in zip(turned, firsts)
                ],
                axis=0,
            )
            for at in (m * CASES, (m + 1) * CASES)
        ]
        result = dot(left, stacked_values(jnp.concatenate(values, axis=1)))
        for i in range(2):
            for h in range(groups):
                outs[h][(m + i) * CASES : (m + i + 1) * CASES, :] = result[
                    h * CASES : (h + 1) * CASES, i * LANES : (i + 1) * LANES
                ]


def ports_kernel(groups, coef, *refs):
    base, image, second = [refs[g * groups : (g + 1) * groups] for g in range(3)]
    x_ref, residual_ref = refs[3 * groups :]
    n = groups * CASES
    dofs = x_ref.shape[0] // CASES
    wide = 4

    def ports(block, carry):
        d0 = block * wide
        own = [pl.ds(pl.multiple_of((d0 + i) * CASES, CASES), CASES) for i in range(wide)]
        x = [jnp.zeros((CASES, LANES), F32)] * wide
        r = [base[0][own[i], :] for i in range(wide)]
        for j in range(n):
            q, c = divmod(j, CASES)
            c0, c1 = coef[j], coef[n + j]
            for i in range(wide):
                row = pl.ds((d0 + i) * CASES + c, 1)
                a = image[q][row, :]
                x[i] = x[i] + (c0 * base[q][row, :] + c1 * a)
                r[i] = r[i] - (c0 * a + c1 * second[q][row, :])
        for i in range(wide):
            x_ref[own[i], :] = x[i]
            residual_ref[own[i], :] = r[i]
        return carry

    lax.fori_loop(0, dofs // wide, ports, 0)


def join_kernel(groups, case_ref, bubble_ref, *refs):
    parts, out_ref = refs[:groups], refs[groups]
    part = parts[0].shape[0]
    for h in range(groups):
        at = pl.ds(pl.multiple_of(lax.rem(case_ref[0] + h, groups) * part, part), part)
        out_ref[at, :] = bubble_ref[at, :] - parts[h][...]


def call(kernel, outs, scratch=(), name=None, flops=0, smem=(), hbm=(), anywhere=(), sems=0, limit=12):
    results = [(pltpu.HBM if far else jax.ShapeDtypeStruct)(shape, dtype) for shape, dtype, far in outs]
    vmem = pl.BlockSpec(memory_space=pltpu.VMEM)
    far_spec = pl.BlockSpec(memory_space=pltpu.HBM)

    def run(*args):
        specs = [
            pl.BlockSpec(memory_space=pltpu.SMEM) if i in smem else far_spec if i in hbm else pl.BlockSpec(memory_space=pl.ANY) if i in anywhere else vmem
            for i in range(len(args))
        ]
        moved = sum(a.size * a.dtype.itemsize for a in args)
        args = [pltpu.with_memory_space_constraint(a, pltpu.HBM) if i in hbm else a for i, a in enumerate(args)]
        return pl.pallas_call(
            kernel,
            out_shape=results,
            in_specs=specs,
            out_specs=[vmem] * len(outs),
            scratch_shapes=[pltpu.VMEM(*shape) if isinstance(shape[0], tuple) else pltpu.VMEM(shape, F32) for shape in scratch]
            + ([pltpu.SemaphoreType.DMA((sems,) if sems > 1 else ())] if sems else []),
            compiler_params=pltpu.CompilerParams(vmem_limit_bytes=limit << 20),
            cost_estimate=pl.CostEstimate(flops=flops, bytes_accessed=moved, transcendentals=0),
            name=name,
        )(*args)

    return run


def exchange(rows, parts):
    moved = lax.all_to_all(rows.reshape(parts, 1, -1), PLANE, split_axis=0, concat_axis=0)
    return moved.reshape(rows.shape)


def local(
    comp_type, stiffness, near_port, far_owner, far_port, bubble_load, port_load,
    bubble_inverse, coupling, port_block,
):
    parts = lax.axis_size("px") * lax.axis_size("py")
    groups = lax.axis_size("case")
    modes, cases, comps = bubble_load.shape
    dofs, _, ports = port_load.shape
    rows, bubbles = dofs * cases, modes * cases
    slot_tiles = -(-SLOTS * parts // LANES)
    coupling = jnp.swapaxes(coupling, 1, 2)
    kind = comp_type.reshape(1, comps)
    stiff = stiffness.reshape(1, comps)
    near = near_port.reshape(1, comps)
    owner = far_owner.reshape(1, comps)
    far = far_port.reshape(1, comps)
    loads = bubble_load.reshape(bubbles, comps)
    field_of = ((rows, ports), F32, True)
    meta_of = ((parts, LANES), F32, False)
    bubble_of = ((bubbles, comps), F32, True)
    given = (kind, stiff, near, owner, far, loads, bubble_inverse, coupling)
    pay, near_sum, meta, where = call(
        functools.partial(condense_kernel, parts),
        [((parts * 10, LANES), F32, False), field_of, meta_of, ((8, LANES), F32, False)],
        [(a.shape, a.dtype) for a in given] + [(rows, comps)] * 2,
        "condense",
        hbm=range(len(given)),
        sems=len(given),
    )(*given)
    near_near, near_far, far_near, far_far, turned_near, turned_far, bubble_base = call(
        tables_kernel,
        [((KINDS * dofs, 3 * dofs), BF16, False)] * 4 + [((KINDS * modes, 3 * dofs), BF16, True)] * 2 + [bubble_of],
        name="tables",
        flops=10**9,
    )(where, loads, bubble_inverse, coupling, port_block)
    base, pay, asked = call(
        functools.partial(rhs_kernel, parts),
        [field_of, ((parts * 18, LANES), F32, False), meta_of],
        name="rhs",
    )(exchange(pay, parts), near_sum, port_load.reshape(rows, ports), meta)

    case = lax.axis_index("case").reshape(1)
    part = bubbles // groups
    part_of = ((part, comps), F32, True)
    slot_scratch = [(slot_tiles, rows, LANES)] * 2

    def to_cases(messages):
        backward = [
            lax.ppermute(message, "case", [(k, (k + h) % groups) for k in range(groups)])
            for h, message in enumerate(messages, 1)
        ]
        return backward[::-1]

    def inner(field):
        return call(inner_kernel, [((rows, ports), F32, False)] * 2, [(rows, comps)] + slot_scratch, "inner", flops=10**9)(
            field, asked, where, near_near, far_far
        )

    arrived = exchange(pay, parts)
    base_all = to_cases([base] * (groups - 1))
    base_inner, base_near = inner(base)
    gram_of = [((cases, LANES), F32, False)]
    (gram,) = call(functools.partial(base_gram_kernel, groups), gram_of, name="base_gram", smem=(0,))(
        case, base, *base_all
    )
    arrived, gram = lax.optimization_barrier((arrived, gram))
    image, base_far, pay = call(
        functools.partial(image_kernel, parts, groups, False),
        [((rows, ports), F32, False), field_of, ((parts * 18, LANES), F32, False)],
        [(rows, comps)] + slot_scratch,
        "image",
    )(arrived, base_inner, asked, where, near_far, far_near, meta)
    arrived = exchange(pay, parts)
    image_all = to_cases([image] * (groups - 1))
    (turned0,) = call(turned_rows, [bubble_of], name="turned", flops=10**9)(
        base_near, base_far, where, turned_near, turned_far
    )
    image_inner, image_near = inner(image)
    (turned1,) = call(turned_near_rows, [bubble_of], name="turned_near", flops=10**9)(image_near, where, turned_near)
    (gram,) = call(functools.partial(gram_kernel, groups), gram_of, name="gram", smem=(0,))(
        case, gram, base, *base_all, image
    )
    arrived, turned0, turned1 = lax.optimization_barrier((arrived, turned0, turned1))
    minor = lax.axis_size("py")
    second, copies, turned_own, *messages = call(
        functools.partial(image_kernel, parts, groups, True),
        [field_of, ((groups * minor, cases, LANES), F32, True), ((2 * part, comps), F32, True)]
        + [((rows + 2 * part, comps), F32, True)] * (groups - 1),
        [(rows, comps)] + slot_scratch + [(rows, comps)] + [(bubbles, comps)] * 3,
        "second",
        smem=(6,),
        hbm=(9, 10),
        sems=2,
    )(
        arrived, image_inner, asked, where, near_far, far_near, case, gram, turned_far, turned0, turned1,
        image, *image_all,
    )
    copies = lax.all_to_all(copies, ("py", "case"), split_axis=0, concat_axis=0)
    messages = pl.pallas_call(
        pass_kernel,
        out_shape=[pltpu.HBM(m.shape, m.dtype) for m in messages],
        in_specs=[pl.BlockSpec(memory_space=pltpu.HBM)] * len(messages),
        out_specs=[pl.BlockSpec(memory_space=pltpu.HBM)] * len(messages),
        input_output_aliases={i: i for i in range(len(messages))},
        cost_estimate=pl.CostEstimate(flops=10**9, bytes_accessed=1 << 20, transcendentals=0),
        name="pass_on",
    )(*messages)
    both1 = to_cases(messages)
    (copies,) = call(sum_kernel, [((parts // minor, groups * cases, LANES), F32, False)], name="sum")(
        copies.reshape(minor, groups, cases, LANES)
    )
    copies = lax.all_to_all(copies, "px", split_axis=0, concat_axis=0)
    coef, coef_rows = call(
        functools.partial(solve_kernel, groups),
        [((2 * groups * cases, cases, LANES), F32, False), ((groups * cases, 2 * LANES), F32, False)],
        [(2, groups * cases, LANES)],
        "solve",
        smem=(0,),
    )(case, copies)
    own, *messages = call(
        functools.partial(bubble_kernel, groups, rows), [((part, comps), F32, False)] * groups, name="bubble"
    )(coef_rows, turned_own, *both1)
    back = to_cases(messages)
    x, residual = call(
        functools.partial(ports_kernel, groups), [field_of, field_of], name="ports", flops=10**9
    )(coef, base, *base_all, image, *image_all, second, *both1)
    (bubble,) = call(functools.partial(join_kernel, groups), [bubble_of], name="join", smem=(0,))(
        case, bubble_base, own, *back
    )
    return (
        x.reshape(port_load.shape),
        residual.reshape(port_load.shape),
        bubble.reshape(bubble_load.shape),
    )


def solution(mesh):
    placed = (
        P(PLANE),
        P(PLANE),
        P(PLANE),
        P(PLANE, None),
        P(PLANE),
        P(None, "case", PLANE),
        P(None, "case", PLANE),
        P(),
        P(),
        P(),
    )
    out = P(None, "case", PLANE)
    return jax.shard_map(
        local, mesh=mesh, in_specs=placed, out_specs=(out, out, out), check_vma=False
    )
```

```python
import functools

import jax
import jax.numpy as jnp
from jax import lax
from jax.experimental import pallas as pl
from jax.experimental.pallas import tpu as pltpu
from jax.sharding import PartitionSpec as P

HIGH = lax.Precision.HIGHEST
PLANE = ("px", "py")
F32 = jnp.float32
BF16 = jnp.bfloat16
KINDS = 8
LANES = 128
CASES = 8
SLOTS = 3
NN = (((1,), (0,)), ((), ()))
NT = (((1,), (1,)), ((), ()))
TN = (((0,), (0,)), ((), ()))


def dot(lhs, rhs, dims=NN):
    return lax.dot_general(lhs, rhs, dims, preferred_element_type=F32)


def dot_high(lhs, rhs, dims=NN):
    return lax.dot_general(lhs, rhs, dims, precision=HIGH, preferred_element_type=F32)


def split2(x):
    high = x.astype(BF16)
    return high, (x - high.astype(F32)).astype(BF16)


def pick_right(x, onehot, dims):
    (left,), (right,) = dims[0]
    return dot(jnp.concatenate(split2(x), axis=left), jnp.concatenate([onehot, onehot], axis=right), dims)


def pick_left(onehot, x, dims):
    (left,), (right,) = dims[0]
    return dot(jnp.concatenate([onehot, onehot], axis=left), jnp.concatenate(split2(x), axis=right), dims)


def stacked_table(table):
    high, low = split2(table)
    return jnp.concatenate([high, high, low], axis=1)


def stacked_values(x):
    high, low = split2(x)
    return jnp.concatenate([high, low, high], axis=0)


def iota(shape, dim):
    return lax.broadcasted_iota(jnp.int32, shape, dim)


def column(row):
    return jnp.transpose(jnp.broadcast_to(row, (8, row.shape[1])))[:, :1]


def onehot(mask):
    return mask.astype(F32).astype(BF16)


KIND, STIFF, NEAR, OWNER = [slice(i, i + 1) for i in range(4)]


def owner_slots(owner, parts):
    count = owner.shape[1]
    owner_f = owner.astype(F32)
    same = (column(owner_f) == owner_f) & (iota((count, count), 0) < iota((count, count), 1))
    rank = jnp.sum(same.astype(F32), axis=0, keepdims=True).astype(jnp.int32)
    to = iota((parts, count), 0).astype(F32) == owner_f
    return [to & (rank == s) for s in range(SLOTS)]


def near_onehot(near):
    count = near.shape[1]
    return onehot(column(near.astype(F32)) == iota((count, LANES), 1).astype(F32))


def stacked_rows(meta, lanes):
    turned = jnp.transpose(meta)
    return jnp.concatenate([turned[lanes + s : lanes + s + 1, :] for s in range(SLOTS)], axis=1)


def port_onehot(meta):
    parts = meta.shape[0]
    ports = (iota((parts, LANES), 1) + 1).astype(F32)
    return onehot(jnp.concatenate([meta[:, s : s + 1] == ports for s in range(SLOTS)], axis=0))


def pad_lanes(x, spare):
    if not spare:
        return x
    return jnp.concatenate([x, jnp.zeros((x.shape[0], spare), x.dtype)], axis=1)


def put(pay_ref, rows, first, pitch):
    parts = pay_ref.shape[0] // pitch
    tiles = rows.shape[1] // LANES
    for g in range(rows.shape[0] // parts):
        for t in range(tiles):
            pay_ref[pl.ds(first + g * tiles + t, parts, stride=pitch), :] = rows[
                g * parts : (g + 1) * parts, t * LANES : (t + 1) * LANES
            ]


def get(pay_ref, first, pitch, tiles):
    parts = pay_ref.shape[0] // pitch
    return jnp.concatenate(
        [
            jnp.concatenate(
                [pay_ref[pl.ds(first + s * tiles + t, parts, stride=pitch), :] for t in range(tiles)],
                axis=1,
            )
            for s in range(SLOTS)
        ],
        axis=0,
    )


def by_kind(products, kind, rows):
    chosen = products[:rows]
    for t in range(1, KINDS):
        chosen = jnp.where(kind == t, products[t * rows : (t + 1) * rows], chosen)
    return chosen


def condense_kernel(
    parts, kind_hbm, stiff_hbm, near_hbm, owner_hbm, far_hbm, load_hbm, inverse_hbm, coupling_hbm,
    pay_ref, near_sum_ref, meta_ref, where_ref,
    kind_ref, stiff_ref, near_ref, owner_ref, far_ref, load_ref, inverse_ref, coupling_ref, near_part, far_part, sems,
):
    copies = [
        pltpu.make_async_copy(source, target, sems.at[i])
        for i, (source, target) in enumerate((
            (inverse_hbm, inverse_ref), (coupling_hbm, coupling_ref), (load_hbm, load_ref), (kind_hbm, kind_ref),
            (stiff_hbm, stiff_ref), (near_hbm, near_ref), (owner_hbm, owner_ref), (far_hbm, far_ref),
        ))
    ]
    for copy in copies:
        copy.start()
    for copy in copies[:2]:
        copy.wait()
    modes = load_ref.shape[0] // CASES
    dofs = near_sum_ref.shape[0] // CASES
    left = stacked_table(
        jnp.concatenate(
            [jnp.transpose(dot_high(inverse_ref[t], coupling_ref[t], TN)) for t in range(KINDS)], axis=0
        )
    )
    for copy in copies[2:]:
        copy.wait()
    kind = kind_ref[...]
    kind2 = jnp.concatenate([kind, kind], axis=1)
    for k in range(0, CASES, 2):
        loads = jnp.concatenate(
            [load_ref[pl.ds(k + i, modes, stride=CASES), :] for i in range(2)], axis=1
        )
        condensed = -by_kind(dot(left, stacked_values(loads)), kind2, 2 * dofs)
        for i in range(2):
            lanes = slice(i * LANES, (i + 1) * LANES)
            near_part[pl.ds(k + i, dofs, stride=CASES), :] = condensed[:dofs, lanes]
            far_part[pl.ds(k + i, dofs, stride=CASES), :] = condensed[dofs:, lanes]
    near = near_ref[...]
    slots = owner_slots(owner_ref[...], parts)
    near_sum_ref[...] = pick_right(near_part[...], near_onehot(near), NN)
    chosen = onehot(jnp.concatenate(slots, axis=0))
    put(pay_ref, pick_left(chosen, far_part[...], NT), 0, 10)
    lane = iota((parts, LANES), 1)
    far_row = (far_ref[...] + 1).astype(F32)
    near_row = (near + 1).astype(F32)
    message = jnp.zeros((parts, LANES), F32)
    own = jnp.zeros((parts, LANES), F32)
    for s in range(SLOTS):
        for at, row in ((0, far_row), (SLOTS, kind.astype(F32)), (2 * SLOTS, stiff_ref[...])):
            value = jnp.sum(jnp.where(slots[s], row, 0.0), axis=1, keepdims=True)
            message = jnp.where(lane == at + s, value, message)
        value = jnp.sum(jnp.where(slots[s], near_row, 0.0), axis=1, keepdims=True)
        own = jnp.where(lane == s, value, own)
    pay_ref[pl.ds(9, parts, stride=10), :] = message
    packed = [kind.astype(F32), stiff_ref[...], near.astype(F32), owner_ref[...].astype(F32)]
    where_ref[...] = jnp.concatenate(packed + packed, axis=0)
    meta_ref[...] = own


def tables_kernel(
    where_ref, load_ref, inverse_ref, coupling_ref, block_ref,
    near_near, near_far, far_near, far_far, turned_near, turned_far, base_ref,
):
    dofs = block_ref.shape[1] // 2
    modes = inverse_ref.shape[1]
    inverses = []
    for t in range(KINDS):
        turned = dot_high(inverse_ref[t], coupling_ref[t], TN)
        schur = block_ref[t] - dot_high(turned, coupling_ref[t], TN)
        at = slice(t * dofs, (t + 1) * dofs)
        near_near[at, :] = stacked_table(schur[:dofs, :dofs])
        near_far[at, :] = stacked_table(schur[:dofs, dofs:])
        far_near[at, :] = stacked_table(schur[dofs:, :dofs])
        far_far[at, :] = stacked_table(schur[dofs:, dofs:])
        at = slice(t * modes, (t + 1) * modes)
        turned_near[at, :] = stacked_table(turned[:, :dofs])
        turned_far[at, :] = stacked_table(turned[:, dofs:])
        inverses.append(inverse_ref[t])
    left = stacked_table(jnp.concatenate(inverses, axis=0))
    kind = where_ref[KIND]
    stiff = where_ref[STIFF]
    kind2 = jnp.concatenate([kind, kind], axis=1)
    stiff2 = jnp.concatenate([stiff, stiff], axis=1)
    for k in range(0, CASES, 2):
        loads = jnp.concatenate(
            [load_ref[pl.ds(k + i, modes, stride=CASES), :] for i in range(2)], axis=1
        )
        result = by_kind(dot(left, stacked_values(loads)), kind2, modes) / stiff2
        for i in range(2):
            base_ref[pl.ds(k + i, modes, stride=CASES), :] = result[:, i * LANES : (i + 1) * LANES]


def send_ports(field, asked, own, pay_ref):
    put(pay_ref, pick_left(jnp.concatenate([asked, own], axis=0), field, NT), 0, 18)


def rhs_kernel(parts, arrived_ref, near_sum_ref, load_ref, meta_ref, field_ref, pay_ref, asked_ref):
    asked = arrived_ref[pl.ds(9, parts, stride=10), :]
    asked_ref[...] = asked
    asked_hot = port_onehot(asked)
    arrived = get(arrived_ref, 0, 10, 3)
    field = load_ref[...] + (near_sum_ref[...] + pick_right(arrived, asked_hot, TN))
    field_ref[...] = field
    send_ports(field, asked_hot, port_onehot(meta_ref[...]), pay_ref)


def component_products(table_ref, part_ref, where_ref, out_ref):
    dofs = part_ref.shape[0] // CASES
    kind, stiff = where_ref[KIND], where_ref[STIFF]
    kind2 = jnp.concatenate([kind, kind], axis=1)
    stiff2 = jnp.concatenate([stiff, stiff], axis=1)
    for k in range(0, CASES, 2):
        values = jnp.concatenate(
            [part_ref[pl.ds(k + i, dofs, stride=CASES), :] for i in range(2)], axis=1
        )
        result = by_kind(dot(table_ref[...], stacked_values(values)), kind2, dofs) * stiff2
        for i in range(2):
            out_ref[pl.ds(k + i, dofs, stride=CASES), :] = result[:, i * LANES : (i + 1) * LANES]


def slot_products(table_ref, slot_ref, asked, out_ref):
    tiles = slot_ref.shape[0]
    dofs = slot_ref.shape[1] // CASES
    spare = tiles * LANES - SLOTS * asked.shape[0]
    kind = pad_lanes(stacked_rows(asked, SLOTS), spare)
    stiff = pad_lanes(stacked_rows(asked, 2 * SLOTS), spare)
    for k in range(CASES):
        values = jnp.concatenate(
            [slot_ref[g, pl.ds(k, dofs, stride=CASES), :] for g in range(tiles)], axis=1
        )
        result = by_kind(dot(table_ref[...], stacked_values(values)), kind, dofs) * stiff
        for g in range(tiles):
            out_ref[g, pl.ds(k, dofs, stride=CASES), :] = result[:, g * LANES : (g + 1) * LANES]


def wide_onehot(asked_hot, tiles):
    spare = tiles * LANES - asked_hot.shape[0]
    if not spare:
        return asked_hot
    return jnp.concatenate([asked_hot, jnp.zeros((spare, LANES), BF16)], axis=0)


def slots_to_ports(part_ref, asked_hot):
    tiles = part_ref.shape[0]
    hot = wide_onehot(asked_hot, tiles)
    total = pick_right(part_ref[0], hot[:LANES], NN)
    for g in range(1, tiles):
        total = total + pick_right(part_ref[g], hot[g * LANES : (g + 1) * LANES], NN)
    return total


def inner_kernel(
    field_ref, asked_ref, where_ref, near_near, far_far,
    inner_ref, near_values, near_part, slot_ref, slot_part,
):
    field, asked = field_ref[...], asked_ref[...]
    near_hot, asked_hot = near_onehot(where_ref[NEAR]), port_onehot(asked)
    tiles = slot_ref.shape[0]
    near_values[...] = pick_right(field, near_hot, NT)
    values = pick_right(field, wide_onehot(asked_hot, tiles), NT)
    for g in range(tiles):
        slot_ref[g] = values[:, g * LANES : (g + 1) * LANES]
    component_products(near_near, near_values, where_ref, near_part)
    slot_products(far_far, slot_ref, asked, slot_part)
    inner_ref[...] = pick_right(near_part[...], near_hot, NN) + slots_to_ports(slot_part, asked_hot)


def near_cross(parts, arrived_ref, pitch, kind_ref, stiff_ref, near_ref, owner_ref, near_far, far_values, near_part):
    slots = onehot(jnp.concatenate(owner_slots(where_ref[OWNER], parts), axis=0))
    far_values[...] = pick_right(get(arrived_ref, 0, pitch, 3), slots, TN)
    component_products(near_far, far_values, where_ref, near_part)
    return pick_right(near_part[...], near_onehot(near_ref[...]), NN)


def far_cross(arrived_ref, first, pitch, asked, asked_hot, far_near, slot_ref, slot_part):
    tiles = slot_ref.shape[0]
    values = jnp.transpose(get(arrived_ref, first, pitch, 3))
    values = pad_lanes(values, tiles * LANES - values.shape[1])
    for g in range(tiles):
        slot_ref[g] = values[:, g * LANES : (g + 1) * LANES]
    slot_products(far_near, slot_ref, asked, slot_part)
    return slots_to_ports(slot_part, asked_hot)


def image_kernel(
    parts, groups, last, arrived_ref, inner_ref, asked_ref, where_ref,
    near_far, far_near, *rest,
):
    if last:
        case_ref, gram_ref, turned_far, turned0_hbm, turned1_hbm = rest[:5]
        images, rest = rest[5 : 5 + groups], rest[5 + groups :]
        image_ref, copies_ref, own_ref = rest[:3]
        messages = rest[3 : 2 + groups]
        near_part, slot_ref, slot_part, far_values, turned_ref, turned0_ref, turned1_ref, sems = rest[2 + groups :]
        fetches = [
            pltpu.make_async_copy(turned1_hbm, turned1_ref, sems.at[0]),
            pltpu.make_async_copy(turned0_hbm, turned0_ref, sems.at[1]),
        ]
        for fetch in fetches:
            fetch.start()
    else:
        meta_ref, image_ref, far_values, pay_ref, near_part, slot_ref, slot_part = rest
    asked = asked_ref[...]
    asked_hot = port_onehot(asked)
    slots = onehot(jnp.concatenate(owner_slots(where_ref[OWNER], parts), axis=0))
    far_values[...] = pick_right(get(arrived_ref, 0, 18, 3), slots, TN)
    component_products(near_far, far_values, where_ref, near_part)
    tiles = slot_ref.shape[0]
    values = jnp.transpose(get(arrived_ref, 9, 18, 3))
    values = pad_lanes(values, tiles * LANES - values.shape[1])
    for g in range(tiles):
        slot_ref[g] = values[:, g * LANES : (g + 1) * LANES]
    slot_products(far_near, slot_ref, asked, slot_part)
    image = inner_ref[...] + pick_right(near_part[...], near_onehot(where_ref[NEAR]), NN)
    image = image + slots_to_ports(slot_part, asked_hot)
    image_ref[...] = image
    if last:
        total = groups * CASES
        gram = add_products(
            LANES, images, [image_ref], [3 * total], case_ref[0], gram_ref[...]
        )
        for p in range(copies_ref.shape[0]):
            copies_ref[p] = gram
        for fetch in fetches:
            fetch.wait()
        turned_sums([(turned_far, far_values)], where_ref, turned_ref, turned1_ref)
        rows, part = image.shape[0], own_ref.shape[0] // 2
        for h in range(groups):
            at = pl.ds(pl.multiple_of(lax.rem(case_ref[0] + h, groups) * part, part), part)
            target, first = (messages[h - 1], rows) if h else (own_ref, 0)
            if h:
                target[:rows, :] = image
            target[first : first + part, :] = turned0_ref[at, :]
            target[first + part :, :] = turned_ref[at, :]
    else:
        send_ports(image, asked_hot, port_onehot(meta_ref[...]), pay_ref)


def turned_sums(pairs, where_ref, out_ref, first=None):
    dofs = pairs[0][1].shape[0] // CASES
    modes = out_ref.shape[0] // CASES
    kind = where_ref[KIND]
    kind2 = jnp.concatenate([kind, kind], axis=1)
    for k in range(0, CASES, 2):
        sums = 0.0
        for table, part in pairs:
            values = jnp.concatenate(
                [part[pl.ds(k + i, dofs, stride=CASES), :] for i in range(2)], axis=1
            )
            sums = sums + dot(table[...], stacked_values(values))
        result = by_kind(sums, kind2, modes)
        for i in range(2):
            rows = pl.ds(k + i, modes, stride=CASES)
            mine = result[:, i * LANES : (i + 1) * LANES]
            out_ref[rows, :] = mine if first is None else first[rows, :] + mine


def turned_rows(near_values, far_values, where_ref, turned_near, turned_far, out_ref):
    turned_sums([(turned_near, near_values), (turned_far, far_values)], where_ref, out_ref)


def turned_near_rows(near_values, where_ref, turned_near, out_ref):
    turned_sums([(turned_near, near_values)], where_ref, out_ref)


def pass_kernel(*refs):
    pass


def add_products(lanes, lefts, rights, first, case, out):
    groups = len(lefts)
    total = groups * CASES
    dofs = lefts[0].shape[0] // CASES
    lane = iota((CASES, LANES), 1)
    for h in range(groups):
        def step(d, sums):
            own = pl.ds(pl.multiple_of(d * CASES, CASES), CASES)
            values = [ref[own, :] for ref in rights]
            new = []
            for i in range(CASES):
                row = lefts[h][pl.ds(d * CASES + i, 1), :]
                new.append(tuple(s + row * v for s, v in zip(sums[i], values)))
            return tuple(new)

        zero = jnp.zeros((CASES, LANES), F32)
        sums = lax.fori_loop(0, dofs, step, ((zero,) * len(rights),) * CASES)
        at = lax.rem(case + h, groups) * CASES
        for i in range(CASES):
            for g in range(len(rights)):
                value = jnp.sum(sums[i][g], axis=1, keepdims=True)
                out = jnp.where(lane == first[g] + at + i, value, out)
    return out


def base_gram_kernel(groups, case_ref, *refs):
    base, out_ref = refs[:groups], refs[groups]
    out_ref[...] = add_products(LANES, base, [base[0]], [0], case_ref[0], jnp.zeros((CASES, LANES), F32))


def gram_kernel(groups, case_ref, gram_ref, *refs):
    base, image_ref, out_ref = refs[:groups], refs[groups], refs[groups + 1]
    out_ref[...] = add_products(LANES, base, [image_ref], [groups * CASES], case_ref[0], gram_ref[...])


def image_gram_kernel(groups, case_ref, gram_ref, *refs):
    image, out_ref = refs[:groups], refs[groups]
    out_ref[...] = add_products(LANES, image, [image[0]], [2 * groups * CASES], case_ref[0], gram_ref[...])


def sum_kernel(in_ref, out_ref):
    for q in range(in_ref.shape[1]):
        total = in_ref[0, q]
        for p in range(1, in_ref.shape[0]):
            total = total + in_ref[p, q]
        for p in range(out_ref.shape[0]):
            out_ref[p, q * CASES : (q + 1) * CASES, :] = total


def inverse2(p, q, r, s):
    scale = 1.0 / (p * s - q * r)
    return s * scale, -q * scale, -r * scale, p * scale


def spd_solve(matrix, target):
    n = matrix.shape[0]
    a = jnp.concatenate([matrix, target], axis=1)
    row_of = iota(a.shape, 0)
    for k in range(0, n, 4):
        c = [jnp.broadcast_to(a[:, k + i : k + i + 1], a.shape) for i in range(4)]
        r = [a[k + i : k + i + 1] for i in range(4)]
        p = [[c[j][k + i : k + i + 1] for j in range(4)] for i in range(4)]
        a00, a01, a10, a11 = inverse2(p[0][0], p[0][1], p[1][0], p[1][1])
        e00, e01 = p[2][0] * a00 + p[2][1] * a10, p[2][0] * a01 + p[2][1] * a11
        e10, e11 = p[3][0] * a00 + p[3][1] * a10, p[3][0] * a01 + p[3][1] * a11
        i00, i01, i10, i11 = inverse2(
            p[2][2] - (e00 * p[0][2] + e01 * p[1][2]),
            p[2][3] - (e00 * p[0][3] + e01 * p[1][3]),
            p[3][2] - (e10 * p[0][2] + e11 * p[1][2]),
            p[3][3] - (e10 * p[0][3] + e11 * p[1][3]),
        )
        t2 = r[2] - (e00 * r[0] + e01 * r[1])
        t3 = r[3] - (e10 * r[0] + e11 * r[1])
        u2, u3 = i00 * t2 + i01 * t3, i10 * t2 + i11 * t3
        w0 = r[0] - (p[0][2] * u2 + p[0][3] * u3)
        w1 = r[1] - (p[1][2] * u2 + p[1][3] * u3)
        u = [a00 * w0 + a01 * w1, a10 * w0 + a11 * w1, u2, u3]
        a = a - ((c[0] * u[0] + c[1] * u[1]) + (c[2] * u[2] + c[3] * u[3]))
        for i in range(4):
            a = jnp.where(row_of == k + i, u[i], a)
    return a[:, n:]


def symmetric(m):
    return 0.5 * (m + jnp.transpose(m))


def solve_kernel(groups, case_ref, gram_ref, coef, coef_rows, turned_coef):
    n = groups * CASES
    total = gram_ref[0]
    for p in range(1, gram_ref.shape[0]):
        total = total + gram_ref[p]
    g00, g01, g11, g12 = [symmetric(total[:, g * n : (g + 1) * n]) for g in range(4)]
    steps = spd_solve(g01, jnp.concatenate([g00, g11], axis=1))
    step0, step1 = steps[:, :n], steps[:, n:]
    both = dot_high(g11, steps)
    second = spd_solve(symmetric(g12 - both[:, n:]), g01 - both[:, :n])
    first = step0 - dot_high(step1, second)
    first, second = jnp.transpose(first), jnp.transpose(second)
    turned_coef[0] = jnp.concatenate([first] * (LANES // n), axis=1)
    turned_coef[1] = jnp.concatenate([second] * (LANES // n), axis=1)
    shift = LANES - case_ref[0] * CASES
    for q in range(groups):
        at = pl.multiple_of(lax.rem(case_ref[0] + q, groups) * CASES, CASES)
        for h in range(2):
            mine = pltpu.roll(turned_coef[h, pl.ds(at, CASES), :], shift, 1)
            coef_rows[q * CASES : (q + 1) * CASES, h * LANES : (h + 1) * LANES] = mine
            if q == 0:
                for j in range(n):
                    coef[h * n + j] = jnp.broadcast_to(mine[:, j : j + 1], (CASES, LANES))


def bubble_kernel(groups, rows, coef_ref, *refs):
    turned, outs = refs[:groups], refs[groups:]
    n = groups * CASES
    part = outs[0].shape[0]
    firsts = [0] + [rows] * (groups - 1)
    left = stacked_table(jnp.concatenate([coef_ref[:, :n], coef_ref[:, LANES : LANES + n]], axis=1))
    for m in range(0, part // CASES, 2):
        values = [
            jnp.concatenate(
                [
                    ref[first + half * part + at : first + half * part + at + CASES, :]
                    for half in range(2)
                    for ref, first in zip(turned, firsts)
                ],
                axis=0,
            )
            for at in (m * CASES, (m + 1) * CASES)
        ]
        result = dot(left, stacked_values(jnp.concatenate(values, axis=1)))
        for i in range(2):
            for h in range(groups):
                outs[h][(m + i) * CASES : (m + i + 1) * CASES, :] = result[
                    h * CASES : (h + 1) * CASES, i * LANES : (i + 1) * LANES
                ]


def ports_kernel(groups, coef, *refs):
    base, image, second = [refs[g * groups : (g + 1) * groups] for g in range(3)]
    x_ref, residual_ref = refs[3 * groups :]
    n = groups * CASES
    dofs = x_ref.shape[0] // CASES
    wide = 4

    def ports(block, carry):
        d0 = block * wide
        own = [pl.ds(pl.multiple_of((d0 + i) * CASES, CASES), CASES) for i in range(wide)]
        x = [jnp.zeros((CASES, LANES), F32)] * wide
        r = [base[0][own[i], :] for i in range(wide)]
        for j in range(n):
            q, c = divmod(j, CASES)
            c0, c1 = coef[j], coef[n + j]
            for i in range(wide):
                row = pl.ds((d0 + i) * CASES + c, 1)
                a = image[q][row, :]
                x[i] = x[i] + (c0 * base[q][row, :] + c1 * a)
                r[i] = r[i] - (c0 * a + c1 * second[q][row, :])
        for i in range(wide):
            x_ref[own[i], :] = x[i]
            residual_ref[own[i], :] = r[i]
        return carry

    lax.fori_loop(0, dofs // wide, ports, 0)


def join_kernel(groups, case_ref, bubble_ref, *refs):
    parts, out_ref = refs[:groups], refs[groups]
    part = parts[0].shape[0]
    for h in range(groups):
        at = pl.ds(pl.multiple_of(lax.rem(case_ref[0] + h, groups) * part, part), part)
        out_ref[at, :] = bubble_ref[at, :] - parts[h][...]


def call(kernel, outs, scratch=(), name=None, flops=0, smem=(), hbm=(), anywhere=(), sems=0, limit=12):
    results = [(pltpu.HBM if far else jax.ShapeDtypeStruct)(shape, dtype) for shape, dtype, far in outs]
    vmem = pl.BlockSpec(memory_space=pltpu.VMEM)
    far_spec = pl.BlockSpec(memory_space=pltpu.HBM)

    def run(*args):
        specs = [
            pl.BlockSpec(memory_space=pltpu.SMEM) if i in smem else far_spec if i in hbm else pl.BlockSpec(memory_space=pl.ANY) if i in anywhere else vmem
            for i in range(len(args))
        ]
        moved = sum(a.size * a.dtype.itemsize for a in args)
        args = [pltpu.with_memory_space_constraint(a, pltpu.HBM) if i in hbm else a for i, a in enumerate(args)]
        return pl.pallas_call(
            kernel,
            out_shape=results,
            in_specs=specs,
            out_specs=[vmem] * len(outs),
            scratch_shapes=[pltpu.VMEM(*shape) if isinstance(shape[0], tuple) else pltpu.VMEM(shape, F32) for shape in scratch]
            + ([pltpu.SemaphoreType.DMA((sems,) if sems > 1 else ())] if sems else []),
            compiler_params=pltpu.CompilerParams(vmem_limit_bytes=limit << 20),
            cost_estimate=pl.CostEstimate(flops=flops, bytes_accessed=moved, transcendentals=0),
            name=name,
        )(*args)

    return run


def exchange(rows, parts):
    moved = lax.all_to_all(rows.reshape(parts, 1, -1), PLANE, split_axis=0, concat_axis=0)
    return moved.reshape(rows.shape)


def local(
    comp_type, stiffness, near_port, far_owner, far_port, bubble_load, port_load,
    bubble_inverse, coupling, port_block,
):
    parts = lax.axis_size("px") * lax.axis_size("py")
    groups = lax.axis_size("case")
    modes, cases, comps = bubble_load.shape
    dofs, _, ports = port_load.shape
    rows, bubbles = dofs * cases, modes * cases
    slot_tiles = -(-SLOTS * parts // LANES)
    coupling = jnp.swapaxes(coupling, 1, 2)
    kind = comp_type.reshape(1, comps)
    stiff = stiffness.reshape(1, comps)
    near = near_port.reshape(1, comps)
    owner = far_owner.reshape(1, comps)
    far = far_port.reshape(1, comps)
    loads = bubble_load.reshape(bubbles, comps)
    field_of = ((rows, ports), F32, True)
    meta_of = ((parts, LANES), F32, False)
    bubble_of = ((bubbles, comps), F32, True)
    given = (kind, stiff, near, owner, far, loads, bubble_inverse, coupling)
    pay, near_sum, meta, where = call(
        functools.partial(condense_kernel, parts),
        [((parts * 10, LANES), F32, False), field_of, meta_of, ((8, LANES), F32, False)],
        [(a.shape, a.dtype) for a in given] + [(rows, comps)] * 2,
        "condense",
        hbm=range(len(given)),
        sems=len(given),
    )(*given)
    near_near, near_far, far_near, far_far, turned_near, turned_far, bubble_base = call(
        tables_kernel,
        [((KINDS * dofs, 3 * dofs), BF16, False)] * 4 + [((KINDS * modes, 3 * dofs), BF16, True)] * 2 + [bubble_of],
        name="tables",
        flops=10**9,
    )(where, loads, bubble_inverse, coupling, port_block)
    base, pay, asked = call(
        functools.partial(rhs_kernel, parts),
        [field_of, ((parts * 18, LANES), F32, False), meta_of],
        name="rhs",
    )(exchange(pay, parts), near_sum, port_load.reshape(rows, ports), meta)

    case = lax.axis_index("case").reshape(1)
    part = bubbles // groups
    part_of = ((part, comps), F32, True)
    slot_scratch = [(slot_tiles, rows, LANES)] * 2

    def to_cases(messages):
        backward = [
            lax.ppermute(message, "case", [(k, (k + h) % groups) for k in range(groups)])
            for h, message in enumerate(messages, 1)
        ]
        return backward[::-1]

    def inner(field):
        return call(inner_kernel, [((rows, ports), F32, False)] * 2, [(rows, comps)] + slot_scratch, "inner", flops=10**9)(
            field, asked, where, near_near, far_far
        )

    arrived = exchange(pay, parts)
    base_all = to_cases([base] * (groups - 1))
    base_inner, base_near = inner(base)
    gram_of = [((cases, LANES), F32, False)]
    (gram,) = call(functools.partial(base_gram_kernel, groups), gram_of, name="base_gram", smem=(0,))(
        case, base, *base_all
    )
    arrived, gram = lax.optimization_barrier((arrived, gram))
    image, base_far, pay = call(
        functools.partial(image_kernel, parts, groups, False),
        [((rows, ports), F32, False), field_of, ((parts * 18, LANES), F32, False)],
        [(rows, comps)] + slot_scratch,
        "image",
    )(arrived, base_inner, asked, where, near_far, far_near, meta)
    arrived = exchange(pay, parts)
    image_all = to_cases([image] * (groups - 1))
    (turned0,) = call(turned_rows, [bubble_of], name="turned", flops=10**9)(
        base_near, base_far, where, turned_near, turned_far
    )
    image_inner, image_near = inner(image)
    (turned1,) = call(turned_near_rows, [bubble_of], name="turned_near", flops=10**9)(image_near, where, turned_near)
    (gram,) = call(functools.partial(gram_kernel, groups), gram_of, name="gram", smem=(0,))(
        case, gram, base, *base_all, image
    )
    (gram,) = call(functools.partial(image_gram_kernel, groups), gram_of, name="image_gram", smem=(0,))(
        case, gram, image, *image_all
    )
    arrived, turned0, turned1, gram = lax.optimization_barrier((arrived, turned0, turned1, gram))
    minor = lax.axis_size("py")
    second, copies, turned_own, *messages = call(
        functools.partial(image_kernel, parts, groups, True),
        [field_of, ((groups * minor, cases, LANES), F32, True), ((2 * part, comps), F32, True)]
        + [((rows + 2 * part, comps), F32, True)] * (groups - 1),
        [(rows, comps)] + slot_scratch + [(rows, comps)] + [(bubbles, comps)] * 3,
        "second",
        smem=(6,),
        hbm=(9, 10),
        sems=2,
    )(
        arrived, image_inner, asked, where, near_far, far_near, case, gram, turned_far, turned0, turned1,
        image, *image_all,
    )
    copies = lax.all_to_all(copies, ("py", "case"), split_axis=0, concat_axis=0)
    messages = pl.pallas_call(
        pass_kernel,
        out_shape=[pltpu.HBM(m.shape, m.dtype) for m in messages],
        in_specs=[pl.BlockSpec(memory_space=pltpu.HBM)] * len(messages),
        out_specs=[pl.BlockSpec(memory_space=pltpu.HBM)] * len(messages),
        input_output_aliases={i: i for i in range(len(messages))},
        cost_estimate=pl.CostEstimate(flops=10**9, bytes_accessed=1 << 20, transcendentals=0),
        name="pass_on",
    )(*messages)
    both1 = to_cases(messages)
    (copies,) = call(sum_kernel, [((parts // minor, groups * cases, LANES), F32, False)], name="sum")(
        copies.reshape(minor, groups, cases, LANES)
    )
    copies = lax.all_to_all(copies, "px", split_axis=0, concat_axis=0)
    coef, coef_rows = call(
        functools.partial(solve_kernel, groups),
        [((2 * groups * cases, cases, LANES), F32, False), ((groups * cases, 2 * LANES), F32, False)],
        [(2, groups * cases, LANES)],
        "solve",
        smem=(0,),
    )(case, copies)
    own, *messages = call(
        functools.partial(bubble_kernel, groups, rows), [((part, comps), F32, False)] * groups, name="bubble"
    )(coef_rows, turned_own, *both1)
    back = to_cases(messages)
    x, residual = call(
        functools.partial(ports_kernel, groups), [field_of, field_of], name="ports", flops=10**9
    )(coef, base, *base_all, image, *image_all, second, *both1)
    (bubble,) = call(functools.partial(join_kernel, groups), [bubble_of], name="join", smem=(0,))(
        case, bubble_base, own, *back
    )
    return (
        x.reshape(port_load.shape),
        residual.reshape(port_load.shape),
        bubble.reshape(bubble_load.shape),
    )


def solution(mesh):
    placed = (
        P(PLANE),
        P(PLANE),
        P(PLANE),
        P(PLANE, None),
        P(PLANE),
        P(None, "case", PLANE),
        P(None, "case", PLANE),
        P(),
        P(),
        P(),
    )
    out = P(None, "case", PLANE)
    return jax.shard_map(
        local, mesh=mesh, in_specs=placed, out_specs=(out, out, out), check_vma=False
    )
```
